32 devices in a mesh: dp: 2 (over core), seq: 16 (over z, y, x).
Axes of the slice: x: 2, y: 2, z: 4, core: 2. Of those that a mesh axis runs over, the one named last changes fastest.
Arguments:
- inputs: bfloat16 [2, 2048, 2048], P('dp', 'seq'), may hold values from -6 to 6
- positions: int32 [2, 2048], P('dp', 'seq'), may hold values from 0 to 4095
- select: int32 [2, 2048], P('dp', 'seq'), may hold values 0 or 1
- cotangent: bfloat16 [2, 2048, 2048], P('dp', 'seq'), may hold values from -6 to 6
- gain_attn: bfloat16 [2048], P('seq'), may hold values from 0.25 to 1.75
- w_query: bfloat16 [2048, 2048], P('seq'), may hold values from -0.1875 to 0.1875
- w_key: bfloat16 [2048, 256], P('seq'), may hold values from -0.1875 to 0.1875
- w_value: bfloat16 [2048, 256], P('seq'), may hold values from -0.125 to 0.125
- w_out: bfloat16 [2048, 2048], P('seq'), may hold values from -0.5 to 0.5
- gain_mlp: bfloat16 [2048], P('seq'), may hold values from 0.25 to 1.75
- w_gate: bfloat16 [2048, 5632], P('seq'), may hold values from -0.125 to 0.125
- w_up: bfloat16 [2048, 5632], P('seq'), may hold values from -0.125 to 0.125
- w_down: bfloat16 [5632, 2048], P('seq'), may hold values from -0.078125 to 0.078125
Outputs:
- outputs: bfloat16 [2, 2048, 2048], P('dp', 'seq')
- grad_inputs: float32 [2, 2048, 2048], P('dp', 'seq')
- grad_gain_attn: float32 [2048], P('seq')
- grad_w_query: float32 [2048, 2048], P('seq')
- grad_w_key: float32 [2048, 256], P('seq')
- grad_w_value: float32 [2048, 256], P('seq')
- grad_w_out: float32 [2048, 2048], P('seq')
- grad_gain_mlp: float32 [2048], P('seq')
- grad_w_gate: float32 [2048, 5632], P('seq')
- grad_w_up: float32 [2048, 5632], P('seq')
- grad_w_down: float32 [5632, 2048], P('seq')
The draws below stay inside these ranges and needn't reach their ends.
All inputs are finite; a program needn't handle non-finite values. No bound on the sum of `select` on one device may be relied on, other than what follows from the above.
Results may differ from the reference program's by a relative error of at most 0.025.
Values may be sent and summed in bfloat16 or wider, within the bound.
No kernel may reach another device: no remote copies, remote signals or barrier semaphores. Data moves between devices by JAX's collectives and lax.ppermute only.
A program may use at most 384 MiB of HBM per device.

```python
import math
import jax
import jax.numpy as jnp
from jax import lax

HEADS = 32
KV_HEADS = 4
HEAD_DIM = 64
FF = 5632
D = 2048
KV_WIDTH = 256
LENGTH = 2048
SEQS_ALL = 2


def touch_ends(values, stream_key, smallest, top_value):
    longest = values.shape.index(max(values.shape))
    spots = []
    for shift in (0, 1):
        where = [jax.random.randint(jax.random.fold_in(stream_key, axis), (), 0, length) for axis, length in enumerate(values.shape)]
        where[longest] = (where[longest] + shift) % values.shape[longest]
        spots.append(tuple(where))
    return values.at[spots[0]].set(smallest).at[spots[1]].set(top_value)


def level_of(rng, shape, split, least, high):
    def one(position, shards_of):
        steps = jax.random.uniform(jax.random.fold_in(jax.random.fold_in(rng, 6), position), (shards_of,), jnp.float32, least / len(split), high / len(split))
        return jnp.repeat(jnp.exp(steps), shape[position] // shards_of).reshape((-1,) + (1,) * (len(shape) - position - 1))

    level = one(*split[0])
    for cut in split[1:]:
        level = level * one(*cut)
    return level


def bell_draw(rng, shape, deviation, reach, split=(), dtype=jnp.bfloat16):
    loudness = level_of(rng, shape, split, -0.22, 0.18) if split else 1.0
    array = jax.random.normal(rng, shape, jnp.float32) * deviation * loudness
    return jnp.minimum(jnp.maximum(array, -reach), reach).astype(dtype)


def setup_inputs(seed: int = 0) -> dict:
    key_list = jax.random.split(jax.random.key(seed), 14)
    return {
        "inputs": bell_draw(key_list[0], (SEQS_ALL, LENGTH, D), 1.0, 6.0, ((0, 2), (1, 16))),
        "positions": touch_ends(jax.random.randint(key_list[1], (SEQS_ALL, LENGTH), 0, 4096), jax.random.fold_in(key_list[1], 1), 0, 4095).astype(jnp.int32),
        "select": touch_ends((jax.random.randint(key_list[2], (SEQS_ALL, LENGTH), 0, 10) < 3).astype(jnp.int32), jax.random.fold_in(key_list[2], 1), 0, 1),
        "cotangent": bell_draw(key_list[3], (SEQS_ALL, LENGTH, D), 1.0, 6.0, ((0, 2), (1, 16))),
        "gain_attn": jnp.clip(1.0 + 0.15 * jax.random.normal(key_list[4], (D,), jnp.float32), 0.25, 1.75).astype(jnp.bfloat16),
        "w_query": bell_draw(key_list[5], (D, D), (D // 2) ** -0.5, 0.1875, ((0, 16),)),
        "w_key": bell_draw(key_list[6], (D, KV_WIDTH), (D // 2) ** -0.5, 0.1875, ((0, 16),)),
        "w_value": bell_draw(key_list[7], (D, KV_WIDTH), D ** -0.5, 0.125, ((0, 16),)),
        "w_out": bell_draw(key_list[8], (D, D), (D // 16) ** -0.5, 0.5, ((0, 16),)),
        "gain_mlp": jnp.clip(1.0 + 0.15 * jax.random.normal(key_list[9], (D,), jnp.float32), 0.25, 1.75).astype(jnp.bfloat16),
        "w_gate": bell_draw(key_list[10], (D, FF), D ** -0.5, 0.125, ((0, 16),)),
        "w_up": bell_draw(key_list[11], (D, FF), D ** -0.5, 0.125, ((0, 16),)),
        "w_down": bell_draw(key_list[12], (FF, D), FF ** -0.5, 0.078125, ((0, 16),)),
    }


epsilon = 1e-05
rope_base = 10000.0
masked_score = -1e+30

@jax.custom_vjp
def low(v):
    return lax.optimization_barrier(v.astype(jnp.bfloat16)).astype(jnp.float32)

@jax.custom_vjp
def low_back(v):
    return v

def low_keep(v):
    return (low(v), None)

def low_pass(kept, grad):
    return (grad,)

def back_keep(v):
    return (v, None)

def back_low(kept, grad):
    return (low(grad),)
low.defvjp(low_keep, low_pass)
low_back.defvjp(back_keep, back_low)

def highest(left, right_side):
    return jnp.einsum('...i,ij->...j', left, right_side, precision=lax.Precision.HIGHEST)

def normalize(values, gain):
    return values * lax.rsqrt(lax.optimization_barrier(jnp.mean(values * values, axis=-1, keepdims=True)) + epsilon) * gain

def rope_tables(positions):
    half_dim = HEAD_DIM // 2
    frequency = rope_base ** (-(jnp.arange(half_dim).astype(jnp.float32) * 2.0 / HEAD_DIM))
    angles = positions.astype(jnp.float32)[..., None] * frequency
    angles = jnp.concatenate([angles, angles], axis=-1)
    return (jnp.cos(angles), jnp.sin(angles))

def rotate(values, cosine, sine):
    half_dim = values.shape[-1] // 2
    turned = jnp.concatenate([-values[..., half_dim:], values[..., :half_dim]], axis=-1)
    return values * cosine + turned * sine

def attend_block(queries, keys, values, start):
    span = queries.shape[1]
    raw_scores = jnp.einsum('nqhd,nkhd->nhqk', queries, keys, precision=lax.Precision.HIGHEST)
    scores = low_back(raw_scores * HEAD_DIM ** (-0.5))
    query_rows = start + jnp.arange(span)
    key_rows = jnp.arange(keys.shape[1])
    allowed = key_rows[None, :] <= query_rows[:, None]
    scores = jnp.where(allowed, scores, masked_score)
    highest_score = lax.optimization_barrier(jnp.max(scores, axis=-1, keepdims=True))
    weights = jnp.exp(scores - highest_score)
    probs = weights / lax.optimization_barrier(jnp.sum(weights, axis=-1, keepdims=True))
    return jnp.einsum('nhqk,nkhd->nqhd', low(probs), values, precision=lax.Precision.HIGHEST)

def layer(x_in, positions, gain_one, query_weight, key_weight, value_weight, out_weight, gain_two, gate_weight, up_weight, down_weight):
    seq_count = x_in.shape[0]
    length = x_in.shape[1]
    low_one = low(normalize(x_in, gain_one))
    cosine, sine = rope_tables(positions)
    cosine = cosine[:, :, None]
    sine = sine[:, :, None]
    query = low_back(highest(low_one, query_weight)).reshape(seq_count, length, HEADS, HEAD_DIM)
    key = low_back(highest(low_one, key_weight)).reshape(seq_count, length, KV_HEADS, HEAD_DIM)
    value = low_back(highest(low_one, value_weight)).reshape(seq_count, length, KV_HEADS, HEAD_DIM)
    query_low = low_back(low(rotate(query, cosine, sine)))
    key_low = low(rotate(key, cosine, sine))
    value_low = low(value)
    repeat = HEADS // KV_HEADS
    key_all = low_back(jnp.repeat(key_low, repeat, axis=2))
    value_all = low_back(jnp.repeat(value_low, repeat, axis=2))
    span = min(512, length)
    block_count = length // span
    blocked = jax.checkpoint(attend_block)

    def one_block(index):
        start = index * span
        queries = lax.dynamic_slice_in_dim(query_low, start, span, 1)
        return blocked(queries, key_all, value_all, start)
    pieces = lax.map(one_block, jnp.arange(block_count).astype(jnp.int32))
    attended = jnp.moveaxis(pieces, 0, 1).reshape(seq_count, length, HEADS * HEAD_DIM)
    attended = low_back(low(attended))
    x_mid = x_in + low_back(highest(attended, out_weight))
    low_two = low(normalize(x_mid, gain_two))
    gate = low_back(highest(low_two, gate_weight))
    up_part = low_back(highest(low_two, up_weight))
    hidden = low(gate / (1.0 + jnp.exp(-gate)) * up_part)
    return x_mid + highest(hidden, down_weight)

def reference(inputs, positions, select, cotangent, gain_attn, w_query, w_key, w_value, w_out, gain_mlp, w_gate, w_up, w_down):
    params = (gain_attn.astype(jnp.float32), w_query.astype(jnp.float32), w_key.astype(jnp.float32), w_value.astype(jnp.float32), w_out.astype(jnp.float32), gain_mlp.astype(jnp.float32), w_gate.astype(jnp.float32), w_up.astype(jnp.float32), w_down.astype(jnp.float32))
    group = math.gcd(SEQS_ALL, max(1, 4096 // LENGTH))
    rounds = SEQS_ALL // group
    x_groups = inputs.astype(jnp.float32).reshape(rounds, group, LENGTH, D)
    pos_groups = positions.reshape(rounds, group, LENGTH)
    weighted = cotangent.astype(jnp.float32) * select.astype(jnp.float32)[..., None]
    cot_groups = weighted.reshape(rounds, group, LENGTH, D)

    def one_round(totals, item):
        x_group, pos_group, cot_group = item

        def run(x_value, gain_one, query_weight, key_weight, value_weight, out_weight, gain_two, gate_weight, up_weight, down_weight):
            return layer(x_value, pos_group, gain_one, query_weight, key_weight, value_weight, out_weight, gain_two, gate_weight, up_weight, down_weight)
        result, pull = jax.vjp(run, x_group, params[0], params[1], params[2], params[3], params[4], params[5], params[6], params[7], params[8])
        grads = pull(cot_group)
        new_totals = tuple((total + grad for total, grad in zip(totals, grads[1:])))
        return (new_totals, (result.astype(jnp.bfloat16), grads[0]))
    zeros = tuple((jnp.zeros(param.shape, jnp.float32) for param in params))
    totals, (results, grad_in) = lax.scan(one_round, zeros, (x_groups, pos_groups, cot_groups))
    return (results.reshape(SEQS_ALL, LENGTH, D), grad_in.reshape(SEQS_ALL, LENGTH, D), totals[0], totals[1], totals[2], totals[3], totals[4], totals[5], totals[6], totals[7], totals[8])
```

```python
import functools

import jax
import jax.numpy as jnp
from jax import lax
from jax.experimental import pallas as pl
from jax.experimental.pallas import tpu as pltpu
from jax.sharding import PartitionSpec as P

HEADS = 32
KV_HEADS = 4
HEAD_DIM = 64
GROUP = KV_HEADS
GROUP_HEADS = HEADS // GROUP
PAIR = 2 * HEAD_DIM

epsilon = 1e-05
rope_base = 10000.0
masked_score = -1e30

f32 = jnp.float32
bf16 = jnp.bfloat16


def dot(left, right, contract=((1,), (0,))):
    return lax.dot_general(left, right, (contract, ((), ())), preferred_element_type=f32)


def stack_heads(block, rows):
    lane = lax.broadcasted_iota(jnp.int32, (rows, PAIR), 1)
    parts = []
    for pair in range(GROUP_HEADS // 2):
        both = block[:, pair * PAIR : (pair + 1) * PAIR]
        parts.append(jnp.where(lane < HEAD_DIM, both, jnp.zeros_like(both)))
        parts.append(jnp.where(lane >= HEAD_DIM, both, jnp.zeros_like(both)))
    return jnp.concatenate(parts, axis=0)


def unstack_heads(stacked, rows):
    lane = lax.broadcasted_iota(jnp.int32, (rows, PAIR), 1)
    parts = []
    for pair in range(GROUP_HEADS // 2):
        low = stacked[2 * pair * rows : (2 * pair + 1) * rows]
        high = stacked[(2 * pair + 1) * rows : (2 * pair + 2) * rows]
        parts.append(jnp.where(lane < HEAD_DIM, low, high))
    return jnp.concatenate(parts, axis=1)


def as_row(column):
    wide = jnp.broadcast_to(column, (column.shape[0], 128))
    return jnp.transpose(wide)[:8]


def attend_kernel(seen_ref, q_ref, kk_ref, vv_ref, qpos_ref, kpos_ref, o_ref, lse_ref):
    rows = q_ref.shape[0]
    stacked = stack_heads(q_ref[...], rows)
    qpos = jnp.concatenate([qpos_ref[...]] * GROUP_HEADS, axis=0)

    def unit(index, carry, masked):
        top, total, acc = carry
        scores = dot(stacked, kk_ref[index], ((1,), (1,)))
        if masked:
            scores = jnp.where(kpos_ref[...] <= qpos, scores, masked_score)
        new_top = jnp.maximum(top, jnp.max(scores, axis=1, keepdims=True))
        weights = jnp.exp(scores - new_top)
        keep = jnp.exp(top - new_top)
        total = total * keep + jnp.sum(weights, axis=1, keepdims=True)
        acc = acc * keep + dot(weights.astype(bf16), vv_ref[index])
        return new_top, total, acc

    count = GROUP_HEADS * rows
    start = (
        jnp.full((count, 1), masked_score, f32),
        jnp.zeros((count, 1), f32),
        jnp.zeros((count, PAIR), f32),
    )
    carry = unit(0, start, True)
    top, total, acc = lax.fori_loop(1, seen_ref[0], lambda i, c: unit(i, c, False), carry)
    o_ref[...] = unstack_heads(acc / total, rows).astype(bf16)
    lse_ref[...] = as_row(top + jnp.log(total))


def attend_back_kernel(
    seen_ref, q_ref, do_ref, o_ref, kk_ref, vv_ref, lse_ref, qpos_ref, kpos_ref,
    dq_ref, dkk_ref, dvv_ref, qs_ref, dos_ref, delta_ref, dqs_ref,
):
    rows = q_ref.shape[0]

    @pl.when(pl.program_id(0) == 0)
    def _():
        dkk_ref[...] = jnp.zeros_like(dkk_ref)
        dvv_ref[...] = jnp.zeros_like(dvv_ref)

    qs_ref[...] = stack_heads(q_ref[...], rows)
    grads = stack_heads(do_ref[...], rows)
    dos_ref[...] = grads
    outs = stack_heads(o_ref[...], rows)
    delta_ref[...] = as_row(jnp.sum(grads.astype(f32) * outs.astype(f32), axis=1, keepdims=True))

    def unit(index, masked):
        keys = kk_ref[index]
        scores = dot(keys, qs_ref[...], ((1,), (1,)))
        if masked:
            qpos = jnp.concatenate([qpos_ref[0:1, :]] * GROUP_HEADS, axis=1)
            scores = jnp.where(kpos_ref[...] <= qpos, scores, masked_score)
        probs = jnp.exp(scores - lse_ref[0:1, :])
        prob_grad = dot(vv_ref[index], dos_ref[...], ((1,), (1,)))
        score_grad = (probs * (prob_grad - delta_ref[0:1, :])).astype(bf16)
        dvv_ref[index] += dot(probs.astype(bf16), dos_ref[...])
        dkk_ref[index] += dot(score_grad, qs_ref[...])
        return dot(score_grad, keys, ((0,), (0,)))

    dqs_ref[...] = unit(0, True)

    @pl.loop(1, seen_ref[0])
    def _(index):
        dqs_ref[...] += unit(index, False)

    dq_ref[...] = unstack_heads(dqs_ref[...], rows)


def block_rows(length):
    return min(128, length)


def whole(shape):
    zeros = (0,) * len(shape)
    return pl.BlockSpec(shape, lambda i, seen: zeros)


def attend(seen, q, kk, vv, order):
    length, width = q.shape
    rows = block_rows(length)
    stacked = GROUP_HEADS * rows
    steps = length // rows
    return pl.pallas_call(
        attend_kernel,
        out_shape=(
            jax.ShapeDtypeStruct((length, width), bf16),
            jax.ShapeDtypeStruct((steps, 8, stacked), f32),
        ),
        grid_spec=pltpu.PrefetchScalarGridSpec(
            num_scalar_prefetch=1,
            grid=(steps,),
            in_specs=[
                pl.BlockSpec((rows, width), lambda i, seen: (i, 0)),
                whole(kk.shape),
                whole(vv.shape),
                pl.BlockSpec((rows, 1), lambda i, seen: (i, 0)),
                whole((1, length)),
            ],
            out_specs=[
                pl.BlockSpec((rows, width), lambda i, seen: (i, 0)),
                pl.BlockSpec((pl.Squeezed(), 8, stacked), lambda i, seen: (i, 0, 0)),
            ],
        ),
        name="attend",
    )(seen, q, kk, vv, order[:, None], order[None, :])


def attend_back(seen, q, do, o, kk, vv, lse, order):
    length, width = q.shape
    rows = block_rows(length)
    stacked = GROUP_HEADS * rows
    steps = length // rows
    return pl.pallas_call(
        attend_back_kernel,
        out_shape=(
            jax.ShapeDtypeStruct((length, width), f32),
            jax.ShapeDtypeStruct(kk.shape, f32),
            jax.ShapeDtypeStruct(vv.shape, f32),
        ),
        grid_spec=pltpu.PrefetchScalarGridSpec(
            num_scalar_prefetch=1,
            grid=(steps,),
            in_specs=[
                pl.BlockSpec((rows, width), lambda i, seen: (i, 0)),
                pl.BlockSpec((rows, width), lambda i, seen: (i, 0)),
                pl.BlockSpec((rows, width), lambda i, seen: (i, 0)),
                whole(kk.shape),
                whole(vv.shape),
                pl.BlockSpec((pl.Squeezed(), 8, stacked), lambda i, seen: (i, 0, 0)),
                pl.BlockSpec((8, rows), lambda i, seen: (0, i)),
                whole((length, 1)),
            ],
            out_specs=[
                pl.BlockSpec((rows, width), lambda i, seen: (i, 0)),
                whole(kk.shape),
                whole(vv.shape),
            ],
            scratch_shapes=[
                pltpu.VMEM((stacked, PAIR), bf16),
                pltpu.VMEM((stacked, PAIR), bf16),
                pltpu.VMEM((8, stacked), f32),
                pltpu.VMEM((stacked, PAIR), f32),
            ],
        ),
        name="attend_back",
    )(seen, q, do, o, kk, vv, lse, jnp.broadcast_to(order[None, :], (8, length)), order[:, None])


def normalize(values):
    inverse = lax.rsqrt(jnp.mean(values * values, axis=-1, keepdims=True) + epsilon)
    return values * inverse, inverse


def norm_back(inner, normed, inverse):
    return inverse * (inner - normed * jnp.mean(inner * normed, axis=-1, keepdims=True))


def rope_tables(positions):
    half_dim = HEAD_DIM // 2
    frequency = rope_base ** (-(jnp.arange(half_dim).astype(f32) * 2.0 / HEAD_DIM))
    angles = positions.astype(f32)[:, None] * frequency
    angles = jnp.concatenate([angles, angles], axis=-1)
    return jnp.cos(angles)[:, None, :], jnp.sin(angles)[:, None, :]


def turn(values):
    half_dim = HEAD_DIM // 2
    return jnp.concatenate([-values[..., half_dim:], values[..., :half_dim]], axis=-1)


def rotate(values, cosine, sine):
    return values * cosine + turn(values) * sine


def unrotate(grads, cosine, sine):
    return grads * cosine - turn(grads * sine)


def solution(mesh):
    n_dp = mesh.shape["dp"]
    n_seq = mesh.shape["seq"]
    planes = n_seq // GROUP
    halves = n_dp // 2
    both = ("dp", "seq")

    in_plane = [[GROUP * p + w for w in range(GROUP)] for p in range(planes)]
    across_dp = [
        [c * n_seq + GROUP * p + w for c in range(n_dp) for p in range(planes)] for w in range(GROUP)
    ]
    in_plane_dp = [
        [c * n_seq + GROUP * p + w for c in range(n_dp) for w in range(GROUP)] for p in range(planes)
    ]
    across = [[GROUP * p + w for p in range(planes)] for w in range(GROUP)]

    def xor_w(value, j):
        return lax.ppermute(value, "seq", [(s, s ^ j) for s in range(n_seq)])

    def shift_z(value, t):
        return lax.ppermute(value, "seq", [(s, (s + GROUP * t) % n_seq) for s in range(n_seq)])

    def shift_dp(value, t):
        return lax.ppermute(value, "dp", [(c, (c + t) % n_dp) for c in range(n_dp)])

    def gather_w(value):
        first = xor_w(value, 1)
        second = xor_w(value, 2)
        half = value.shape[0] // 2
        third = jnp.concatenate([xor_w(first[:half], 2), xor_w(second[half:], 1)], axis=0)
        return jnp.concatenate([value, first, second, third], axis=0)

    def scatter_w(slots):
        got = [xor_w(slots[j], j) for j in range(1, GROUP)]
        return functools.reduce(jnp.add, [g.astype(f32) for g in got], slots[0].astype(f32))

    def gather_z(value):
        return [value] + [shift_z(value, t) for t in range(1, planes)]

    def scatter_z(slots):
        got = [shift_z(slots[t], -t) for t in range(1, planes)]
        return functools.reduce(jnp.add, [g.astype(f32) for g in got], slots[0].astype(f32))

    def gather_dp(value):
        return jnp.concatenate([value] + [shift_dp(value, t) for t in range(1, n_dp)], axis=0)

    def pick(value, index, count, axis):
        size = value.shape[axis] // count
        return lax.dynamic_slice_in_dim(value, index * size, size, axis)

    def exchange_dp(value, c, axis):
        parts = [pick(value, c, n_dp, axis)]
        for t in range(1, n_dp):
            parts.append(shift_dp(pick(value, (c + t) % n_dp, n_dp, axis), t))
        return jnp.concatenate(parts, axis=0)

    def collect_dp(value, c):
        out = jnp.zeros((n_dp,) + value.shape, value.dtype)
        out = lax.dynamic_update_index_in_dim(out, value, c, 0)
        for t in range(1, n_dp):
            out = lax.dynamic_update_index_in_dim(out, shift_dp(value, t), (c - t) % n_dp, 0)
        return out

    def body(
        inputs, positions, select, cotangent, gain_attn, w_query, w_key, w_value, w_out, gain_mlp,
        w_gate, w_up, w_down,
    ):
        seqs, rows, width = inputs.shape
        tokens = seqs * rows
        shard = w_query.shape[0]
        ff_rows = w_down.shape[0]
        ff_block = w_gate.shape[1] // planes
        q_width = GROUP_HEADS * HEAD_DIM
        s = lax.axis_index("seq")
        c = lax.axis_index("dp")
        p = s // GROUP
        w = s % GROUP

        gain_one = gain_attn.astype(f32)[:, None]
        gain_two = gain_mlp.astype(f32)[:, None]

        def scaled(weight, gain):
            return (weight.astype(f32) * gain).astype(bf16)

        q_cols = scaled(w_query, gain_one).reshape(shard, GROUP, n_dp, q_width // n_dp)
        kv_cols = jnp.concatenate(
            [
                scaled(w_key, gain_one).reshape(shard, GROUP, HEAD_DIM),
                scaled(w_value, gain_one).reshape(shard, GROUP, HEAD_DIM),
            ],
            axis=-1,
        ).reshape(shard, GROUP, n_dp, PAIR // n_dp)
        qkv_cols = jnp.concatenate([q_cols, kv_cols], axis=-1)
        qkv_part = lax.dynamic_index_in_dim(qkv_cols, c, 2, keepdims=False)
        qkv_part = lax.all_to_all(
            jnp.transpose(qkv_part, (1, 0, 2)), "seq", 0, 0, axis_index_groups=in_plane, tiled=True
        )
        part_width = (q_width + PAIR) // n_dp
        qkv_part = qkv_part.reshape(GROUP * shard, part_width)
        qkv_full = lax.all_gather(qkv_part, both, axis_index_groups=across_dp, tiled=False)
        qkv_full = qkv_full.reshape(n_dp, width, part_width)

        out_part = pick(w_out, c, n_dp, 1)
        out_part = lax.ppermute(
            out_part, "seq", [(i, GROUP * (i % planes) + i // planes) for i in range(n_seq)]
        )
        out_full = lax.all_gather(out_part, both, axis_index_groups=across_dp, tiled=False)
        out_full = out_full.reshape(n_dp, planes * shard, width // n_dp)

        piece = shard // halves
        gate_up = jnp.where(c // halves == 0, scaled(w_gate, gain_two), scaled(w_up, gain_two))
        gate_up = pick(gate_up, c % halves, halves, 0)
        gate_up_part = jnp.zeros((planes, piece, ff_block), bf16)
        for t in range(planes):
            block = pick(gate_up, (p + t) % planes, planes, 1)
            block = shift_z(block, t) if t else block
            gate_up_part = lax.dynamic_update_index_in_dim(gate_up_part, block, (p - t) % planes, 0)
        gate_up_full = lax.all_gather(gate_up_part, both, axis_index_groups=in_plane_dp, tiled=False)
        gate_up_full = gate_up_full.reshape(2, width, ff_block)
        gate_full = gate_up_full[0]
        up_full = gate_up_full[1]

        down_full = lax.all_gather(
            pick(w_down, c, n_dp, 1), both, axis_index_groups=in_plane_dp, tiled=False
        )
        down_full = down_full.reshape(n_dp, ff_block, width // n_dp)

        def reorder(value):
            value = value.reshape(tokens, planes, GROUP, halves, piece)
            return jnp.transpose(value, (0, 3, 2, 1, 4)).reshape(tokens, width)

        def order_back(value):
            value = value.reshape(tokens, halves, GROUP, planes, piece)
            return jnp.transpose(value, (0, 3, 2, 1, 4)).reshape(tokens, width)

        x_in = inputs.reshape(tokens, width).astype(f32)
        normed_one, inverse_one = normalize(x_in)
        low_one = gather_w(normed_one.astype(bf16))
        own_pos = positions.reshape(1, tokens)
        plane_pos = jnp.concatenate([own_pos] + [xor_w(own_pos, j) for j in range(1, GROUP)], axis=1)
        cosine, sine = rope_tables(plane_pos.reshape(GROUP * tokens))

        grad_y = (
            cotangent.astype(f32) * select.astype(f32)[..., None]
        ).reshape(tokens, width)
        grad_y_all = jnp.concatenate(gather_z(grad_y.astype(bf16)), axis=0)

        projected = [dot(low_one, qkv_full[i]) for i in range(n_dp)]
        cut = q_width // n_dp
        q = jnp.concatenate([one[:, :cut] for one in projected], axis=1)
        kv = jnp.concatenate([one[:, cut:] for one in projected], axis=1)
        plane_tokens = GROUP * tokens
        q = rotate(q.reshape(plane_tokens, GROUP_HEADS, HEAD_DIM), cosine, sine)
        q = (q.astype(bf16).astype(f32) * HEAD_DIM ** (-0.5)).astype(bf16).reshape(plane_tokens, q_width)
        k = rotate(kv[:, None, :HEAD_DIM], cosine, sine)[:, 0]
        kv_low = jnp.concatenate([k, kv[:, HEAD_DIM:]], axis=1).astype(bf16)
        kv_all = jnp.stack(gather_z(kv_low))
        kk = jnp.concatenate([kv_all[..., :HEAD_DIM]] * 2, axis=-1)
        vv = jnp.concatenate([kv_all[..., HEAD_DIM:]] * 2, axis=-1)

        def by_seq(value, axis):
            shape = value.shape
            value = value.reshape(shape[:axis] + (GROUP, seqs, rows) + shape[axis + 1 :])
            value = jnp.moveaxis(value, axis + 1, 0)
            return value.reshape((seqs,) + shape[:axis] + (GROUP * rows,) + shape[axis + 1 :])

        def from_seq(value, axis):
            shape = value.shape[1:]
            value = value.reshape((seqs,) + shape[:axis] + (GROUP, rows) + shape[axis + 1 :])
            value = jnp.moveaxis(value, 0, axis + 1)
            return value.reshape(shape[:axis] + (GROUP * seqs * rows,) + shape[axis + 1 :])

        order = jnp.concatenate([(w ^ j) * rows + jnp.arange(rows) for j in range(GROUP)])
        order = order.astype(jnp.int32)
        seen = (p + 1).astype(jnp.int32).reshape(1)
        q_seq = by_seq(q, 0)
        kk_seq = by_seq(kk, 1)
        vv_seq = by_seq(vv, 1)
        pieces = [attend(seen, q_seq[i], kk_seq[i], vv_seq[i], order) for i in range(seqs)]
        o_seq = [one[0] for one in pieces]
        lse_seq = [one[1] for one in pieces]
        o = from_seq(jnp.stack(o_seq), 0)

        branch = jnp.concatenate([dot(o, out_full[i]).astype(bf16) for i in range(n_dp)], axis=1)
        branch = scatter_w([branch[j * tokens : (j + 1) * tokens] for j in range(GROUP)])
        x_mid = x_in + branch

        normed_two, inverse_two = normalize(x_mid)
        low_two = jnp.concatenate(gather_z(reorder(normed_two.astype(bf16))), axis=0)
        gate = dot(low_two, gate_full)
        up_part = dot(low_two, up_full)
        sigmoid_gate = 1.0 / (1.0 + jnp.exp(-gate))
        hidden = (gate * sigmoid_gate * up_part).astype(bf16)

        grad_hidden = functools.reduce(
            jnp.add,
            [
                dot(pick(grad_y_all, i, n_dp, 1), down_full[i], ((1,), (1,)))
                for i in range(n_dp)
            ],
        )
        grad_gate = (
            grad_hidden * up_part * sigmoid_gate * (1.0 + gate * (1.0 - sigmoid_gate))
        ).astype(bf16)
        grad_up = (grad_hidden * gate * sigmoid_gate).astype(bf16)
        grad_low_two = dot(grad_gate, gate_full, ((1,), (1,))) + dot(
            grad_up, up_full, ((1,), (1,))
        )
        grad_low_two = grad_low_two.astype(bf16)
        inner_two = scatter_z([grad_low_two[t * tokens : (t + 1) * tokens] for t in range(planes)])
        grad_x_mid = grad_y + norm_back(order_back(inner_two), normed_two, inverse_two)

        mixed = jnp.concatenate([dot(hidden, down_full[i]).astype(bf16) for i in range(n_dp)], axis=1)
        mixed = scatter_z([mixed[t * tokens : (t + 1) * tokens] for t in range(planes)])
        outputs = (x_mid + mixed).astype(bf16).reshape(seqs, rows, width)

        hidden_all = gather_dp(hidden)
        down_sum = dot(hidden_all, exchange_dp(grad_y_all, c, 1), ((0,), (0,))).astype(bf16)
        down_sum = lax.psum_scatter(down_sum, "seq", axis_index_groups=in_plane, tiled=True)
        down_sum = collect_dp(down_sum, c)
        grad_w_down = jnp.moveaxis(down_sum, 0, 1).reshape(ff_rows, width).astype(f32)

        low_two_all = gather_dp(low_two)
        if halves > 1:
            low_two_all = pick(low_two_all, c % halves, halves, 1)

        def of_member(member):
            return jnp.where(member // halves == 0, grad_gate, grad_up)

        gate_up_grads = [of_member(c)]
        for t in range(1, n_dp):
            gate_up_grads.append(shift_dp(of_member((c + t) % n_dp), t))
        gate_up_sum = dot(low_two_all, jnp.concatenate(gate_up_grads, axis=0), ((0,), (0,)))
        gate_up_sum = lax.psum_scatter(
            gate_up_sum.astype(bf16), "seq", axis_index_groups=in_plane, tiled=True
        ).reshape(planes, piece, ff_block)
        gate_up_rows = jnp.zeros((piece, planes, ff_block), bf16)
        for t in range(planes):
            block = lax.dynamic_index_in_dim(gate_up_sum, (p + t) % planes, 0, keepdims=False)
            block = shift_z(block, t) if t else block
            gate_up_rows = lax.dynamic_update_index_in_dim(gate_up_rows, block, (p - t) % planes, 1)
        gate_up_rows = collect_dp(gate_up_rows.reshape(piece, planes * ff_block), c)
        gate_up_rows = gate_up_rows.reshape(2, shard, planes * ff_block).astype(f32)
        grad_w_gate = gate_up_rows[0] * gain_two
        grad_w_up = gate_up_rows[1] * gain_two
        grad_gain_mlp = jnp.sum(
            gate_up_rows[0] * w_gate.astype(f32) + gate_up_rows[1] * w_up.astype(f32), axis=1
        )

        grad_branch = gather_w(grad_x_mid.astype(bf16))
        grad_o = functools.reduce(
            jnp.add,
            [dot(pick(grad_branch, i, n_dp, 1), out_full[i], ((1,), (1,))) for i in range(n_dp)],
        ).astype(bf16)

        out_sum = dot(gather_dp(o), exchange_dp(grad_branch, c, 1), ((0,), (0,))).astype(bf16)
        out_sum = lax.psum_scatter(out_sum, "seq", axis_index_groups=across, tiled=True)
        out_sum = lax.ppermute(
            out_sum, "seq", [(GROUP * (i % planes) + i // planes, i) for i in range(n_seq)]
        )
        grad_w_out = jnp.moveaxis(collect_dp(out_sum, c), 0, 1).reshape(shard, width).astype(f32)

        grad_o_seq = by_seq(grad_o, 0)
        pieces = [
            attend_back(
                seen, q_seq[i], grad_o_seq[i], o_seq[i], kk_seq[i], vv_seq[i], lse_seq[i], order
            )
            for i in range(seqs)
        ]
        grad_q = from_seq(jnp.stack([one[0] for one in pieces]), 0) * HEAD_DIM ** (-0.5)
        grad_kk = from_seq(jnp.stack([one[1] for one in pieces]), 1)
        grad_vv = from_seq(jnp.stack([one[2] for one in pieces]), 1)
        grad_kv = jnp.concatenate(
            [
                grad_kk[..., :HEAD_DIM] + grad_kk[..., HEAD_DIM:],
                grad_vv[..., :HEAD_DIM] + grad_vv[..., HEAD_DIM:],
            ],
            axis=-1,
        ).astype(bf16)
        grad_kv = scatter_z([grad_kv[t] for t in range(planes)])
        query_pre = unrotate(grad_q.reshape(plane_tokens, GROUP_HEADS, HEAD_DIM), cosine, sine)
        query_pre = query_pre.reshape(plane_tokens, q_width).astype(bf16)
        key_pre = unrotate(grad_kv[:, None, :HEAD_DIM], cosine, sine)[:, 0]
        kv_pre = jnp.concatenate([key_pre, grad_kv[:, HEAD_DIM:]], axis=1).astype(bf16)
        pre = [
            jnp.concatenate(
                [query_pre[:, i * cut : (i + 1) * cut], pick(kv_pre, i, n_dp, 1)], axis=1
            )
            for i in range(n_dp)
        ]
        grad_low_one = functools.reduce(
            jnp.add, [dot(pre[i], qkv_full[i], ((1,), (1,))) for i in range(n_dp)]
        ).astype(bf16)
        inner_one = scatter_w([grad_low_one[j * tokens : (j + 1) * tokens] for j in range(GROUP)])
        grad_inputs = grad_x_mid + norm_back(inner_one, normed_one, inverse_one)
        grad_inputs = grad_inputs.reshape(seqs, rows, width)

        qkv_sum = dot(
            gather_dp(low_one), exchange_dp(jnp.concatenate(pre, axis=1), c, 1), ((0,), (0,))
        ).astype(bf16)
        qkv_sum = lax.psum_scatter(qkv_sum, "seq", axis_index_groups=across, tiled=True)
        qkv_sum = qkv_sum.reshape(GROUP, shard, part_width)
        qkv_sum = lax.all_to_all(qkv_sum, "seq", 0, 0, axis_index_groups=in_plane, tiled=True)
        qkv_sum = collect_dp(qkv_sum, c).astype(f32)
        q_sum = jnp.transpose(qkv_sum[..., :cut], (2, 1, 0, 3)).reshape(shard, width)
        kv_sum = jnp.transpose(qkv_sum[..., cut:], (2, 1, 0, 3)).reshape(shard, GROUP, PAIR)
        k_sum = kv_sum[..., :HEAD_DIM].reshape(shard, GROUP * HEAD_DIM)
        v_sum = kv_sum[..., HEAD_DIM:].reshape(shard, GROUP * HEAD_DIM)
        grad_gain_attn = (
            jnp.sum(q_sum * w_query.astype(f32), axis=1)
            + jnp.sum(k_sum * w_key.astype(f32), axis=1)
            + jnp.sum(v_sum * w_value.astype(f32), axis=1)
        )

        return (
            outputs,
            grad_inputs,
            grad_gain_attn,
            q_sum * gain_one,
            k_sum * gain_one,
            v_sum * gain_one,
            grad_w_out,
            grad_gain_mlp,
            grad_w_gate,
            grad_w_up,
            grad_w_down,
        )

    tokens_spec = P("dp", "seq", None)
    in_specs = (
        tokens_spec,
        P("dp", "seq"),
        P("dp", "seq"),
        tokens_spec,
        P("seq"),
        P("seq", None),
        P("seq", None),
        P("seq", None),
        P("seq", None),
        P("seq"),
        P("seq", None),
        P("seq", None),
        P("seq", None),
    )
    out_specs = (
        tokens_spec,
        tokens_spec,
        P("seq"),
        P("seq", None),
        P("seq", None),
        P("seq", None),
        P("seq", None),
        P("seq"),
        P("seq", None),
        P("seq", None),
        P("seq", None),
    )
    return jax.shard_map(body, mesh=mesh, in_specs=in_specs, out_specs=out_specs, check_vma=False)
```

```python
import functools

import jax
import jax.numpy as jnp
from jax import lax
from jax.experimental import pallas as pl
from jax.experimental.pallas import tpu as pltpu
from jax.sharding import PartitionSpec as P

HEADS = 32
KV_HEADS = 4
HEAD_DIM = 64
GROUP = KV_HEADS
GROUP_HEADS = HEADS // GROUP
PAIR = 2 * HEAD_DIM

epsilon = 1e-05
rope_base = 10000.0
masked_score = -1e30

f32 = jnp.float32
bf16 = jnp.bfloat16


def dot(left, right, contract=((1,), (0,))):
    return lax.dot_general(left, right, (contract, ((), ())), preferred_element_type=f32)


def stack_heads(block, rows):
    lane = lax.broadcasted_iota(jnp.int32, (rows, PAIR), 1)
    parts = []
    for pair in range(GROUP_HEADS // 2):
        both = block[:, pair * PAIR : (pair + 1) * PAIR]
        parts.append(jnp.where(lane < HEAD_DIM, both, jnp.zeros_like(both)))
        parts.append(jnp.where(lane >= HEAD_DIM, both, jnp.zeros_like(both)))
    return jnp.concatenate(parts, axis=0)


def unstack_heads(stacked, rows):
    lane = lax.broadcasted_iota(jnp.int32, (rows, PAIR), 1)
    parts = []
    for pair in range(GROUP_HEADS // 2):
        low = stacked[2 * pair * rows : (2 * pair + 1) * rows]
        high = stacked[(2 * pair + 1) * rows : (2 * pair + 2) * rows]
        parts.append(jnp.where(lane < HEAD_DIM, low, high))
    return jnp.concatenate(parts, axis=1)


def as_row(column):
    wide = jnp.broadcast_to(column, (column.shape[0], 128))
    return jnp.transpose(wide)[:8]


def attend_kernel(seen_ref, q_ref, kk_ref, vv_ref, qpos_ref, kpos_ref, o_ref, lse_ref):
    rows = q_ref.shape[0]
    stacked = stack_heads(q_ref[...], rows)
    qpos = jnp.concatenate([qpos_ref[...]] * GROUP_HEADS, axis=0)

    def unit(index, carry, masked):
        top, total, acc = carry
        scores = dot(stacked, kk_ref[index], ((1,), (1,)))
        if masked:
            scores = jnp.where(kpos_ref[...] <= qpos, scores, masked_score)
        new_top = jnp.maximum(top, jnp.max(scores, axis=1, keepdims=True))
        weights = jnp.exp(scores - new_top)
        keep = jnp.exp(top - new_top)
        total = total * keep + jnp.sum(weights, axis=1, keepdims=True)
        acc = acc * keep + dot(weights.astype(bf16), vv_ref[index])
        return new_top, total, acc

    count = GROUP_HEADS * rows
    start = (
        jnp.full((count, 1), masked_score, f32),
        jnp.zeros((count, 1), f32),
        jnp.zeros((count, PAIR), f32),
    )
    carry = unit(0, start, True)
    top, total, acc = lax.fori_loop(1, seen_ref[0], lambda i, c: unit(i, c, False), carry)
    o_ref[...] = unstack_heads(acc / total, rows).astype(bf16)
    lse_ref[...] = as_row(top + jnp.log(total))


def attend_back_kernel(
    seen_ref, q_ref, do_ref, o_ref, kk_ref, vv_ref, lse_ref, qpos_ref, kpos_ref,
    dq_ref, dkk_ref, dvv_ref, qs_ref, dos_ref, delta_ref, dqs_ref,
):
    rows = q_ref.shape[0]

    @pl.when(pl.program_id(0) == 0)
    def _():
        dkk_ref[...] = jnp.zeros_like(dkk_ref)
        dvv_ref[...] = jnp.zeros_like(dvv_ref)

    qs_ref[...] = stack_heads(q_ref[...], rows)
    grads = stack_heads(do_ref[...], rows)
    dos_ref[...] = grads
    outs = stack_heads(o_ref[...], rows)
    delta_ref[...] = as_row(jnp.sum(grads.astype(f32) * outs.astype(f32), axis=1, keepdims=True))

    def unit(index, masked):
        keys = kk_ref[index]
        scores = dot(keys, qs_ref[...], ((1,), (1,)))
        if masked:
            qpos = jnp.concatenate([qpos_ref[0:1, :]] * GROUP_HEADS, axis=1)
            scores = jnp.where(kpos_ref[...] <= qpos, scores, masked_score)
        probs = jnp.exp(scores - lse_ref[0:1, :])
        prob_grad = dot(vv_ref[index], dos_ref[...], ((1,), (1,)))
        score_grad = (probs * (prob_grad - delta_ref[0:1, :])).astype(bf16)
        dvv_ref[index] += dot(probs.astype(bf16), dos_ref[...])
        dkk_ref[index] += dot(score_grad, qs_ref[...])
        return dot(score_grad, keys, ((0,), (0,)))

    dqs_ref[...] = unit(0, True)

    @pl.loop(1, seen_ref[0])
    def _(index):
        dqs_ref[...] += unit(index, False)

    dq_ref[...] = unstack_heads(dqs_ref[...], rows)


def block_rows(length):
    return min(128, length)


def whole(shape):
    zeros = (0,) * len(shape)
    return pl.BlockSpec(shape, lambda i, seen: zeros)


def attend(seen, q, kk, vv, order):
    length, width = q.shape
    rows = block_rows(length)
    stacked = GROUP_HEADS * rows
    steps = length // rows
    return pl.pallas_call(
        attend_kernel,
        out_shape=(
            jax.ShapeDtypeStruct((length, width), bf16),
            jax.ShapeDtypeStruct((steps, 8, stacked), f32),
        ),
        grid_spec=pltpu.PrefetchScalarGridSpec(
            num_scalar_prefetch=1,
            grid=(steps,),
            in_specs=[
                pl.BlockSpec((rows, width), lambda i, seen: (i, 0)),
                whole(kk.shape),
                whole(vv.shape),
                pl.BlockSpec((rows, 1), lambda i, seen: (i, 0)),
                whole((1, length)),
            ],
            out_specs=[
                pl.BlockSpec((rows, width), lambda i, seen: (i, 0)),
                pl.BlockSpec((pl.Squeezed(), 8, stacked), lambda i, seen: (i, 0, 0)),
            ],
        ),
        name="attend",
    )(seen, q, kk, vv, order[:, None], order[None, :])


def attend_back(seen, q, do, o, kk, vv, lse, order):
    length, width = q.shape
    rows = block_rows(length)
    stacked = GROUP_HEADS * rows
    steps = length // rows
    return pl.pallas_call(
        attend_back_kernel,
        out_shape=(
            jax.ShapeDtypeStruct((length, width), f32),
            jax.ShapeDtypeStruct(kk.shape, f32),
            jax.ShapeDtypeStruct(vv.shape, f32),
        ),
        grid_spec=pltpu.PrefetchScalarGridSpec(
            num_scalar_prefetch=1,
            grid=(steps,),
            in_specs=[
                pl.BlockSpec((rows, width), lambda i, seen: (i, 0)),
                pl.BlockSpec((rows, width), lambda i, seen: (i, 0)),
                pl.BlockSpec((rows, width), lambda i, seen: (i, 0)),
                whole(kk.shape),
                whole(vv.shape),
                pl.BlockSpec((pl.Squeezed(), 8, stacked), lambda i, seen: (i, 0, 0)),
                pl.BlockSpec((8, rows), lambda i, seen: (0, i)),
                whole((length, 1)),
            ],
            out_specs=[
                pl.BlockSpec((rows, width), lambda i, seen: (i, 0)),
                whole(kk.shape),
                whole(vv.shape),
            ],
            scratch_shapes=[
                pltpu.VMEM((stacked, PAIR), bf16),
                pltpu.VMEM((stacked, PAIR), bf16),
                pltpu.VMEM((8, stacked), f32),
                pltpu.VMEM((stacked, PAIR), f32),
            ],
        ),
        name="attend_back",
    )(seen, q, do, o, kk, vv, lse, jnp.broadcast_to(order[None, :], (8, length)), order[:, None])


def normalize(values):
    inverse = lax.rsqrt(jnp.mean(values * values, axis=-1, keepdims=True) + epsilon)
    return values * inverse, inverse


def norm_back(inner, normed, inverse):
    return inverse * (inner - normed * jnp.mean(inner * normed, axis=-1, keepdims=True))


def rope_tables(positions):
    half_dim = HEAD_DIM // 2
    frequency = rope_base ** (-(jnp.arange(half_dim).astype(f32) * 2.0 / HEAD_DIM))
    angles = positions.astype(f32)[:, None] * frequency
    angles = jnp.concatenate([angles, angles], axis=-1)
    return jnp.cos(angles)[:, None, :], jnp.sin(angles)[:, None, :]


def turn(values):
    half_dim = HEAD_DIM // 2
    return jnp.concatenate([-values[..., half_dim:], values[..., :half_dim]], axis=-1)


def rotate(values, cosine, sine):
    return values * cosine + turn(values) * sine


def unrotate(grads, cosine, sine):
    return grads * cosine - turn(grads * sine)


def after(value, *earlier):
    return lax.optimization_barrier((value,) + earlier)[0]


def solution(mesh):
    n_dp = mesh.shape["dp"]
    n_seq = mesh.shape["seq"]
    planes = n_seq // GROUP
    halves = n_dp // 2
    both = ("dp", "seq")

    in_plane = [[GROUP * p + w for w in range(GROUP)] for p in range(planes)]
    across_dp = [
        [c * n_seq + GROUP * p + w for c in range(n_dp) for p in range(planes)] for w in range(GROUP)
    ]
    in_plane_dp = [
        [c * n_seq + GROUP * p + w for c in range(n_dp) for w in range(GROUP)] for p in range(planes)
    ]
    across = [[GROUP * p + w for p in range(planes)] for w in range(GROUP)]

    def xor_w(value, j):
        return lax.ppermute(value, "seq", [(s, s ^ j) for s in range(n_seq)])

    def shift_z(value, t):
        return lax.ppermute(value, "seq", [(s, (s + GROUP * t) % n_seq) for s in range(n_seq)])

    def shift_dp(value, t):
        return lax.ppermute(value, "dp", [(c, (c + t) % n_dp) for c in range(n_dp)])

    def gather_w(value):
        first = xor_w(value, 1)
        second = xor_w(value, 2)
        half = value.shape[0] // 2
        third = jnp.concatenate([xor_w(first[:half], 2), xor_w(second[half:], 1)], axis=0)
        return jnp.concatenate([value, first, second, third], axis=0)

    def scatter_w(slots):
        got = [xor_w(slots[j], j) for j in range(1, GROUP)]
        return functools.reduce(jnp.add, [g.astype(f32) for g in got], slots[0].astype(f32))

    def gather_z(value):
        return [value] + [shift_z(value, t) for t in range(1, planes)]

    def scatter_z(slots):
        got = [shift_z(slots[t], -t) for t in range(1, planes)]
        return functools.reduce(jnp.add, [g.astype(f32) for g in got], slots[0].astype(f32))

    def gather_dp(value):
        return jnp.concatenate([value] + [shift_dp(value, t) for t in range(1, n_dp)], axis=0)

    def pick(value, index, count, axis):
        size = value.shape[axis] // count
        return lax.dynamic_slice_in_dim(value, index * size, size, axis)

    def exchange_dp(value, c, axis):
        parts = [pick(value, c, n_dp, axis)]
        for t in range(1, n_dp):
            parts.append(shift_dp(pick(value, (c + t) % n_dp, n_dp, axis), t))
        return jnp.concatenate(parts, axis=0)

    def collect_dp(value, c):
        slots = [value] + [shift_dp(value, t) for t in range(1, n_dp)]
        out = []
        for member in range(n_dp):
            chosen = slots[0]
            for t in range(1, n_dp):
                chosen = jnp.where((c - t) % n_dp == member, slots[t], chosen)
            out.append(chosen)
        return out

    def body(
        inputs, positions, select, cotangent, gain_attn, w_query, w_key, w_value, w_out, gain_mlp,
        w_gate, w_up, w_down,
    ):
        seqs, rows, width = inputs.shape
        tokens = seqs * rows
        shard = w_query.shape[0]
        ff_rows = w_down.shape[0]
        ff_block = w_gate.shape[1] // planes
        q_width = GROUP_HEADS * HEAD_DIM
        s = lax.axis_index("seq")
        c = lax.axis_index("dp")
        p = s // GROUP
        w = s % GROUP

        gain_one = gain_attn.astype(f32)[:, None]
        gain_two = gain_mlp.astype(f32)[:, None]

        def scaled(weight, gain):
            return (weight.astype(f32) * gain).astype(bf16)

        q_cols = scaled(w_query, gain_one).reshape(shard, GROUP, n_dp, q_width // n_dp)
        kv_cols = jnp.concatenate(
            [
                scaled(w_key, gain_one).reshape(shard, GROUP, HEAD_DIM),
                scaled(w_value, gain_one).reshape(shard, GROUP, HEAD_DIM),
            ],
            axis=-1,
        ).reshape(shard, GROUP, n_dp, PAIR // n_dp)
        qkv_cols = jnp.concatenate([q_cols, kv_cols], axis=-1)
        qkv_part = lax.dynamic_index_in_dim(qkv_cols, c, 2, keepdims=False)
        qkv_part = lax.all_to_all(
            jnp.transpose(qkv_part, (1, 0, 2)), "seq", 0, 0, axis_index_groups=in_plane, tiled=True
        )
        part_width = (q_width + PAIR) // n_dp
        qkv_part = qkv_part.reshape(GROUP * shard, part_width)
        qkv_full = lax.all_gather(qkv_part, both, axis_index_groups=across_dp, tiled=False)
        qkv_full = qkv_full.reshape(n_dp, width, part_width)

        x_in = inputs.reshape(tokens, width).astype(f32)
        normed_one, inverse_one = normalize(x_in)
        low_one = gather_w(after(normed_one.astype(bf16), qkv_part))

        out_part = after(pick(w_out, c, n_dp, 1), low_one)
        out_part = lax.ppermute(
            out_part, "seq", [(i, GROUP * (i % planes) + i // planes) for i in range(n_seq)]
        )
        out_full = lax.all_gather(out_part, both, axis_index_groups=across_dp, tiled=False)
        out_full = out_full.reshape(n_dp, planes * shard, width // n_dp)

        piece = shard // halves
        gate_up = jnp.where(c // halves == 0, scaled(w_gate, gain_two), scaled(w_up, gain_two))
        gate_up = after(pick(gate_up, c % halves, halves, 0), low_one, qkv_full)
        gate_up_part = jnp.zeros((planes, piece, ff_block), bf16)
        for t in range(planes):
            block = pick(gate_up, (p + t) % planes, planes, 1)
            block = shift_z(block, t) if t else block
            gate_up_part = lax.dynamic_update_index_in_dim(gate_up_part, block, (p - t) % planes, 0)
        gate_up_full = lax.all_gather(gate_up_part, both, axis_index_groups=in_plane_dp, tiled=False)
        gate_up_full = gate_up_full.reshape(2, width, ff_block)
        gate_full = gate_up_full[0]
        up_full = gate_up_full[1]

        down_full = lax.all_gather(
            after(pick(w_down, c, n_dp, 1), gate_up_part), both, axis_index_groups=in_plane_dp, tiled=False
        )
        down_full = down_full.reshape(n_dp, ff_block, width // n_dp)

        blocks = [
            (i * GROUP + j) * halves + h
            for h in range(halves) for j in range(GROUP) for i in range(planes)
        ]

        def column_blocks(value, which):
            return jnp.concatenate([value[:, i * piece : (i + 1) * piece] for i in which], axis=1)

        def reorder(value):
            return column_blocks(value, blocks)

        def order_back(value):
            return column_blocks(value, [blocks.index(i) for i in range(len(blocks))])

        own_pos = positions.reshape(1, tokens)
        plane_pos = jnp.concatenate([own_pos] + [xor_w(own_pos, j) for j in range(1, GROUP)], axis=1)
        cosine, sine = rope_tables(plane_pos.reshape(GROUP * tokens))

        grad_y = (
            cotangent.astype(f32) * select.astype(f32)[..., None]
        ).reshape(tokens, width)
        projected = [dot(low_one, qkv_full[i]) for i in range(n_dp)]
        cut = q_width // n_dp
        q = jnp.concatenate([one[:, :cut] for one in projected], axis=1)
        kv = jnp.concatenate([one[:, cut:] for one in projected], axis=1)
        plane_tokens = GROUP * tokens
        q = rotate(q.reshape(plane_tokens, GROUP_HEADS, HEAD_DIM), cosine, sine)
        q = (q.astype(bf16).astype(f32) * HEAD_DIM ** (-0.5)).astype(bf16).reshape(plane_tokens, q_width)
        k = rotate(kv[:, None, :HEAD_DIM], cosine, sine)[:, 0]
        kv_low = jnp.concatenate([k, kv[:, HEAD_DIM:]], axis=1).astype(bf16)
        kv_all = jnp.stack(gather_z(kv_low))
        grad_y_all = jnp.concatenate(gather_z(after(grad_y.astype(bf16), kv_all)), axis=0)
        kk = jnp.concatenate([kv_all[..., :HEAD_DIM]] * 2, axis=-1)
        vv = jnp.concatenate([kv_all[..., HEAD_DIM:]] * 2, axis=-1)

        def by_seq(value, axis):
            shape = value.shape
            value = value.reshape(shape[:axis] + (GROUP, seqs, rows) + shape[axis + 1 :])
            value = jnp.moveaxis(value, axis + 1, 0)
            return value.reshape((seqs,) + shape[:axis] + (GROUP * rows,) + shape[axis + 1 :])

        def from_seq(value, axis):
            shape = value.shape[1:]
            value = value.reshape((seqs,) + shape[:axis] + (GROUP, rows) + shape[axis + 1 :])
            value = jnp.moveaxis(value, 0, axis + 1)
            return value.reshape(shape[:axis] + (GROUP * seqs * rows,) + shape[axis + 1 :])

        order = jnp.concatenate([(w ^ j) * rows + jnp.arange(rows) for j in range(GROUP)])
        order = order.astype(jnp.int32)
        seen = (p + 1).astype(jnp.int32).reshape(1)
        q_seq = by_seq(q, 0)
        kk_seq = by_seq(kk, 1)
        vv_seq = by_seq(vv, 1)
        pieces = [attend(seen, q_seq[i], kk_seq[i], vv_seq[i], order) for i in range(seqs)]
        o_seq = [one[0] for one in pieces]
        lse_seq = [one[1] for one in pieces]
        o = from_seq(jnp.stack(o_seq), 0)

        branch = jnp.concatenate([dot(o, out_full[i]).astype(bf16) for i in range(n_dp)], axis=1)
        branch = scatter_w([branch[j * tokens : (j + 1) * tokens] for j in range(GROUP)])
        x_mid = x_in + branch

        normed_two, inverse_two = normalize(x_mid)
        low_two = jnp.concatenate(gather_z(reorder(normed_two.astype(bf16))), axis=0)
        gate = dot(low_two, gate_full)
        up_part = dot(low_two, up_full)
        sigmoid_gate = 1.0 / (1.0 + jnp.exp(-gate))
        hidden = (gate * sigmoid_gate * up_part).astype(bf16)

        grad_hidden = functools.reduce(
            jnp.add,
            [
                dot(pick(grad_y_all, i, n_dp, 1), down_full[i], ((1,), (1,)))
                for i in range(n_dp)
            ],
        )
        grad_gate = (
            grad_hidden * up_part * sigmoid_gate * (1.0 + gate * (1.0 - sigmoid_gate))
        ).astype(bf16)
        grad_up = (grad_hidden * gate * sigmoid_gate).astype(bf16)
        grad_low_two = dot(grad_gate, gate_full, ((1,), (1,))) + dot(
            grad_up, up_full, ((1,), (1,))
        )
        grad_low_two = grad_low_two.astype(bf16)
        inner_two = scatter_z([grad_low_two[t * tokens : (t + 1) * tokens] for t in range(planes)])

        hidden_later = after(hidden, grad_low_two)
        hidden_all = gather_dp(hidden_later)
        down_sum = dot(hidden_all, exchange_dp(grad_y_all, c, 1), ((0,), (0,))).astype(bf16)

        low_two_all = gather_dp(low_two)
        if halves > 1:
            low_two_all = pick(low_two_all, c % halves, halves, 1)

        def of_member(member):
            return jnp.where(member // halves == 0, grad_gate, grad_up)

        gate_up_grads = [of_member(c)]
        for t in range(1, n_dp):
            gate_up_grads.append(shift_dp(of_member((c + t) % n_dp), t))
        gate_up_grads = after(jnp.concatenate(gate_up_grads, axis=0), grad_low_two)
        gate_up_sum = dot(low_two_all, gate_up_grads, ((0,), (0,))).astype(bf16)

        mixed = jnp.concatenate(
            [dot(hidden_later, down_full[i]).astype(bf16) for i in range(n_dp)], axis=1
        )
        inner_two = after(inner_two, down_sum, gate_up_sum, mixed)
        grad_x_mid = grad_y + norm_back(order_back(inner_two), normed_two, inverse_two)

        mixed = after(mixed, inner_two)
        mixed = scatter_z([mixed[t * tokens : (t + 1) * tokens] for t in range(planes)])
        down_sum = lax.psum_scatter(down_sum, "seq", axis_index_groups=in_plane, tiled=True)
        gate_up_sum = lax.psum_scatter(
            gate_up_sum, "seq", axis_index_groups=in_plane, tiled=True
        ).reshape(planes, piece, ff_block)

        grad_branch = gather_w(grad_x_mid.astype(bf16))
        grad_o = functools.reduce(
            jnp.add,
            [dot(pick(grad_branch, i, n_dp, 1), out_full[i], ((1,), (1,))) for i in range(n_dp)],
        ).astype(bf16)

        out_part_sum = dot(gather_dp(o), exchange_dp(grad_branch, c, 1), ((0,), (0,))).astype(bf16)
        out_sum = lax.psum_scatter(out_part_sum, "seq", axis_index_groups=across, tiled=True)
        out_sum = lax.ppermute(
            out_sum, "seq", [(GROUP * (i % planes) + i // planes, i) for i in range(n_seq)]
        )
        grad_w_out = jnp.concatenate(collect_dp(out_sum, c), axis=1).astype(f32)

        grad_o_seq = by_seq(grad_o, 0)
        grad_o_seq = after(grad_o_seq, out_part_sum)
        pieces = [
            attend_back(
                seen, q_seq[i], grad_o_seq[i], o_seq[i], kk_seq[i], vv_seq[i], lse_seq[i], order
            )
            for i in range(seqs)
        ]
        grad_q = from_seq(jnp.stack([one[0] for one in pieces]), 0) * HEAD_DIM ** (-0.5)
        grad_kk = from_seq(jnp.stack([one[1] for one in pieces]), 1)
        grad_vv = from_seq(jnp.stack([one[2] for one in pieces]), 1)
        grad_kv = jnp.concatenate(
            [
                grad_kk[..., :HEAD_DIM] + grad_kk[..., HEAD_DIM:],
                grad_vv[..., :HEAD_DIM] + grad_vv[..., HEAD_DIM:],
            ],
            axis=-1,
        ).astype(bf16)
        grad_kv = scatter_z([grad_kv[t] for t in range(planes)])
        query_pre = unrotate(grad_q.reshape(plane_tokens, GROUP_HEADS, HEAD_DIM), cosine, sine)
        query_pre = query_pre.reshape(plane_tokens, q_width).astype(bf16)
        key_pre = unrotate(grad_kv[:, None, :HEAD_DIM], cosine, sine)[:, 0]
        kv_pre = jnp.concatenate([key_pre, grad_kv[:, HEAD_DIM:]], axis=1).astype(bf16)
        pre = [
            jnp.concatenate(
                [query_pre[:, i * cut : (i + 1) * cut], pick(kv_pre, i, n_dp, 1)], axis=1
            )
            for i in range(n_dp)
        ]
        mixed = after(mixed, kv_pre)
        outputs = (x_mid + mixed).astype(bf16).reshape(seqs, rows, width)

        grad_low_one = functools.reduce(
            jnp.add, [dot(pre[i], qkv_full[i], ((1,), (1,))) for i in range(n_dp)]
        ).astype(bf16)
        inner_one = scatter_w([grad_low_one[j * tokens : (j + 1) * tokens] for j in range(GROUP)])
        grad_inputs = grad_x_mid + norm_back(inner_one, normed_one, inverse_one)
        grad_inputs = grad_inputs.reshape(seqs, rows, width)

        qkv_sum = dot(
            gather_dp(low_one),
            exchange_dp(after(jnp.concatenate(pre, axis=1), grad_low_one), c, 1),
            ((0,), (0,)),
        ).astype(bf16)
        qkv_sum = lax.psum_scatter(qkv_sum, "seq", axis_index_groups=across, tiled=True)
        qkv_sum = qkv_sum.reshape(GROUP, shard, part_width)
        qkv_sum = lax.all_to_all(qkv_sum, "seq", 0, 0, axis_index_groups=in_plane, tiled=True)
        qkv_sum = collect_dp(qkv_sum, c)
        q_sum = jnp.concatenate(
            [one[j][:, :cut] for j in range(GROUP) for one in qkv_sum], axis=1
        ).astype(f32)
        kv_sum = jnp.concatenate(
            [one[j][:, cut:] for j in range(GROUP) for one in qkv_sum], axis=1
        ).astype(f32).reshape(shard, GROUP, PAIR)
        k_sum = kv_sum[..., :HEAD_DIM].reshape(shard, GROUP * HEAD_DIM)
        v_sum = kv_sum[..., HEAD_DIM:].reshape(shard, GROUP * HEAD_DIM)

        grad_w_down = jnp.concatenate(collect_dp(down_sum, c), axis=1).astype(f32)
        gate_up_rows = jnp.zeros((planes, piece, ff_block), bf16)
        for t in range(planes):
            block = lax.dynamic_index_in_dim(gate_up_sum, (p + t) % planes, 0, keepdims=False)
            block = shift_z(block, t) if t else block
            gate_up_rows = lax.dynamic_update_index_in_dim(gate_up_rows, block, (p - t) % planes, 0)
        gate_up_rows = collect_dp(gate_up_rows, c)

        def rows_of(members):
            wide = [jnp.concatenate([one[i] for i in range(planes)], axis=1) for one in members]
            return jnp.concatenate(wide, axis=0).astype(f32)

        gate_rows = rows_of(gate_up_rows[:halves])
        up_rows = rows_of(gate_up_rows[halves:])
        grad_w_gate = gate_rows * gain_two
        grad_w_up = up_rows * gain_two
        grad_gain_mlp = jnp.sum(
            gate_rows * w_gate.astype(f32) + up_rows * w_up.astype(f32), axis=1
        )
        grad_gain_attn = (
            jnp.sum(q_sum * w_query.astype(f32), axis=1)
            + jnp.sum(k_sum * w_key.astype(f32), axis=1)
            + jnp.sum(v_sum * w_value.astype(f32), axis=1)
        )

        return (
            outputs,
            grad_inputs,
            grad_gain_attn,
            q_sum * gain_one,
            k_sum * gain_one,
            v_sum * gain_one,
            grad_w_out,
            grad_gain_mlp,
            grad_w_gate,
            grad_w_up,
            grad_w_down,
        )

    tokens_spec = P("dp", "seq", None)
    in_specs = (
        tokens_spec,
        P("dp", "seq"),
        P("dp", "seq"),
        tokens_spec,
        P("seq"),
        P("seq", None),
        P("seq", None),
        P("seq", None),
        P("seq", None),
        P("seq"),
        P("seq", None),
        P("seq", None),
        P("seq", None),
    )
    out_specs = (
        tokens_spec,
        tokens_spec,
        P("seq"),
        P("seq", None),
        P("seq", None),
        P("seq", None),
        P("seq", None),
        P("seq"),
        P("seq", None),
        P("seq", None),
        P("seq", None),
    )
    return jax.shard_map(body, mesh=mesh, in_specs=in_specs, out_specs=out_specs, check_vma=False)
```

```python
import functools

import jax
import jax.numpy as jnp
from jax import lax
from jax.experimental import pallas as pl
from jax.experimental.pallas import tpu as pltpu
from jax.sharding import PartitionSpec as P

HEADS = 32
KV_HEADS = 4
HEAD_DIM = 64
GROUP = KV_HEADS
GROUP_HEADS = HEADS // GROUP
PAIR = 2 * HEAD_DIM

epsilon = 1e-05
rope_base = 10000.0
masked_score = -1e30

f32 = jnp.float32
bf16 = jnp.bfloat16


def dot(left, right, contract=((1,), (0,))):
    return lax.dot_general(left, right, (contract, ((), ())), preferred_element_type=f32)


def stack_heads(block, rows):
    lane = lax.broadcasted_iota(jnp.int32, (rows, PAIR), 1)
    parts = []
    for pair in range(GROUP_HEADS // 2):
        both = block[:, pair * PAIR : (pair + 1) * PAIR]
        parts.append(jnp.where(lane < HEAD_DIM, both, jnp.zeros_like(both)))
        parts.append(jnp.where(lane >= HEAD_DIM, both, jnp.zeros_like(both)))
    return jnp.concatenate(parts, axis=0)


def unstack_heads(stacked, rows):
    lane = lax.broadcasted_iota(jnp.int32, (rows, PAIR), 1)
    parts = []
    for pair in range(GROUP_HEADS // 2):
        low = stacked[2 * pair * rows : (2 * pair + 1) * rows]
        high = stacked[(2 * pair + 1) * rows : (2 * pair + 2) * rows]
        parts.append(jnp.where(lane < HEAD_DIM, low, high))
    return jnp.concatenate(parts, axis=1)


def as_row(column):
    wide = jnp.broadcast_to(column, (column.shape[0], 128))
    return jnp.transpose(wide)[:8]


def attend_kernel(seen_ref, q_ref, kk_ref, vv_ref, qpos_ref, kpos_ref, o_ref, lse_ref):
    rows = q_ref.shape[0]
    stacked = stack_heads(q_ref[...], rows)
    qpos = jnp.concatenate([qpos_ref[...]] * GROUP_HEADS, axis=0)

    def unit(index, carry, masked):
        top, total, acc = carry
        scores = dot(stacked, kk_ref[index], ((1,), (1,)))
        if masked:
            scores = jnp.where(kpos_ref[...] <= qpos, scores, masked_score)
        new_top = jnp.maximum(top, jnp.max(scores, axis=1, keepdims=True))
        weights = jnp.exp(scores - new_top)
        keep = jnp.exp(top - new_top)
        total = total * keep + jnp.sum(weights, axis=1, keepdims=True)
        acc = acc * keep + dot(weights.astype(bf16), vv_ref[index])
        return new_top, total, acc

    count = GROUP_HEADS * rows
    start = (
        jnp.full((count, 1), masked_score, f32),
        jnp.zeros((count, 1), f32),
        jnp.zeros((count, PAIR), f32),
    )
    carry = unit(0, start, True)
    top, total, acc = lax.fori_loop(1, seen_ref[0], lambda i, c: unit(i, c, False), carry)
    o_ref[...] = unstack_heads(acc / total, rows).astype(bf16)
    lse_ref[...] = as_row(top + jnp.log(total))


def attend_back_kernel(
    seen_ref, q_ref, do_ref, o_ref, kk_ref, vv_ref, lse_ref, qpos_ref, kpos_ref,
    dq_ref, dkk_ref, dvv_ref, qs_ref, dos_ref, delta_ref, dqs_ref,
):
    rows = q_ref.shape[0]

    @pl.when(pl.program_id(0) == 0)
    def _():
        dkk_ref[...] = jnp.zeros_like(dkk_ref)
        dvv_ref[...] = jnp.zeros_like(dvv_ref)

    qs_ref[...] = stack_heads(q_ref[...], rows)
    grads = stack_heads(do_ref[...], rows)
    dos_ref[...] = grads
    outs = stack_heads(o_ref[...], rows)
    delta_ref[...] = as_row(jnp.sum(grads.astype(f32) * outs.astype(f32), axis=1, keepdims=True))

    def unit(index, masked):
        keys = kk_ref[index]
        scores = dot(keys, qs_ref[...], ((1,), (1,)))
        if masked:
            qpos = jnp.concatenate([qpos_ref[0:1, :]] * GROUP_HEADS, axis=1)
            scores = jnp.where(kpos_ref[...] <= qpos, scores, masked_score)
        probs = jnp.exp(scores - lse_ref[0:1, :])
        prob_grad = dot(vv_ref[index], dos_ref[...], ((1,), (1,)))
        score_grad = (probs * (prob_grad - delta_ref[0:1, :])).astype(bf16)
        dvv_ref[index] += dot(probs.astype(bf16), dos_ref[...])
        dkk_ref[index] += dot(score_grad, qs_ref[...])
        return dot(score_grad, keys, ((0,), (0,)))

    dqs_ref[...] = unit(0, True)

    @pl.loop(1, seen_ref[0])
    def _(index):
        dqs_ref[...] += unit(index, False)

    dq_ref[...] = unstack_heads(dqs_ref[...], rows)


def block_rows(length):
    return min(128, length)


def whole(shape):
    zeros = (0,) * len(shape)
    return pl.BlockSpec(shape, lambda i, seen: zeros)


def attend(seen, q, kk, vv, order):
    length, width = q.shape
    rows = block_rows(length)
    stacked = GROUP_HEADS * rows
    steps = length // rows
    return pl.pallas_call(
        attend_kernel,
        out_shape=(
            jax.ShapeDtypeStruct((length, width), bf16),
            jax.ShapeDtypeStruct((steps, 8, stacked), f32),
        ),
        grid_spec=pltpu.PrefetchScalarGridSpec(
            num_scalar_prefetch=1,
            grid=(steps,),
            in_specs=[
                pl.BlockSpec((rows, width), lambda i, seen: (i, 0)),
                whole(kk.shape),
                whole(vv.shape),
                pl.BlockSpec((rows, 1), lambda i, seen: (i, 0)),
                whole((1, length)),
            ],
            out_specs=[
                pl.BlockSpec((rows, width), lambda i, seen: (i, 0)),
                pl.BlockSpec((pl.Squeezed(), 8, stacked), lambda i, seen: (i, 0, 0)),
            ],
        ),
        name="attend",
    )(seen, q, kk, vv, order[:, None], order[None, :])


def attend_back(seen, q, do, o, kk, vv, lse, order):
    length, width = q.shape
    rows = block_rows(length)
    stacked = GROUP_HEADS * rows
    steps = length // rows
    return pl.pallas_call(
        attend_back_kernel,
        out_shape=(
            jax.ShapeDtypeStruct((length, width), f32),
            jax.ShapeDtypeStruct(kk.shape, f32),
            jax.ShapeDtypeStruct(vv.shape, f32),
        ),
        grid_spec=pltpu.PrefetchScalarGridSpec(
            num_scalar_prefetch=1,
            grid=(steps,),
            in_specs=[
                pl.BlockSpec((rows, width), lambda i, seen: (i, 0)),
                pl.BlockSpec((rows, width), lambda i, seen: (i, 0)),
                pl.BlockSpec((rows, width), lambda i, seen: (i, 0)),
                whole(kk.shape),
                whole(vv.shape),
                pl.BlockSpec((pl.Squeezed(), 8, stacked), lambda i, seen: (i, 0, 0)),
                pl.BlockSpec((8, rows), lambda i, seen: (0, i)),
                whole((length, 1)),
            ],
            out_specs=[
                pl.BlockSpec((rows, width), lambda i, seen: (i, 0)),
                whole(kk.shape),
                whole(vv.shape),
            ],
            scratch_shapes=[
                pltpu.VMEM((stacked, PAIR), bf16),
                pltpu.VMEM((stacked, PAIR), bf16),
                pltpu.VMEM((8, stacked), f32),
                pltpu.VMEM((stacked, PAIR), f32),
            ],
        ),
        name="attend_back",
    )(seen, q, do, o, kk, vv, lse, jnp.broadcast_to(order[None, :], (8, length)), order[:, None])


def normalize(values):
    inverse = lax.rsqrt(jnp.mean(values * values, axis=-1, keepdims=True) + epsilon)
    return values * inverse, inverse


def norm_back(inner, normed, inverse):
    return inverse * (inner - normed * jnp.mean(inner * normed, axis=-1, keepdims=True))


def rope_tables(positions):
    half_dim = HEAD_DIM // 2
    frequency = rope_base ** (-(jnp.arange(half_dim).astype(f32) * 2.0 / HEAD_DIM))
    angles = positions.astype(f32)[:, None] * frequency
    angles = jnp.concatenate([angles, angles], axis=-1)
    return jnp.cos(angles)[:, None, :], jnp.sin(angles)[:, None, :]


def turn(values):
    half_dim = HEAD_DIM // 2
    return jnp.concatenate([-values[..., half_dim:], values[..., :half_dim]], axis=-1)


def rotate(values, cosine, sine):
    return values * cosine + turn(values) * sine


def unrotate(grads, cosine, sine):
    return grads * cosine - turn(grads * sine)


def after(value, *earlier):
    return lax.optimization_barrier((value,) + earlier)[0]


def solution(mesh):
    n_dp = mesh.shape["dp"]
    n_seq = mesh.shape["seq"]
    planes = n_seq // GROUP
    halves = n_dp // 2
    both = ("dp", "seq")

    in_plane = [[GROUP * p + w for w in range(GROUP)] for p in range(planes)]
    across_dp = [
        [c * n_seq + GROUP * p + w for c in range(n_dp) for p in range(planes)] for w in range(GROUP)
    ]
    in_plane_dp = [
        [c * n_seq + GROUP * p + w for c in range(n_dp) for w in range(GROUP)] for p in range(planes)
    ]
    across = [[GROUP * p + w for p in range(planes)] for w in range(GROUP)]

    def xor_w(value, j):
        return lax.ppermute(value, "seq", [(s, s ^ j) for s in range(n_seq)])

    def shift_z(value, t):
        return lax.ppermute(value, "seq", [(s, (s + GROUP * t) % n_seq) for s in range(n_seq)])

    def shift_dp(value, t):
        return lax.ppermute(value, "dp", [(c, (c + t) % n_dp) for c in range(n_dp)])

    def gather_w(value):
        first = xor_w(value, 1)
        second = xor_w(value, 2)
        half = value.shape[0] // 2
        third = jnp.concatenate([xor_w(first[:half], 2), xor_w(second[half:], 1)], axis=0)
        return jnp.concatenate([value, first, second, third], axis=0)

    def scatter_w(slots):
        got = [xor_w(slots[j], j) for j in range(1, GROUP)]
        return functools.reduce(jnp.add, [g.astype(f32) for g in got], slots[0].astype(f32))

    def gather_z(value):
        return [value] + [shift_z(value, t) for t in range(1, planes)]

    def scatter_z(slots):
        got = [shift_z(slots[t], -t) for t in range(1, planes)]
        return functools.reduce(jnp.add, [g.astype(f32) for g in got], slots[0].astype(f32))

    def gather_dp(value):
        return jnp.concatenate([value] + [shift_dp(value, t) for t in range(1, n_dp)], axis=0)

    def pick(value, index, count, axis):
        size = value.shape[axis] // count
        return lax.dynamic_slice_in_dim(value, index * size, size, axis)

    def exchange_dp(value, c, axis):
        parts = [pick(value, c, n_dp, axis)]
        for t in range(1, n_dp):
            parts.append(shift_dp(pick(value, (c + t) % n_dp, n_dp, axis), t))
        return jnp.concatenate(parts, axis=0)

    def collect_dp(value, c):
        slots = [value] + [shift_dp(value, t) for t in range(1, n_dp)]
        out = []
        for member in range(n_dp):
            chosen = slots[0]
            for t in range(1, n_dp):
                chosen = jnp.where((c - t) % n_dp == member, slots[t], chosen)
            out.append(chosen)
        return out

    def body(
        inputs, positions, select, cotangent, gain_attn, w_query, w_key, w_value, w_out, gain_mlp,
        w_gate, w_up, w_down,
    ):
        seqs, rows, width = inputs.shape
        tokens = seqs * rows
        shard = w_query.shape[0]
        ff_rows = w_down.shape[0]
        ff_block = w_gate.shape[1] // planes
        q_width = GROUP_HEADS * HEAD_DIM
        s = lax.axis_index("seq")
        c = lax.axis_index("dp")
        p = s // GROUP
        w = s % GROUP

        gain_one = gain_attn.astype(f32)[:, None]
        gain_two = gain_mlp.astype(f32)[:, None]

        def scaled(weight, gain):
            return (weight.astype(f32) * gain).astype(bf16)

        q_cols = scaled(w_query, gain_one).reshape(shard, GROUP, n_dp, q_width // n_dp)
        kv_cols = jnp.concatenate(
            [
                scaled(w_key, gain_one).reshape(shard, GROUP, HEAD_DIM),
                scaled(w_value, gain_one).reshape(shard, GROUP, HEAD_DIM),
            ],
            axis=-1,
        ).reshape(shard, GROUP, n_dp, PAIR // n_dp)
        qkv_cols = jnp.concatenate([q_cols, kv_cols], axis=-1)
        qkv_part = lax.dynamic_index_in_dim(qkv_cols, c, 2, keepdims=False)
        qkv_part = lax.all_to_all(
            jnp.transpose(qkv_part, (1, 0, 2)), "seq", 0, 0, axis_index_groups=in_plane, tiled=True
        )
        part_width = (q_width + PAIR) // n_dp
        qkv_part = qkv_part.reshape(GROUP * shard, part_width)
        ring = [qkv_part] + [shift_z(qkv_part, -t) for t in range(1, planes)]
        qkv_ring = jnp.concatenate(ring + ring[: planes - 1], axis=0)
        qkv_mine = lax.dynamic_slice_in_dim(
            qkv_ring, ((planes - p) % planes) * GROUP * shard, width, 0
        )
        qkv_full = collect_dp(qkv_mine, c)

        x_in = inputs.reshape(tokens, width).astype(f32)
        normed_one, inverse_one = normalize(x_in)
        low_one = gather_w(normed_one.astype(bf16))

        out_part = lax.ppermute(
            pick(w_out, c, n_dp, 1),
            "seq",
            [(i, GROUP * (i % planes) + i // planes) for i in range(n_seq)],
        )
        out_full = lax.all_gather(out_part, both, axis_index_groups=across_dp, tiled=False)
        out_full = out_full.reshape(n_dp, planes * shard, width // n_dp)

        piece = shard // halves
        gate_up = jnp.where(c // halves == 0, scaled(w_gate, gain_two), scaled(w_up, gain_two))
        gate_up = after(pick(gate_up, c % halves, halves, 0), low_one, qkv_mine)
        gate_up_part = jnp.zeros((planes, piece, ff_block), bf16)
        for t in range(planes):
            block = pick(gate_up, (p + t) % planes, planes, 1)
            block = shift_z(block, t) if t else block
            gate_up_part = lax.dynamic_update_index_in_dim(gate_up_part, block, (p - t) % planes, 0)
        gate_up_full = lax.all_gather(gate_up_part, both, axis_index_groups=in_plane_dp, tiled=False)
        gate_up_full = gate_up_full.reshape(2, width, ff_block)
        gate_full = gate_up_full[0]
        up_full = gate_up_full[1]

        down_full = lax.all_gather(
            pick(w_down, c, n_dp, 1), both, axis_index_groups=in_plane_dp, tiled=False
        )
        down_full = down_full.reshape(n_dp, ff_block, width // n_dp)

        blocks = [
            (i * GROUP + j) * halves + h
            for h in range(halves) for j in range(GROUP) for i in range(planes)
        ]

        def column_blocks(value, which):
            return jnp.concatenate([value[:, i * piece : (i + 1) * piece] for i in which], axis=1)

        def reorder(value):
            return column_blocks(value, blocks)

        def order_back(value):
            return column_blocks(value, [blocks.index(i) for i in range(len(blocks))])

        own_pos = positions.reshape(1, tokens)
        plane_pos = jnp.concatenate([own_pos] + [xor_w(own_pos, j) for j in range(1, GROUP)], axis=1)
        cosine, sine = rope_tables(plane_pos.reshape(GROUP * tokens))

        grad_y = (
            cotangent.astype(f32) * select.astype(f32)[..., None]
        ).reshape(tokens, width)
        projected = [dot(low_one, qkv_full[i]) for i in range(n_dp)]
        cut = q_width // n_dp
        q = jnp.concatenate([one[:, :cut] for one in projected], axis=1)
        kv = jnp.concatenate([one[:, cut:] for one in projected], axis=1)
        plane_tokens = GROUP * tokens
        q = rotate(q.reshape(plane_tokens, GROUP_HEADS, HEAD_DIM), cosine, sine)
        q = (q.astype(bf16).astype(f32) * HEAD_DIM ** (-0.5)).astype(bf16).reshape(plane_tokens, q_width)
        k = rotate(kv[:, None, :HEAD_DIM], cosine, sine)[:, 0]
        kv_low = jnp.concatenate([k, kv[:, HEAD_DIM:]], axis=1).astype(bf16)
        kv_all = jnp.stack(gather_z(kv_low))
        grad_y_all = jnp.concatenate(gather_z(after(grad_y.astype(bf16), kv_all, gate_up_part)), axis=0)
        kk = jnp.concatenate([kv_all[..., :HEAD_DIM]] * 2, axis=-1)
        vv = jnp.concatenate([kv_all[..., HEAD_DIM:]] * 2, axis=-1)

        def by_seq(value, axis):
            shape = value.shape
            value = value.reshape(shape[:axis] + (GROUP, seqs, rows) + shape[axis + 1 :])
            value = jnp.moveaxis(value, axis + 1, 0)
            return value.reshape((seqs,) + shape[:axis] + (GROUP * rows,) + shape[axis + 1 :])

        def from_seq(value, axis):
            shape = value.shape[1:]
            value = value.reshape((seqs,) + shape[:axis] + (GROUP, rows) + shape[axis + 1 :])
            value = jnp.moveaxis(value, 0, axis + 1)
            return value.reshape(shape[:axis] + (GROUP * seqs * rows,) + shape[axis + 1 :])

        order = jnp.concatenate([(w ^ j) * rows + jnp.arange(rows) for j in range(GROUP)])
        order = order.astype(jnp.int32)
        seen = (p + 1).astype(jnp.int32).reshape(1)
        q_seq = by_seq(q, 0)
        kk_seq = by_seq(kk, 1)
        vv_seq = by_seq(vv, 1)
        pieces = [attend(seen, q_seq[i], kk_seq[i], vv_seq[i], order) for i in range(seqs)]
        o_seq = [one[0] for one in pieces]
        lse_seq = [one[1] for one in pieces]
        o = from_seq(jnp.stack(o_seq), 0)

        branch = jnp.concatenate([dot(o, out_full[i]).astype(bf16) for i in range(n_dp)], axis=1)
        branch = scatter_w([branch[j * tokens : (j + 1) * tokens] for j in range(GROUP)])
        x_mid = x_in + branch

        normed_two, inverse_two = normalize(x_mid)
        low_two = reorder(normed_two.astype(bf16))
        low_two = jnp.concatenate(gather_z(after(low_two, grad_y_all)), axis=0)
        gate = dot(low_two, gate_full)
        up_part = dot(low_two, up_full)
        sigmoid_gate = 1.0 / (1.0 + jnp.exp(-gate))
        hidden = (gate * sigmoid_gate * up_part).astype(bf16)

        grad_hidden = functools.reduce(
            jnp.add,
            [
                dot(pick(grad_y_all, i, n_dp, 1), down_full[i], ((1,), (1,)))
                for i in range(n_dp)
            ],
        )
        grad_gate = (
            grad_hidden * up_part * sigmoid_gate * (1.0 + gate * (1.0 - sigmoid_gate))
        ).astype(bf16)
        grad_up = (grad_hidden * gate * sigmoid_gate).astype(bf16)
        grad_low_two = dot(grad_gate, gate_full, ((1,), (1,))) + dot(
            grad_up, up_full, ((1,), (1,))
        )
        grad_low_two = grad_low_two.astype(bf16)
        inner_two = scatter_z([grad_low_two[t * tokens : (t + 1) * tokens] for t in range(planes)])

        hidden_later = after(hidden, grad_low_two)
        hidden_all = gather_dp(hidden_later)
        down_sum = dot(hidden_all, exchange_dp(grad_y_all, c, 1), ((0,), (0,))).astype(bf16)

        low_two_all = gather_dp(low_two)
        if halves > 1:
            low_two_all = pick(low_two_all, c % halves, halves, 1)

        def of_member(member):
            return jnp.where(member // halves == 0, grad_gate, grad_up)

        gate_up_grads = [of_member(c)]
        for t in range(1, n_dp):
            gate_up_grads.append(shift_dp(of_member((c + t) % n_dp), t))
        gate_up_grads = after(jnp.concatenate(gate_up_grads, axis=0), grad_low_two)
        gate_up_sum = dot(low_two_all, gate_up_grads, ((0,), (0,))).astype(bf16)

        mixed = jnp.concatenate(
            [dot(hidden_later, down_full[i]).astype(bf16) for i in range(n_dp)], axis=1
        )
        inner_two = after(inner_two, down_sum, gate_up_sum, mixed)
        grad_x_mid = grad_y + norm_back(order_back(inner_two), normed_two, inverse_two)

        mixed = after(mixed, inner_two)
        mixed = scatter_z([mixed[t * tokens : (t + 1) * tokens] for t in range(planes)])
        gate_up_sum = lax.psum_scatter(gate_up_sum, "seq", axis_index_groups=in_plane, tiled=True)
        down_sum = lax.psum_scatter(
            after(down_sum, gate_up_sum), "seq", axis_index_groups=in_plane, tiled=True
        )
        gate_up_sum = gate_up_sum.reshape(planes, piece, ff_block)

        grad_branch = gather_w(grad_x_mid.astype(bf16))
        grad_o = functools.reduce(
            jnp.add,
            [dot(pick(grad_branch, i, n_dp, 1), out_full[i], ((1,), (1,))) for i in range(n_dp)],
        ).astype(bf16)

        out_part_sum = dot(gather_dp(o), exchange_dp(grad_branch, c, 1), ((0,), (0,))).astype(bf16)
        out_sum = lax.psum_scatter(
            after(out_part_sum, down_sum), "seq", axis_index_groups=across, tiled=True
        )
        out_sum = lax.ppermute(
            out_sum, "seq", [(GROUP * (i % planes) + i // planes, i) for i in range(n_seq)]
        )
        grad_w_out = jnp.concatenate(collect_dp(out_sum, c), axis=1).astype(f32)

        grad_o_seq = by_seq(grad_o, 0)
        grad_o_seq = after(grad_o_seq, out_part_sum)
        pieces = [
            attend_back(
                seen, q_seq[i], grad_o_seq[i], o_seq[i], kk_seq[i], vv_seq[i], lse_seq[i], order
            )
            for i in range(seqs)
        ]
        grad_q = from_seq(jnp.stack([one[0] for one in pieces]), 0) * HEAD_DIM ** (-0.5)
        grad_kk = from_seq(jnp.stack([one[1] for one in pieces]), 1)
        grad_vv = from_seq(jnp.stack([one[2] for one in pieces]), 1)
        grad_kv = jnp.concatenate(
            [
                grad_kk[..., :HEAD_DIM] + grad_kk[..., HEAD_DIM:],
                grad_vv[..., :HEAD_DIM] + grad_vv[..., HEAD_DIM:],
            ],
            axis=-1,
        ).astype(bf16)
        grad_kv = scatter_z([grad_kv[t] for t in range(planes)])
        query_pre = unrotate(grad_q.reshape(plane_tokens, GROUP_HEADS, HEAD_DIM), cosine, sine)
        query_pre = query_pre.reshape(plane_tokens, q_width).astype(bf16)
        key_pre = unrotate(grad_kv[:, None, :HEAD_DIM], cosine, sine)[:, 0]
        kv_pre = jnp.concatenate([key_pre, grad_kv[:, HEAD_DIM:]], axis=1).astype(bf16)
        pre = [
            jnp.concatenate(
                [query_pre[:, i * cut : (i + 1) * cut], pick(kv_pre, i, n_dp, 1)], axis=1
            )
            for i in range(n_dp)
        ]
        mixed = after(mixed, kv_pre)
        outputs = (x_mid + mixed).astype(bf16).reshape(seqs, rows, width)

        grad_low_one = functools.reduce(
            jnp.add, [dot(pre[i], qkv_full[i], ((1,), (1,))) for i in range(n_dp)]
        ).astype(bf16)
        inner_one = scatter_w([grad_low_one[j * tokens : (j + 1) * tokens] for j in range(GROUP)])
        grad_inputs = grad_x_mid + norm_back(inner_one, normed_one, inverse_one)
        grad_inputs = grad_inputs.reshape(seqs, rows, width)

        qkv_sum = dot(
            gather_dp(low_one),
            exchange_dp(after(jnp.concatenate(pre, axis=1), grad_low_one), c, 1),
            ((0,), (0,)),
        ).astype(bf16)
        qkv_sum = lax.psum_scatter(
            after(qkv_sum, out_sum), "seq", axis_index_groups=across, tiled=True
        )
        qkv_sum = qkv_sum.reshape(GROUP, shard, part_width)
        qkv_sum = lax.all_to_all(qkv_sum, "seq", 0, 0, axis_index_groups=in_plane, tiled=True)
        qkv_sum = collect_dp(qkv_sum, c)
        q_sum = jnp.concatenate(
            [one[j][:, :cut] for j in range(GROUP) for one in qkv_sum], axis=1
        ).astype(f32)
        kv_sum = jnp.concatenate(
            [one[j][:, cut:] for j in range(GROUP) for one in qkv_sum], axis=1
        ).astype(f32).reshape(shard, GROUP, PAIR)
        k_sum = kv_sum[..., :HEAD_DIM].reshape(shard, GROUP * HEAD_DIM)
        v_sum = kv_sum[..., HEAD_DIM:].reshape(shard, GROUP * HEAD_DIM)

        grad_w_down = jnp.concatenate(collect_dp(down_sum, c), axis=1).astype(f32)
        gate_up_rows = jnp.zeros((planes, piece, ff_block), bf16)
        for t in range(planes):
            block = lax.dynamic_index_in_dim(gate_up_sum, (p + t) % planes, 0, keepdims=False)
            block = shift_z(block, t) if t else block
            gate_up_rows = lax.dynamic_update_index_in_dim(gate_up_rows, block, (p - t) % planes, 0)
        gate_up_rows = collect_dp(gate_up_rows, c)

        def rows_of(members):
            wide = [jnp.concatenate([one[i] for i in range(planes)], axis=1) for one in members]
            return jnp.concatenate(wide, axis=0).astype(f32)

        gate_rows = rows_of(gate_up_rows[:halves])
        up_rows = rows_of(gate_up_rows[halves:])
        grad_w_gate = gate_rows * gain_two
        grad_w_up = up_rows * gain_two
        grad_gain_mlp = jnp.sum(
            gate_rows * w_gate.astype(f32) + up_rows * w_up.astype(f32), axis=1
        )
        grad_gain_attn = (
            jnp.sum(q_sum * w_query.astype(f32), axis=1)
            + jnp.sum(k_sum * w_key.astype(f32), axis=1)
            + jnp.sum(v_sum * w_value.astype(f32), axis=1)
        )

        return (
            outputs,
            grad_inputs,
            grad_gain_attn,
            q_sum * gain_one,
            k_sum * gain_one,
            v_sum * gain_one,
            grad_w_out,
            grad_gain_mlp,
            grad_w_gate,
            grad_w_up,
            grad_w_down,
        )

    tokens_spec = P("dp", "seq", None)
    in_specs = (
        tokens_spec,
        P("dp", "seq"),
        P("dp", "seq"),
        tokens_spec,
        P("seq"),
        P("seq", None),
        P("seq", None),
        P("seq", None),
        P("seq", None),
        P("seq"),
        P("seq", None),
        P("seq", None),
        P("seq", None),
    )
    out_specs = (
        tokens_spec,
        tokens_spec,
        P("seq"),
        P("seq", None),
        P("seq", None),
        P("seq", None),
        P("seq", None),
        P("seq"),
        P("seq", None),
        P("seq", None),
        P("seq", None),
    )
    return jax.shard_map(body, mesh=mesh, in_specs=in_specs, out_specs=out_specs, check_vma=False)
```

```python
import functools

import jax
import jax.numpy as jnp
from jax import lax
from jax.experimental import pallas as pl
from jax.experimental.pallas import tpu as pltpu
from jax.sharding import PartitionSpec as P

HEADS = 32
KV_HEADS = 4
HEAD_DIM = 64
GROUP = KV_HEADS
GROUP_HEADS = HEADS // GROUP
PAIR = 2 * HEAD_DIM

epsilon = 1e-05
rope_base = 10000.0
masked_score = -1e30

f32 = jnp.float32
bf16 = jnp.bfloat16


def dot(left, right, contract=((1,), (0,))):
    return lax.dot_general(left, right, (contract, ((), ())), preferred_element_type=f32)


def stack_heads(block, rows):
    lane = lax.broadcasted_iota(jnp.int32, (rows, PAIR), 1)
    parts = []
    for pair in range(GROUP_HEADS // 2):
        both = block[:, pair * PAIR : (pair + 1) * PAIR]
        parts.append(jnp.where(lane < HEAD_DIM, both, jnp.zeros_like(both)))
        parts.append(jnp.where(lane >= HEAD_DIM, both, jnp.zeros_like(both)))
    return jnp.concatenate(parts, axis=0)


def unstack_heads(stacked, rows):
    lane = lax.broadcasted_iota(jnp.int32, (rows, PAIR), 1)
    parts = []
    for pair in range(GROUP_HEADS // 2):
        low = stacked[2 * pair * rows : (2 * pair + 1) * rows]
        high = stacked[(2 * pair + 1) * rows : (2 * pair + 2) * rows]
        parts.append(jnp.where(lane < HEAD_DIM, low, high))
    return jnp.concatenate(parts, axis=1)


def as_row(column):
    wide = jnp.broadcast_to(column, (column.shape[0], 128))
    return jnp.transpose(wide)[:8]


def attend_kernel(seen_ref, q_ref, kk_ref, vv_ref, qpos_ref, kpos_ref, o_ref, lse_ref):
    rows = q_ref.shape[0]
    stacked = stack_heads(q_ref[...], rows)
    qpos = jnp.concatenate([qpos_ref[...]] * GROUP_HEADS, axis=0)

    def unit(index, carry, masked):
        top, total, acc = carry
        scores = dot(stacked, kk_ref[index], ((1,), (1,)))
        if masked:
            scores = jnp.where(kpos_ref[...] <= qpos, scores, masked_score)
        new_top = jnp.maximum(top, jnp.max(scores, axis=1, keepdims=True))
        weights = jnp.exp(scores - new_top)
        keep = jnp.exp(top - new_top)
        total = total * keep + jnp.sum(weights, axis=1, keepdims=True)
        acc = acc * keep + dot(weights.astype(bf16), vv_ref[index])
        return new_top, total, acc

    count = GROUP_HEADS * rows
    start = (
        jnp.full((count, 1), masked_score, f32),
        jnp.zeros((count, 1), f32),
        jnp.zeros((count, PAIR), f32),
    )
    carry = unit(0, start, True)
    top, total, acc = lax.fori_loop(1, seen_ref[0], lambda i, c: unit(i, c, False), carry)
    o_ref[...] = unstack_heads(acc / total, rows).astype(bf16)
    lse_ref[...] = as_row(top + jnp.log(total))


def attend_back_kernel(
    seen_ref, q_ref, do_ref, o_ref, kk_ref, vv_ref, lse_ref, qpos_ref, kpos_ref,
    dq_ref, dkk_ref, dvv_ref, qs_ref, dos_ref, delta_ref, dqs_ref,
):
    rows = q_ref.shape[0]

    @pl.when(pl.program_id(0) == 0)
    def _():
        dkk_ref[...] = jnp.zeros_like(dkk_ref)
        dvv_ref[...] = jnp.zeros_like(dvv_ref)

    qs_ref[...] = stack_heads(q_ref[...], rows)
    grads = stack_heads(do_ref[...], rows)
    dos_ref[...] = grads
    outs = stack_heads(o_ref[...], rows)
    delta_ref[...] = as_row(jnp.sum(grads.astype(f32) * outs.astype(f32), axis=1, keepdims=True))

    def unit(index, masked):
        keys = kk_ref[index]
        scores = dot(keys, qs_ref[...], ((1,), (1,)))
        if masked:
            qpos = jnp.concatenate([qpos_ref[0:1, :]] * GROUP_HEADS, axis=1)
            scores = jnp.where(kpos_ref[...] <= qpos, scores, masked_score)
        probs = jnp.exp(scores - lse_ref[0:1, :])
        prob_grad = dot(vv_ref[index], dos_ref[...], ((1,), (1,)))
        score_grad = (probs * (prob_grad - delta_ref[0:1, :])).astype(bf16)
        dvv_ref[index] += dot(probs.astype(bf16), dos_ref[...])
        dkk_ref[index] += dot(score_grad, qs_ref[...])
        return dot(score_grad, keys, ((0,), (0,)))

    dqs_ref[...] = unit(0, True)

    @pl.loop(1, seen_ref[0])
    def _(index):
        dqs_ref[...] += unit(index, False)

    dq_ref[...] = unstack_heads(dqs_ref[...], rows)


def block_rows(length):
    return min(128, length)


def whole(shape):
    zeros = (0,) * len(shape)
    return pl.BlockSpec(shape, lambda i, seen: zeros)


def attend(seen, q, kk, vv, order):
    length, width = q.shape
    rows = block_rows(length)
    stacked = GROUP_HEADS * rows
    steps = length // rows
    return pl.pallas_call(
        attend_kernel,
        out_shape=(
            jax.ShapeDtypeStruct((length, width), bf16),
            jax.ShapeDtypeStruct((steps, 8, stacked), f32),
        ),
        grid_spec=pltpu.PrefetchScalarGridSpec(
            num_scalar_prefetch=1,
            grid=(steps,),
            in_specs=[
                pl.BlockSpec((rows, width), lambda i, seen: (i, 0)),
                whole(kk.shape),
                whole(vv.shape),
                pl.BlockSpec((rows, 1), lambda i, seen: (i, 0)),
                whole((1, length)),
            ],
            out_specs=[
                pl.BlockSpec((rows, width), lambda i, seen: (i, 0)),
                pl.BlockSpec((pl.Squeezed(), 8, stacked), lambda i, seen: (i, 0, 0)),
            ],
        ),
        name="attend",
    )(seen, q, kk, vv, order[:, None], order[None, :])


def attend_back(seen, q, do, o, kk, vv, lse, order):
    length, width = q.shape
    rows = block_rows(length)
    stacked = GROUP_HEADS * rows
    steps = length // rows
    return pl.pallas_call(
        attend_back_kernel,
        out_shape=(
            jax.ShapeDtypeStruct((length, width), f32),
            jax.ShapeDtypeStruct(kk.shape, f32),
            jax.ShapeDtypeStruct(vv.shape, f32),
        ),
        grid_spec=pltpu.PrefetchScalarGridSpec(
            num_scalar_prefetch=1,
            grid=(steps,),
            in_specs=[
                pl.BlockSpec((rows, width), lambda i, seen: (i, 0)),
                pl.BlockSpec((rows, width), lambda i, seen: (i, 0)),
                pl.BlockSpec((rows, width), lambda i, seen: (i, 0)),
                whole(kk.shape),
                whole(vv.shape),
                pl.BlockSpec((pl.Squeezed(), 8, stacked), lambda i, seen: (i, 0, 0)),
                pl.BlockSpec((8, rows), lambda i, seen: (0, i)),
                whole((length, 1)),
            ],
            out_specs=[
                pl.BlockSpec((rows, width), lambda i, seen: (i, 0)),
                whole(kk.shape),
                whole(vv.shape),
            ],
            scratch_shapes=[
                pltpu.VMEM((stacked, PAIR), bf16),
                pltpu.VMEM((stacked, PAIR), bf16),
                pltpu.VMEM((8, stacked), f32),
                pltpu.VMEM((stacked, PAIR), f32),
            ],
        ),
        name="attend_back",
    )(seen, q, do, o, kk, vv, lse, jnp.broadcast_to(order[None, :], (8, length)), order[:, None])


def normalize(values):
    inverse = lax.rsqrt(jnp.mean(values * values, axis=-1, keepdims=True) + epsilon)
    return values * inverse, inverse


def norm_back(inner, normed, inverse):
    return inverse * (inner - normed * jnp.mean(inner * normed, axis=-1, keepdims=True))


def rope_tables(positions):
    half_dim = HEAD_DIM // 2
    frequency = rope_base ** (-(jnp.arange(half_dim).astype(f32) * 2.0 / HEAD_DIM))
    angles = positions.astype(f32)[:, None] * frequency
    angles = jnp.concatenate([angles, angles], axis=-1)
    return jnp.cos(angles)[:, None, :], jnp.sin(angles)[:, None, :]


def turn(values):
    half_dim = HEAD_DIM // 2
    return jnp.concatenate([-values[..., half_dim:], values[..., :half_dim]], axis=-1)


def rotate(values, cosine, sine):
    return values * cosine + turn(values) * sine


def unrotate(grads, cosine, sine):
    return grads * cosine - turn(grads * sine)


def after(value, *earlier):
    return lax.optimization_barrier((value,) + earlier)[0]


def solution(mesh):
    n_dp = mesh.shape["dp"]
    n_seq = mesh.shape["seq"]
    planes = n_seq // GROUP
    halves = n_dp // 2
    both = ("dp", "seq")

    in_plane = [[GROUP * p + w for w in range(GROUP)] for p in range(planes)]
    across_dp = [
        [c * n_seq + GROUP * p + w for c in range(n_dp) for p in range(planes)] for w in range(GROUP)
    ]
    in_plane_dp = [
        [c * n_seq + GROUP * p + w for c in range(n_dp) for w in range(GROUP)] for p in range(planes)
    ]
    across = [[GROUP * p + w for p in range(planes)] for w in range(GROUP)]

    def xor_w(value, j):
        return lax.ppermute(value, "seq", [(s, s ^ j) for s in range(n_seq)])

    def shift_z(value, t):
        return lax.ppermute(value, "seq", [(s, (s + GROUP * t) % n_seq) for s in range(n_seq)])

    def shift_dp(value, t):
        return lax.ppermute(value, "dp", [(c, (c + t) % n_dp) for c in range(n_dp)])

    def gather_w(value):
        first = xor_w(value, 1)
        second = xor_w(value, 2)
        half = value.shape[0] // 2
        third = jnp.concatenate([xor_w(first[:half], 2), xor_w(second[half:], 1)], axis=0)
        return jnp.concatenate([value, first, second, third], axis=0)

    def scatter_w(slots):
        got = [xor_w(slots[j], j) for j in range(1, GROUP)]
        return functools.reduce(jnp.add, [g.astype(f32) for g in got], slots[0].astype(f32))

    def gather_z(value):
        return [value] + [shift_z(value, t) for t in range(1, planes)]

    def scatter_z(slots):
        got = [shift_z(slots[t], -t) for t in range(1, planes)]
        return functools.reduce(jnp.add, [g.astype(f32) for g in got], slots[0].astype(f32))

    def gather_dp(value):
        return jnp.concatenate([value] + [shift_dp(value, t) for t in range(1, n_dp)], axis=0)

    def pick(value, index, count, axis):
        size = value.shape[axis] // count
        return lax.dynamic_slice_in_dim(value, index * size, size, axis)

    def exchange_dp(value, c, axis):
        parts = [pick(value, c, n_dp, axis)]
        for t in range(1, n_dp):
            parts.append(shift_dp(pick(value, (c + t) % n_dp, n_dp, axis), t))
        return jnp.concatenate(parts, axis=0)

    def collect_dp(value, c):
        slots = [value] + [shift_dp(value, t) for t in range(1, n_dp)]
        out = []
        for member in range(n_dp):
            chosen = slots[0]
            for t in range(1, n_dp):
                chosen = jnp.where((c - t) % n_dp == member, slots[t], chosen)
            out.append(chosen)
        return out

    def body(
        inputs, positions, select, cotangent, gain_attn, w_query, w_key, w_value, w_out, gain_mlp,
        w_gate, w_up, w_down,
    ):
        seqs, rows, width = inputs.shape
        tokens = seqs * rows
        shard = w_query.shape[0]
        ff_rows = w_down.shape[0]
        ff_block = w_gate.shape[1] // planes
        q_width = GROUP_HEADS * HEAD_DIM
        s = lax.axis_index("seq")
        c = lax.axis_index("dp")
        p = s // GROUP
        w = s % GROUP

        gain_one = gain_attn.astype(f32)[:, None]
        gain_two = gain_mlp.astype(f32)[:, None]

        def scaled(weight, gain):
            return (weight.astype(f32) * gain).astype(bf16)

        q_cols = scaled(w_query, gain_one).reshape(shard, GROUP, n_dp, q_width // n_dp)
        kv_cols = jnp.concatenate(
            [
                scaled(w_key, gain_one).reshape(shard, GROUP, HEAD_DIM),
                scaled(w_value, gain_one).reshape(shard, GROUP, HEAD_DIM),
            ],
            axis=-1,
        ).reshape(shard, GROUP, n_dp, PAIR // n_dp)
        qkv_cols = jnp.concatenate([q_cols, kv_cols], axis=-1)
        qkv_part = lax.dynamic_index_in_dim(qkv_cols, c, 2, keepdims=False)
        qkv_part = lax.all_to_all(
            jnp.transpose(qkv_part, (1, 0, 2)), "seq", 0, 0, axis_index_groups=in_plane, tiled=True
        )
        part_width = (q_width + PAIR) // n_dp
        qkv_part = qkv_part.reshape(GROUP * shard, part_width)
        ring = [qkv_part] + [shift_z(qkv_part, -t) for t in range(1, planes)]
        qkv_ring = jnp.concatenate(ring + ring[: planes - 1], axis=0)
        qkv_mine = lax.dynamic_slice_in_dim(
            qkv_ring, ((planes - p) % planes) * GROUP * shard, width, 0
        )
        qkv_full = collect_dp(qkv_mine, c)

        x_in = inputs.reshape(tokens, width).astype(f32)
        normed_one, inverse_one = normalize(x_in)
        low_one = gather_w(after(normed_one.astype(bf16), qkv_part))

        out_part = lax.ppermute(
            after(pick(w_out, c, n_dp, 1), low_one, qkv_mine),
            "seq",
            [(i, GROUP * (i % planes) + i // planes) for i in range(n_seq)],
        )
        down_full = lax.all_gather(
            pick(w_down, c, n_dp, 1), both, axis_index_groups=in_plane_dp, tiled=False
        )
        down_full = down_full.reshape(n_dp, ff_block, width // n_dp)
        out_full = lax.all_gather(
            after(out_part, down_full), both, axis_index_groups=across_dp, tiled=False
        )
        out_full = out_full.reshape(n_dp, planes * shard, width // n_dp)

        piece = shard // halves
        gate_up = jnp.where(c // halves == 0, scaled(w_gate, gain_two), scaled(w_up, gain_two))
        gate_up = after(pick(gate_up, c % halves, halves, 0), low_one, qkv_mine)
        gate_up_sent = [
            shift_z(pick(gate_up, (p + t) % planes, planes, 1), t) if t
            else pick(gate_up, p, planes, 1)
            for t in range(planes)
        ]

        blocks = [
            (i * GROUP + j) * halves + h
            for h in range(halves) for j in range(GROUP) for i in range(planes)
        ]

        def column_blocks(value, which):
            return jnp.concatenate([value[:, i * piece : (i + 1) * piece] for i in which], axis=1)

        def reorder(value):
            return column_blocks(value, blocks)

        def order_back(value):
            return column_blocks(value, [blocks.index(i) for i in range(len(blocks))])

        own_pos = positions.reshape(1, tokens)
        plane_pos = jnp.concatenate([own_pos] + [xor_w(own_pos, j) for j in range(1, GROUP)], axis=1)
        cosine, sine = rope_tables(plane_pos.reshape(GROUP * tokens))

        grad_y = (
            cotangent.astype(f32) * select.astype(f32)[..., None]
        ).reshape(tokens, width)
        projected = [dot(low_one, qkv_full[i]) for i in range(n_dp)]
        cut = q_width // n_dp
        q = jnp.concatenate([one[:, :cut] for one in projected], axis=1)
        kv = jnp.concatenate([one[:, cut:] for one in projected], axis=1)
        plane_tokens = GROUP * tokens
        q = rotate(q.reshape(plane_tokens, GROUP_HEADS, HEAD_DIM), cosine, sine)
        q = (q.astype(bf16).astype(f32) * HEAD_DIM ** (-0.5)).astype(bf16).reshape(plane_tokens, q_width)
        k = rotate(kv[:, None, :HEAD_DIM], cosine, sine)[:, 0]
        kv_low = jnp.concatenate([k, kv[:, HEAD_DIM:]], axis=1).astype(bf16)
        kv_sent = gather_z(kv_low)
        gate_up_part = jnp.zeros((planes, piece, ff_block), bf16)
        for t in range(planes):
            gate_up_part = lax.dynamic_update_index_in_dim(
                gate_up_part, after(gate_up_sent[t], kv_low), (p - t) % planes, 0
            )
        gate_up_full = lax.all_gather(
            after(gate_up_part, out_part), both, axis_index_groups=in_plane_dp, tiled=False
        )
        gate_up_full = gate_up_full.reshape(2, width, ff_block)
        gate_full = gate_up_full[0]
        up_full = gate_up_full[1]
        kv_all = jnp.stack(kv_sent)
        grad_y_all = jnp.concatenate(gather_z(after(grad_y.astype(bf16), kv_all, gate_up_part)), axis=0)
        kk = jnp.concatenate([kv_all[..., :HEAD_DIM]] * 2, axis=-1)
        vv = jnp.concatenate([kv_all[..., HEAD_DIM:]] * 2, axis=-1)

        def by_seq(value, axis):
            shape = value.shape
            value = value.reshape(shape[:axis] + (GROUP, seqs, rows) + shape[axis + 1 :])
            value = jnp.moveaxis(value, axis + 1, 0)
            return value.reshape((seqs,) + shape[:axis] + (GROUP * rows,) + shape[axis + 1 :])

        def from_seq(value, axis):
            shape = value.shape[1:]
            value = value.reshape((seqs,) + shape[:axis] + (GROUP, rows) + shape[axis + 1 :])
            value = jnp.moveaxis(value, 0, axis + 1)
            return value.reshape(shape[:axis] + (GROUP * seqs * rows,) + shape[axis + 1 :])

        order = jnp.concatenate([(w ^ j) * rows + jnp.arange(rows) for j in range(GROUP)])
        order = order.astype(jnp.int32)
        seen = (p + 1).astype(jnp.int32).reshape(1)
        q_seq = by_seq(q, 0)
        kk_seq = by_seq(kk, 1)
        vv_seq = by_seq(vv, 1)
        pieces = [attend(seen, q_seq[i], kk_seq[i], vv_seq[i], order) for i in range(seqs)]
        o_seq = [one[0] for one in pieces]
        lse_seq = [one[1] for one in pieces]
        o = from_seq(jnp.stack(o_seq), 0)

        branch = jnp.concatenate([dot(o, out_full[i]).astype(bf16) for i in range(n_dp)], axis=1)
        branch = scatter_w([branch[j * tokens : (j + 1) * tokens] for j in range(GROUP)])
        x_mid = x_in + branch

        normed_two, inverse_two = normalize(x_mid)
        low_two = reorder(normed_two.astype(bf16))
        low_two = jnp.concatenate(gather_z(after(low_two, grad_y_all)), axis=0)
        gate = dot(low_two, gate_full)
        up_part = dot(low_two, up_full)
        sigmoid_gate = 1.0 / (1.0 + jnp.exp(-gate))
        hidden = (gate * sigmoid_gate * up_part).astype(bf16)

        grad_hidden = functools.reduce(
            jnp.add,
            [
                dot(pick(grad_y_all, i, n_dp, 1), down_full[i], ((1,), (1,)))
                for i in range(n_dp)
            ],
        )
        grad_gate = (
            grad_hidden * up_part * sigmoid_gate * (1.0 + gate * (1.0 - sigmoid_gate))
        ).astype(bf16)
        grad_up = (grad_hidden * gate * sigmoid_gate).astype(bf16)
        grad_low_two = dot(grad_gate, gate_full, ((1,), (1,))) + dot(
            grad_up, up_full, ((1,), (1,))
        )
        grad_low_two = grad_low_two.astype(bf16)
        inner_two = scatter_z([grad_low_two[t * tokens : (t + 1) * tokens] for t in range(planes)])

        hidden_later = after(hidden, grad_low_two)
        hidden_all = gather_dp(hidden_later)
        down_sum = dot(hidden_all, exchange_dp(grad_y_all, c, 1), ((0,), (0,))).astype(bf16)

        low_two_all = gather_dp(low_two)
        if halves > 1:
            low_two_all = pick(low_two_all, c % halves, halves, 1)

        def of_member(member):
            return jnp.where(member // halves == 0, grad_gate, grad_up)

        gate_up_grads = [of_member(c)]
        for t in range(1, n_dp):
            gate_up_grads.append(shift_dp(of_member((c + t) % n_dp), t))
        gate_up_grads = after(jnp.concatenate(gate_up_grads, axis=0), grad_low_two)
        gate_up_sum = dot(low_two_all, gate_up_grads, ((0,), (0,))).astype(bf16)

        mixed = jnp.concatenate(
            [dot(hidden_later, down_full[i]).astype(bf16) for i in range(n_dp)], axis=1
        )
        inner_two = after(inner_two, down_sum, gate_up_sum, mixed)
        grad_x_mid = grad_y + norm_back(order_back(inner_two), normed_two, inverse_two)

        mixed = after(mixed, grad_x_mid)
        mixed_sent = [shift_z(mixed[t * tokens : (t + 1) * tokens], -t) for t in range(1, planes)]
        gate_up_sum = lax.psum_scatter(gate_up_sum, "seq", axis_index_groups=in_plane, tiled=True)
        down_sum = lax.psum_scatter(
            down_sum, "seq", axis_index_groups=in_plane, tiled=True
        )
        gate_up_sum = gate_up_sum.reshape(planes, piece, ff_block)

        grad_branch = gather_w(grad_x_mid.astype(bf16))
        grad_o = functools.reduce(
            jnp.add,
            [dot(pick(grad_branch, i, n_dp, 1), out_full[i], ((1,), (1,))) for i in range(n_dp)],
        ).astype(bf16)

        out_part_sum = dot(gather_dp(o), exchange_dp(grad_branch, c, 1), ((0,), (0,))).astype(bf16)
        out_sum = lax.psum_scatter(
            after(out_part_sum, down_sum, gate_up_sum), "seq", axis_index_groups=across, tiled=True
        )
        out_sum = lax.ppermute(
            out_sum, "seq", [(GROUP * (i % planes) + i // planes, i) for i in range(n_seq)]
        )
        grad_w_out = jnp.concatenate(collect_dp(out_sum, c), axis=1).astype(f32)

        grad_o_seq = by_seq(grad_o, 0)
        mixed = functools.reduce(
            jnp.add,
            [after(g, grad_branch).astype(f32) for g in mixed_sent],
            mixed[:tokens].astype(f32),
        )
        grad_o_seq = after(grad_o_seq, out_part_sum, mixed)
        pieces = [
            attend_back(
                seen, q_seq[i], grad_o_seq[i], o_seq[i], kk_seq[i], vv_seq[i], lse_seq[i], order
            )
            for i in range(seqs)
        ]
        grad_q = from_seq(jnp.stack([one[0] for one in pieces]), 0) * HEAD_DIM ** (-0.5)
        grad_kk = from_seq(jnp.stack([one[1] for one in pieces]), 1)
        grad_vv = from_seq(jnp.stack([one[2] for one in pieces]), 1)
        grad_kv = jnp.concatenate(
            [
                grad_kk[..., :HEAD_DIM] + grad_kk[..., HEAD_DIM:],
                grad_vv[..., :HEAD_DIM] + grad_vv[..., HEAD_DIM:],
            ],
            axis=-1,
        ).astype(bf16)
        grad_kv = scatter_z([grad_kv[t] for t in range(planes)])
        query_pre = unrotate(grad_q.reshape(plane_tokens, GROUP_HEADS, HEAD_DIM), cosine, sine)
        query_pre = query_pre.reshape(plane_tokens, q_width).astype(bf16)
        key_pre = unrotate(grad_kv[:, None, :HEAD_DIM], cosine, sine)[:, 0]
        kv_pre = jnp.concatenate([key_pre, grad_kv[:, HEAD_DIM:]], axis=1).astype(bf16)
        pre = [
            jnp.concatenate(
                [query_pre[:, i * cut : (i + 1) * cut], pick(kv_pre, i, n_dp, 1)], axis=1
            )
            for i in range(n_dp)
        ]
        mixed = after(mixed, kv_pre)
        outputs = (x_mid + mixed).astype(bf16).reshape(seqs, rows, width)

        grad_low_one = functools.reduce(
            jnp.add, [dot(pre[i], qkv_full[i], ((1,), (1,))) for i in range(n_dp)]
        ).astype(bf16)
        inner_one = scatter_w([grad_low_one[j * tokens : (j + 1) * tokens] for j in range(GROUP)])
        grad_inputs = grad_x_mid + norm_back(inner_one, normed_one, inverse_one)
        grad_inputs = grad_inputs.reshape(seqs, rows, width)

        qkv_sum = dot(
            gather_dp(low_one),
            exchange_dp(after(jnp.concatenate(pre, axis=1), grad_low_one), c, 1),
            ((0,), (0,)),
        ).astype(bf16)
        gate_up_late = after(gate_up_sum, qkv_sum)
        qkv_sum = lax.psum_scatter(
            after(qkv_sum, out_sum), "seq", axis_index_groups=across, tiled=True
        )
        qkv_sum = qkv_sum.reshape(GROUP, shard, part_width)
        qkv_sum = lax.all_to_all(qkv_sum, "seq", 0, 0, axis_index_groups=in_plane, tiled=True)
        qkv_sum = collect_dp(qkv_sum, c)
        q_sum = jnp.concatenate(
            [one[j][:, :cut] for j in range(GROUP) for one in qkv_sum], axis=1
        ).astype(f32)
        kv_sum = jnp.concatenate(
            [one[j][:, cut:] for j in range(GROUP) for one in qkv_sum], axis=1
        ).astype(f32).reshape(shard, GROUP, PAIR)
        k_sum = kv_sum[..., :HEAD_DIM].reshape(shard, GROUP * HEAD_DIM)
        v_sum = kv_sum[..., HEAD_DIM:].reshape(shard, GROUP * HEAD_DIM)

        grad_w_down = jnp.concatenate(collect_dp(down_sum, c), axis=1).astype(f32)
        gate_up_rows = jnp.zeros((planes, piece, ff_block), bf16)
        sent = []
        for t in range(planes):
            block = lax.dynamic_index_in_dim(gate_up_late, (p + t) % planes, 0, keepdims=False)
            sent.append(shift_z(block, t) if t else block)
        sent = lax.optimization_barrier(tuple(sent))
        for t in range(planes):
            gate_up_rows = lax.dynamic_update_index_in_dim(
                gate_up_rows, sent[t], (p - t) % planes, 0
            )
        gate_up_rows = collect_dp(gate_up_rows, c)

        def rows_of(members):
            wide = [jnp.concatenate([one[i] for i in range(planes)], axis=1) for one in members]
            return jnp.concatenate(wide, axis=0).astype(f32)

        gate_rows = rows_of(gate_up_rows[:halves])
        up_rows = rows_of(gate_up_rows[halves:])
        grad_w_gate = gate_rows * gain_two
        grad_w_up = up_rows * gain_two
        grad_gain_mlp = jnp.sum(
            gate_rows * w_gate.astype(f32) + up_rows * w_up.astype(f32), axis=1
        )
        grad_gain_attn = (
            jnp.sum(q_sum * w_query.astype(f32), axis=1)
            + jnp.sum(k_sum * w_key.astype(f32), axis=1)
            + jnp.sum(v_sum * w_value.astype(f32), axis=1)
        )

        return (
            outputs,
            grad_inputs,
            grad_gain_attn,
            q_sum * gain_one,
            k_sum * gain_one,
            v_sum * gain_one,
            grad_w_out,
            grad_gain_mlp,
            grad_w_gate,
            grad_w_up,
            grad_w_down,
        )

    tokens_spec = P("dp", "seq", None)
    in_specs = (
        tokens_spec,
        P("dp", "seq"),
        P("dp", "seq"),
        tokens_spec,
        P("seq"),
        P("seq", None),
        P("seq", None),
        P("seq", None),
        P("seq", None),
        P("seq"),
        P("seq", None),
        P("seq", None),
        P("seq", None),
    )
    out_specs = (
        tokens_spec,
        tokens_spec,
        P("seq"),
        P("seq", None),
        P("seq", None),
        P("seq", None),
        P("seq", None),
        P("seq"),
        P("seq", None),
        P("seq", None),
        P("seq", None),
    )
    return jax.shard_map(body, mesh=mesh, in_specs=in_specs, out_specs=out_specs, check_vma=False)
```

```python
import functools

import jax
import jax.numpy as jnp
from jax import lax
from jax.experimental import pallas as pl
from jax.experimental.pallas import tpu as pltpu
from jax.sharding import PartitionSpec as P

HEADS = 32
KV_HEADS = 4
HEAD_DIM = 64
GROUP = KV_HEADS
GROUP_HEADS = HEADS // GROUP
PAIR = 2 * HEAD_DIM

epsilon = 1e-05
rope_base = 10000.0
masked_score = -1e30

f32 = jnp.float32
bf16 = jnp.bfloat16


def dot(left, right, contract=((1,), (0,))):
    return lax.dot_general(left, right, (contract, ((), ())), preferred_element_type=f32)


def stack_heads(block, rows):
    lane = lax.broadcasted_iota(jnp.int32, (rows, PAIR), 1)
    parts = []
    for pair in range(GROUP_HEADS // 2):
        both = block[:, pair * PAIR : (pair + 1) * PAIR]
        parts.append(jnp.where(lane < HEAD_DIM, both, jnp.zeros_like(both)))
        parts.append(jnp.where(lane >= HEAD_DIM, both, jnp.zeros_like(both)))
    return jnp.concatenate(parts, axis=0)


def unstack_heads(stacked, rows):
    lane = lax.broadcasted_iota(jnp.int32, (rows, PAIR), 1)
    parts = []
    for pair in range(GROUP_HEADS // 2):
        low = stacked[2 * pair * rows : (2 * pair + 1) * rows]
        high = stacked[(2 * pair + 1) * rows : (2 * pair + 2) * rows]
        parts.append(jnp.where(lane < HEAD_DIM, low, high))
    return jnp.concatenate(parts, axis=1)


def as_row(column):
    wide = jnp.broadcast_to(column, (column.shape[0], 128))
    return jnp.transpose(wide)[:8]


def attend_kernel(seen_ref, q_ref, kk_ref, vv_ref, qpos_ref, kpos_ref, o_ref, lse_ref):
    rows = q_ref.shape[0]
    stacked = stack_heads(q_ref[...], rows)
    qpos = jnp.concatenate([qpos_ref[...]] * GROUP_HEADS, axis=0)

    def unit(index, carry, masked):
        top, total, acc = carry
        scores = dot(stacked, kk_ref[index], ((1,), (1,)))
        if masked:
            scores = jnp.where(kpos_ref[...] <= qpos, scores, masked_score)
        new_top = jnp.maximum(top, jnp.max(scores, axis=1, keepdims=True))
        weights = jnp.exp(scores - new_top)
        keep = jnp.exp(top - new_top)
        total = total * keep + jnp.sum(weights, axis=1, keepdims=True)
        acc = acc * keep + dot(weights.astype(bf16), vv_ref[index])
        return new_top, total, acc

    count = GROUP_HEADS * rows
    start = (
        jnp.full((count, 1), masked_score, f32),
        jnp.zeros((count, 1), f32),
        jnp.zeros((count, PAIR), f32),
    )
    carry = unit(0, start, True)
    top, total, acc = lax.fori_loop(1, seen_ref[0], lambda i, c: unit(i, c, False), carry)
    o_ref[...] = unstack_heads(acc / total, rows).astype(bf16)
    lse_ref[...] = as_row(top + jnp.log(total))


def attend_back_kernel(
    seen_ref, q_ref, do_ref, o_ref, kk_ref, vv_ref, lse_ref, qpos_ref, kpos_ref,
    dq_ref, dkk_ref, dvv_ref, qs_ref, dos_ref, delta_ref, dqs_ref,
):
    rows = q_ref.shape[0]

    @pl.when(pl.program_id(0) == 0)
    def _():
        dkk_ref[...] = jnp.zeros_like(dkk_ref)
        dvv_ref[...] = jnp.zeros_like(dvv_ref)

    qs_ref[...] = stack_heads(q_ref[...], rows)
    grads = stack_heads(do_ref[...], rows)
    dos_ref[...] = grads
    outs = stack_heads(o_ref[...], rows)
    delta_ref[...] = as_row(jnp.sum(grads.astype(f32) * outs.astype(f32), axis=1, keepdims=True))

    def unit(index, masked):
        keys = kk_ref[index]
        scores = dot(keys, qs_ref[...], ((1,), (1,)))
        if masked:
            qpos = jnp.concatenate([qpos_ref[0:1, :]] * GROUP_HEADS, axis=1)
            scores = jnp.where(kpos_ref[...] <= qpos, scores, masked_score)
        probs = jnp.exp(scores - lse_ref[0:1, :])
        prob_grad = dot(vv_ref[index], dos_ref[...], ((1,), (1,)))
        score_grad = (probs * (prob_grad - delta_ref[0:1, :])).astype(bf16)
        dvv_ref[index] += dot(probs.astype(bf16), dos_ref[...])
        dkk_ref[index] += dot(score_grad, qs_ref[...])
        return dot(score_grad, keys, ((0,), (0,)))

    dqs_ref[...] = unit(0, True)

    @pl.loop(1, seen_ref[0])
    def _(index):
        dqs_ref[...] += unit(index, False)

    dq_ref[...] = unstack_heads(dqs_ref[...], rows)


def block_rows(length):
    return min(128, length)


def whole(shape):
    zeros = (0,) * len(shape)
    return pl.BlockSpec(shape, lambda i, seen: zeros)


def attend(seen, q, kk, vv, order):
    length, width = q.shape
    rows = block_rows(length)
    stacked = GROUP_HEADS * rows
    steps = length // rows
    return pl.pallas_call(
        attend_kernel,
        out_shape=(
            jax.ShapeDtypeStruct((length, width), bf16),
            jax.ShapeDtypeStruct((steps, 8, stacked), f32),
        ),
        grid_spec=pltpu.PrefetchScalarGridSpec(
            num_scalar_prefetch=1,
            grid=(steps,),
            in_specs=[
                pl.BlockSpec((rows, width), lambda i, seen: (i, 0)),
                whole(kk.shape),
                whole(vv.shape),
                pl.BlockSpec((rows, 1), lambda i, seen: (i, 0)),
                whole((1, length)),
            ],
            out_specs=[
                pl.BlockSpec((rows, width), lambda i, seen: (i, 0)),
                pl.BlockSpec((pl.Squeezed(), 8, stacked), lambda i, seen: (i, 0, 0)),
            ],
        ),
        name="attend",
    )(seen, q, kk, vv, order[:, None], order[None, :])


def attend_back(seen, q, do, o, kk, vv, lse, order):
    length, width = q.shape
    rows = block_rows(length)
    stacked = GROUP_HEADS * rows
    steps = length // rows
    return pl.pallas_call(
        attend_back_kernel,
        out_shape=(
            jax.ShapeDtypeStruct((length, width), f32),
            jax.ShapeDtypeStruct(kk.shape, f32),
            jax.ShapeDtypeStruct(vv.shape, f32),
        ),
        grid_spec=pltpu.PrefetchScalarGridSpec(
            num_scalar_prefetch=1,
            grid=(steps,),
            in_specs=[
                pl.BlockSpec((rows, width), lambda i, seen: (i, 0)),
                pl.BlockSpec((rows, width), lambda i, seen: (i, 0)),
                pl.BlockSpec((rows, width), lambda i, seen: (i, 0)),
                whole(kk.shape),
                whole(vv.shape),
                pl.BlockSpec((pl.Squeezed(), 8, stacked), lambda i, seen: (i, 0, 0)),
                pl.BlockSpec((8, rows), lambda i, seen: (0, i)),
                whole((length, 1)),
            ],
            out_specs=[
                pl.BlockSpec((rows, width), lambda i, seen: (i, 0)),
                whole(kk.shape),
                whole(vv.shape),
            ],
            scratch_shapes=[
                pltpu.VMEM((stacked, PAIR), bf16),
                pltpu.VMEM((stacked, PAIR), bf16),
                pltpu.VMEM((8, stacked), f32),
                pltpu.VMEM((stacked, PAIR), f32),
            ],
        ),
        name="attend_back",
    )(seen, q, do, o, kk, vv, lse, jnp.broadcast_to(order[None, :], (8, length)), order[:, None])


def normalize(values):
    inverse = lax.rsqrt(jnp.mean(values * values, axis=-1, keepdims=True) + epsilon)
    return values * inverse, inverse


def norm_back(inner, normed, inverse):
    return inverse * (inner - normed * jnp.mean(inner * normed, axis=-1, keepdims=True))


def rope_tables(positions):
    half_dim = HEAD_DIM // 2
    frequency = rope_base ** (-(jnp.arange(half_dim).astype(f32) * 2.0 / HEAD_DIM))
    angles = positions.astype(f32)[:, None] * frequency
    angles = jnp.concatenate([angles, angles], axis=-1)
    return jnp.cos(angles)[:, None, :], jnp.sin(angles)[:, None, :]


def turn(values):
    half_dim = HEAD_DIM // 2
    return jnp.concatenate([-values[..., half_dim:], values[..., :half_dim]], axis=-1)


def rotate(values, cosine, sine):
    return values * cosine + turn(values) * sine


def unrotate(grads, cosine, sine):
    return grads * cosine - turn(grads * sine)


def tie(*values):
    return lax.optimization_barrier(values)


def solution(mesh):
    n_dp = mesh.shape["dp"]
    n_seq = mesh.shape["seq"]
    planes = n_seq // GROUP
    halves = n_dp // 2
    both = ("dp", "seq")

    in_plane = [[GROUP * p + w for w in range(GROUP)] for p in range(planes)]
    across_dp = [
        [c * n_seq + GROUP * p + w for c in range(n_dp) for p in range(planes)] for w in range(GROUP)
    ]
    in_plane_dp = [
        [c * n_seq + GROUP * p + w for c in range(n_dp) for w in range(GROUP)] for p in range(planes)
    ]
    across = [[GROUP * p + w for p in range(planes)] for w in range(GROUP)]

    def xor_w(value, j):
        return lax.ppermute(value, "seq", [(s, s ^ j) for s in range(n_seq)])

    def shift_z(value, t):
        return lax.ppermute(value, "seq", [(s, (s + GROUP * t) % n_seq) for s in range(n_seq)])

    def shift_dp(value, t):
        return lax.ppermute(value, "dp", [(c, (c + t) % n_dp) for c in range(n_dp)])

    def gather_w(value):
        first = xor_w(value, 1)
        second = xor_w(value, 2)
        half = value.shape[0] // 2
        third = jnp.concatenate([xor_w(first[:half], 2), xor_w(second[half:], 1)], axis=0)
        return jnp.concatenate([value, first, second, third], axis=0)

    def scatter_w(slots):
        got = [xor_w(slots[j], j) for j in range(1, GROUP)]
        return functools.reduce(jnp.add, [g.astype(f32) for g in got], slots[0].astype(f32))

    def gather_z(value):
        return [value] + [shift_z(value, t) for t in range(1, planes)]

    def scatter_z(slots):
        got = [shift_z(slots[t], -t) for t in range(1, planes)]
        return functools.reduce(jnp.add, [g.astype(f32) for g in got], slots[0].astype(f32))

    def gather_dp(value):
        return jnp.concatenate([value] + [shift_dp(value, t) for t in range(1, n_dp)], axis=0)

    def pick(value, index, count, axis):
        size = value.shape[axis] // count
        return lax.dynamic_slice_in_dim(value, index * size, size, axis)

    def exchange_dp(value, c, axis):
        parts = [pick(value, c, n_dp, axis)]
        for t in range(1, n_dp):
            parts.append(shift_dp(pick(value, (c + t) % n_dp, n_dp, axis), t))
        return jnp.concatenate(parts, axis=0)

    def collect_dp(value, c):
        slots = [value] + [shift_dp(value, t) for t in range(1, n_dp)]
        out = []
        for member in range(n_dp):
            chosen = slots[0]
            for t in range(1, n_dp):
                chosen = jnp.where((c - t) % n_dp == member, slots[t], chosen)
            out.append(chosen)
        return out

    def body(
        inputs, positions, select, cotangent, gain_attn, w_query, w_key, w_value, w_out, gain_mlp,
        w_gate, w_up, w_down,
    ):
        seqs, rows, width = inputs.shape
        tokens = seqs * rows
        shard = w_query.shape[0]
        ff_rows = w_down.shape[0]
        ff_block = w_gate.shape[1] // planes
        q_width = GROUP_HEADS * HEAD_DIM
        s = lax.axis_index("seq")
        c = lax.axis_index("dp")
        p = s // GROUP
        w = s % GROUP

        gain_one = gain_attn.astype(f32)[:, None]
        gain_two = gain_mlp.astype(f32)[:, None]

        def scaled(weight, gain):
            return (weight.astype(f32) * gain).astype(bf16)

        q_cols = scaled(w_query, gain_one).reshape(shard, GROUP, n_dp, q_width // n_dp)
        kv_cols = jnp.concatenate(
            [
                scaled(w_key, gain_one).reshape(shard, GROUP, HEAD_DIM),
                scaled(w_value, gain_one).reshape(shard, GROUP, HEAD_DIM),
            ],
            axis=-1,
        ).reshape(shard, GROUP, n_dp, PAIR // n_dp)
        qkv_cols = jnp.concatenate([q_cols, kv_cols], axis=-1)
        qkv_part = lax.dynamic_index_in_dim(qkv_cols, c, 2, keepdims=False)
        qkv_part = lax.all_to_all(
            jnp.transpose(qkv_part, (1, 0, 2)), "seq", 0, 0, axis_index_groups=in_plane, tiled=True
        )
        part_width = (q_width + PAIR) // n_dp
        qkv_part = qkv_part.reshape(GROUP * shard, part_width)
        own_pos = positions.reshape(1, tokens)
        plane_pos = jnp.concatenate([own_pos] + [xor_w(own_pos, j) for j in range(1, GROUP)], axis=1)
        x_in = inputs.reshape(tokens, width).astype(f32)
        normed_one, inverse_one = normalize(x_in)
        low_one, qkv_part, plane_pos = tie(normed_one.astype(bf16), qkv_part, plane_pos)

        ring = [qkv_part] + [shift_z(qkv_part, -t) for t in range(1, planes)]
        qkv_ring = jnp.concatenate(ring + ring[: planes - 1], axis=0)
        qkv_mine = lax.dynamic_slice_in_dim(
            qkv_ring, ((planes - p) % planes) * GROUP * shard, width, 0
        )
        low_one = gather_w(low_one)

        piece = shard // halves
        gate_up = jnp.where(c // halves == 0, scaled(w_gate, gain_two), scaled(w_up, gain_two))
        out_part, gate_up, qkv_mine = tie(
            pick(w_out, c, n_dp, 1), pick(gate_up, c % halves, halves, 0), qkv_mine
        )
        qkv_full = collect_dp(qkv_mine, c)
        out_part = lax.ppermute(
            out_part, "seq", [(i, GROUP * (i % planes) + i // planes) for i in range(n_seq)]
        )
        gate_up_sent = [
            shift_z(pick(gate_up, (p + t) % planes, planes, 1), t) if t
            else pick(gate_up, p, planes, 1)
            for t in range(planes)
        ]
        down_full = lax.all_gather(
            pick(w_down, c, n_dp, 1), both, axis_index_groups=in_plane_dp, tiled=False
        )
        out_part, down_full = tie(out_part, down_full)
        down_full = down_full.reshape(n_dp, ff_block, width // n_dp)
        out_full = lax.all_gather(out_part, both, axis_index_groups=across_dp, tiled=False)
        out_full = out_full.reshape(n_dp, planes * shard, width // n_dp)

        blocks = [
            (i * GROUP + j) * halves + h
            for h in range(halves) for j in range(GROUP) for i in range(planes)
        ]

        def column_blocks(value, which):
            return jnp.concatenate([value[:, i * piece : (i + 1) * piece] for i in which], axis=1)

        def reorder(value):
            return column_blocks(value, blocks)

        def order_back(value):
            return column_blocks(value, [blocks.index(i) for i in range(len(blocks))])

        cosine, sine = rope_tables(plane_pos.reshape(GROUP * tokens))

        grad_y = (
            cotangent.astype(f32) * select.astype(f32)[..., None]
        ).reshape(tokens, width)
        projected = [dot(low_one, qkv_full[i]) for i in range(n_dp)]
        cut = q_width // n_dp
        q = jnp.concatenate([one[:, :cut] for one in projected], axis=1)
        kv = jnp.concatenate([one[:, cut:] for one in projected], axis=1)
        plane_tokens = GROUP * tokens
        q = rotate(q.reshape(plane_tokens, GROUP_HEADS, HEAD_DIM), cosine, sine)
        q = (q.astype(bf16).astype(f32) * HEAD_DIM ** (-0.5)).astype(bf16).reshape(plane_tokens, q_width)
        k = rotate(kv[:, None, :HEAD_DIM], cosine, sine)[:, 0]
        kv_low = jnp.concatenate([k, kv[:, HEAD_DIM:]], axis=1).astype(bf16)
        kv_all = jnp.stack(gather_z(kv_low))
        grad_y_low, kv_all = tie(grad_y.astype(bf16), kv_all)
        *gate_up_sent, q = tie(*gate_up_sent, q)
        gate_up_part = jnp.zeros((planes, piece, ff_block), bf16)
        for t in range(planes):
            gate_up_part = lax.dynamic_update_index_in_dim(
                gate_up_part, gate_up_sent[t], (p - t) % planes, 0
            )
        gate_up_full = lax.all_gather(
            gate_up_part, both, axis_index_groups=in_plane_dp, tiled=False
        )
        gate_up_full = gate_up_full.reshape(2, width, ff_block)
        gate_full = gate_up_full[0]
        up_full = gate_up_full[1]
        grad_y_all = jnp.concatenate(gather_z(grad_y_low), axis=0)
        kk = jnp.concatenate([kv_all[..., :HEAD_DIM]] * 2, axis=-1)
        vv = jnp.concatenate([kv_all[..., HEAD_DIM:]] * 2, axis=-1)

        def by_seq(value, axis):
            shape = value.shape
            value = value.reshape(shape[:axis] + (GROUP, seqs, rows) + shape[axis + 1 :])
            value = jnp.moveaxis(value, axis + 1, 0)
            return value.reshape((seqs,) + shape[:axis] + (GROUP * rows,) + shape[axis + 1 :])

        def from_seq(value, axis):
            shape = value.shape[1:]
            value = value.reshape((seqs,) + shape[:axis] + (GROUP, rows) + shape[axis + 1 :])
            value = jnp.moveaxis(value, 0, axis + 1)
            return value.reshape(shape[:axis] + (GROUP * seqs * rows,) + shape[axis + 1 :])

        order = jnp.concatenate([(w ^ j) * rows + jnp.arange(rows) for j in range(GROUP)])
        order = order.astype(jnp.int32)
        seen = (p + 1).astype(jnp.int32).reshape(1)
        q_seq = by_seq(q, 0)
        kk_seq = by_seq(kk, 1)
        vv_seq = by_seq(vv, 1)
        pieces = [attend(seen, q_seq[i], kk_seq[i], vv_seq[i], order) for i in range(seqs)]
        o_seq = [one[0] for one in pieces]
        lse_seq = [one[1] for one in pieces]
        o = from_seq(jnp.stack(o_seq), 0)

        branch = jnp.concatenate([dot(o, out_full[i]).astype(bf16) for i in range(n_dp)], axis=1)
        branch = scatter_w([branch[j * tokens : (j + 1) * tokens] for j in range(GROUP)])
        x_mid = x_in + branch

        normed_two, inverse_two = normalize(x_mid)
        low_two = reorder(normed_two.astype(bf16))
        low_two, grad_y_all = tie(low_two, grad_y_all)
        low_two = jnp.concatenate(gather_z(low_two), axis=0)
        gate = dot(low_two, gate_full)
        up_part = dot(low_two, up_full)
        sigmoid_gate = 1.0 / (1.0 + jnp.exp(-gate))
        hidden = (gate * sigmoid_gate * up_part).astype(bf16)

        grad_hidden = functools.reduce(
            jnp.add,
            [
                dot(pick(grad_y_all, i, n_dp, 1), down_full[i], ((1,), (1,)))
                for i in range(n_dp)
            ],
        )
        grad_gate = (
            grad_hidden * up_part * sigmoid_gate * (1.0 + gate * (1.0 - sigmoid_gate))
        ).astype(bf16)
        grad_up = (grad_hidden * gate * sigmoid_gate).astype(bf16)
        grad_low_two = dot(grad_gate, gate_full, ((1,), (1,))) + dot(
            grad_up, up_full, ((1,), (1,))
        )
        grad_low_two = grad_low_two.astype(bf16)
        hidden_later, grad_gate_later, grad_up_later, grad_low_two = tie(
            hidden, grad_gate, grad_up, grad_low_two
        )
        inner_sent = [
            shift_z(grad_low_two[t * tokens : (t + 1) * tokens], -t) for t in range(1, planes)
        ]

        hidden_all = gather_dp(hidden_later)
        down_sum = dot(hidden_all, exchange_dp(grad_y_all, c, 1), ((0,), (0,))).astype(bf16)

        low_two_all = gather_dp(low_two)
        if halves > 1:
            low_two_all = pick(low_two_all, c % halves, halves, 1)

        def of_member(member):
            return jnp.where(member // halves == 0, grad_gate_later, grad_up_later)

        gate_up_grads = [of_member(c)]
        for t in range(1, n_dp):
            gate_up_grads.append(shift_dp(of_member((c + t) % n_dp), t))
        gate_up_grads = jnp.concatenate(gate_up_grads, axis=0)
        gate_up_sum = dot(low_two_all, gate_up_grads, ((0,), (0,))).astype(bf16)

        hidden_last, down_sum, gate_up_sum = tie(hidden_later, down_sum, gate_up_sum)
        mixed = jnp.concatenate(
            [dot(hidden_last, down_full[i]).astype(bf16) for i in range(n_dp)], axis=1
        )
        *inner_sent, mixed = tie(*inner_sent, mixed)
        inner_two = functools.reduce(
            jnp.add, [g.astype(f32) for g in inner_sent], grad_low_two[:tokens].astype(f32)
        )
        grad_x_mid = grad_y + norm_back(order_back(inner_two), normed_two, inverse_two)

        mixed, grad_x_low = tie(mixed, grad_x_mid.astype(bf16))
        mixed_sent = [shift_z(mixed[t * tokens : (t + 1) * tokens], -t) for t in range(1, planes)]
        gate_up_sum = lax.psum_scatter(gate_up_sum, "seq", axis_index_groups=in_plane, tiled=True)
        down_sum = lax.psum_scatter(
            down_sum, "seq", axis_index_groups=in_plane, tiled=True
        )
        gate_up_sum = gate_up_sum.reshape(planes, piece, ff_block)

        grad_branch = gather_w(grad_x_low)
        mixed_sent[0], grad_branch = tie(mixed_sent[0], grad_branch)
        grad_o = functools.reduce(
            jnp.add,
            [dot(pick(grad_branch, i, n_dp, 1), out_full[i], ((1,), (1,))) for i in range(n_dp)],
        ).astype(bf16)

        out_part_sum = dot(gather_dp(o), exchange_dp(grad_branch, c, 1), ((0,), (0,))).astype(bf16)
        grad_o_seq = by_seq(grad_o, 0)
        *mixed_sent, grad_o_seq, out_part_sum = tie(*mixed_sent, grad_o_seq, out_part_sum)
        out_sum = lax.psum_scatter(out_part_sum, "seq", axis_index_groups=across, tiled=True)
        out_sum = lax.ppermute(
            out_sum, "seq", [(GROUP * (i % planes) + i // planes, i) for i in range(n_seq)]
        )
        grad_w_out = jnp.concatenate(collect_dp(out_sum, c), axis=1).astype(f32)

        mixed = functools.reduce(
            jnp.add, [g.astype(f32) for g in mixed_sent], mixed[:tokens].astype(f32)
        )
        pieces = [
            attend_back(
                seen, q_seq[i], grad_o_seq[i], o_seq[i], kk_seq[i], vv_seq[i], lse_seq[i], order
            )
            for i in range(seqs)
        ]
        grad_q = from_seq(jnp.stack([one[0] for one in pieces]), 0) * HEAD_DIM ** (-0.5)
        grad_kk = from_seq(jnp.stack([one[1] for one in pieces]), 1)
        grad_vv = from_seq(jnp.stack([one[2] for one in pieces]), 1)
        grad_kv = jnp.concatenate(
            [
                grad_kk[..., :HEAD_DIM] + grad_kk[..., HEAD_DIM:],
                grad_vv[..., :HEAD_DIM] + grad_vv[..., HEAD_DIM:],
            ],
            axis=-1,
        ).astype(bf16)
        grad_kv = scatter_z([grad_kv[t] for t in range(planes)])
        query_pre = unrotate(grad_q.reshape(plane_tokens, GROUP_HEADS, HEAD_DIM), cosine, sine)
        query_pre = query_pre.reshape(plane_tokens, q_width).astype(bf16)
        key_pre = unrotate(grad_kv[:, None, :HEAD_DIM], cosine, sine)[:, 0]
        kv_pre = jnp.concatenate([key_pre, grad_kv[:, HEAD_DIM:]], axis=1).astype(bf16)
        pre = [
            jnp.concatenate(
                [query_pre[:, i * cut : (i + 1) * cut], pick(kv_pre, i, n_dp, 1)], axis=1
            )
            for i in range(n_dp)
        ]
        outputs = (x_mid + mixed).astype(bf16).reshape(seqs, rows, width)

        grad_low_one = functools.reduce(
            jnp.add, [dot(pre[i], qkv_full[i], ((1,), (1,))) for i in range(n_dp)]
        ).astype(bf16)
        inner_one = scatter_w([grad_low_one[j * tokens : (j + 1) * tokens] for j in range(GROUP)])
        grad_inputs = grad_x_mid + norm_back(inner_one, normed_one, inverse_one)
        grad_inputs = grad_inputs.reshape(seqs, rows, width)

        qkv_sum = dot(
            gather_dp(low_one),
            exchange_dp(jnp.concatenate(pre, axis=1), c, 1),
            ((0,), (0,)),
        ).astype(bf16)
        gate_up_late, qkv_sum = tie(gate_up_sum, qkv_sum)
        qkv_sum = lax.psum_scatter(
            qkv_sum, "seq", axis_index_groups=across, tiled=True
        )
        qkv_sum = qkv_sum.reshape(GROUP, shard, part_width)
        qkv_sum = lax.all_to_all(qkv_sum, "seq", 0, 0, axis_index_groups=in_plane, tiled=True)
        qkv_sum = collect_dp(qkv_sum, c)
        q_sum = jnp.concatenate(
            [one[j][:, :cut] for j in range(GROUP) for one in qkv_sum], axis=1
        ).astype(f32)
        kv_sum = jnp.concatenate(
            [one[j][:, cut:] for j in range(GROUP) for one in qkv_sum], axis=1
        ).astype(f32).reshape(shard, GROUP, PAIR)
        k_sum = kv_sum[..., :HEAD_DIM].reshape(shard, GROUP * HEAD_DIM)
        v_sum = kv_sum[..., HEAD_DIM:].reshape(shard, GROUP * HEAD_DIM)

        grad_w_down = jnp.concatenate(collect_dp(down_sum, c), axis=1).astype(f32)
        gate_up_rows = jnp.zeros((planes, piece, ff_block), bf16)
        sent = []
        for t in range(planes):
            block = lax.dynamic_index_in_dim(gate_up_late, (p + t) % planes, 0, keepdims=False)
            sent.append(shift_z(block, t) if t else block)
        sent = lax.optimization_barrier(tuple(sent))
        for t in range(planes):
            gate_up_rows = lax.dynamic_update_index_in_dim(
                gate_up_rows, sent[t], (p - t) % planes, 0
            )
        gate_up_rows = collect_dp(gate_up_rows, c)

        def rows_of(members):
            wide = [jnp.concatenate([one[i] for i in range(planes)], axis=1) for one in members]
            return jnp.concatenate(wide, axis=0).astype(f32)

        gate_rows = rows_of(gate_up_rows[:halves])
        up_rows = rows_of(gate_up_rows[halves:])
        grad_w_gate = gate_rows * gain_two
        grad_w_up = up_rows * gain_two
        grad_gain_mlp = jnp.sum(
            gate_rows * w_gate.astype(f32) + up_rows * w_up.astype(f32), axis=1
        )
        grad_gain_attn = (
            jnp.sum(q_sum * w_query.astype(f32), axis=1)
            + jnp.sum(k_sum * w_key.astype(f32), axis=1)
            + jnp.sum(v_sum * w_value.astype(f32), axis=1)
        )

        return (
            outputs,
            grad_inputs,
            grad_gain_attn,
            q_sum * gain_one,
            k_sum * gain_one,
            v_sum * gain_one,
            grad_w_out,
            grad_gain_mlp,
            grad_w_gate,
            grad_w_up,
            grad_w_down,
        )

    tokens_spec = P("dp", "seq", None)
    in_specs = (
        tokens_spec,
        P("dp", "seq"),
        P("dp", "seq"),
        tokens_spec,
        P("seq"),
        P("seq", None),
        P("seq", None),
        P("seq", None),
        P("seq", None),
        P("seq"),
        P("seq", None),
        P("seq", None),
        P("seq", None),
    )
    out_specs = (
        tokens_spec,
        tokens_spec,
        P("seq"),
        P("seq", None),
        P("seq", None),
        P("seq", None),
        P("seq", None),
        P("seq"),
        P("seq", None),
        P("seq", None),
        P("seq", None),
    )
    return jax.shard_map(body, mesh=mesh, in_specs=in_specs, out_specs=out_specs, check_vma=False)
```

```python
import functools

import jax
import jax.numpy as jnp
from jax import lax
from jax.experimental import pallas as pl
from jax.experimental.pallas import tpu as pltpu
from jax.sharding import PartitionSpec as P

HEADS = 32
KV_HEADS = 4
HEAD_DIM = 64
GROUP = KV_HEADS
GROUP_HEADS = HEADS // GROUP
PAIR = 2 * HEAD_DIM

epsilon = 1e-05
rope_base = 10000.0
masked_score = -1e30

f32 = jnp.float32
bf16 = jnp.bfloat16


def dot(left, right, contract=((1,), (0,))):
    return lax.dot_general(left, right, (contract, ((), ())), preferred_element_type=f32)


def stack_heads(block, rows):
    lane = lax.broadcasted_iota(jnp.int32, (rows, PAIR), 1)
    parts = []
    for pair in range(GROUP_HEADS // 2):
        both = block[:, pair * PAIR : (pair + 1) * PAIR]
        parts.append(jnp.where(lane < HEAD_DIM, both, jnp.zeros_like(both)))
        parts.append(jnp.where(lane >= HEAD_DIM, both, jnp.zeros_like(both)))
    return jnp.concatenate(parts, axis=0)


def unstack_heads(stacked, rows):
    lane = lax.broadcasted_iota(jnp.int32, (rows, PAIR), 1)
    parts = []
    for pair in range(GROUP_HEADS // 2):
        low = stacked[2 * pair * rows : (2 * pair + 1) * rows]
        high = stacked[(2 * pair + 1) * rows : (2 * pair + 2) * rows]
        parts.append(jnp.where(lane < HEAD_DIM, low, high))
    return jnp.concatenate(parts, axis=1)


def as_row(column):
    wide = jnp.broadcast_to(column, (column.shape[0], 128))
    return jnp.transpose(wide)[:8]


def attend_kernel(seen_ref, q_ref, kk_ref, vv_ref, qpos_ref, kpos_ref, o_ref, lse_ref):
    rows = q_ref.shape[0]
    stacked = stack_heads(q_ref[...], rows)
    qpos = jnp.concatenate([qpos_ref[...]] * GROUP_HEADS, axis=0)

    def unit(index, carry, masked):
        top, total, acc = carry
        scores = dot(stacked, kk_ref[index], ((1,), (1,)))
        if masked:
            scores = jnp.where(kpos_ref[...] <= qpos, scores, masked_score)
        new_top = jnp.maximum(top, jnp.max(scores, axis=1, keepdims=True))
        weights = jnp.exp(scores - new_top)
        keep = jnp.exp(top - new_top)
        total = total * keep + jnp.sum(weights, axis=1, keepdims=True)
        acc = acc * keep + dot(weights.astype(bf16), vv_ref[index])
        return new_top, total, acc

    count = GROUP_HEADS * rows
    start = (
        jnp.full((count, 1), masked_score, f32),
        jnp.zeros((count, 1), f32),
        jnp.zeros((count, PAIR), f32),
    )
    carry = unit(0, start, True)
    top, total, acc = lax.fori_loop(1, seen_ref[0], lambda i, c: unit(i, c, False), carry)
    o_ref[...] = unstack_heads(acc / total, rows).astype(bf16)
    lse_ref[...] = as_row(top + jnp.log(total))


def attend_back_kernel(
    seen_ref, q_ref, do_ref, o_ref, kk_ref, vv_ref, lse_ref, qpos_ref, kpos_ref,
    dq_ref, dkk_ref, dvv_ref, qs_ref, dos_ref, delta_ref, dqs_ref,
):
    rows = q_ref.shape[0]

    @pl.when(pl.program_id(0) == 0)
    def _():
        dkk_ref[...] = jnp.zeros_like(dkk_ref)
        dvv_ref[...] = jnp.zeros_like(dvv_ref)

    qs_ref[...] = stack_heads(q_ref[...], rows)
    grads = stack_heads(do_ref[...], rows)
    dos_ref[...] = grads
    outs = stack_heads(o_ref[...], rows)
    delta_ref[...] = as_row(jnp.sum(grads.astype(f32) * outs.astype(f32), axis=1, keepdims=True))

    def unit(index, masked):
        keys = kk_ref[index]
        scores = dot(keys, qs_ref[...], ((1,), (1,)))
        if masked:
            qpos = jnp.concatenate([qpos_ref[0:1, :]] * GROUP_HEADS, axis=1)
            scores = jnp.where(kpos_ref[...] <= qpos, scores, masked_score)
        probs = jnp.exp(scores - lse_ref[0:1, :])
        prob_grad = dot(vv_ref[index], dos_ref[...], ((1,), (1,)))
        score_grad = (probs * (prob_grad - delta_ref[0:1, :])).astype(bf16)
        dvv_ref[index] += dot(probs.astype(bf16), dos_ref[...])
        dkk_ref[index] += dot(score_grad, qs_ref[...])
        return dot(score_grad, keys, ((0,), (0,)))

    dqs_ref[...] = unit(0, True)

    @pl.loop(1, seen_ref[0])
    def _(index):
        dqs_ref[...] += unit(index, False)

    dq_ref[...] = unstack_heads(dqs_ref[...], rows)


def block_rows(length):
    return min(128, length)


def whole(shape):
    zeros = (0,) * len(shape)
    return pl.BlockSpec(shape, lambda i, seen: zeros)


def attend(seen, q, kk, vv, order):
    length, width = q.shape
    rows = block_rows(length)
    stacked = GROUP_HEADS * rows
    steps = length // rows
    return pl.pallas_call(
        attend_kernel,
        out_shape=(
            jax.ShapeDtypeStruct((length, width), bf16),
            jax.ShapeDtypeStruct((steps, 8, stacked), f32),
        ),
        grid_spec=pltpu.PrefetchScalarGridSpec(
            num_scalar_prefetch=1,
            grid=(steps,),
            in_specs=[
                pl.BlockSpec((rows, width), lambda i, seen: (i, 0)),
                whole(kk.shape),
                whole(vv.shape),
                pl.BlockSpec((rows, 1), lambda i, seen: (i, 0)),
                whole((1, length)),
            ],
            out_specs=[
                pl.BlockSpec((rows, width), lambda i, seen: (i, 0)),
                pl.BlockSpec((pl.Squeezed(), 8, stacked), lambda i, seen: (i, 0, 0)),
            ],
        ),
        name="attend",
    )(seen, q, kk, vv, order[:, None], order[None, :])


def attend_back(seen, q, do, o, kk, vv, lse, order):
    length, width = q.shape
    rows = block_rows(length)
    stacked = GROUP_HEADS * rows
    steps = length // rows
    return pl.pallas_call(
        attend_back_kernel,
        out_shape=(
            jax.ShapeDtypeStruct((length, width), f32),
            jax.ShapeDtypeStruct(kk.shape, f32),
            jax.ShapeDtypeStruct(vv.shape, f32),
        ),
        grid_spec=pltpu.PrefetchScalarGridSpec(
            num_scalar_prefetch=1,
            grid=(steps,),
            in_specs=[
                pl.BlockSpec((rows, width), lambda i, seen: (i, 0)),
                pl.BlockSpec((rows, width), lambda i, seen: (i, 0)),
                pl.BlockSpec((rows, width), lambda i, seen: (i, 0)),
                whole(kk.shape),
                whole(vv.shape),
                pl.BlockSpec((pl.Squeezed(), 8, stacked), lambda i, seen: (i, 0, 0)),
                pl.BlockSpec((8, rows), lambda i, seen: (0, i)),
                whole((length, 1)),
            ],
            out_specs=[
                pl.BlockSpec((rows, width), lambda i, seen: (i, 0)),
                whole(kk.shape),
                whole(vv.shape),
            ],
            scratch_shapes=[
                pltpu.VMEM((stacked, PAIR), bf16),
                pltpu.VMEM((stacked, PAIR), bf16),
                pltpu.VMEM((8, stacked), f32),
                pltpu.VMEM((stacked, PAIR), f32),
            ],
        ),
        name="attend_back",
    )(seen, q, do, o, kk, vv, lse, jnp.broadcast_to(order[None, :], (8, length)), order[:, None])


def normalize(values):
    inverse = lax.rsqrt(jnp.mean(values * values, axis=-1, keepdims=True) + epsilon)
    return values * inverse, inverse


def norm_back(inner, normed, inverse):
    return inverse * (inner - normed * jnp.mean(inner * normed, axis=-1, keepdims=True))


def rope_tables(positions):
    half_dim = HEAD_DIM // 2
    frequency = rope_base ** (-(jnp.arange(half_dim).astype(f32) * 2.0 / HEAD_DIM))
    angles = positions.astype(f32)[:, None] * frequency
    angles = jnp.concatenate([angles, angles], axis=-1)
    return jnp.cos(angles)[:, None, :], jnp.sin(angles)[:, None, :]


def turn(values):
    half_dim = HEAD_DIM // 2
    return jnp.concatenate([-values[..., half_dim:], values[..., :half_dim]], axis=-1)


def rotate(values, cosine, sine):
    return values * cosine + turn(values) * sine


def unrotate(grads, cosine, sine):
    return grads * cosine - turn(grads * sine)


def tie(*values):
    return lax.optimization_barrier(values)


def solution(mesh):
    n_dp = mesh.shape["dp"]
    n_seq = mesh.shape["seq"]
    planes = n_seq // GROUP
    halves = n_dp // 2
    both = ("dp", "seq")

    in_plane = [[GROUP * p + w for w in range(GROUP)] for p in range(planes)]
    across_dp = [
        [c * n_seq + GROUP * p + w for c in range(n_dp) for p in range(planes)] for w in range(GROUP)
    ]
    in_plane_dp = [
        [c * n_seq + GROUP * p + w for c in range(n_dp) for w in range(GROUP)] for p in range(planes)
    ]
    across = [[GROUP * p + w for p in range(planes)] for w in range(GROUP)]

    def xor_w(value, j):
        return lax.ppermute(value, "seq", [(s, s ^ j) for s in range(n_seq)])

    def shift_z(value, t):
        return lax.ppermute(value, "seq", [(s, (s + GROUP * t) % n_seq) for s in range(n_seq)])

    def shift_dp(value, t):
        return lax.ppermute(value, "dp", [(c, (c + t) % n_dp) for c in range(n_dp)])

    def gather_w(value):
        first = xor_w(value, 1)
        second = xor_w(value, 2)
        half = value.shape[0] // 2
        third = jnp.concatenate([xor_w(first[:half], 2), xor_w(second[half:], 1)], axis=0)
        return jnp.concatenate([value, first, second, third], axis=0)

    def scatter_w(slots):
        got = [xor_w(slots[j], j) for j in range(1, GROUP)]
        return functools.reduce(jnp.add, [g.astype(f32) for g in got], slots[0].astype(f32))

    def gather_z(value):
        return [value] + [shift_z(value, t) for t in range(1, planes)]

    def scatter_z(slots):
        got = [shift_z(slots[t], -t) for t in range(1, planes)]
        return functools.reduce(jnp.add, [g.astype(f32) for g in got], slots[0].astype(f32))

    def gather_dp(value):
        return jnp.concatenate([value] + [shift_dp(value, t) for t in range(1, n_dp)], axis=0)

    def pick(value, index, count, axis):
        size = value.shape[axis] // count
        return lax.dynamic_slice_in_dim(value, index * size, size, axis)

    def exchange_dp(value, c, axis):
        parts = [pick(value, c, n_dp, axis)]
        for t in range(1, n_dp):
            parts.append(shift_dp(pick(value, (c + t) % n_dp, n_dp, axis), t))
        return jnp.concatenate(parts, axis=0)

    def collect_dp(value, c):
        slots = [value] + [shift_dp(value, t) for t in range(1, n_dp)]
        out = []
        for member in range(n_dp):
            chosen = slots[0]
            for t in range(1, n_dp):
                chosen = jnp.where((c - t) % n_dp == member, slots[t], chosen)
            out.append(chosen)
        return out

    def body(
        inputs, positions, select, cotangent, gain_attn, w_query, w_key, w_value, w_out, gain_mlp,
        w_gate, w_up, w_down,
    ):
        seqs, rows, width = inputs.shape
        tokens = seqs * rows
        shard = w_query.shape[0]
        ff_rows = w_down.shape[0]
        ff_block = w_gate.shape[1] // planes
        q_width = GROUP_HEADS * HEAD_DIM
        s = lax.axis_index("seq")
        c = lax.axis_index("dp")
        p = s // GROUP
        w = s % GROUP

        gain_one = gain_attn.astype(f32)[:, None]
        gain_two = gain_mlp.astype(f32)[:, None]

        def scaled(weight, gain):
            return (weight.astype(f32) * gain).astype(bf16)

        q_cols = scaled(w_query, gain_one).reshape(shard, GROUP, n_dp, q_width // n_dp)
        kv_cols = jnp.concatenate(
            [
                scaled(w_key, gain_one).reshape(shard, GROUP, HEAD_DIM),
                scaled(w_value, gain_one).reshape(shard, GROUP, HEAD_DIM),
            ],
            axis=-1,
        ).reshape(shard, GROUP, n_dp, PAIR // n_dp)
        qkv_cols = jnp.concatenate([q_cols, kv_cols], axis=-1)
        qkv_part = lax.dynamic_index_in_dim(qkv_cols, c, 2, keepdims=False)
        qkv_part = lax.all_to_all(
            jnp.transpose(qkv_part, (1, 0, 2)), "seq", 0, 0, axis_index_groups=in_plane, tiled=True
        )
        part_width = (q_width + PAIR) // n_dp
        qkv_part = qkv_part.reshape(GROUP * shard, part_width)
        own_pos = positions.reshape(1, tokens)
        plane_pos = jnp.concatenate([own_pos] + [xor_w(own_pos, j) for j in range(1, GROUP)], axis=1)
        x_in = inputs.reshape(tokens, width).astype(f32)
        normed_one, inverse_one = normalize(x_in)
        low_one, qkv_part, plane_pos = tie(normed_one.astype(bf16), qkv_part, plane_pos)

        ring = [qkv_part] + [shift_z(qkv_part, -t) for t in range(1, planes)]
        qkv_ring = jnp.concatenate(ring + ring[: planes - 1], axis=0)
        qkv_mine = lax.dynamic_slice_in_dim(
            qkv_ring, ((planes - p) % planes) * GROUP * shard, width, 0
        )
        low_one = gather_w(low_one)

        piece = shard // halves
        gate_up = jnp.where(c // halves == 0, scaled(w_gate, gain_two), scaled(w_up, gain_two))
        out_part, gate_up, qkv_mine = tie(
            pick(w_out, c, n_dp, 1), pick(gate_up, c % halves, halves, 0), qkv_mine
        )
        qkv_full = collect_dp(qkv_mine, c)
        out_part = lax.ppermute(
            out_part, "seq", [(i, GROUP * (i % planes) + i // planes) for i in range(n_seq)]
        )
        gate_up_sent = [
            shift_z(pick(gate_up, (p + t) % planes, planes, 1), t) if t
            else pick(gate_up, p, planes, 1)
            for t in range(planes)
        ]
        down_full = lax.all_gather(
            pick(w_down, c, n_dp, 1), both, axis_index_groups=in_plane_dp, tiled=False
        )
        out_part, down_full = tie(out_part, down_full)
        down_full = down_full.reshape(n_dp, ff_block, width // n_dp)
        out_full = lax.all_gather(out_part, both, axis_index_groups=across_dp, tiled=False)
        out_full = out_full.reshape(n_dp, planes * shard, width // n_dp)

        blocks = [
            (i * GROUP + j) * halves + h
            for h in range(halves) for j in range(GROUP) for i in range(planes)
        ]

        def column_blocks(value, which):
            return jnp.concatenate([value[:, i * piece : (i + 1) * piece] for i in which], axis=1)

        def reorder(value):
            return column_blocks(value, blocks)

        def order_back(value):
            return column_blocks(value, [blocks.index(i) for i in range(len(blocks))])

        cosine, sine = rope_tables(plane_pos.reshape(GROUP * tokens))

        grad_y = (
            cotangent.astype(f32) * select.astype(f32)[..., None]
        ).reshape(tokens, width)
        projected = [dot(low_one, qkv_full[i]) for i in range(n_dp)]
        cut = q_width // n_dp
        q = jnp.concatenate([one[:, :cut] for one in projected], axis=1)
        kv = jnp.concatenate([one[:, cut:] for one in projected], axis=1)
        plane_tokens = GROUP * tokens
        q = rotate(q.reshape(plane_tokens, GROUP_HEADS, HEAD_DIM), cosine, sine)
        q = (q.astype(bf16).astype(f32) * HEAD_DIM ** (-0.5)).astype(bf16).reshape(plane_tokens, q_width)
        k = rotate(kv[:, None, :HEAD_DIM], cosine, sine)[:, 0]
        kv_low = jnp.concatenate([k, kv[:, HEAD_DIM:]], axis=1).astype(bf16)
        kv_all = jnp.stack(gather_z(kv_low))
        grad_y_low, kv_all = tie(grad_y.astype(bf16), kv_all)
        *gate_up_sent, q = tie(*gate_up_sent, q)
        gate_up_part = jnp.zeros((planes, piece, ff_block), bf16)
        for t in range(planes):
            gate_up_part = lax.dynamic_update_index_in_dim(
                gate_up_part, gate_up_sent[t], (p - t) % planes, 0
            )
        gate_up_full = lax.all_gather(
            gate_up_part, both, axis_index_groups=in_plane_dp, tiled=False
        )
        gate_up_full = gate_up_full.reshape(2, width, ff_block)
        gate_full = gate_up_full[0]
        up_full = gate_up_full[1]
        grad_y_all = jnp.concatenate(gather_z(grad_y_low), axis=0)
        kk = jnp.concatenate([kv_all[..., :HEAD_DIM]] * 2, axis=-1)
        vv = jnp.concatenate([kv_all[..., HEAD_DIM:]] * 2, axis=-1)

        def by_seq(value, axis):
            shape = value.shape
            value = value.reshape(shape[:axis] + (GROUP, seqs, rows) + shape[axis + 1 :])
            value = jnp.moveaxis(value, axis + 1, 0)
            return value.reshape((seqs,) + shape[:axis] + (GROUP * rows,) + shape[axis + 1 :])

        def from_seq(value, axis):
            shape = value.shape[1:]
            value = value.reshape((seqs,) + shape[:axis] + (GROUP, rows) + shape[axis + 1 :])
            value = jnp.moveaxis(value, 0, axis + 1)
            return value.reshape(shape[:axis] + (GROUP * seqs * rows,) + shape[axis + 1 :])

        order = jnp.concatenate([(w ^ j) * rows + jnp.arange(rows) for j in range(GROUP)])
        order = order.astype(jnp.int32)
        seen = (p + 1).astype(jnp.int32).reshape(1)
        q_seq = by_seq(q, 0)
        kk_seq = by_seq(kk, 1)
        vv_seq = by_seq(vv, 1)
        pieces = [attend(seen, q_seq[i], kk_seq[i], vv_seq[i], order) for i in range(seqs)]
        o_seq = [one[0] for one in pieces]
        lse_seq = [one[1] for one in pieces]
        o = from_seq(jnp.stack(o_seq), 0)

        branch = jnp.concatenate([dot(o, out_full[i]).astype(bf16) for i in range(n_dp)], axis=1)
        branch = scatter_w([branch[j * tokens : (j + 1) * tokens] for j in range(GROUP)])
        x_mid = x_in + branch

        normed_two, inverse_two = normalize(x_mid)
        low_two = reorder(normed_two.astype(bf16))
        low_two, grad_y_all = tie(low_two, grad_y_all)
        low_two = jnp.concatenate(gather_z(low_two), axis=0)
        gate = dot(low_two, gate_full)
        up_part = dot(low_two, up_full)
        sigmoid_gate = 1.0 / (1.0 + jnp.exp(-gate))
        hidden = (gate * sigmoid_gate * up_part).astype(bf16)

        grad_hidden = functools.reduce(
            jnp.add,
            [
                dot(pick(grad_y_all, i, n_dp, 1), down_full[i], ((1,), (1,)))
                for i in range(n_dp)
            ],
        )
        grad_gate = (
            grad_hidden * up_part * sigmoid_gate * (1.0 + gate * (1.0 - sigmoid_gate))
        ).astype(bf16)
        grad_up = (grad_hidden * gate * sigmoid_gate).astype(bf16)
        grad_low_two = dot(grad_gate, gate_full, ((1,), (1,))) + dot(
            grad_up, up_full, ((1,), (1,))
        )
        grad_low_two = grad_low_two.astype(bf16)
        hidden_later, grad_gate_later, grad_up_later, grad_low_two = tie(
            hidden, grad_gate, grad_up, grad_low_two
        )
        inner_sent = [
            shift_z(grad_low_two[t * tokens : (t + 1) * tokens], -t) for t in range(1, planes)
        ]

        hidden_all = gather_dp(hidden_later)
        down_sum = dot(hidden_all, exchange_dp(grad_y_all, c, 1), ((0,), (0,))).astype(bf16)

        low_two_all = gather_dp(low_two)
        if halves > 1:
            low_two_all = pick(low_two_all, c % halves, halves, 1)

        def of_member(member):
            return jnp.where(member // halves == 0, grad_gate_later, grad_up_later)

        gate_up_grads = [of_member(c)]
        for t in range(1, n_dp):
            gate_up_grads.append(shift_dp(of_member((c + t) % n_dp), t))
        gate_up_grads = jnp.concatenate(gate_up_grads, axis=0)
        gate_up_sum = dot(low_two_all, gate_up_grads, ((0,), (0,))).astype(bf16)

        inner_sent[0], gate_up_sum = tie(inner_sent[0], gate_up_sum)
        *inner_rest, down_sum = tie(*inner_sent[1:], down_sum)
        inner_sent = [inner_sent[0]] + inner_rest
        inner_two = functools.reduce(
            jnp.add, [g.astype(f32) for g in inner_sent], grad_low_two[:tokens].astype(f32)
        )
        grad_x_mid = grad_y + norm_back(order_back(inner_two), normed_two, inverse_two)

        hidden_last, grad_x_low = tie(hidden_later, grad_x_mid.astype(bf16))
        mixed = jnp.concatenate(
            [dot(hidden_last, down_full[i]).astype(bf16) for i in range(n_dp)], axis=1
        )
        gate_up_sum = lax.psum_scatter(gate_up_sum, "seq", axis_index_groups=in_plane, tiled=True)
        down_sum = lax.psum_scatter(
            down_sum, "seq", axis_index_groups=in_plane, tiled=True
        )
        gate_up_sum = gate_up_sum.reshape(planes, piece, ff_block)

        grad_branch = gather_w(grad_x_low)
        mixed, grad_branch = tie(mixed, grad_branch)
        mixed_sent = [shift_z(mixed[t * tokens : (t + 1) * tokens], -t) for t in range(1, planes)]
        grad_o = functools.reduce(
            jnp.add,
            [dot(pick(grad_branch, i, n_dp, 1), out_full[i], ((1,), (1,))) for i in range(n_dp)],
        ).astype(bf16)

        out_part_sum = dot(gather_dp(o), exchange_dp(grad_branch, c, 1), ((0,), (0,))).astype(bf16)
        grad_o_seq = by_seq(grad_o, 0)
        gate_up_sum, out_part_sum = tie(gate_up_sum, out_part_sum)
        out_sum = lax.psum_scatter(out_part_sum, "seq", axis_index_groups=across, tiled=True)
        pieces = [
            attend_back(
                seen, q_seq[i], grad_o_seq[i], o_seq[i], kk_seq[i], vv_seq[i], lse_seq[i], order
            )
            for i in range(seqs)
        ]
        *mixed_sent, grad_q = tie(*mixed_sent, jnp.stack([one[0] for one in pieces]))
        mixed = functools.reduce(
            jnp.add, [g.astype(f32) for g in mixed_sent], mixed[:tokens].astype(f32)
        )
        grad_q = from_seq(grad_q, 0) * HEAD_DIM ** (-0.5)
        grad_kk = from_seq(jnp.stack([one[1] for one in pieces]), 1)
        grad_vv = from_seq(jnp.stack([one[2] for one in pieces]), 1)
        grad_kv = jnp.concatenate(
            [
                grad_kk[..., :HEAD_DIM] + grad_kk[..., HEAD_DIM:],
                grad_vv[..., :HEAD_DIM] + grad_vv[..., HEAD_DIM:],
            ],
            axis=-1,
        ).astype(bf16)
        grad_kv = scatter_z([grad_kv[t] for t in range(planes)])
        query_pre = unrotate(grad_q.reshape(plane_tokens, GROUP_HEADS, HEAD_DIM), cosine, sine)
        query_pre = query_pre.reshape(plane_tokens, q_width).astype(bf16)
        key_pre = unrotate(grad_kv[:, None, :HEAD_DIM], cosine, sine)[:, 0]
        kv_pre = jnp.concatenate([key_pre, grad_kv[:, HEAD_DIM:]], axis=1).astype(bf16)
        pre = [
            jnp.concatenate(
                [query_pre[:, i * cut : (i + 1) * cut], pick(kv_pre, i, n_dp, 1)], axis=1
            )
            for i in range(n_dp)
        ]
        outputs = (x_mid + mixed).astype(bf16).reshape(seqs, rows, width)

        grad_low_one = functools.reduce(
            jnp.add, [dot(pre[i], qkv_full[i], ((1,), (1,))) for i in range(n_dp)]
        ).astype(bf16)
        inner_one = scatter_w([grad_low_one[j * tokens : (j + 1) * tokens] for j in range(GROUP)])
        grad_inputs = grad_x_mid + norm_back(inner_one, normed_one, inverse_one)
        grad_inputs = grad_inputs.reshape(seqs, rows, width)

        qkv_sum = dot(
            gather_dp(low_one),
            exchange_dp(jnp.concatenate(pre, axis=1), c, 1),
            ((0,), (0,)),
        ).astype(bf16)
        gate_up_late, down_sum, out_sum, qkv_sum = tie(gate_up_sum, down_sum, out_sum, qkv_sum)
        out_sum = lax.ppermute(
            out_sum, "seq", [(GROUP * (i % planes) + i // planes, i) for i in range(n_seq)]
        )
        grad_w_out = jnp.concatenate(collect_dp(out_sum, c), axis=1).astype(f32)

        qkv_sum = lax.psum_scatter(
            qkv_sum, "seq", axis_index_groups=across, tiled=True
        )
        qkv_sum = qkv_sum.reshape(GROUP, shard, part_width)
        qkv_sum = lax.all_to_all(qkv_sum, "seq", 0, 0, axis_index_groups=in_plane, tiled=True)
        qkv_sum = collect_dp(qkv_sum, c)
        q_sum = jnp.concatenate(
            [one[j][:, :cut] for j in range(GROUP) for one in qkv_sum], axis=1
        ).astype(f32)
        kv_sum = jnp.concatenate(
            [one[j][:, cut:] for j in range(GROUP) for one in qkv_sum], axis=1
        ).astype(f32).reshape(shard, GROUP, PAIR)
        k_sum = kv_sum[..., :HEAD_DIM].reshape(shard, GROUP * HEAD_DIM)
        v_sum = kv_sum[..., HEAD_DIM:].reshape(shard, GROUP * HEAD_DIM)

        grad_w_down = jnp.concatenate(collect_dp(down_sum, c), axis=1).astype(f32)
        gate_up_rows = jnp.zeros((planes, piece, ff_block), bf16)
        sent = []
        for t in range(planes):
            block = lax.dynamic_index_in_dim(gate_up_late, (p + t) % planes, 0, keepdims=False)
            sent.append(shift_z(block, t) if t else block)
        sent = lax.optimization_barrier(tuple(sent))
        for t in range(planes):
            gate_up_rows = lax.dynamic_update_index_in_dim(
                gate_up_rows, sent[t], (p - t) % planes, 0
            )
        gate_up_rows = collect_dp(gate_up_rows, c)

        def rows_of(members):
            wide = [jnp.concatenate([one[i] for i in range(planes)], axis=1) for one in members]
            return jnp.concatenate(wide, axis=0).astype(f32)

        gate_rows = rows_of(gate_up_rows[:halves])
        up_rows = rows_of(gate_up_rows[halves:])
        grad_w_gate = gate_rows * gain_two
        grad_w_up = up_rows * gain_two
        grad_gain_mlp = jnp.sum(
            gate_rows * w_gate.astype(f32) + up_rows * w_up.astype(f32), axis=1
        )
        grad_gain_attn = (
            jnp.sum(q_sum * w_query.astype(f32), axis=1)
            + jnp.sum(k_sum * w_key.astype(f32), axis=1)
            + jnp.sum(v_sum * w_value.astype(f32), axis=1)
        )

        return (
            outputs,
            grad_inputs,
            grad_gain_attn,
            q_sum * gain_one,
            k_sum * gain_one,
            v_sum * gain_one,
            grad_w_out,
            grad_gain_mlp,
            grad_w_gate,
            grad_w_up,
            grad_w_down,
        )

    tokens_spec = P("dp", "seq", None)
    in_specs = (
        tokens_spec,
        P("dp", "seq"),
        P("dp", "seq"),
        tokens_spec,
        P("seq"),
        P("seq", None),
        P("seq", None),
        P("seq", None),
        P("seq", None),
        P("seq"),
        P("seq", None),
        P("seq", None),
        P("seq", None),
    )
    out_specs = (
        tokens_spec,
        tokens_spec,
        P("seq"),
        P("seq", None),
        P("seq", None),
        P("seq", None),
        P("seq", None),
        P("seq"),
        P("seq", None),
        P("seq", None),
        P("seq", None),
    )
    return jax.shard_map(body, mesh=mesh, in_specs=in_specs, out_specs=out_specs, check_vma=False)
```

```python
import functools

import jax
import jax.numpy as jnp
from jax import lax
from jax.experimental import pallas as pl
from jax.experimental.pallas import tpu as pltpu
from jax.sharding import PartitionSpec as P

HEADS = 32
KV_HEADS = 4
HEAD_DIM = 64
GROUP = KV_HEADS
GROUP_HEADS = HEADS // GROUP
PAIR = 2 * HEAD_DIM

epsilon = 1e-05
rope_base = 10000.0
masked_score = -1e30

f32 = jnp.float32
bf16 = jnp.bfloat16


def dot(left, right, contract=((1,), (0,))):
    return lax.dot_general(left, right, (contract, ((), ())), preferred_element_type=f32)


def stack_heads(block, rows):
    lane = lax.broadcasted_iota(jnp.int32, (rows, PAIR), 1)
    parts = []
    for pair in range(GROUP_HEADS // 2):
        both = block[:, pair * PAIR : (pair + 1) * PAIR]
        parts.append(jnp.where(lane < HEAD_DIM, both, jnp.zeros_like(both)))
        parts.append(jnp.where(lane >= HEAD_DIM, both, jnp.zeros_like(both)))
    return jnp.concatenate(parts, axis=0)


def unstack_heads(stacked, rows):
    lane = lax.broadcasted_iota(jnp.int32, (rows, PAIR), 1)
    parts = []
    for pair in range(GROUP_HEADS // 2):
        low = stacked[2 * pair * rows : (2 * pair + 1) * rows]
        high = stacked[(2 * pair + 1) * rows : (2 * pair + 2) * rows]
        parts.append(jnp.where(lane < HEAD_DIM, low, high))
    return jnp.concatenate(parts, axis=1)


def as_row(column):
    wide = jnp.broadcast_to(column, (column.shape[0], 128))
    return jnp.transpose(wide)[:8]


def attend_kernel(seen_ref, q_ref, kk_ref, vv_ref, qpos_ref, kpos_ref, o_ref, lse_ref):
    rows = q_ref.shape[0]
    stacked = stack_heads(q_ref[...], rows)
    qpos = jnp.concatenate([qpos_ref[...]] * GROUP_HEADS, axis=0)

    def unit(index, carry, masked):
        top, total, acc = carry
        scores = dot(stacked, kk_ref[index], ((1,), (1,)))
        if masked:
            scores = jnp.where(kpos_ref[...] <= qpos, scores, masked_score)
        new_top = jnp.maximum(top, jnp.max(scores, axis=1, keepdims=True))
        weights = jnp.exp(scores - new_top)
        keep = jnp.exp(top - new_top)
        total = total * keep + jnp.sum(weights, axis=1, keepdims=True)
        acc = acc * keep + dot(weights.astype(bf16), vv_ref[index])
        return new_top, total, acc

    count = GROUP_HEADS * rows
    start = (
        jnp.full((count, 1), masked_score, f32),
        jnp.zeros((count, 1), f32),
        jnp.zeros((count, PAIR), f32),
    )
    carry = unit(0, start, True)
    top, total, acc = lax.fori_loop(1, seen_ref[0], lambda i, c: unit(i, c, False), carry)
    o_ref[...] = unstack_heads(acc / total, rows).astype(bf16)
    lse_ref[...] = as_row(top + jnp.log(total))


def attend_back_kernel(
    seen_ref, q_ref, do_ref, o_ref, kk_ref, vv_ref, lse_ref, qpos_ref, kpos_ref,
    dq_ref, dkk_ref, dvv_ref, qs_ref, dos_ref, delta_ref, dqs_ref,
):
    rows = q_ref.shape[0]

    @pl.when(pl.program_id(0) == 0)
    def _():
        dkk_ref[...] = jnp.zeros_like(dkk_ref)
        dvv_ref[...] = jnp.zeros_like(dvv_ref)

    qs_ref[...] = stack_heads(q_ref[...], rows)
    grads = stack_heads(do_ref[...], rows)
    dos_ref[...] = grads
    outs = stack_heads(o_ref[...], rows)
    delta_ref[...] = as_row(jnp.sum(grads.astype(f32) * outs.astype(f32), axis=1, keepdims=True))

    def unit(index, masked):
        keys = kk_ref[index]
        scores = dot(keys, qs_ref[...], ((1,), (1,)))
        if masked:
            qpos = jnp.concatenate([qpos_ref[0:1, :]] * GROUP_HEADS, axis=1)
            scores = jnp.where(kpos_ref[...] <= qpos, scores, masked_score)
        probs = jnp.exp(scores - lse_ref[0:1, :])
        prob_grad = dot(vv_ref[index], dos_ref[...], ((1,), (1,)))
        score_grad = (probs * (prob_grad - delta_ref[0:1, :])).astype(bf16)
        dvv_ref[index] += dot(probs.astype(bf16), dos_ref[...])
        dkk_ref[index] += dot(score_grad, qs_ref[...])
        return dot(score_grad, keys, ((0,), (0,)))

    dqs_ref[...] = unit(0, True)

    @pl.loop(1, seen_ref[0])
    def _(index):
        dqs_ref[...] += unit(index, False)

    dq_ref[...] = unstack_heads(dqs_ref[...], rows)


def block_rows(length):
    return min(128, length)


def whole(shape):
    zeros = (0,) * len(shape)
    return pl.BlockSpec(shape, lambda i, seen: zeros)


def attend(seen, q, kk, vv, order):
    length, width = q.shape
    rows = block_rows(length)
    stacked = GROUP_HEADS * rows
    steps = length // rows
    return pl.pallas_call(
        attend_kernel,
        out_shape=(
            jax.ShapeDtypeStruct((length, width), bf16),
            jax.ShapeDtypeStruct((steps, 8, stacked), f32),
        ),
        grid_spec=pltpu.PrefetchScalarGridSpec(
            num_scalar_prefetch=1,
            grid=(steps,),
            in_specs=[
                pl.BlockSpec((rows, width), lambda i, seen: (i, 0)),
                whole(kk.shape),
                whole(vv.shape),
                pl.BlockSpec((rows, 1), lambda i, seen: (i, 0)),
                whole((1, length)),
            ],
            out_specs=[
                pl.BlockSpec((rows, width), lambda i, seen: (i, 0)),
                pl.BlockSpec((pl.Squeezed(), 8, stacked), lambda i, seen: (i, 0, 0)),
            ],
        ),
        name="attend",
    )(seen, q, kk, vv, order[:, None], order[None, :])


def attend_back(seen, q, do, o, kk, vv, lse, order):
    length, width = q.shape
    rows = block_rows(length)
    stacked = GROUP_HEADS * rows
    steps = length // rows
    return pl.pallas_call(
        attend_back_kernel,
        out_shape=(
            jax.ShapeDtypeStruct((length, width), f32),
            jax.ShapeDtypeStruct(kk.shape, f32),
            jax.ShapeDtypeStruct(vv.shape, f32),
        ),
        grid_spec=pltpu.PrefetchScalarGridSpec(
            num_scalar_prefetch=1,
            grid=(steps,),
            in_specs=[
                pl.BlockSpec((rows, width), lambda i, seen: (i, 0)),
                pl.BlockSpec((rows, width), lambda i, seen: (i, 0)),
                pl.BlockSpec((rows, width), lambda i, seen: (i, 0)),
                whole(kk.shape),
                whole(vv.shape),
                pl.BlockSpec((pl.Squeezed(), 8, stacked), lambda i, seen: (i, 0, 0)),
                pl.BlockSpec((8, rows), lambda i, seen: (0, i)),
                whole((length, 1)),
            ],
            out_specs=[
                pl.BlockSpec((rows, width), lambda i, seen: (i, 0)),
                whole(kk.shape),
                whole(vv.shape),
            ],
            scratch_shapes=[
                pltpu.VMEM((stacked, PAIR), bf16),
                pltpu.VMEM((stacked, PAIR), bf16),
                pltpu.VMEM((8, stacked), f32),
                pltpu.VMEM((stacked, PAIR), f32),
            ],
        ),
        name="attend_back",
    )(seen, q, do, o, kk, vv, lse, jnp.broadcast_to(order[None, :], (8, length)), order[:, None])


def normalize(values):
    inverse = lax.rsqrt(jnp.mean(values * values, axis=-1, keepdims=True) + epsilon)
    return values * inverse, inverse


def norm_back(inner, normed, inverse):
    return inverse * (inner - normed * jnp.mean(inner * normed, axis=-1, keepdims=True))


def rope_tables(positions):
    half_dim = HEAD_DIM // 2
    frequency = rope_base ** (-(jnp.arange(half_dim).astype(f32) * 2.0 / HEAD_DIM))
    angles = positions.astype(f32)[:, None] * frequency
    angles = jnp.concatenate([angles, angles], axis=-1)
    return jnp.cos(angles)[:, None, :], jnp.sin(angles)[:, None, :]


def turn(values):
    half_dim = HEAD_DIM // 2
    return jnp.concatenate([-values[..., half_dim:], values[..., :half_dim]], axis=-1)


def rotate(values, cosine, sine):
    return values * cosine + turn(values) * sine


def unrotate(grads, cosine, sine):
    return grads * cosine - turn(grads * sine)


def tie(*values):
    return lax.optimization_barrier(values)


def solution(mesh):
    n_dp = mesh.shape["dp"]
    n_seq = mesh.shape["seq"]
    planes = n_seq // GROUP
    halves = n_dp // 2
    both = ("dp", "seq")

    in_plane = [[GROUP * p + w for w in range(GROUP)] for p in range(planes)]
    across_dp = [
        [c * n_seq + GROUP * p + w for c in range(n_dp) for p in range(planes)] for w in range(GROUP)
    ]
    in_plane_dp = [
        [c * n_seq + GROUP * p + w for c in range(n_dp) for w in range(GROUP)] for p in range(planes)
    ]
    across = [[GROUP * p + w for p in range(planes)] for w in range(GROUP)]

    def xor_w(value, j):
        return lax.ppermute(value, "seq", [(s, s ^ j) for s in range(n_seq)])

    def shift_z(value, t):
        return lax.ppermute(value, "seq", [(s, (s + GROUP * t) % n_seq) for s in range(n_seq)])

    def shift_dp(value, t):
        return lax.ppermute(value, "dp", [(c, (c + t) % n_dp) for c in range(n_dp)])

    def gather_w(value):
        first = xor_w(value, 1)
        second = xor_w(value, 2)
        half = value.shape[0] // 2
        third = jnp.concatenate([xor_w(first[:half], 2), xor_w(second[half:], 1)], axis=0)
        return jnp.concatenate([value, first, second, third], axis=0)

    def scatter_w(slots):
        got = [xor_w(slots[j], j) for j in range(1, GROUP)]
        return functools.reduce(jnp.add, [g.astype(f32) for g in got], slots[0].astype(f32))

    def gather_z(value):
        return [value] + [shift_z(value, t) for t in range(1, planes)]

    def scatter_z(slots):
        got = [shift_z(slots[t], -t) for t in range(1, planes)]
        return functools.reduce(jnp.add, [g.astype(f32) for g in got], slots[0].astype(f32))

    def gather_dp(value):
        return jnp.concatenate([value] + [shift_dp(value, t) for t in range(1, n_dp)], axis=0)

    def pick(value, index, count, axis):
        size = value.shape[axis] // count
        return lax.dynamic_slice_in_dim(value, index * size, size, axis)

    def exchange_dp(value, c, axis):
        parts = [pick(value, c, n_dp, axis)]
        for t in range(1, n_dp):
            parts.append(shift_dp(pick(value, (c + t) % n_dp, n_dp, axis), t))
        return jnp.concatenate(parts, axis=0)

    def collect_dp(value, c):
        slots = [value] + [shift_dp(value, t) for t in range(1, n_dp)]
        out = []
        for member in range(n_dp):
            chosen = slots[0]
            for t in range(1, n_dp):
                chosen = jnp.where((c - t) % n_dp == member, slots[t], chosen)
            out.append(chosen)
        return out

    def body(
        inputs, positions, select, cotangent, gain_attn, w_query, w_key, w_value, w_out, gain_mlp,
        w_gate, w_up, w_down,
    ):
        seqs, rows, width = inputs.shape
        tokens = seqs * rows
        shard = w_query.shape[0]
        ff_rows = w_down.shape[0]
        ff_block = w_gate.shape[1] // planes
        q_width = GROUP_HEADS * HEAD_DIM
        s = lax.axis_index("seq")
        c = lax.axis_index("dp")
        p = s // GROUP
        w = s % GROUP

        gain_one = gain_attn.astype(f32)[:, None]
        gain_two = gain_mlp.astype(f32)[:, None]

        def scaled(weight, gain):
            return (weight.astype(f32) * gain).astype(bf16)

        q_cols = scaled(w_query, gain_one).reshape(shard, GROUP, n_dp, q_width // n_dp)
        kv_cols = jnp.concatenate(
            [
                scaled(w_key, gain_one).reshape(shard, GROUP, HEAD_DIM),
                scaled(w_value, gain_one).reshape(shard, GROUP, HEAD_DIM),
            ],
            axis=-1,
        ).reshape(shard, GROUP, n_dp, PAIR // n_dp)
        qkv_cols = jnp.concatenate([q_cols, kv_cols], axis=-1)
        qkv_part = lax.dynamic_index_in_dim(qkv_cols, c, 2, keepdims=False)
        qkv_part = lax.all_to_all(
            jnp.transpose(qkv_part, (1, 0, 2)), "seq", 0, 0, axis_index_groups=in_plane, tiled=True
        )
        part_width = (q_width + PAIR) // n_dp
        qkv_part = qkv_part.reshape(GROUP * shard, part_width)
        own_pos = positions.reshape(1, tokens)
        plane_pos = jnp.concatenate([own_pos] + [xor_w(own_pos, j) for j in range(1, GROUP)], axis=1)
        x_in = inputs.reshape(tokens, width).astype(f32)
        normed_one, inverse_one = normalize(x_in)
        low_one, qkv_part, plane_pos = tie(normed_one.astype(bf16), qkv_part, plane_pos)

        ring = [qkv_part] + [shift_z(qkv_part, -t) for t in range(1, planes)]
        qkv_ring = jnp.concatenate(ring + ring[: planes - 1], axis=0)
        qkv_mine = lax.dynamic_slice_in_dim(
            qkv_ring, ((planes - p) % planes) * GROUP * shard, width, 0
        )
        low_one = gather_w(low_one)

        piece = shard // halves
        gate_up = jnp.where(c // halves == 0, scaled(w_gate, gain_two), scaled(w_up, gain_two))
        out_part, gate_up, qkv_mine = tie(
            pick(w_out, c, n_dp, 1), pick(gate_up, c % halves, halves, 0), qkv_mine
        )
        qkv_full = collect_dp(qkv_mine, c)
        out_part = lax.ppermute(
            out_part, "seq", [(i, GROUP * (i % planes) + i // planes) for i in range(n_seq)]
        )
        gate_up_sent = [
            shift_z(pick(gate_up, (p + t) % planes, planes, 1), t) if t
            else pick(gate_up, p, planes, 1)
            for t in range(planes)
        ]
        down_full = lax.all_gather(
            pick(w_down, c, n_dp, 1), both, axis_index_groups=in_plane_dp, tiled=False
        )
        out_part, down_full = tie(out_part, down_full)
        down_full = down_full.reshape(n_dp, ff_block, width // n_dp)
        out_full = lax.all_gather(out_part, both, axis_index_groups=across_dp, tiled=False)
        out_full = out_full.reshape(n_dp, planes * shard, width // n_dp)

        blocks = [
            (i * GROUP + j) * halves + h
            for h in range(halves) for j in range(GROUP) for i in range(planes)
        ]

        def column_blocks(value, which):
            return jnp.concatenate([value[:, i * piece : (i + 1) * piece] for i in which], axis=1)

        def reorder(value):
            return column_blocks(value, blocks)

        def order_back(value):
            return column_blocks(value, [blocks.index(i) for i in range(len(blocks))])

        cosine, sine = rope_tables(plane_pos.reshape(GROUP * tokens))

        grad_y = (
            cotangent.astype(f32) * select.astype(f32)[..., None]
        ).reshape(tokens, width)
        projected = [dot(low_one, qkv_full[i]) for i in range(n_dp)]
        cut = q_width // n_dp
        q = jnp.concatenate([one[:, :cut] for one in projected], axis=1)
        kv = jnp.concatenate([one[:, cut:] for one in projected], axis=1)
        plane_tokens = GROUP * tokens
        q = rotate(q.reshape(plane_tokens, GROUP_HEADS, HEAD_DIM), cosine, sine)
        q = (q.astype(bf16).astype(f32) * HEAD_DIM ** (-0.5)).astype(bf16).reshape(plane_tokens, q_width)
        k = rotate(kv[:, None, :HEAD_DIM], cosine, sine)[:, 0]
        kv_low = jnp.concatenate([k, kv[:, HEAD_DIM:]], axis=1).astype(bf16)
        kv_all = jnp.stack(gather_z(kv_low))
        grad_y_low, kv_all = tie(grad_y.astype(bf16), kv_all)
        *gate_up_sent, q = tie(*gate_up_sent, q)
        gate_up_part = jnp.zeros((planes, piece, ff_block), bf16)
        for t in range(planes):
            gate_up_part = lax.dynamic_update_index_in_dim(
                gate_up_part, gate_up_sent[t], (p - t) % planes, 0
            )
        gate_up_full = lax.all_gather(
            gate_up_part, both, axis_index_groups=in_plane_dp, tiled=False
        )
        gate_up_full = gate_up_full.reshape(2, width, ff_block)
        gate_full = gate_up_full[0]
        up_full = gate_up_full[1]
        grad_y_all = jnp.concatenate(gather_z(grad_y_low), axis=0)
        kk = jnp.concatenate([kv_all[..., :HEAD_DIM]] * 2, axis=-1)
        vv = jnp.concatenate([kv_all[..., HEAD_DIM:]] * 2, axis=-1)

        def by_seq(value, axis):
            shape = value.shape
            value = value.reshape(shape[:axis] + (GROUP, seqs, rows) + shape[axis + 1 :])
            value = jnp.moveaxis(value, axis + 1, 0)
            return value.reshape((seqs,) + shape[:axis] + (GROUP * rows,) + shape[axis + 1 :])

        def from_seq(value, axis):
            shape = value.shape[1:]
            value = value.reshape((seqs,) + shape[:axis] + (GROUP, rows) + shape[axis + 1 :])
            value = jnp.moveaxis(value, 0, axis + 1)
            return value.reshape(shape[:axis] + (GROUP * seqs * rows,) + shape[axis + 1 :])

        order = jnp.concatenate([(w ^ j) * rows + jnp.arange(rows) for j in range(GROUP)])
        order = order.astype(jnp.int32)
        seen = (p + 1).astype(jnp.int32).reshape(1)
        q_seq = by_seq(q, 0)
        kk_seq = by_seq(kk, 1)
        vv_seq = by_seq(vv, 1)
        pieces = [attend(seen, q_seq[i], kk_seq[i], vv_seq[i], order) for i in range(seqs)]
        o_seq = [one[0] for one in pieces]
        lse_seq = [one[1] for one in pieces]
        o = from_seq(jnp.stack(o_seq), 0)

        branch = jnp.concatenate([dot(o, out_full[i]).astype(bf16) for i in range(n_dp)], axis=1)
        branch = scatter_w([branch[j * tokens : (j + 1) * tokens] for j in range(GROUP)])
        x_mid = x_in + branch

        normed_two, inverse_two = normalize(x_mid)
        low_two = reorder(normed_two.astype(bf16))
        low_two, grad_y_all = tie(low_two, grad_y_all)
        low_two = jnp.concatenate(gather_z(low_two), axis=0)
        gate = dot(low_two, gate_full)
        up_part = dot(low_two, up_full)
        sigmoid_gate = 1.0 / (1.0 + jnp.exp(-gate))
        hidden = (gate * sigmoid_gate * up_part).astype(bf16)

        grad_hidden = functools.reduce(
            jnp.add,
            [
                dot(pick(grad_y_all, i, n_dp, 1), down_full[i], ((1,), (1,)))
                for i in range(n_dp)
            ],
        )
        grad_gate = (
            grad_hidden * up_part * sigmoid_gate * (1.0 + gate * (1.0 - sigmoid_gate))
        ).astype(bf16)
        grad_up = (grad_hidden * gate * sigmoid_gate).astype(bf16)
        grad_low_two = dot(grad_gate, gate_full, ((1,), (1,))) + dot(
            grad_up, up_full, ((1,), (1,))
        )
        grad_low_two = grad_low_two.astype(bf16)
        hidden_later, grad_gate_later, grad_up_later, grad_low_two = tie(
            hidden, grad_gate, grad_up, grad_low_two
        )
        inner_sent = [
            shift_z(grad_low_two[t * tokens : (t + 1) * tokens], -t) for t in range(1, planes)
        ]

        hidden_all = gather_dp(hidden_later)
        down_sum = dot(hidden_all, exchange_dp(grad_y_all, c, 1), ((0,), (0,))).astype(bf16)

        low_two_all = gather_dp(low_two)
        if halves > 1:
            low_two_all = pick(low_two_all, c % halves, halves, 1)

        def of_member(member):
            return jnp.where(member // halves == 0, grad_gate_later, grad_up_later)

        gate_up_grads = [of_member(c)]
        for t in range(1, n_dp):
            gate_up_grads.append(shift_dp(of_member((c + t) % n_dp), t))
        gate_up_grads = jnp.concatenate(gate_up_grads, axis=0)
        gate_up_sum = dot(low_two_all, gate_up_grads, ((0,), (0,))).astype(bf16)

        inner_sent[0], gate_up_sum = tie(inner_sent[0], gate_up_sum)
        *inner_rest, down_sum = tie(*inner_sent[1:], down_sum)
        inner_sent = [inner_sent[0]] + inner_rest
        mixed = jnp.concatenate(
            [dot(hidden_later, down_full[i]).astype(bf16) for i in range(n_dp)], axis=1
        )
        *inner_sent, mixed = tie(*inner_sent, mixed)
        inner_two = functools.reduce(
            jnp.add, [g.astype(f32) for g in inner_sent], grad_low_two[:tokens].astype(f32)
        )
        grad_x_mid = grad_y + norm_back(order_back(inner_two), normed_two, inverse_two)

        mixed, grad_x_low = tie(mixed, grad_x_mid.astype(bf16))
        mixed_sent = [shift_z(mixed[t * tokens : (t + 1) * tokens], -t) for t in range(1, planes)]
        gate_up_sum = lax.psum_scatter(gate_up_sum, "seq", axis_index_groups=in_plane, tiled=True)
        down_sum = lax.psum_scatter(
            down_sum, "seq", axis_index_groups=in_plane, tiled=True
        )
        gate_up_sum = gate_up_sum.reshape(planes, piece, ff_block)

        grad_branch = gather_w(grad_x_low)
        early = planes - 2
        *mixed_sent[:early], grad_branch = tie(*mixed_sent[:early], grad_branch)
        grad_o = functools.reduce(
            jnp.add,
            [dot(pick(grad_branch, i, n_dp, 1), out_full[i], ((1,), (1,))) for i in range(n_dp)],
        ).astype(bf16)

        out_part_sum = dot(gather_dp(o), exchange_dp(grad_branch, c, 1), ((0,), (0,))).astype(bf16)
        grad_o_seq = by_seq(grad_o, 0)
        *late, grad_o_seq, out_part_sum = tie(*mixed_sent[early:], grad_o_seq, out_part_sum)
        mixed_sent = mixed_sent[:early] + list(late)
        gate_up_sum, out_part_sum = tie(gate_up_sum, out_part_sum)
        out_sum = lax.psum_scatter(out_part_sum, "seq", axis_index_groups=across, tiled=True)
        pieces = [
            attend_back(
                seen, q_seq[i], grad_o_seq[i], o_seq[i], kk_seq[i], vv_seq[i], lse_seq[i], order
            )
            for i in range(seqs)
        ]
        grad_q = jnp.stack([one[0] for one in pieces])
        mixed = functools.reduce(
            jnp.add, [g.astype(f32) for g in mixed_sent], mixed[:tokens].astype(f32)
        )
        grad_q = from_seq(grad_q, 0) * HEAD_DIM ** (-0.5)
        grad_kk = from_seq(jnp.stack([one[1] for one in pieces]), 1)
        grad_vv = from_seq(jnp.stack([one[2] for one in pieces]), 1)
        grad_kv = jnp.concatenate(
            [
                grad_kk[..., :HEAD_DIM] + grad_kk[..., HEAD_DIM:],
                grad_vv[..., :HEAD_DIM] + grad_vv[..., HEAD_DIM:],
            ],
            axis=-1,
        ).astype(bf16)
        grad_kv = scatter_z([grad_kv[t] for t in range(planes)])
        grad_kv, gate_up_late = tie(grad_kv, gate_up_sum)
        gate_up_sent = []
        for t in range(planes):
            block = lax.dynamic_index_in_dim(gate_up_late, (p + t) % planes, 0, keepdims=False)
            gate_up_sent.append(shift_z(block, t) if t else block)
        query_pre = unrotate(grad_q.reshape(plane_tokens, GROUP_HEADS, HEAD_DIM), cosine, sine)
        query_pre = query_pre.reshape(plane_tokens, q_width).astype(bf16)
        query_pre, out_sum = tie(query_pre, out_sum)
        key_pre = unrotate(grad_kv[:, None, :HEAD_DIM], cosine, sine)[:, 0]
        kv_pre = jnp.concatenate([key_pre, grad_kv[:, HEAD_DIM:]], axis=1).astype(bf16)
        pre = [
            jnp.concatenate(
                [query_pre[:, i * cut : (i + 1) * cut], pick(kv_pre, i, n_dp, 1)], axis=1
            )
            for i in range(n_dp)
        ]
        outputs = (x_mid + mixed).astype(bf16).reshape(seqs, rows, width)

        grad_low_one = functools.reduce(
            jnp.add, [dot(pre[i], qkv_full[i], ((1,), (1,))) for i in range(n_dp)]
        ).astype(bf16)
        inner_one = scatter_w([grad_low_one[j * tokens : (j + 1) * tokens] for j in range(GROUP)])
        grad_inputs = grad_x_mid + norm_back(inner_one, normed_one, inverse_one)
        grad_inputs = grad_inputs.reshape(seqs, rows, width)

        qkv_sum = dot(
            gather_dp(low_one),
            exchange_dp(jnp.concatenate(pre, axis=1), c, 1),
            ((0,), (0,)),
        ).astype(bf16)
        *gate_up_sent, down_sum, qkv_sum = tie(*gate_up_sent, down_sum, qkv_sum)
        out_sum = lax.ppermute(
            out_sum, "seq", [(GROUP * (i % planes) + i // planes, i) for i in range(n_seq)]
        )
        grad_w_out = jnp.concatenate(collect_dp(out_sum, c), axis=1).astype(f32)

        qkv_sum = lax.psum_scatter(
            qkv_sum, "seq", axis_index_groups=across, tiled=True
        )
        qkv_sum = qkv_sum.reshape(GROUP, shard, part_width)
        qkv_sum = lax.all_to_all(qkv_sum, "seq", 0, 0, axis_index_groups=in_plane, tiled=True)
        qkv_sum = collect_dp(qkv_sum, c)
        q_sum = jnp.concatenate(
            [one[j][:, :cut] for j in range(GROUP) for one in qkv_sum], axis=1
        ).astype(f32)
        kv_sum = jnp.concatenate(
            [one[j][:, cut:] for j in range(GROUP) for one in qkv_sum], axis=1
        ).astype(f32).reshape(shard, GROUP, PAIR)
        k_sum = kv_sum[..., :HEAD_DIM].reshape(shard, GROUP * HEAD_DIM)
        v_sum = kv_sum[..., HEAD_DIM:].reshape(shard, GROUP * HEAD_DIM)

        grad_w_down = jnp.concatenate(collect_dp(down_sum, c), axis=1).astype(f32)
        gate_up_rows = jnp.zeros((planes, piece, ff_block), bf16)
        for t in range(planes):
            gate_up_rows = lax.dynamic_update_index_in_dim(
                gate_up_rows, gate_up_sent[t], (p - t) % planes, 0
            )
        gate_up_rows = collect_dp(gate_up_rows, c)

        def rows_of(members):
            wide = [jnp.concatenate([one[i] for i in range(planes)], axis=1) for one in members]
            return jnp.concatenate(wide, axis=0).astype(f32)

        gate_rows = rows_of(gate_up_rows[:halves])
        up_rows = rows_of(gate_up_rows[halves:])
        grad_w_gate = gate_rows * gain_two
        grad_w_up = up_rows * gain_two
        grad_gain_mlp = jnp.sum(
            gate_rows * w_gate.astype(f32) + up_rows * w_up.astype(f32), axis=1
        )
        grad_gain_attn = (
            jnp.sum(q_sum * w_query.astype(f32), axis=1)
            + jnp.sum(k_sum * w_key.astype(f32), axis=1)
            + jnp.sum(v_sum * w_value.astype(f32), axis=1)
        )

        return (
            outputs,
            grad_inputs,
            grad_gain_attn,
            q_sum * gain_one,
            k_sum * gain_one,
            v_sum * gain_one,
            grad_w_out,
            grad_gain_mlp,
            grad_w_gate,
            grad_w_up,
            grad_w_down,
        )

    tokens_spec = P("dp", "seq", None)
    in_specs = (
        tokens_spec,
        P("dp", "seq"),
        P("dp", "seq"),
        tokens_spec,
        P("seq"),
        P("seq", None),
        P("seq", None),
        P("seq", None),
        P("seq", None),
        P("seq"),
        P("seq", None),
        P("seq", None),
        P("seq", None),
    )
    out_specs = (
        tokens_spec,
        tokens_spec,
        P("seq"),
        P("seq", None),
        P("seq", None),
        P("seq", None),
        P("seq", None),
        P("seq"),
        P("seq", None),
        P("seq", None),
        P("seq", None),
    )
    return jax.shard_map(body, mesh=mesh, in_specs=in_specs, out_specs=out_specs, check_vma=False)
```

```python
import functools

import jax
import jax.numpy as jnp
from jax import lax
from jax.experimental import pallas as pl
from jax.experimental.pallas import tpu as pltpu
from jax.sharding import PartitionSpec as P

HEADS = 32
KV_HEADS = 4
HEAD_DIM = 64
GROUP = KV_HEADS
GROUP_HEADS = HEADS // GROUP
PAIR = 2 * HEAD_DIM

epsilon = 1e-05
rope_base = 10000.0
masked_score = -1e30

f32 = jnp.float32
bf16 = jnp.bfloat16


def dot(left, right, contract=((1,), (0,))):
    return lax.dot_general(left, right, (contract, ((), ())), preferred_element_type=f32)


def stack_heads(block, rows):
    lane = lax.broadcasted_iota(jnp.int32, (rows, PAIR), 1)
    parts = []
    for pair in range(GROUP_HEADS // 2):
        both = block[:, pair * PAIR : (pair + 1) * PAIR]
        parts.append(jnp.where(lane < HEAD_DIM, both, jnp.zeros_like(both)))
        parts.append(jnp.where(lane >= HEAD_DIM, both, jnp.zeros_like(both)))
    return jnp.concatenate(parts, axis=0)


def unstack_heads(stacked, rows):
    lane = lax.broadcasted_iota(jnp.int32, (rows, PAIR), 1)
    parts = []
    for pair in range(GROUP_HEADS // 2):
        low = stacked[2 * pair * rows : (2 * pair + 1) * rows]
        high = stacked[(2 * pair + 1) * rows : (2 * pair + 2) * rows]
        parts.append(jnp.where(lane < HEAD_DIM, low, high))
    return jnp.concatenate(parts, axis=1)


def as_row(column):
    wide = jnp.broadcast_to(column, (column.shape[0], 128))
    return jnp.transpose(wide)[:8]


def turn(values):
    width = values.shape[1]
    half_dim = HEAD_DIM // 2
    lane = lax.broadcasted_iota(jnp.int32, values.shape, 1)
    ahead = pltpu.roll(values, width - half_dim, 1)
    behind = pltpu.roll(values, half_dim, 1)
    return jnp.where(lane % HEAD_DIM < half_dim, -ahead, behind)


def rotate(values, cosine, sine):
    return values * cosine + turn(values) * sine


def unrotate(grads, cosine, sine):
    return grads * cosine - turn(grads * sine)


def project_kernel(low_ref, w_ref, cos_ref, sin_ref, q_ref, kv_ref):
    made = dot(low_ref[...], w_ref[...])
    cosine, sine = cos_ref[...], sin_ref[...]
    for i in range(q_ref.shape[1] // PAIR):
        q = rotate(made[:, i * PAIR : (i + 1) * PAIR], cosine, sine).astype(bf16)
        q_ref[:, i * PAIR : (i + 1) * PAIR] = (q.astype(f32) * HEAD_DIM ** (-0.5)).astype(bf16)
    kv = made[:, q_ref.shape[1] :]
    lane = lax.broadcasted_iota(jnp.int32, kv.shape, 1)
    kv_ref[...] = jnp.where(lane < HEAD_DIM, rotate(kv, cosine, sine), kv).astype(bf16)


def project(low, weights, cosine, sine):
    tokens, width = low.shape
    q_width = weights.shape[1] - PAIR
    rows = block_rows(tokens)
    return pl.pallas_call(
        project_kernel,
        out_shape=(
            jax.ShapeDtypeStruct((tokens, q_width), bf16),
            jax.ShapeDtypeStruct((tokens, PAIR), bf16),
        ),
        grid=(tokens // rows,),
        in_specs=[
            pl.BlockSpec((rows, width), lambda i: (i, 0)),
            pl.BlockSpec(weights.shape, lambda i: (0, 0)),
            pl.BlockSpec((rows, PAIR), lambda i: (i, 0)),
            pl.BlockSpec((rows, PAIR), lambda i: (i, 0)),
        ],
        out_specs=[
            pl.BlockSpec((rows, q_width), lambda i: (i, 0)),
            pl.BlockSpec((rows, PAIR), lambda i: (i, 0)),
        ],
        name="project",
    )(low, weights, cosine, sine)


def feed_kernel(low_ref, w_ref, grad_hidden_ref, hidden_ref, grad_gate_ref, grad_up_ref, back_ref):
    low = low_ref[...]
    gate = dot(low, w_ref[0])
    up = dot(low, w_ref[1])
    grad_hidden = grad_hidden_ref[...]
    sigmoid_gate = 1.0 / (1.0 + jnp.exp(-gate))
    silu = gate * sigmoid_gate
    hidden_ref[...] = (silu * up).astype(bf16)
    grad_gate = (
        grad_hidden * up * sigmoid_gate * (1.0 + gate * (1.0 - sigmoid_gate))
    ).astype(bf16)
    grad_up = (grad_hidden * silu).astype(bf16)
    grad_gate_ref[...] = grad_gate
    grad_up_ref[...] = grad_up
    back_ref[...] = (
        dot(grad_gate, w_ref[0], ((1,), (1,))) + dot(grad_up, w_ref[1], ((1,), (1,)))
    ).astype(bf16)


def feed(low, weights, grad_hidden):
    tokens, width = low.shape
    block = weights.shape[2]
    rows = block_rows(tokens)
    narrow = pl.BlockSpec((rows, block), lambda i: (i, 0))
    wide = pl.BlockSpec((rows, width), lambda i: (i, 0))
    return pl.pallas_call(
        feed_kernel,
        out_shape=(
            jax.ShapeDtypeStruct((tokens, block), bf16),
            jax.ShapeDtypeStruct((tokens, block), bf16),
            jax.ShapeDtypeStruct((tokens, block), bf16),
            jax.ShapeDtypeStruct((tokens, width), bf16),
        ),
        grid=(tokens // rows,),
        in_specs=[wide, pl.BlockSpec(weights.shape, lambda i: (0, 0, 0)), narrow],
        out_specs=[narrow, narrow, narrow, wide],
        name="feed",
    )(low, weights, grad_hidden)


def both_lanes(kv_ref, kk_ref, vv_ref):
    @pl.when(pl.program_id(0) == 0)
    def _():
        for index in range(kv_ref.shape[0]):
            kv = kv_ref[index].astype(f32)
            swapped = pltpu.roll(kv, HEAD_DIM, 1)
            lane = lax.broadcasted_iota(jnp.int32, kv.shape, 1)
            kk_ref[index] = jnp.where(lane < HEAD_DIM, kv, swapped).astype(bf16)
            vv_ref[index] = jnp.where(lane < HEAD_DIM, swapped, kv).astype(bf16)


def attend_kernel(seen_ref, q_ref, kv_ref, qpos_ref, kpos_ref, o_ref, lse_ref, kk_ref, vv_ref):
    rows = q_ref.shape[0]
    both_lanes(kv_ref, kk_ref, vv_ref)
    stacked = stack_heads(q_ref[...], rows)
    qpos = jnp.concatenate([qpos_ref[...]] * GROUP_HEADS, axis=0)

    def unit(index, carry, masked):
        top, total, acc = carry
        scores = dot(stacked, kk_ref[index], ((1,), (1,)))
        if masked:
            scores = jnp.where(kpos_ref[...] <= qpos, scores, masked_score)
        new_top = jnp.maximum(top, jnp.max(scores, axis=1, keepdims=True))
        weights = jnp.exp(scores - new_top)
        keep = jnp.exp(top - new_top)
        total = total * keep + jnp.sum(weights, axis=1, keepdims=True)
        acc = acc * keep + dot(weights.astype(bf16), vv_ref[index])
        return new_top, total, acc

    count = GROUP_HEADS * rows
    start = (
        jnp.full((count, 1), masked_score, f32),
        jnp.zeros((count, 1), f32),
        jnp.zeros((count, PAIR), f32),
    )
    carry = unit(0, start, True)
    top, total, acc = lax.fori_loop(1, seen_ref[0], lambda i, c: unit(i, c, False), carry)
    o_ref[...] = unstack_heads(acc / total, rows).astype(bf16)
    lse_ref[...] = as_row(top + jnp.log(total))


def attend_back_kernel(
    seen_ref, q_ref, do_ref, o_ref, kv_ref, lse_ref, qpos_ref, kpos_ref, cos_ref, sin_ref,
    dq_ref, dkv_ref, qs_ref, dos_ref, delta_ref, dqs_ref, kk_ref, vv_ref, dkk_ref, dvv_ref,
):
    rows = q_ref.shape[0]
    both_lanes(kv_ref, kk_ref, vv_ref)

    @pl.when(pl.program_id(0) == 0)
    def _():
        dkk_ref[...] = jnp.zeros_like(dkk_ref)
        dvv_ref[...] = jnp.zeros_like(dvv_ref)

    qs_ref[...] = stack_heads(q_ref[...], rows)
    grads = stack_heads(do_ref[...], rows)
    dos_ref[...] = grads
    outs = stack_heads(o_ref[...], rows)
    delta_ref[...] = as_row(jnp.sum(grads.astype(f32) * outs.astype(f32), axis=1, keepdims=True))

    def unit(index, masked):
        keys = kk_ref[index]
        scores = dot(keys, qs_ref[...], ((1,), (1,)))
        if masked:
            qpos = jnp.concatenate([qpos_ref[0:1, :]] * GROUP_HEADS, axis=1)
            scores = jnp.where(kpos_ref[...] <= qpos, scores, masked_score)
        probs = jnp.exp(scores - lse_ref[0:1, :])
        prob_grad = dot(vv_ref[index], dos_ref[...], ((1,), (1,)))
        score_grad = (probs * (prob_grad - delta_ref[0:1, :])).astype(bf16)
        dvv_ref[index] += dot(probs.astype(bf16), dos_ref[...])
        dkk_ref[index] += dot(score_grad, qs_ref[...])
        return dot(score_grad, keys, ((0,), (0,)))

    dqs_ref[...] = unit(0, True)

    @pl.loop(1, seen_ref[0])
    def _(index):
        dqs_ref[...] += unit(index, False)

    grads = unstack_heads(dqs_ref[...], rows) * HEAD_DIM ** (-0.5)
    cosine, sine = cos_ref[...], sin_ref[...]
    for i in range(dq_ref.shape[1] // PAIR):
        part = unrotate(grads[:, i * PAIR : (i + 1) * PAIR], cosine, sine)
        dq_ref[:, i * PAIR : (i + 1) * PAIR] = part.astype(bf16)

    @pl.when(pl.program_id(0) == pl.num_programs(0) - 1)
    def _():
        for index in range(kv_ref.shape[0]):
            keys, values = dkk_ref[index], dvv_ref[index]
            keys = keys + pltpu.roll(keys, HEAD_DIM, 1)
            values = values + pltpu.roll(values, HEAD_DIM, 1)
            lane = lax.broadcasted_iota(jnp.int32, keys.shape, 1)
            dkv_ref[index] = jnp.where(lane < HEAD_DIM, keys, values).astype(bf16)


def block_rows(length):
    return min(128, length)


def whole(shape):
    zeros = (0,) * len(shape)
    return pl.BlockSpec(shape, lambda i, seen: zeros)


def attend(seen, q, kv, order):
    length, width = q.shape
    rows = block_rows(length)
    stacked = GROUP_HEADS * rows
    steps = length // rows
    return pl.pallas_call(
        attend_kernel,
        out_shape=(
            jax.ShapeDtypeStruct((length, width), bf16),
            jax.ShapeDtypeStruct((steps, 8, stacked), f32),
        ),
        grid_spec=pltpu.PrefetchScalarGridSpec(
            num_scalar_prefetch=1,
            grid=(steps,),
            in_specs=[
                pl.BlockSpec((rows, width), lambda i, seen: (i, 0)),
                whole(kv.shape),
                pl.BlockSpec((rows, 1), lambda i, seen: (i, 0)),
                whole((1, length)),
            ],
            out_specs=[
                pl.BlockSpec((rows, width), lambda i, seen: (i, 0)),
                pl.BlockSpec((pl.Squeezed(), 8, stacked), lambda i, seen: (i, 0, 0)),
            ],
            scratch_shapes=[pltpu.VMEM(kv.shape, bf16), pltpu.VMEM(kv.shape, bf16)],
        ),
        name="attend",
    )(seen, q, kv, order[:, None], order[None, :])


def attend_back(seen, q, do, o, kv, lse, order, cosine, sine):
    length, width = q.shape
    rows = block_rows(length)
    stacked = GROUP_HEADS * rows
    steps = length // rows
    return pl.pallas_call(
        attend_back_kernel,
        out_shape=(
            jax.ShapeDtypeStruct((length, width), bf16),
            jax.ShapeDtypeStruct(kv.shape, bf16),
        ),
        grid_spec=pltpu.PrefetchScalarGridSpec(
            num_scalar_prefetch=1,
            grid=(steps,),
            in_specs=[
                pl.BlockSpec((rows, width), lambda i, seen: (i, 0)),
                pl.BlockSpec((rows, width), lambda i, seen: (i, 0)),
                pl.BlockSpec((rows, width), lambda i, seen: (i, 0)),
                whole(kv.shape),
                pl.BlockSpec((pl.Squeezed(), 8, stacked), lambda i, seen: (i, 0, 0)),
                pl.BlockSpec((8, rows), lambda i, seen: (0, i)),
                whole((length, 1)),
                pl.BlockSpec((rows, PAIR), lambda i, seen: (i, 0)),
                pl.BlockSpec((rows, PAIR), lambda i, seen: (i, 0)),
            ],
            out_specs=[
                pl.BlockSpec((rows, width), lambda i, seen: (i, 0)),
                whole(kv.shape),
            ],
            scratch_shapes=[
                pltpu.VMEM((stacked, PAIR), bf16),
                pltpu.VMEM((stacked, PAIR), bf16),
                pltpu.VMEM((8, stacked), f32),
                pltpu.VMEM((stacked, PAIR), f32),
                pltpu.VMEM(kv.shape, bf16),
                pltpu.VMEM(kv.shape, bf16),
                pltpu.VMEM(kv.shape, f32),
                pltpu.VMEM(kv.shape, f32),
            ],
        ),
        name="attend_back",
    )(
        seen, q, do, o, kv, lse, jnp.broadcast_to(order[None, :], (8, length)), order[:, None],
        cosine, sine,
    )


def normalize(values):
    inverse = lax.rsqrt(jnp.mean(values * values, axis=-1, keepdims=True) + epsilon)
    return values * inverse, inverse


def norm_back(inner, normed, inverse):
    return inverse * (inner - normed * jnp.mean(inner * normed, axis=-1, keepdims=True))


def rope_tables(positions):
    half_dim = HEAD_DIM // 2
    frequency = rope_base ** (-(jnp.arange(half_dim).astype(f32) * 2.0 / HEAD_DIM))
    angles = positions.astype(f32)[:, None] * frequency
    times = PAIR // half_dim
    return jnp.tile(jnp.cos(angles), (1, times)), jnp.tile(jnp.sin(angles), (1, times))


def unrotate_keys(grads, cosine, sine):
    half_dim = HEAD_DIM // 2
    sines = grads * sine
    turned = jnp.concatenate([-sines[:, half_dim:], sines[:, :half_dim]], axis=1)
    return grads * cosine - turned


def tie(*values):
    return lax.optimization_barrier(values)


def solution(mesh):
    n_dp = mesh.shape["dp"]
    n_seq = mesh.shape["seq"]
    planes = n_seq // GROUP
    halves = n_dp // 2
    both = ("dp", "seq")

    in_plane = [[GROUP * p + w for w in range(GROUP)] for p in range(planes)]
    across_dp = [
        [c * n_seq + GROUP * p + w for c in range(n_dp) for p in range(planes)] for w in range(GROUP)
    ]
    in_plane_dp = [
        [c * n_seq + GROUP * p + w for c in range(n_dp) for w in range(GROUP)] for p in range(planes)
    ]
    across = [[GROUP * p + w for p in range(planes)] for w in range(GROUP)]

    def xor_w(value, j):
        return lax.ppermute(value, "seq", [(s, s ^ j) for s in range(n_seq)])

    def shift_z(value, t):
        return lax.ppermute(value, "seq", [(s, (s + GROUP * t) % n_seq) for s in range(n_seq)])

    def shift_dp(value, t):
        return lax.ppermute(value, "dp", [(c, (c + t) % n_dp) for c in range(n_dp)])

    def gather_w(value):
        first = xor_w(value, 1)
        second = xor_w(value, 2)
        half = value.shape[0] // 2
        third = jnp.concatenate([xor_w(first[:half], 2), xor_w(second[half:], 1)], axis=0)
        return jnp.concatenate([value, first, second, third], axis=0)

    def scatter_w(slots):
        got = [xor_w(slots[j], j) for j in range(1, GROUP)]
        return functools.reduce(jnp.add, [g.astype(f32) for g in got], slots[0].astype(f32))

    def gather_z(value):
        return [value] + [shift_z(value, t) for t in range(1, planes)]

    def scatter_z(slots):
        got = [shift_z(slots[t], -t) for t in range(1, planes)]
        return functools.reduce(jnp.add, [g.astype(f32) for g in got], slots[0].astype(f32))

    def gather_dp(value):
        return jnp.concatenate([value] + [shift_dp(value, t) for t in range(1, n_dp)], axis=0)

    def pick(value, index, count, axis):
        size = value.shape[axis] // count
        return lax.dynamic_slice_in_dim(value, index * size, size, axis)

    def exchange_dp(value, c, axis):
        parts = [pick(value, c, n_dp, axis)]
        for t in range(1, n_dp):
            parts.append(shift_dp(pick(value, (c + t) % n_dp, n_dp, axis), t))
        return jnp.concatenate(parts, axis=0)

    def collect_dp(value, c):
        slots = [value] + [shift_dp(value, t) for t in range(1, n_dp)]
        out = []
        for member in range(n_dp):
            chosen = slots[0]
            for t in range(1, n_dp):
                chosen = jnp.where((c - t) % n_dp == member, slots[t], chosen)
            out.append(chosen)
        return out

    def body(
        inputs, positions, select, cotangent, gain_attn, w_query, w_key, w_value, w_out, gain_mlp,
        w_gate, w_up, w_down,
    ):
        seqs, rows, width = inputs.shape
        tokens = seqs * rows
        shard = w_query.shape[0]
        ff_rows = w_down.shape[0]
        ff_block = w_gate.shape[1] // planes
        q_width = GROUP_HEADS * HEAD_DIM
        s = lax.axis_index("seq")
        c = lax.axis_index("dp")
        p = s // GROUP
        w = s % GROUP

        gain_one = gain_attn.astype(f32)[:, None]
        gain_two = gain_mlp.astype(f32)[:, None]

        def scaled(weight, gain):
            return (weight.astype(f32) * gain).astype(bf16)

        q_cols = scaled(w_query, gain_one).reshape(shard, GROUP, n_dp, q_width // n_dp)
        kv_cols = jnp.concatenate(
            [
                scaled(w_key, gain_one).reshape(shard, GROUP, HEAD_DIM),
                scaled(w_value, gain_one).reshape(shard, GROUP, HEAD_DIM),
            ],
            axis=-1,
        ).reshape(shard, GROUP, n_dp, PAIR // n_dp)
        qkv_cols = jnp.concatenate([q_cols, kv_cols], axis=-1)
        qkv_part = lax.dynamic_index_in_dim(qkv_cols, c, 2, keepdims=False)
        qkv_part = lax.all_to_all(
            jnp.transpose(qkv_part, (1, 0, 2)), "seq", 0, 0, axis_index_groups=in_plane, tiled=True
        )
        part_width = (q_width + PAIR) // n_dp
        qkv_part = qkv_part.reshape(GROUP * shard, part_width)
        own_pos = positions.reshape(1, tokens)
        plane_pos = jnp.concatenate([own_pos] + [xor_w(own_pos, j) for j in range(1, GROUP)], axis=1)
        x_in = inputs.reshape(tokens, width).astype(f32)
        normed_one, inverse_one = normalize(x_in)
        low_one, qkv_part, plane_pos = tie(normed_one.astype(bf16), qkv_part, plane_pos)

        ring = [qkv_part] + [shift_z(qkv_part, -t) for t in range(1, planes)]
        qkv_ring = jnp.concatenate(ring + ring[: planes - 1], axis=0)
        qkv_mine = lax.dynamic_slice_in_dim(
            qkv_ring, ((planes - p) % planes) * GROUP * shard, width, 0
        )
        low_one = gather_w(low_one)

        piece = shard // halves
        gate_up = jnp.where(c // halves == 0, scaled(w_gate, gain_two), scaled(w_up, gain_two))
        out_part, gate_up, qkv_mine = tie(
            pick(w_out, c, n_dp, 1), pick(gate_up, c % halves, halves, 0), qkv_mine
        )
        qkv_full = collect_dp(qkv_mine, c)
        out_part = lax.ppermute(
            out_part, "seq", [(i, GROUP * (i % planes) + i // planes) for i in range(n_seq)]
        )
        gate_up_sent = [
            shift_z(pick(gate_up, (p + t) % planes, planes, 1), t) if t
            else pick(gate_up, p, planes, 1)
            for t in range(planes)
        ]
        down_full = lax.all_gather(
            pick(w_down, c, n_dp, 1), both, axis_index_groups=in_plane_dp, tiled=False
        )
        out_part, down_full = tie(out_part, down_full)
        down_full = down_full.reshape(n_dp, ff_block, width // n_dp)
        out_full = lax.all_gather(out_part, both, axis_index_groups=across_dp, tiled=False)
        out_full = out_full.reshape(n_dp, planes * shard, width // n_dp)

        blocks = [
            (i * GROUP + j) * halves + h
            for h in range(halves) for j in range(GROUP) for i in range(planes)
        ]

        def column_blocks(value, which):
            return jnp.concatenate([value[:, i * piece : (i + 1) * piece] for i in which], axis=1)

        def reorder(value):
            return column_blocks(value, blocks)

        def order_back(value):
            return column_blocks(value, [blocks.index(i) for i in range(len(blocks))])

        cosine, sine = rope_tables(plane_pos.reshape(GROUP * tokens))

        grad_y = (
            cotangent.astype(f32) * select.astype(f32)[..., None]
        ).reshape(tokens, width)
        cut = q_width // n_dp
        plane_tokens = GROUP * tokens
        qkv_weights = jnp.concatenate(
            [one[:, :cut] for one in qkv_full] + [one[:, cut:] for one in qkv_full], axis=1
        )
        q, kv_low = project(low_one, qkv_weights, cosine, sine)
        kv_all = jnp.stack(gather_z(kv_low))
        grad_y_low, kv_all = tie(grad_y.astype(bf16), kv_all)
        *gate_up_sent, q = tie(*gate_up_sent, q)
        gate_up_part = jnp.zeros((planes, piece, ff_block), bf16)
        for t in range(planes):
            gate_up_part = lax.dynamic_update_index_in_dim(
                gate_up_part, gate_up_sent[t], (p - t) % planes, 0
            )
        gate_up_full = lax.all_gather(
            gate_up_part, both, axis_index_groups=in_plane_dp, tiled=False
        )
        gate_up_full = gate_up_full.reshape(2, width, ff_block)
        grad_y_all = jnp.concatenate(gather_z(grad_y_low), axis=0)

        def by_seq(value, axis):
            shape = value.shape
            value = value.reshape(shape[:axis] + (GROUP, seqs, rows) + shape[axis + 1 :])
            value = jnp.moveaxis(value, axis + 1, 0)
            return value.reshape((seqs,) + shape[:axis] + (GROUP * rows,) + shape[axis + 1 :])

        def from_seq(value, axis):
            shape = value.shape[1:]
            value = value.reshape((seqs,) + shape[:axis] + (GROUP, rows) + shape[axis + 1 :])
            value = jnp.moveaxis(value, 0, axis + 1)
            return value.reshape(shape[:axis] + (GROUP * seqs * rows,) + shape[axis + 1 :])

        order = jnp.concatenate([(w ^ j) * rows + jnp.arange(rows) for j in range(GROUP)])
        order = order.astype(jnp.int32)
        seen = (p + 1).astype(jnp.int32).reshape(1)
        q_seq = by_seq(q, 0)
        kv_seq = by_seq(kv_all, 1)
        cos_seq = by_seq(cosine, 0)
        sin_seq = by_seq(sine, 0)
        pieces = [attend(seen, q_seq[i], kv_seq[i], order) for i in range(seqs)]
        o_seq = [one[0] for one in pieces]
        lse_seq = [one[1] for one in pieces]
        o = from_seq(jnp.stack(o_seq), 0)

        branch = jnp.concatenate([dot(o, out_full[i]).astype(bf16) for i in range(n_dp)], axis=1)
        branch = scatter_w([branch[j * tokens : (j + 1) * tokens] for j in range(GROUP)])
        x_mid = x_in + branch

        normed_two, inverse_two = normalize(x_mid)
        low_two = reorder(normed_two.astype(bf16))
        low_two, grad_y_all = tie(low_two, grad_y_all)
        low_two_own, *low_two_sent = gather_z(low_two)
        grad_hidden = functools.reduce(
            jnp.add,
            [
                dot(pick(grad_y_all, i, n_dp, 1), down_full[i], ((1,), (1,)))
                for i in range(n_dp)
            ],
        )
        *low_two_sent, grad_hidden = tie(*low_two_sent, grad_hidden)
        low_two = jnp.concatenate([low_two_own] + low_two_sent, axis=0)
        hidden, grad_gate, grad_up, grad_low_two = feed(low_two, gate_up_full, grad_hidden)
        hidden_later, grad_gate_later, grad_up_later, grad_low_two = tie(
            hidden, grad_gate, grad_up, grad_low_two
        )
        inner_sent = [
            shift_z(grad_low_two[t * tokens : (t + 1) * tokens], -t) for t in range(1, planes)
        ]

        hidden_all = gather_dp(hidden_later)
        down_sum = dot(hidden_all, exchange_dp(grad_y_all, c, 1), ((0,), (0,))).astype(bf16)

        low_two_all = gather_dp(low_two)
        if halves > 1:
            low_two_all = pick(low_two_all, c % halves, halves, 1)

        def of_member(member):
            return jnp.where(member // halves == 0, grad_gate_later, grad_up_later)

        gate_up_grads = [of_member(c)]
        for t in range(1, n_dp):
            gate_up_grads.append(shift_dp(of_member((c + t) % n_dp), t))
        gate_up_grads = jnp.concatenate(gate_up_grads, axis=0)
        gate_up_sum = dot(low_two_all, gate_up_grads, ((0,), (0,))).astype(bf16)

        inner_sent[0], gate_up_sum = tie(inner_sent[0], gate_up_sum)
        *inner_rest, down_sum = tie(*inner_sent[1:], down_sum)
        inner_sent = [inner_sent[0]] + inner_rest
        mixed = jnp.concatenate(
            [dot(hidden_later, down_full[i]).astype(bf16) for i in range(n_dp)], axis=1
        )
        *inner_sent, mixed = tie(*inner_sent, mixed)
        inner_two = functools.reduce(
            jnp.add, [g.astype(f32) for g in inner_sent], grad_low_two[:tokens].astype(f32)
        )
        grad_x_mid = grad_y + norm_back(order_back(inner_two), normed_two, inverse_two)

        mixed, grad_x_low = tie(mixed, grad_x_mid.astype(bf16))
        mixed_sent = [shift_z(mixed[t * tokens : (t + 1) * tokens], -t) for t in range(1, planes)]
        gate_up_sum = lax.psum_scatter(gate_up_sum, "seq", axis_index_groups=in_plane, tiled=True)
        down_sum = lax.psum_scatter(
            down_sum, "seq", axis_index_groups=in_plane, tiled=True
        )
        gate_up_sum = gate_up_sum.reshape(planes, piece, ff_block)

        grad_branch = gather_w(grad_x_low)
        early = planes - 2
        *mixed_sent[:early], grad_branch = tie(*mixed_sent[:early], grad_branch)
        grad_o = functools.reduce(
            jnp.add,
            [dot(pick(grad_branch, i, n_dp, 1), out_full[i], ((1,), (1,))) for i in range(n_dp)],
        ).astype(bf16)

        out_part_sum = dot(gather_dp(o), exchange_dp(grad_branch, c, 1), ((0,), (0,))).astype(bf16)
        grad_o_seq = by_seq(grad_o, 0)
        *late, grad_o_seq, out_part_sum = tie(*mixed_sent[early:], grad_o_seq, out_part_sum)
        mixed_sent = mixed_sent[:early] + list(late)
        gate_up_sum, out_part_sum = tie(gate_up_sum, out_part_sum)
        out_sum = lax.psum_scatter(out_part_sum, "seq", axis_index_groups=across, tiled=True)
        pieces = [
            attend_back(
                seen, q_seq[i], grad_o_seq[i], o_seq[i], kv_seq[i], lse_seq[i], order,
                cos_seq[i], sin_seq[i],
            )
            for i in range(seqs)
        ]
        grad_q = jnp.stack([one[0] for one in pieces])
        mixed = functools.reduce(
            jnp.add, [g.astype(f32) for g in mixed_sent], mixed[:tokens].astype(f32)
        )
        query_pre = from_seq(grad_q, 0)
        grad_kv = from_seq(jnp.stack([one[1] for one in pieces]), 1)
        grad_kv = scatter_z([grad_kv[t] for t in range(planes)])
        grad_kv, gate_up_late = tie(grad_kv, gate_up_sum)
        gate_up_sent = []
        for t in range(planes):
            block = lax.dynamic_index_in_dim(gate_up_late, (p + t) % planes, 0, keepdims=False)
            gate_up_sent.append(shift_z(block, t) if t else block)
        query_pre, out_sum = tie(query_pre, out_sum)
        key_pre = unrotate_keys(
            grad_kv[:, :HEAD_DIM], cosine[:, :HEAD_DIM], sine[:, :HEAD_DIM]
        )
        kv_pre = jnp.concatenate([key_pre, grad_kv[:, HEAD_DIM:]], axis=1).astype(bf16)
        pre = [
            jnp.concatenate(
                [query_pre[:, i * cut : (i + 1) * cut], pick(kv_pre, i, n_dp, 1)], axis=1
            )
            for i in range(n_dp)
        ]
        outputs = (x_mid + mixed).astype(bf16).reshape(seqs, rows, width)

        grad_low_one = dot(
            jnp.concatenate([query_pre, kv_pre], axis=1), qkv_weights, ((1,), (1,))
        ).astype(bf16)
        inner_one = scatter_w([grad_low_one[j * tokens : (j + 1) * tokens] for j in range(GROUP)])
        grad_inputs = grad_x_mid + norm_back(inner_one, normed_one, inverse_one)
        grad_inputs = grad_inputs.reshape(seqs, rows, width)

        qkv_sum = dot(
            gather_dp(low_one),
            exchange_dp(jnp.concatenate(pre, axis=1), c, 1),
            ((0,), (0,)),
        ).astype(bf16)
        *gate_up_sent, down_sum, qkv_sum = tie(*gate_up_sent, down_sum, qkv_sum)
        out_sum = lax.ppermute(
            out_sum, "seq", [(GROUP * (i % planes) + i // planes, i) for i in range(n_seq)]
        )
        grad_w_out = jnp.concatenate(collect_dp(out_sum, c), axis=1).astype(f32)

        qkv_sum = lax.psum_scatter(
            qkv_sum, "seq", axis_index_groups=across, tiled=True
        )
        qkv_sum = qkv_sum.reshape(GROUP, shard, part_width)
        qkv_sum = lax.all_to_all(qkv_sum, "seq", 0, 0, axis_index_groups=in_plane, tiled=True)
        qkv_sum = collect_dp(qkv_sum, c)
        q_sum = jnp.concatenate(
            [one[j][:, :cut] for j in range(GROUP) for one in qkv_sum], axis=1
        ).astype(f32)
        kv_sum = jnp.concatenate(
            [one[j][:, cut:] for j in range(GROUP) for one in qkv_sum], axis=1
        ).astype(f32).reshape(shard, GROUP, PAIR)
        k_sum = kv_sum[..., :HEAD_DIM].reshape(shard, GROUP * HEAD_DIM)
        v_sum = kv_sum[..., HEAD_DIM:].reshape(shard, GROUP * HEAD_DIM)

        grad_w_down = jnp.concatenate(collect_dp(down_sum, c), axis=1).astype(f32)
        gate_up_rows = jnp.zeros((planes, piece, ff_block), bf16)
        for t in range(planes):
            gate_up_rows = lax.dynamic_update_index_in_dim(
                gate_up_rows, gate_up_sent[t], (p - t) % planes, 0
            )
        gate_up_rows = collect_dp(gate_up_rows, c)

        def rows_of(members):
            wide = [jnp.concatenate([one[i] for i in range(planes)], axis=1) for one in members]
            return jnp.concatenate(wide, axis=0).astype(f32)

        gate_rows = rows_of(gate_up_rows[:halves])
        up_rows = rows_of(gate_up_rows[halves:])
        grad_w_gate = gate_rows * gain_two
        grad_w_up = up_rows * gain_two
        grad_gain_mlp = jnp.sum(
            gate_rows * w_gate.astype(f32) + up_rows * w_up.astype(f32), axis=1
        )
        grad_gain_attn = (
            jnp.sum(q_sum * w_query.astype(f32), axis=1)
            + jnp.sum(k_sum * w_key.astype(f32), axis=1)
            + jnp.sum(v_sum * w_value.astype(f32), axis=1)
        )

        return (
            outputs,
            grad_inputs,
            grad_gain_attn,
            q_sum * gain_one,
            k_sum * gain_one,
            v_sum * gain_one,
            grad_w_out,
            grad_gain_mlp,
            grad_w_gate,
            grad_w_up,
            grad_w_down,
        )

    tokens_spec = P("dp", "seq", None)
    in_specs = (
        tokens_spec,
        P("dp", "seq"),
        P("dp", "seq"),
        tokens_spec,
        P("seq"),
        P("seq", None),
        P("seq", None),
        P("seq", None),
        P("seq", None),
        P("seq"),
        P("seq", None),
        P("seq", None),
        P("seq", None),
    )
    out_specs = (
        tokens_spec,
        tokens_spec,
        P("seq"),
        P("seq", None),
        P("seq", None),
        P("seq", None),
        P("seq", None),
        P("seq"),
        P("seq", None),
        P("seq", None),
        P("seq", None),
    )
    return jax.shard_map(body, mesh=mesh, in_specs=in_specs, out_specs=out_specs, check_vma=False)
```

```python
import functools

import jax
import jax.numpy as jnp
from jax import lax
from jax.experimental import pallas as pl
from jax.experimental.pallas import tpu as pltpu
from jax.sharding import PartitionSpec as P

HEADS = 32
KV_HEADS = 4
HEAD_DIM = 64
GROUP = KV_HEADS
GROUP_HEADS = HEADS // GROUP
PAIR = 2 * HEAD_DIM

epsilon = 1e-05
rope_base = 10000.0
masked_score = -1e30

f32 = jnp.float32
bf16 = jnp.bfloat16


def dot(left, right, contract=((1,), (0,))):
    return lax.dot_general(left, right, (contract, ((), ())), preferred_element_type=f32)


def stack_heads(block, rows):
    lane = lax.broadcasted_iota(jnp.int32, (rows, PAIR), 1)
    parts = []
    for pair in range(GROUP_HEADS // 2):
        both = block[:, pair * PAIR : (pair + 1) * PAIR]
        parts.append(jnp.where(lane < HEAD_DIM, both, jnp.zeros_like(both)))
        parts.append(jnp.where(lane >= HEAD_DIM, both, jnp.zeros_like(both)))
    return jnp.concatenate(parts, axis=0)


def unstack_heads(stacked, rows):
    lane = lax.broadcasted_iota(jnp.int32, (rows, PAIR), 1)
    parts = []
    for pair in range(GROUP_HEADS // 2):
        low = stacked[2 * pair * rows : (2 * pair + 1) * rows]
        high = stacked[(2 * pair + 1) * rows : (2 * pair + 2) * rows]
        parts.append(jnp.where(lane < HEAD_DIM, low, high))
    return jnp.concatenate(parts, axis=1)


def as_row(column):
    wide = jnp.broadcast_to(column, (column.shape[0], 128))
    return jnp.transpose(wide)[:8]


def turn(values):
    width = values.shape[1]
    half_dim = HEAD_DIM // 2
    lane = lax.broadcasted_iota(jnp.int32, values.shape, 1)
    ahead = pltpu.roll(values, width - half_dim, 1)
    behind = pltpu.roll(values, half_dim, 1)
    return jnp.where(lane % HEAD_DIM < half_dim, -ahead, behind)


def rotate(values, cosine, sine):
    return values * cosine + turn(values) * sine


def unrotate(grads, cosine, sine):
    return grads * cosine - turn(grads * sine)


def project_kernel(low_ref, w_ref, cos_ref, sin_ref, q_ref, kv_ref):
    made = dot(low_ref[...], w_ref[...])
    cosine, sine = cos_ref[...], sin_ref[...]
    for i in range(q_ref.shape[1] // PAIR):
        q = rotate(made[:, i * PAIR : (i + 1) * PAIR], cosine, sine).astype(bf16)
        q_ref[:, i * PAIR : (i + 1) * PAIR] = (q.astype(f32) * HEAD_DIM ** (-0.5)).astype(bf16)
    kv = made[:, q_ref.shape[1] :]
    lane = lax.broadcasted_iota(jnp.int32, kv.shape, 1)
    kv_ref[...] = jnp.where(lane < HEAD_DIM, rotate(kv, cosine, sine), kv).astype(bf16)


def project(low, weights, cosine, sine):
    tokens, width = low.shape
    q_width = weights.shape[1] - PAIR
    rows = min(256, tokens)
    return pl.pallas_call(
        project_kernel,
        out_shape=(
            jax.ShapeDtypeStruct((tokens, q_width), bf16),
            jax.ShapeDtypeStruct((tokens, PAIR), bf16),
        ),
        grid=(tokens // rows,),
        in_specs=[
            pl.BlockSpec((rows, width), lambda i: (i, 0)),
            pl.BlockSpec(weights.shape, lambda i: (0, 0)),
            pl.BlockSpec((rows, PAIR), lambda i: (i, 0)),
            pl.BlockSpec((rows, PAIR), lambda i: (i, 0)),
        ],
        out_specs=[
            pl.BlockSpec((rows, q_width), lambda i: (i, 0)),
            pl.BlockSpec((rows, PAIR), lambda i: (i, 0)),
        ],
        name="project",
    )(low, weights, cosine, sine)


def feed_kernel(low_ref, w_ref, grad_hidden_ref, hidden_ref, grad_gate_ref, grad_up_ref, back_ref):
    low = low_ref[...]
    gate = dot(low, w_ref[0])
    up = dot(low, w_ref[1])
    grad_hidden = grad_hidden_ref[...]
    sigmoid_gate = 1.0 / (1.0 + jnp.exp(-gate))
    silu = gate * sigmoid_gate
    hidden_ref[...] = (silu * up).astype(bf16)
    grad_gate = (
        grad_hidden * up * sigmoid_gate * (1.0 + gate * (1.0 - sigmoid_gate))
    ).astype(bf16)
    grad_up = (grad_hidden * silu).astype(bf16)
    grad_gate_ref[...] = grad_gate
    grad_up_ref[...] = grad_up
    back_ref[...] = (
        dot(grad_gate, w_ref[0], ((1,), (1,))) + dot(grad_up, w_ref[1], ((1,), (1,)))
    ).astype(bf16)


def feed(low, weights, grad_hidden):
    tokens, width = low.shape
    block = weights.shape[2]
    rows = min(256, tokens)
    narrow = pl.BlockSpec((rows, block), lambda i: (i, 0))
    wide = pl.BlockSpec((rows, width), lambda i: (i, 0))
    return pl.pallas_call(
        feed_kernel,
        out_shape=(
            jax.ShapeDtypeStruct((tokens, block), bf16),
            jax.ShapeDtypeStruct((tokens, block), bf16),
            jax.ShapeDtypeStruct((tokens, block), bf16),
            jax.ShapeDtypeStruct((tokens, width), bf16),
        ),
        grid=(tokens // rows,),
        in_specs=[wide, pl.BlockSpec(weights.shape, lambda i: (0, 0, 0)), narrow],
        out_specs=[narrow, narrow, narrow, wide],
        name="feed",
    )(low, weights, grad_hidden)


def both_lanes(kv_ref, kk_ref, vv_ref):
    @pl.when(pl.program_id(0) == 0)
    def _():
        for index in range(kv_ref.shape[0]):
            kv = kv_ref[index].astype(f32)
            swapped = pltpu.roll(kv, HEAD_DIM, 1)
            lane = lax.broadcasted_iota(jnp.int32, kv.shape, 1)
            kk_ref[index] = jnp.where(lane < HEAD_DIM, kv, swapped).astype(bf16)
            vv_ref[index] = jnp.where(lane < HEAD_DIM, swapped, kv).astype(bf16)


def attend_kernel(seen_ref, q_ref, kv_ref, qpos_ref, kpos_ref, o_ref, lse_ref, kk_ref, vv_ref):
    rows = q_ref.shape[0]
    both_lanes(kv_ref, kk_ref, vv_ref)
    stacked = stack_heads(q_ref[...], rows)
    qpos = jnp.concatenate([qpos_ref[...]] * GROUP_HEADS, axis=0)

    def unit(index, carry, masked):
        top, total, acc = carry
        scores = dot(stacked, kk_ref[index], ((1,), (1,)))
        if masked:
            scores = jnp.where(kpos_ref[...] <= qpos, scores, masked_score)
        new_top = jnp.maximum(top, jnp.max(scores, axis=1, keepdims=True))
        weights = jnp.exp(scores - new_top)
        keep = jnp.exp(top - new_top)
        total = total * keep + jnp.sum(weights, axis=1, keepdims=True)
        acc = acc * keep + dot(weights.astype(bf16), vv_ref[index])
        return new_top, total, acc

    count = GROUP_HEADS * rows
    start = (
        jnp.full((count, 1), masked_score, f32),
        jnp.zeros((count, 1), f32),
        jnp.zeros((count, PAIR), f32),
    )
    carry = unit(0, start, True)
    top, total, acc = lax.fori_loop(1, seen_ref[0], lambda i, c: unit(i, c, False), carry)
    o_ref[...] = unstack_heads(acc / total, rows).astype(bf16)
    lse_ref[...] = as_row(top + jnp.log(total))


def attend_back_kernel(
    seen_ref, q_ref, do_ref, o_ref, kv_ref, lse_ref, qpos_ref, kpos_ref, cos_ref, sin_ref,
    dq_ref, dkv_ref, qs_ref, dos_ref, delta_ref, dqs_ref, kk_ref, vv_ref, dkk_ref, dvv_ref,
):
    rows = q_ref.shape[0]
    both_lanes(kv_ref, kk_ref, vv_ref)

    @pl.when(pl.program_id(0) == 0)
    def _():
        dkk_ref[...] = jnp.zeros_like(dkk_ref)
        dvv_ref[...] = jnp.zeros_like(dvv_ref)

    qs_ref[...] = stack_heads(q_ref[...], rows)
    grads = stack_heads(do_ref[...], rows)
    dos_ref[...] = grads
    outs = stack_heads(o_ref[...], rows)
    delta_ref[...] = as_row(jnp.sum(grads.astype(f32) * outs.astype(f32), axis=1, keepdims=True))

    def unit(index, masked):
        keys = kk_ref[index]
        scores = dot(keys, qs_ref[...], ((1,), (1,)))
        if masked:
            qpos = jnp.concatenate([qpos_ref[0:1, :]] * GROUP_HEADS, axis=1)
            scores = jnp.where(kpos_ref[...] <= qpos, scores, masked_score)
        probs = jnp.exp(scores - lse_ref[0:1, :])
        prob_grad = dot(vv_ref[index], dos_ref[...], ((1,), (1,)))
        score_grad = (probs * (prob_grad - delta_ref[0:1, :])).astype(bf16)
        dvv_ref[index] += dot(probs.astype(bf16), dos_ref[...])
        dkk_ref[index] += dot(score_grad, qs_ref[...])
        return dot(score_grad, keys, ((0,), (0,)))

    dqs_ref[...] = unit(0, True)

    @pl.loop(1, seen_ref[0])
    def _(index):
        dqs_ref[...] += unit(index, False)

    grads = unstack_heads(dqs_ref[...], rows) * HEAD_DIM ** (-0.5)
    cosine, sine = cos_ref[...], sin_ref[...]
    for i in range(dq_ref.shape[1] // PAIR):
        part = unrotate(grads[:, i * PAIR : (i + 1) * PAIR], cosine, sine)
        dq_ref[:, i * PAIR : (i + 1) * PAIR] = part.astype(bf16)

    @pl.when(pl.program_id(0) == pl.num_programs(0) - 1)
    def _():
        for index in range(kv_ref.shape[0]):
            keys, values = dkk_ref[index], dvv_ref[index]
            keys = keys + pltpu.roll(keys, HEAD_DIM, 1)
            values = values + pltpu.roll(values, HEAD_DIM, 1)
            lane = lax.broadcasted_iota(jnp.int32, keys.shape, 1)
            dkv_ref[index] = jnp.where(lane < HEAD_DIM, keys, values).astype(bf16)


def block_rows(length):
    return min(128, length)


def whole(shape):
    zeros = (0,) * len(shape)
    return pl.BlockSpec(shape, lambda i, seen: zeros)


def attend(seen, q, kv, order):
    length, width = q.shape
    rows = block_rows(length)
    stacked = GROUP_HEADS * rows
    steps = length // rows
    return pl.pallas_call(
        attend_kernel,
        out_shape=(
            jax.ShapeDtypeStruct((length, width), bf16),
            jax.ShapeDtypeStruct((steps, 8, stacked), f32),
        ),
        grid_spec=pltpu.PrefetchScalarGridSpec(
            num_scalar_prefetch=1,
            grid=(steps,),
            in_specs=[
                pl.BlockSpec((rows, width), lambda i, seen: (i, 0)),
                whole(kv.shape),
                pl.BlockSpec((rows, 1), lambda i, seen: (i, 0)),
                whole((1, length)),
            ],
            out_specs=[
                pl.BlockSpec((rows, width), lambda i, seen: (i, 0)),
                pl.BlockSpec((pl.Squeezed(), 8, stacked), lambda i, seen: (i, 0, 0)),
            ],
            scratch_shapes=[pltpu.VMEM(kv.shape, bf16), pltpu.VMEM(kv.shape, bf16)],
        ),
        name="attend",
    )(seen, q, kv, order[:, None], order[None, :])


def attend_back(seen, q, do, o, kv, lse, order, cosine, sine):
    length, width = q.shape
    rows = block_rows(length)
    stacked = GROUP_HEADS * rows
    steps = length // rows
    return pl.pallas_call(
        attend_back_kernel,
        out_shape=(
            jax.ShapeDtypeStruct((length, width), bf16),
            jax.ShapeDtypeStruct(kv.shape, bf16),
        ),
        grid_spec=pltpu.PrefetchScalarGridSpec(
            num_scalar_prefetch=1,
            grid=(steps,),
            in_specs=[
                pl.BlockSpec((rows, width), lambda i, seen: (i, 0)),
                pl.BlockSpec((rows, width), lambda i, seen: (i, 0)),
                pl.BlockSpec((rows, width), lambda i, seen: (i, 0)),
                whole(kv.shape),
                pl.BlockSpec((pl.Squeezed(), 8, stacked), lambda i, seen: (i, 0, 0)),
                pl.BlockSpec((8, rows), lambda i, seen: (0, i)),
                whole((length, 1)),
                pl.BlockSpec((rows, PAIR), lambda i, seen: (i, 0)),
                pl.BlockSpec((rows, PAIR), lambda i, seen: (i, 0)),
            ],
            out_specs=[
                pl.BlockSpec((rows, width), lambda i, seen: (i, 0)),
                whole(kv.shape),
            ],
            scratch_shapes=[
                pltpu.VMEM((stacked, PAIR), bf16),
                pltpu.VMEM((stacked, PAIR), bf16),
                pltpu.VMEM((8, stacked), f32),
                pltpu.VMEM((stacked, PAIR), f32),
                pltpu.VMEM(kv.shape, bf16),
                pltpu.VMEM(kv.shape, bf16),
                pltpu.VMEM(kv.shape, f32),
                pltpu.VMEM(kv.shape, f32),
            ],
        ),
        name="attend_back",
    )(
        seen, q, do, o, kv, lse, jnp.broadcast_to(order[None, :], (8, length)), order[:, None],
        cosine, sine,
    )


def normalize(values):
    inverse = lax.rsqrt(jnp.mean(values * values, axis=-1, keepdims=True) + epsilon)
    return values * inverse, inverse


def norm_back(inner, normed, inverse):
    return inverse * (inner - normed * jnp.mean(inner * normed, axis=-1, keepdims=True))


def rope_tables(positions):
    half_dim = HEAD_DIM // 2
    frequency = rope_base ** (-(jnp.arange(half_dim).astype(f32) * 2.0 / HEAD_DIM))
    angles = positions.astype(f32)[:, None] * frequency
    times = PAIR // half_dim
    return jnp.tile(jnp.cos(angles), (1, times)), jnp.tile(jnp.sin(angles), (1, times))


def unrotate_keys(grads, cosine, sine):
    half_dim = HEAD_DIM // 2
    sines = grads * sine
    turned = jnp.concatenate([-sines[:, half_dim:], sines[:, :half_dim]], axis=1)
    return grads * cosine - turned


def tie(*values):
    return lax.optimization_barrier(values)


def solution(mesh):
    n_dp = mesh.shape["dp"]
    n_seq = mesh.shape["seq"]
    planes = n_seq // GROUP
    halves = n_dp // 2
    both = ("dp", "seq")

    in_plane = [[GROUP * p + w for w in range(GROUP)] for p in range(planes)]
    across_dp = [
        [c * n_seq + GROUP * p + w for c in range(n_dp) for p in range(planes)] for w in range(GROUP)
    ]
    in_plane_dp = [
        [c * n_seq + GROUP * p + w for c in range(n_dp) for w in range(GROUP)] for p in range(planes)
    ]
    across = [[GROUP * p + w for p in range(planes)] for w in range(GROUP)]

    def xor_w(value, j):
        return lax.ppermute(value, "seq", [(s, s ^ j) for s in range(n_seq)])

    def shift_z(value, t):
        return lax.ppermute(value, "seq", [(s, (s + GROUP * t) % n_seq) for s in range(n_seq)])

    def shift_dp(value, t):
        return lax.ppermute(value, "dp", [(c, (c + t) % n_dp) for c in range(n_dp)])

    def gather_w(value):
        first = xor_w(value, 1)
        second = xor_w(value, 2)
        half = value.shape[0] // 2
        third = jnp.concatenate([xor_w(first[:half], 2), xor_w(second[half:], 1)], axis=0)
        return jnp.concatenate([value, first, second, third], axis=0)

    def scatter_w(slots):
        got = [xor_w(slots[j], j) for j in range(1, GROUP)]
        return functools.reduce(jnp.add, [g.astype(f32) for g in got], slots[0].astype(f32))

    def gather_z(value):
        return [value] + [shift_z(value, t) for t in range(1, planes)]

    def scatter_z(slots):
        got = [shift_z(slots[t], -t) for t in range(1, planes)]
        return functools.reduce(jnp.add, [g.astype(f32) for g in got], slots[0].astype(f32))

    def gather_dp(value):
        return jnp.concatenate([value] + [shift_dp(value, t) for t in range(1, n_dp)], axis=0)

    def pick(value, index, count, axis):
        size = value.shape[axis] // count
        return lax.dynamic_slice_in_dim(value, index * size, size, axis)

    def exchange_dp(value, c, axis):
        parts = [pick(value, c, n_dp, axis)]
        for t in range(1, n_dp):
            parts.append(shift_dp(pick(value, (c + t) % n_dp, n_dp, axis), t))
        return jnp.concatenate(parts, axis=0)

    def collect_dp(value, c):
        slots = [value] + [shift_dp(value, t) for t in range(1, n_dp)]
        out = []
        for member in range(n_dp):
            chosen = slots[0]
            for t in range(1, n_dp):
                chosen = jnp.where((c - t) % n_dp == member, slots[t], chosen)
            out.append(chosen)
        return out

    def body(
        inputs, positions, select, cotangent, gain_attn, w_query, w_key, w_value, w_out, gain_mlp,
        w_gate, w_up, w_down,
    ):
        seqs, rows, width = inputs.shape
        tokens = seqs * rows
        shard = w_query.shape[0]
        ff_rows = w_down.shape[0]
        ff_block = w_gate.shape[1] // planes
        q_width = GROUP_HEADS * HEAD_DIM
        s = lax.axis_index("seq")
        c = lax.axis_index("dp")
        p = s // GROUP
        w = s % GROUP

        gain_one = gain_attn.astype(f32)[:, None]
        gain_two = gain_mlp.astype(f32)[:, None]

        def scaled(weight, gain):
            return (weight.astype(f32) * gain).astype(bf16)

        q_cols = scaled(w_query, gain_one).reshape(shard, GROUP, n_dp, q_width // n_dp)
        kv_cols = jnp.concatenate(
            [
                scaled(w_key, gain_one).reshape(shard, GROUP, HEAD_DIM),
                scaled(w_value, gain_one).reshape(shard, GROUP, HEAD_DIM),
            ],
            axis=-1,
        ).reshape(shard, GROUP, n_dp, PAIR // n_dp)
        qkv_cols = jnp.concatenate([q_cols, kv_cols], axis=-1)
        qkv_part = lax.dynamic_index_in_dim(qkv_cols, c, 2, keepdims=False)
        qkv_part = lax.all_to_all(
            jnp.transpose(qkv_part, (1, 0, 2)), "seq", 0, 0, axis_index_groups=in_plane, tiled=True
        )
        part_width = (q_width + PAIR) // n_dp
        qkv_part = qkv_part.reshape(GROUP * shard, part_width)
        own_pos = positions.reshape(1, tokens)
        plane_pos = jnp.concatenate([own_pos] + [xor_w(own_pos, j) for j in range(1, GROUP)], axis=1)
        x_in = inputs.reshape(tokens, width).astype(f32)
        normed_one, inverse_one = normalize(x_in)
        low_one, qkv_part, plane_pos = tie(normed_one.astype(bf16), qkv_part, plane_pos)

        ring = [qkv_part] + [shift_z(qkv_part, -t) for t in range(1, planes)]
        low_one, *ring = tie(gather_w(low_one), *ring)
        qkv_ring = jnp.concatenate(ring + ring[: planes - 1], axis=0)
        qkv_mine = lax.dynamic_slice_in_dim(
            qkv_ring, ((planes - p) % planes) * GROUP * shard, width, 0
        )
        piece = shard // halves
        gate_up = jnp.where(c // halves == 0, scaled(w_gate, gain_two), scaled(w_up, gain_two))
        gate_up = pick(gate_up, c % halves, halves, 0)
        grad_y = (
            cotangent.astype(f32) * select.astype(f32)[..., None]
        ).reshape(tokens, width)
        out_part, grad_y_low, qkv_mine = tie(
            pick(w_out, c, n_dp, 1), grad_y.astype(bf16), qkv_mine
        )
        grad_y_sent = gather_z(grad_y_low)
        qkv_full = collect_dp(qkv_mine, c)
        out_part = lax.ppermute(
            out_part, "seq", [(i, GROUP * (i % planes) + i // planes) for i in range(n_seq)]
        )
        down_full = lax.all_gather(
            pick(w_down, c, n_dp, 1), both, axis_index_groups=in_plane_dp, tiled=False
        )
        down_full = down_full.reshape(n_dp, ff_block, width // n_dp)
        out_full = lax.all_gather(out_part, both, axis_index_groups=across_dp, tiled=False)
        out_full = out_full.reshape(n_dp, planes * shard, width // n_dp)

        blocks = [
            (i * GROUP + j) * halves + h
            for h in range(halves) for j in range(GROUP) for i in range(planes)
        ]

        def column_blocks(value, which):
            return jnp.concatenate([value[:, i * piece : (i + 1) * piece] for i in which], axis=1)

        def reorder(value):
            return column_blocks(value, blocks)

        def order_back(value):
            return column_blocks(value, [blocks.index(i) for i in range(len(blocks))])

        cosine, sine = rope_tables(plane_pos.reshape(GROUP * tokens))

        cut = q_width // n_dp
        plane_tokens = GROUP * tokens
        qkv_weights = jnp.concatenate(
            [one[:, :cut] for one in qkv_full] + [one[:, cut:] for one in qkv_full], axis=1
        )
        q, kv_low = project(low_one, qkv_weights, cosine, sine)
        kv_all = jnp.stack(gather_z(kv_low))
        *grad_y_sent, q = tie(*grad_y_sent, q)
        grad_y_all = jnp.concatenate(grad_y_sent, axis=0)
        gate_up, kv_all = tie(gate_up, kv_all)
        gate_up_sent = [
            shift_z(pick(gate_up, (p + t) % planes, planes, 1), t) if t
            else pick(gate_up, p, planes, 1)
            for t in range(planes)
        ]

        def by_seq(value, axis):
            shape = value.shape
            value = value.reshape(shape[:axis] + (GROUP, seqs, rows) + shape[axis + 1 :])
            value = jnp.moveaxis(value, axis + 1, 0)
            return value.reshape((seqs,) + shape[:axis] + (GROUP * rows,) + shape[axis + 1 :])

        def from_seq(value, axis):
            shape = value.shape[1:]
            value = value.reshape((seqs,) + shape[:axis] + (GROUP, rows) + shape[axis + 1 :])
            value = jnp.moveaxis(value, 0, axis + 1)
            return value.reshape(shape[:axis] + (GROUP * seqs * rows,) + shape[axis + 1 :])

        order = jnp.concatenate([(w ^ j) * rows + jnp.arange(rows) for j in range(GROUP)])
        order = order.astype(jnp.int32)
        seen = (p + 1).astype(jnp.int32).reshape(1)
        q_seq = by_seq(q, 0)
        kv_seq = by_seq(kv_all, 1)
        cos_seq = by_seq(cosine, 0)
        sin_seq = by_seq(sine, 0)
        pieces = [attend(seen, q_seq[i], kv_seq[i], order) for i in range(seqs)]
        o_seq = [one[0] for one in pieces]
        lse_seq = [one[1] for one in pieces]
        o = from_seq(jnp.stack(o_seq), 0)

        branch = jnp.concatenate([dot(o, out_full[i]).astype(bf16) for i in range(n_dp)], axis=1)
        *gate_up_sent, branch = tie(*gate_up_sent, branch)
        gate_up_part = jnp.zeros((planes, piece, ff_block), bf16)
        for t in range(planes):
            gate_up_part = lax.dynamic_update_index_in_dim(
                gate_up_part, gate_up_sent[t], (p - t) % planes, 0
            )
        gate_up_full = lax.all_gather(
            gate_up_part, both, axis_index_groups=in_plane_dp, tiled=False
        )
        gate_up_full = gate_up_full.reshape(2, width, ff_block)
        branch = scatter_w([branch[j * tokens : (j + 1) * tokens] for j in range(GROUP)])
        x_mid = x_in + branch

        normed_two, inverse_two = normalize(x_mid)
        low_two = reorder(normed_two.astype(bf16))
        low_two, grad_y_all = tie(low_two, grad_y_all)
        low_two_own, *low_two_sent = gather_z(low_two)
        grad_hidden = functools.reduce(
            jnp.add,
            [
                dot(pick(grad_y_all, i, n_dp, 1), down_full[i], ((1,), (1,)))
                for i in range(n_dp)
            ],
        )
        *low_two_sent, grad_hidden = tie(*low_two_sent, grad_hidden)
        low_two = jnp.concatenate([low_two_own] + low_two_sent, axis=0)
        hidden, grad_gate, grad_up, grad_low_two = feed(low_two, gate_up_full, grad_hidden)
        hidden_later, grad_gate_later, grad_up_later, grad_low_two = tie(
            hidden, grad_gate, grad_up, grad_low_two
        )
        inner_sent = [
            shift_z(grad_low_two[t * tokens : (t + 1) * tokens], -t) for t in range(1, planes)
        ]

        hidden_all = gather_dp(hidden_later)
        down_sum = dot(hidden_all, exchange_dp(grad_y_all, c, 1), ((0,), (0,))).astype(bf16)

        low_two_all = gather_dp(low_two)
        if halves > 1:
            low_two_all = pick(low_two_all, c % halves, halves, 1)

        def of_member(member):
            return jnp.where(member // halves == 0, grad_gate_later, grad_up_later)

        gate_up_grads = [of_member(c)]
        for t in range(1, n_dp):
            gate_up_grads.append(shift_dp(of_member((c + t) % n_dp), t))
        gate_up_grads = jnp.concatenate(gate_up_grads, axis=0)
        gate_up_sum = dot(low_two_all, gate_up_grads, ((0,), (0,))).astype(bf16)

        inner_sent[0], gate_up_sum = tie(inner_sent[0], gate_up_sum)
        *inner_rest, down_sum = tie(*inner_sent[1:], down_sum)
        inner_sent = [inner_sent[0]] + inner_rest
        mixed = jnp.concatenate(
            [dot(hidden_later, down_full[i]).astype(bf16) for i in range(n_dp)], axis=1
        )
        *inner_sent, mixed = tie(*inner_sent, mixed)
        inner_two = functools.reduce(
            jnp.add, [g.astype(f32) for g in inner_sent], grad_low_two[:tokens].astype(f32)
        )
        grad_x_mid = grad_y + norm_back(order_back(inner_two), normed_two, inverse_two)

        mixed, grad_x_low = tie(mixed, grad_x_mid.astype(bf16))
        mixed_sent = [shift_z(mixed[t * tokens : (t + 1) * tokens], -t) for t in range(1, planes)]
        gate_up_sum = lax.psum_scatter(gate_up_sum, "seq", axis_index_groups=in_plane, tiled=True)
        down_sum = lax.psum_scatter(
            down_sum, "seq", axis_index_groups=in_plane, tiled=True
        )
        gate_up_sum = gate_up_sum.reshape(planes, piece, ff_block)

        grad_branch = gather_w(grad_x_low)
        early = planes - 2
        *mixed_sent[:early], grad_branch = tie(*mixed_sent[:early], grad_branch)
        grad_o = functools.reduce(
            jnp.add,
            [dot(pick(grad_branch, i, n_dp, 1), out_full[i], ((1,), (1,))) for i in range(n_dp)],
        ).astype(bf16)

        out_part_sum = dot(gather_dp(o), exchange_dp(grad_branch, c, 1), ((0,), (0,))).astype(bf16)
        grad_o_seq = by_seq(grad_o, 0)
        *late, grad_o_seq, out_part_sum = tie(*mixed_sent[early:], grad_o_seq, out_part_sum)
        mixed_sent = mixed_sent[:early] + list(late)
        gate_up_sum, out_part_sum = tie(gate_up_sum, out_part_sum)
        out_sum = lax.psum_scatter(out_part_sum, "seq", axis_index_groups=across, tiled=True)
        pieces = [
            attend_back(
                seen, q_seq[i], grad_o_seq[i], o_seq[i], kv_seq[i], lse_seq[i], order,
                cos_seq[i], sin_seq[i],
            )
            for i in range(seqs)
        ]
        grad_q = jnp.stack([one[0] for one in pieces])
        mixed = functools.reduce(
            jnp.add, [g.astype(f32) for g in mixed_sent], mixed[:tokens].astype(f32)
        )
        query_pre = from_seq(grad_q, 0)
        grad_kv = from_seq(jnp.stack([one[1] for one in pieces]), 1)
        grad_kv = scatter_z([grad_kv[t] for t in range(planes)])
        grad_kv, gate_up_late = tie(grad_kv, gate_up_sum)
        gate_up_sent = []
        for t in range(planes):
            block = lax.dynamic_index_in_dim(gate_up_late, (p + t) % planes, 0, keepdims=False)
            gate_up_sent.append(shift_z(block, t) if t else block)
        query_pre, out_sum = tie(query_pre, out_sum)
        key_pre = unrotate_keys(
            grad_kv[:, :HEAD_DIM], cosine[:, :HEAD_DIM], sine[:, :HEAD_DIM]
        )
        kv_pre = jnp.concatenate([key_pre, grad_kv[:, HEAD_DIM:]], axis=1).astype(bf16)
        pre = [
            jnp.concatenate(
                [query_pre[:, i * cut : (i + 1) * cut], pick(kv_pre, i, n_dp, 1)], axis=1
            )
            for i in range(n_dp)
        ]
        outputs = (x_mid + mixed).astype(bf16).reshape(seqs, rows, width)

        grad_low_one = dot(
            jnp.concatenate([query_pre, kv_pre], axis=1), qkv_weights, ((1,), (1,))
        ).astype(bf16)
        inner_one = scatter_w([grad_low_one[j * tokens : (j + 1) * tokens] for j in range(GROUP)])
        grad_inputs = grad_x_mid + norm_back(inner_one, normed_one, inverse_one)
        grad_inputs = grad_inputs.reshape(seqs, rows, width)

        qkv_sum = dot(
            gather_dp(low_one),
            exchange_dp(jnp.concatenate(pre, axis=1), c, 1),
            ((0,), (0,)),
        ).astype(bf16)
        *gate_up_sent, down_sum, qkv_sum = tie(*gate_up_sent, down_sum, qkv_sum)
        out_sum = lax.ppermute(
            out_sum, "seq", [(GROUP * (i % planes) + i // planes, i) for i in range(n_seq)]
        )
        grad_w_out = jnp.concatenate(collect_dp(out_sum, c), axis=1).astype(f32)

        qkv_sum = lax.psum_scatter(
            qkv_sum, "seq", axis_index_groups=across, tiled=True
        )
        qkv_sum = qkv_sum.reshape(GROUP, shard, part_width)
        qkv_sum = lax.all_to_all(qkv_sum, "seq", 0, 0, axis_index_groups=in_plane, tiled=True)
        qkv_sum = collect_dp(qkv_sum, c)
        q_sum = jnp.concatenate(
            [one[j][:, :cut] for j in range(GROUP) for one in qkv_sum], axis=1
        ).astype(f32)
        kv_sum = jnp.concatenate(
            [one[j][:, cut:] for j in range(GROUP) for one in qkv_sum], axis=1
        ).astype(f32).reshape(shard, GROUP, PAIR)
        k_sum = kv_sum[..., :HEAD_DIM].reshape(shard, GROUP * HEAD_DIM)
        v_sum = kv_sum[..., HEAD_DIM:].reshape(shard, GROUP * HEAD_DIM)

        grad_w_down = jnp.concatenate(collect_dp(down_sum, c), axis=1).astype(f32)
        gate_up_rows = jnp.zeros((planes, piece, ff_block), bf16)
        for t in range(planes):
            gate_up_rows = lax.dynamic_update_index_in_dim(
                gate_up_rows, gate_up_sent[t], (p - t) % planes, 0
            )
        gate_up_rows = collect_dp(gate_up_rows, c)

        def rows_of(members):
            wide = [jnp.concatenate([one[i] for i in range(planes)], axis=1) for one in members]
            return jnp.concatenate(wide, axis=0).astype(f32)

        gate_rows = rows_of(gate_up_rows[:halves])
        up_rows = rows_of(gate_up_rows[halves:])
        grad_w_gate = gate_rows * gain_two
        grad_w_up = up_rows * gain_two
        grad_gain_mlp = jnp.sum(
            gate_rows * w_gate.astype(f32) + up_rows * w_up.astype(f32), axis=1
        )
        grad_gain_attn = (
            jnp.sum(q_sum * w_query.astype(f32), axis=1)
            + jnp.sum(k_sum * w_key.astype(f32), axis=1)
            + jnp.sum(v_sum * w_value.astype(f32), axis=1)
        )

        return (
            outputs,
            grad_inputs,
            grad_gain_attn,
            q_sum * gain_one,
            k_sum * gain_one,
            v_sum * gain_one,
            grad_w_out,
            grad_gain_mlp,
            grad_w_gate,
            grad_w_up,
            grad_w_down,
        )

    tokens_spec = P("dp", "seq", None)
    in_specs = (
        tokens_spec,
        P("dp", "seq"),
        P("dp", "seq"),
        tokens_spec,
        P("seq"),
        P("seq", None),
        P("seq", None),
        P("seq", None),
        P("seq", None),
        P("seq"),
        P("seq", None),
        P("seq", None),
        P("seq", None),
    )
    out_specs = (
        tokens_spec,
        tokens_spec,
        P("seq"),
        P("seq", None),
        P("seq", None),
        P("seq", None),
        P("seq", None),
        P("seq"),
        P("seq", None),
        P("seq", None),
        P("seq", None),
    )
    return jax.shard_map(body, mesh=mesh, in_specs=in_specs, out_specs=out_specs, check_vma=False)
```

```python
import functools

import jax
import jax.numpy as jnp
from jax import lax
from jax.experimental import pallas as pl
from jax.experimental.pallas import tpu as pltpu
from jax.sharding import PartitionSpec as P

HEADS = 32
KV_HEADS = 4
HEAD_DIM = 64
GROUP = KV_HEADS
GROUP_HEADS = HEADS // GROUP
PAIR = 2 * HEAD_DIM

epsilon = 1e-05
rope_base = 10000.0
masked_score = -1e30

f32 = jnp.float32
bf16 = jnp.bfloat16


def dot(left, right, contract=((1,), (0,))):
    return lax.dot_general(left, right, (contract, ((), ())), preferred_element_type=f32)


def stack_heads(block, rows):
    lane = lax.broadcasted_iota(jnp.int32, (rows, PAIR), 1)
    parts = []
    for pair in range(GROUP_HEADS // 2):
        both = block[:, pair * PAIR : (pair + 1) * PAIR]
        parts.append(jnp.where(lane < HEAD_DIM, both, jnp.zeros_like(both)))
        parts.append(jnp.where(lane >= HEAD_DIM, both, jnp.zeros_like(both)))
    return jnp.concatenate(parts, axis=0)


def unstack_heads(stacked, rows):
    lane = lax.broadcasted_iota(jnp.int32, (rows, PAIR), 1)
    parts = []
    for pair in range(GROUP_HEADS // 2):
        low = stacked[2 * pair * rows : (2 * pair + 1) * rows]
        high = stacked[(2 * pair + 1) * rows : (2 * pair + 2) * rows]
        parts.append(jnp.where(lane < HEAD_DIM, low, high))
    return jnp.concatenate(parts, axis=1)


def as_row(column):
    wide = jnp.broadcast_to(column, (column.shape[0], 128))
    return jnp.transpose(wide)[:8]


def turn(values):
    width = values.shape[1]
    half_dim = HEAD_DIM // 2
    lane = lax.broadcasted_iota(jnp.int32, values.shape, 1)
    ahead = pltpu.roll(values, width - half_dim, 1)
    behind = pltpu.roll(values, half_dim, 1)
    return jnp.where(lane % HEAD_DIM < half_dim, -ahead, behind)


def rotate(values, cosine, sine):
    return values * cosine + turn(values) * sine


def unrotate(grads, cosine, sine):
    return grads * cosine - turn(grads * sine)


def project_kernel(low_ref, w_ref, cos_ref, sin_ref, q_ref, kv_ref):
    made = dot(low_ref[...], w_ref[...])
    cosine, sine = cos_ref[...], sin_ref[...]
    for i in range(q_ref.shape[1] // PAIR):
        q = rotate(made[:, i * PAIR : (i + 1) * PAIR], cosine, sine).astype(bf16)
        q_ref[:, i * PAIR : (i + 1) * PAIR] = (q.astype(f32) * HEAD_DIM ** (-0.5)).astype(bf16)
    kv = made[:, q_ref.shape[1] :]
    lane = lax.broadcasted_iota(jnp.int32, kv.shape, 1)
    kv_ref[...] = jnp.where(lane < HEAD_DIM, rotate(kv, cosine, sine), kv).astype(bf16)


def project(low, weights, cosine, sine):
    tokens, width = low.shape
    q_width = weights.shape[1] - PAIR
    rows = min(256, tokens)
    return pl.pallas_call(
        project_kernel,
        out_shape=(
            jax.ShapeDtypeStruct((tokens, q_width), bf16),
            jax.ShapeDtypeStruct((tokens, PAIR), bf16),
        ),
        grid=(tokens // rows,),
        in_specs=[
            pl.BlockSpec((rows, width), lambda i: (i, 0)),
            pl.BlockSpec(weights.shape, lambda i: (0, 0)),
            pl.BlockSpec((rows, PAIR), lambda i: (i, 0)),
            pl.BlockSpec((rows, PAIR), lambda i: (i, 0)),
        ],
        out_specs=[
            pl.BlockSpec((rows, q_width), lambda i: (i, 0)),
            pl.BlockSpec((rows, PAIR), lambda i: (i, 0)),
        ],
        name="project",
    )(low, weights, cosine, sine)


def feed_kernel(low_ref, w_ref, grad_hidden_ref, hidden_ref, grad_gate_ref, grad_up_ref, back_ref):
    low = low_ref[...]
    gate = dot(low, w_ref[0])
    up = dot(low, w_ref[1])
    grad_hidden = grad_hidden_ref[...]
    sigmoid_gate = 1.0 / (1.0 + jnp.exp(-gate))
    silu = gate * sigmoid_gate
    hidden_ref[...] = (silu * up).astype(bf16)
    grad_gate = (
        grad_hidden * up * sigmoid_gate * (1.0 + gate * (1.0 - sigmoid_gate))
    ).astype(bf16)
    grad_up = (grad_hidden * silu).astype(bf16)
    grad_gate_ref[...] = grad_gate
    grad_up_ref[...] = grad_up
    back_ref[...] = (
        dot(grad_gate, w_ref[0], ((1,), (1,))) + dot(grad_up, w_ref[1], ((1,), (1,)))
    ).astype(bf16)


def feed(low, weights, grad_hidden):
    tokens, width = low.shape
    block = weights.shape[2]
    rows = min(256, tokens)
    narrow = pl.BlockSpec((rows, block), lambda i: (i, 0))
    wide = pl.BlockSpec((rows, width), lambda i: (i, 0))
    return pl.pallas_call(
        feed_kernel,
        out_shape=(
            jax.ShapeDtypeStruct((tokens, block), bf16),
            jax.ShapeDtypeStruct((tokens, block), bf16),
            jax.ShapeDtypeStruct((tokens, block), bf16),
            jax.ShapeDtypeStruct((tokens, width), bf16),
        ),
        grid=(tokens // rows,),
        in_specs=[wide, pl.BlockSpec(weights.shape, lambda i: (0, 0, 0)), narrow],
        out_specs=[narrow, narrow, narrow, wide],
        name="feed",
    )(low, weights, grad_hidden)


def both_lanes(kv_ref, kk_ref, vv_ref):
    @pl.when(pl.program_id(0) == 0)
    def _():
        for index in range(kv_ref.shape[0]):
            kv = kv_ref[index].astype(f32)
            swapped = pltpu.roll(kv, HEAD_DIM, 1)
            lane = lax.broadcasted_iota(jnp.int32, kv.shape, 1)
            kk_ref[index] = jnp.where(lane < HEAD_DIM, kv, swapped).astype(bf16)
            vv_ref[index] = jnp.where(lane < HEAD_DIM, swapped, kv).astype(bf16)


def attend_kernel(seen_ref, q_ref, kv_ref, qpos_ref, kpos_ref, o_ref, lse_ref, kk_ref, vv_ref):
    rows = q_ref.shape[0]
    both_lanes(kv_ref, kk_ref, vv_ref)
    stacked = stack_heads(q_ref[...], rows)
    qpos = jnp.concatenate([qpos_ref[...]] * GROUP_HEADS, axis=0)

    def unit(index, carry, masked):
        top, total, acc = carry
        scores = dot(stacked, kk_ref[index], ((1,), (1,)))
        if masked:
            scores = jnp.where(kpos_ref[...] <= qpos, scores, masked_score)
        new_top = jnp.maximum(top, jnp.max(scores, axis=1, keepdims=True))
        weights = jnp.exp(scores - new_top)
        keep = jnp.exp(top - new_top)
        total = total * keep + jnp.sum(weights, axis=1, keepdims=True)
        acc = acc * keep + dot(weights.astype(bf16), vv_ref[index])
        return new_top, total, acc

    count = GROUP_HEADS * rows
    start = (
        jnp.full((count, 1), masked_score, f32),
        jnp.zeros((count, 1), f32),
        jnp.zeros((count, PAIR), f32),
    )
    carry = unit(0, start, True)
    top, total, acc = lax.fori_loop(1, seen_ref[0], lambda i, c: unit(i, c, False), carry)
    o_ref[...] = unstack_heads(acc / total, rows).astype(bf16)
    lse_ref[...] = as_row(top + jnp.log(total))


def attend_back_kernel(
    seen_ref, q_ref, do_ref, o_ref, kv_ref, lse_ref, qpos_ref, kpos_ref, cos_ref, sin_ref,
    dq_ref, dkv_ref, qs_ref, dos_ref, delta_ref, dqs_ref, kk_ref, vv_ref, dkk_ref, dvv_ref,
):
    rows = q_ref.shape[0]
    both_lanes(kv_ref, kk_ref, vv_ref)

    @pl.when(pl.program_id(0) == 0)
    def _():
        dkk_ref[...] = jnp.zeros_like(dkk_ref)
        dvv_ref[...] = jnp.zeros_like(dvv_ref)

    qs_ref[...] = stack_heads(q_ref[...], rows)
    grads = stack_heads(do_ref[...], rows)
    dos_ref[...] = grads
    outs = stack_heads(o_ref[...], rows)
    delta_ref[...] = as_row(jnp.sum(grads.astype(f32) * outs.astype(f32), axis=1, keepdims=True))

    def unit(index, masked):
        keys = kk_ref[index]
        scores = dot(keys, qs_ref[...], ((1,), (1,)))
        if masked:
            qpos = jnp.concatenate([qpos_ref[0:1, :]] * GROUP_HEADS, axis=1)
            scores = jnp.where(kpos_ref[...] <= qpos, scores, masked_score)
        probs = jnp.exp(scores - lse_ref[0:1, :])
        prob_grad = dot(vv_ref[index], dos_ref[...], ((1,), (1,)))
        score_grad = (probs * (prob_grad - delta_ref[0:1, :])).astype(bf16)
        dvv_ref[index] += dot(probs.astype(bf16), dos_ref[...])
        dkk_ref[index] += dot(score_grad, qs_ref[...])
        return dot(score_grad, keys, ((0,), (0,)))

    dqs_ref[...] = unit(0, True)

    @pl.loop(1, seen_ref[0])
    def _(index):
        dqs_ref[...] += unit(index, False)

    grads = unstack_heads(dqs_ref[...], rows) * HEAD_DIM ** (-0.5)
    cosine, sine = cos_ref[...], sin_ref[...]
    for i in range(dq_ref.shape[1] // PAIR):
        part = unrotate(grads[:, i * PAIR : (i + 1) * PAIR], cosine, sine)
        dq_ref[:, i * PAIR : (i + 1) * PAIR] = part.astype(bf16)

    @pl.when(pl.program_id(0) == pl.num_programs(0) - 1)
    def _():
        for index in range(kv_ref.shape[0]):
            keys, values = dkk_ref[index], dvv_ref[index]
            keys = keys + pltpu.roll(keys, HEAD_DIM, 1)
            values = values + pltpu.roll(values, HEAD_DIM, 1)
            lane = lax.broadcasted_iota(jnp.int32, keys.shape, 1)
            dkv_ref[index] = jnp.where(lane < HEAD_DIM, keys, values).astype(bf16)


def block_rows(length):
    return min(128, length)


def whole(shape):
    zeros = (0,) * len(shape)
    return pl.BlockSpec(shape, lambda i, seen: zeros)


def attend(seen, q, kv, order):
    length, width = q.shape
    rows = block_rows(length)
    stacked = GROUP_HEADS * rows
    steps = length // rows
    return pl.pallas_call(
        attend_kernel,
        out_shape=(
            jax.ShapeDtypeStruct((length, width), bf16),
            jax.ShapeDtypeStruct((steps, 8, stacked), f32),
        ),
        grid_spec=pltpu.PrefetchScalarGridSpec(
            num_scalar_prefetch=1,
            grid=(steps,),
            in_specs=[
                pl.BlockSpec((rows, width), lambda i, seen: (i, 0)),
                whole(kv.shape),
                pl.BlockSpec((rows, 1), lambda i, seen: (i, 0)),
                whole((1, length)),
            ],
            out_specs=[
                pl.BlockSpec((rows, width), lambda i, seen: (i, 0)),
                pl.BlockSpec((pl.Squeezed(), 8, stacked), lambda i, seen: (i, 0, 0)),
            ],
            scratch_shapes=[pltpu.VMEM(kv.shape, bf16), pltpu.VMEM(kv.shape, bf16)],
        ),
        name="attend",
    )(seen, q, kv, order[:, None], order[None, :])


def attend_back(seen, q, do, o, kv, lse, order, cosine, sine):
    length, width = q.shape
    rows = block_rows(length)
    stacked = GROUP_HEADS * rows
    steps = length // rows
    return pl.pallas_call(
        attend_back_kernel,
        out_shape=(
            jax.ShapeDtypeStruct((length, width), bf16),
            jax.ShapeDtypeStruct(kv.shape, bf16),
        ),
        grid_spec=pltpu.PrefetchScalarGridSpec(
            num_scalar_prefetch=1,
            grid=(steps,),
            in_specs=[
                pl.BlockSpec((rows, width), lambda i, seen: (i, 0)),
                pl.BlockSpec((rows, width), lambda i, seen: (i, 0)),
                pl.BlockSpec((rows, width), lambda i, seen: (i, 0)),
                whole(kv.shape),
                pl.BlockSpec((pl.Squeezed(), 8, stacked), lambda i, seen: (i, 0, 0)),
                pl.BlockSpec((8, rows), lambda i, seen: (0, i)),
                whole((length, 1)),
                pl.BlockSpec((rows, PAIR), lambda i, seen: (i, 0)),
                pl.BlockSpec((rows, PAIR), lambda i, seen: (i, 0)),
            ],
            out_specs=[
                pl.BlockSpec((rows, width), lambda i, seen: (i, 0)),
                whole(kv.shape),
            ],
            scratch_shapes=[
                pltpu.VMEM((stacked, PAIR), bf16),
                pltpu.VMEM((stacked, PAIR), bf16),
                pltpu.VMEM((8, stacked), f32),
                pltpu.VMEM((stacked, PAIR), f32),
                pltpu.VMEM(kv.shape, bf16),
                pltpu.VMEM(kv.shape, bf16),
                pltpu.VMEM(kv.shape, f32),
                pltpu.VMEM(kv.shape, f32),
            ],
        ),
        name="attend_back",
    )(
        seen, q, do, o, kv, lse, jnp.broadcast_to(order[None, :], (8, length)), order[:, None],
        cosine, sine,
    )


def normalize(values):
    inverse = lax.rsqrt(jnp.mean(values * values, axis=-1, keepdims=True) + epsilon)
    return values * inverse, inverse


def norm_back(inner, normed, inverse):
    return inverse * (inner - normed * jnp.mean(inner * normed, axis=-1, keepdims=True))


def rope_tables(positions):
    half_dim = HEAD_DIM // 2
    frequency = rope_base ** (-(jnp.arange(half_dim).astype(f32) * 2.0 / HEAD_DIM))
    angles = positions.astype(f32)[:, None] * frequency
    times = PAIR // half_dim
    return jnp.tile(jnp.cos(angles), (1, times)), jnp.tile(jnp.sin(angles), (1, times))


def unrotate_keys(grads, cosine, sine):
    half_dim = HEAD_DIM // 2
    sines = grads * sine
    turned = jnp.concatenate([-sines[:, half_dim:], sines[:, :half_dim]], axis=1)
    return grads * cosine - turned


def tie(*values):
    return lax.optimization_barrier(values)


def solution(mesh):
    n_dp = mesh.shape["dp"]
    n_seq = mesh.shape["seq"]
    planes = n_seq // GROUP
    halves = n_dp // 2
    both = ("dp", "seq")

    in_plane = [[GROUP * p + w for w in range(GROUP)] for p in range(planes)]
    across_dp = [
        [c * n_seq + GROUP * p + w for c in range(n_dp) for p in range(planes)] for w in range(GROUP)
    ]
    in_plane_dp = [
        [c * n_seq + GROUP * p + w for c in range(n_dp) for w in range(GROUP)] for p in range(planes)
    ]
    across = [[GROUP * p + w for p in range(planes)] for w in range(GROUP)]

    def xor_w(value, j):
        return lax.ppermute(value, "seq", [(s, s ^ j) for s in range(n_seq)])

    def shift_z(value, t):
        return lax.ppermute(value, "seq", [(s, (s + GROUP * t) % n_seq) for s in range(n_seq)])

    def shift_dp(value, t):
        return lax.ppermute(value, "dp", [(c, (c + t) % n_dp) for c in range(n_dp)])

    def gather_w(value):
        first = xor_w(value, 1)
        second = xor_w(value, 2)
        half = value.shape[0] // 2
        third = jnp.concatenate([xor_w(first[:half], 2), xor_w(second[half:], 1)], axis=0)
        return jnp.concatenate([value, first, second, third], axis=0)

    def scatter_w(slots):
        got = [xor_w(slots[j], j) for j in range(1, GROUP)]
        return functools.reduce(jnp.add, [g.astype(f32) for g in got], slots[0].astype(f32))

    def gather_z(value):
        return [value] + [shift_z(value, t) for t in range(1, planes)]

    def scatter_z(slots):
        got = [shift_z(slots[t], -t) for t in range(1, planes)]
        return functools.reduce(jnp.add, [g.astype(f32) for g in got], slots[0].astype(f32))

    def gather_dp(value):
        return jnp.concatenate([value] + [shift_dp(value, t) for t in range(1, n_dp)], axis=0)

    def pick(value, index, count, axis):
        size = value.shape[axis] // count
        return lax.dynamic_slice_in_dim(value, index * size, size, axis)

    def exchange_dp(value, c, axis):
        parts = [pick(value, c, n_dp, axis)]
        for t in range(1, n_dp):
            parts.append(shift_dp(pick(value, (c + t) % n_dp, n_dp, axis), t))
        return jnp.concatenate(parts, axis=0)

    def collect_dp(value, c):
        slots = [value] + [shift_dp(value, t) for t in range(1, n_dp)]
        out = []
        for member in range(n_dp):
            chosen = slots[0]
            for t in range(1, n_dp):
                chosen = jnp.where((c - t) % n_dp == member, slots[t], chosen)
            out.append(chosen)
        return out

    def body(
        inputs, positions, select, cotangent, gain_attn, w_query, w_key, w_value, w_out, gain_mlp,
        w_gate, w_up, w_down,
    ):
        seqs, rows, width = inputs.shape
        tokens = seqs * rows
        shard = w_query.shape[0]
        ff_rows = w_down.shape[0]
        ff_block = w_gate.shape[1] // planes
        q_width = GROUP_HEADS * HEAD_DIM
        s = lax.axis_index("seq")
        c = lax.axis_index("dp")
        p = s // GROUP
        w = s % GROUP

        gain_one = gain_attn.astype(f32)[:, None]
        gain_two = gain_mlp.astype(f32)[:, None]

        def scaled(weight, gain):
            return (weight.astype(f32) * gain).astype(bf16)

        q_cols = scaled(w_query, gain_one).reshape(shard, GROUP, n_dp, q_width // n_dp)
        kv_cols = jnp.concatenate(
            [
                scaled(w_key, gain_one).reshape(shard, GROUP, HEAD_DIM),
                scaled(w_value, gain_one).reshape(shard, GROUP, HEAD_DIM),
            ],
            axis=-1,
        ).reshape(shard, GROUP, n_dp, PAIR // n_dp)
        qkv_cols = jnp.concatenate([q_cols, kv_cols], axis=-1)
        qkv_part = lax.dynamic_index_in_dim(qkv_cols, c, 2, keepdims=False)
        qkv_part = lax.all_to_all(
            jnp.transpose(qkv_part, (1, 0, 2)), "seq", 0, 0, axis_index_groups=in_plane, tiled=True
        )
        part_width = (q_width + PAIR) // n_dp
        qkv_part = qkv_part.reshape(GROUP * shard, part_width)
        own_pos = positions.reshape(1, tokens)
        plane_pos = jnp.concatenate([own_pos] + [xor_w(own_pos, j) for j in range(1, GROUP)], axis=1)
        x_in = inputs.reshape(tokens, width).astype(f32)
        normed_one, inverse_one = normalize(x_in)
        low_one, qkv_part, plane_pos = tie(normed_one.astype(bf16), qkv_part, plane_pos)

        ring = [qkv_part] + [shift_z(qkv_part, -t) for t in range(1, planes)]
        low_one, *ring = tie(gather_w(low_one), *ring)
        qkv_ring = jnp.concatenate(ring + ring[: planes - 1], axis=0)
        qkv_mine = lax.dynamic_slice_in_dim(
            qkv_ring, ((planes - p) % planes) * GROUP * shard, width, 0
        )
        piece = shard // halves
        gate_up = jnp.where(c // halves == 0, scaled(w_gate, gain_two), scaled(w_up, gain_two))
        out_part, gate_up, qkv_mine = tie(
            pick(w_out, c, n_dp, 1), pick(gate_up, c % halves, halves, 0), qkv_mine
        )
        qkv_full = collect_dp(qkv_mine, c)
        out_part = lax.ppermute(
            out_part, "seq", [(i, GROUP * (i % planes) + i // planes) for i in range(n_seq)]
        )
        gate_up_sent = [
            shift_z(pick(gate_up, (p + t) % planes, planes, 1), t) if t
            else pick(gate_up, p, planes, 1)
            for t in range(planes)
        ]
        down_full = lax.all_gather(
            pick(w_down, c, n_dp, 1), both, axis_index_groups=in_plane_dp, tiled=False
        )
        out_part, down_full = tie(out_part, down_full)
        down_full = down_full.reshape(n_dp, ff_block, width // n_dp)
        out_full = lax.all_gather(out_part, both, axis_index_groups=across_dp, tiled=False)
        out_full = out_full.reshape(n_dp, planes * shard, width // n_dp)

        blocks = [
            (i * GROUP + j) * halves + h
            for h in range(halves) for j in range(GROUP) for i in range(planes)
        ]

        def column_blocks(value, which):
            return jnp.concatenate([value[:, i * piece : (i + 1) * piece] for i in which], axis=1)

        def reorder(value):
            return column_blocks(value, blocks)

        def order_back(value):
            return column_blocks(value, [blocks.index(i) for i in range(len(blocks))])

        cosine, sine = rope_tables(plane_pos.reshape(GROUP * tokens))

        grad_y = (
            cotangent.astype(f32) * select.astype(f32)[..., None]
        ).reshape(tokens, width)
        cut = q_width // n_dp
        plane_tokens = GROUP * tokens
        qkv_weights = jnp.concatenate(
            [one[:, :cut] for one in qkv_full] + [one[:, cut:] for one in qkv_full], axis=1
        )
        q, kv_low = project(low_one, qkv_weights, cosine, sine)
        kv_all = jnp.stack(gather_z(kv_low))
        grad_y_low, kv_all = tie(grad_y.astype(bf16), kv_all)
        *gate_up_sent, q = tie(*gate_up_sent, q)
        gate_up_part = jnp.zeros((planes, piece, ff_block), bf16)
        for t in range(planes):
            gate_up_part = lax.dynamic_update_index_in_dim(
                gate_up_part, gate_up_sent[t], (p - t) % planes, 0
            )
        gate_up_full = lax.all_gather(
            gate_up_part, both, axis_index_groups=in_plane_dp, tiled=False
        )
        gate_up_full = gate_up_full.reshape(2, width, ff_block)
        grad_y_all = jnp.concatenate(gather_z(grad_y_low), axis=0)

        def by_seq(value, axis):
            shape = value.shape
            value = value.reshape(shape[:axis] + (GROUP, seqs, rows) + shape[axis + 1 :])
            value = jnp.moveaxis(value, axis + 1, 0)
            return value.reshape((seqs,) + shape[:axis] + (GROUP * rows,) + shape[axis + 1 :])

        def from_seq(value, axis):
            shape = value.shape[1:]
            value = value.reshape((seqs,) + shape[:axis] + (GROUP, rows) + shape[axis + 1 :])
            value = jnp.moveaxis(value, 0, axis + 1)
            return value.reshape(shape[:axis] + (GROUP * seqs * rows,) + shape[axis + 1 :])

        order = jnp.concatenate([(w ^ j) * rows + jnp.arange(rows) for j in range(GROUP)])
        order = order.astype(jnp.int32)
        seen = (p + 1).astype(jnp.int32).reshape(1)
        q_seq = by_seq(q, 0)
        kv_seq = by_seq(kv_all, 1)
        cos_seq = by_seq(cosine, 0)
        sin_seq = by_seq(sine, 0)
        pieces = [attend(seen, q_seq[i], kv_seq[i], order) for i in range(seqs)]
        o_seq = [one[0] for one in pieces]
        lse_seq = [one[1] for one in pieces]
        o = from_seq(jnp.stack(o_seq), 0)

        branch = jnp.concatenate([dot(o, out_full[i]).astype(bf16) for i in range(n_dp)], axis=1)
        branch = scatter_w([branch[j * tokens : (j + 1) * tokens] for j in range(GROUP)])
        x_mid = x_in + branch

        normed_two, inverse_two = normalize(x_mid)
        low_two = reorder(normed_two.astype(bf16))
        low_two, grad_y_all = tie(low_two, grad_y_all)
        low_two_own, *low_two_sent = gather_z(low_two)
        grad_hidden = functools.reduce(
            jnp.add,
            [
                dot(pick(grad_y_all, i, n_dp, 1), down_full[i], ((1,), (1,)))
                for i in range(n_dp)
            ],
        )
        *low_two_sent, grad_hidden = tie(*low_two_sent, grad_hidden)
        low_two = jnp.concatenate([low_two_own] + low_two_sent, axis=0)
        hidden, grad_gate, grad_up, grad_low_two = feed(low_two, gate_up_full, grad_hidden)
        hidden_later, grad_gate_later, grad_up_later, grad_low_two = tie(
            hidden, grad_gate, grad_up, grad_low_two
        )
        inner_sent = [
            shift_z(grad_low_two[t * tokens : (t + 1) * tokens], -t) for t in range(1, planes)
        ]

        hidden_all = gather_dp(hidden_later)
        down_sum = dot(hidden_all, exchange_dp(grad_y_all, c, 1), ((0,), (0,))).astype(bf16)

        low_two_all = gather_dp(low_two)
        if halves > 1:
            low_two_all = pick(low_two_all, c % halves, halves, 1)

        def of_member(member):
            return jnp.where(member // halves == 0, grad_gate_later, grad_up_later)

        gate_up_grads = [of_member(c)]
        for t in range(1, n_dp):
            gate_up_grads.append(shift_dp(of_member((c + t) % n_dp), t))
        gate_up_grads = jnp.concatenate(gate_up_grads, axis=0)
        gate_up_sum = dot(low_two_all, gate_up_grads, ((0,), (0,))).astype(bf16)

        inner_sent[0], gate_up_sum = tie(inner_sent[0], gate_up_sum)
        *inner_rest, down_sum = tie(*inner_sent[1:], down_sum)
        inner_sent = [inner_sent[0]] + inner_rest
        mixed = jnp.concatenate(
            [dot(hidden_later, down_full[i]).astype(bf16) for i in range(n_dp)], axis=1
        )
        *inner_sent, mixed = tie(*inner_sent, mixed)
        inner_two = functools.reduce(
            jnp.add, [g.astype(f32) for g in inner_sent], grad_low_two[:tokens].astype(f32)
        )
        grad_x_mid = grad_y + norm_back(order_back(inner_two), normed_two, inverse_two)

        mixed, grad_x_low = tie(mixed, grad_x_mid.astype(bf16))
        mixed_sent = [shift_z(mixed[t * tokens : (t + 1) * tokens], -t) for t in range(1, planes)]
        gate_up_sum = lax.psum_scatter(gate_up_sum, "seq", axis_index_groups=in_plane, tiled=True)
        down_sum = lax.psum_scatter(
            down_sum, "seq", axis_index_groups=in_plane, tiled=True
        )
        gate_up_sum = gate_up_sum.reshape(planes, piece, ff_block)

        grad_branch = gather_w(grad_x_low)
        early = planes - 2
        *mixed_sent[:early], grad_branch = tie(*mixed_sent[:early], grad_branch)
        grad_o = functools.reduce(
            jnp.add,
            [dot(pick(grad_branch, i, n_dp, 1), out_full[i], ((1,), (1,))) for i in range(n_dp)],
        ).astype(bf16)

        out_part_sum = dot(gather_dp(o), exchange_dp(grad_branch, c, 1), ((0,), (0,))).astype(bf16)
        grad_o_seq = by_seq(grad_o, 0)
        *late, grad_o_seq, out_part_sum = tie(*mixed_sent[early:], grad_o_seq, out_part_sum)
        mixed_sent = mixed_sent[:early] + list(late)
        gate_up_sum, out_part_sum = tie(gate_up_sum, out_part_sum)
        out_sum = lax.psum_scatter(out_part_sum, "seq", axis_index_groups=across, tiled=True)
        pieces = [
            attend_back(
                seen, q_seq[i], grad_o_seq[i], o_seq[i], kv_seq[i], lse_seq[i], order,
                cos_seq[i], sin_seq[i],
            )
            for i in range(seqs)
        ]
        grad_q = jnp.stack([one[0] for one in pieces])
        mixed = functools.reduce(
            jnp.add, [g.astype(f32) for g in mixed_sent], mixed[:tokens].astype(f32)
        )
        query_pre = from_seq(grad_q, 0)
        grad_kv = from_seq(jnp.stack([one[1] for one in pieces]), 1)
        grad_kv = scatter_z([grad_kv[t] for t in range(planes)])
        grad_kv, gate_up_late = tie(grad_kv, gate_up_sum)
        gate_up_sent = []
        for t in range(planes):
            block = lax.dynamic_index_in_dim(gate_up_late, (p + t) % planes, 0, keepdims=False)
            gate_up_sent.append(shift_z(block, t) if t else block)
        query_pre, out_sum = tie(query_pre, out_sum)
        key_pre = unrotate_keys(
            grad_kv[:, :HEAD_DIM], cosine[:, :HEAD_DIM], sine[:, :HEAD_DIM]
        )
        kv_pre = jnp.concatenate([key_pre, grad_kv[:, HEAD_DIM:]], axis=1).astype(bf16)
        pre = [
            jnp.concatenate(
                [query_pre[:, i * cut : (i + 1) * cut], pick(kv_pre, i, n_dp, 1)], axis=1
            )
            for i in range(n_dp)
        ]
        outputs = (x_mid + mixed).astype(bf16).reshape(seqs, rows, width)

        grad_low_one = dot(
            jnp.concatenate([query_pre, kv_pre], axis=1), qkv_weights, ((1,), (1,))
        ).astype(bf16)
        inner_one = scatter_w([grad_low_one[j * tokens : (j + 1) * tokens] for j in range(GROUP)])
        grad_inputs = grad_x_mid + norm_back(inner_one, normed_one, inverse_one)
        grad_inputs = grad_inputs.reshape(seqs, rows, width)

        qkv_sum = dot(
            gather_dp(low_one),
            exchange_dp(jnp.concatenate(pre, axis=1), c, 1),
            ((0,), (0,)),
        ).astype(bf16)
        *gate_up_sent, down_sum, qkv_sum = tie(*gate_up_sent, down_sum, qkv_sum)
        out_sum = lax.ppermute(
            out_sum, "seq", [(GROUP * (i % planes) + i // planes, i) for i in range(n_seq)]
        )
        grad_w_out = jnp.concatenate(collect_dp(out_sum, c), axis=1).astype(f32)

        qkv_sum = lax.psum_scatter(
            qkv_sum, "seq", axis_index_groups=across, tiled=True
        )
        grad_w_down = jnp.concatenate(collect_dp(down_sum, c), axis=1).astype(f32)
        gate_up_rows = jnp.zeros((planes, piece, ff_block), bf16)
        for t in range(planes):
            gate_up_rows = lax.dynamic_update_index_in_dim(
                gate_up_rows, gate_up_sent[t], (p - t) % planes, 0
            )
        gate_up_rows = collect_dp(gate_up_rows, c)

        def rows_of(members):
            wide = [jnp.concatenate([one[i] for i in range(planes)], axis=1) for one in members]
            return jnp.concatenate(wide, axis=0).astype(f32)

        gate_rows = rows_of(gate_up_rows[:halves])
        up_rows = rows_of(gate_up_rows[halves:])
        grad_w_gate = gate_rows * gain_two
        grad_w_up = up_rows * gain_two
        grad_gain_mlp = jnp.sum(
            gate_rows * w_gate.astype(f32) + up_rows * w_up.astype(f32), axis=1
        )
        qkv_sum, grad_w_gate, grad_w_up, grad_w_down, grad_gain_mlp = tie(
            qkv_sum, grad_w_gate, grad_w_up, grad_w_down, grad_gain_mlp
        )
        qkv_sum = qkv_sum.reshape(GROUP, shard, part_width)
        qkv_sum = lax.all_to_all(qkv_sum, "seq", 0, 0, axis_index_groups=in_plane, tiled=True)
        qkv_sum = collect_dp(qkv_sum, c)
        q_sum = jnp.concatenate(
            [one[j][:, :cut] for j in range(GROUP) for one in qkv_sum], axis=1
        ).astype(f32)
        kv_sum = jnp.concatenate(
            [one[j][:, cut:] for j in range(GROUP) for one in qkv_sum], axis=1
        ).astype(f32).reshape(shard, GROUP, PAIR)
        k_sum = kv_sum[..., :HEAD_DIM].reshape(shard, GROUP * HEAD_DIM)
        v_sum = kv_sum[..., HEAD_DIM:].reshape(shard, GROUP * HEAD_DIM)

        grad_gain_attn = (
            jnp.sum(q_sum * w_query.astype(f32), axis=1)
            + jnp.sum(k_sum * w_key.astype(f32), axis=1)
            + jnp.sum(v_sum * w_value.astype(f32), axis=1)
        )

        return (
            outputs,
            grad_inputs,
            grad_gain_attn,
            q_sum * gain_one,
            k_sum * gain_one,
            v_sum * gain_one,
            grad_w_out,
            grad_gain_mlp,
            grad_w_gate,
            grad_w_up,
            grad_w_down,
        )

    tokens_spec = P("dp", "seq", None)
    in_specs = (
        tokens_spec,
        P("dp", "seq"),
        P("dp", "seq"),
        tokens_spec,
        P("seq"),
        P("seq", None),
        P("seq", None),
        P("seq", None),
        P("seq", None),
        P("seq"),
        P("seq", None),
        P("seq", None),
        P("seq", None),
    )
    out_specs = (
        tokens_spec,
        tokens_spec,
        P("seq"),
        P("seq", None),
        P("seq", None),
        P("seq", None),
        P("seq", None),
        P("seq"),
        P("seq", None),
        P("seq", None),
        P("seq", None),
    )
    return jax.shard_map(body, mesh=mesh, in_specs=in_specs, out_specs=out_specs, check_vma=False)
```

```python
import functools

import jax
import jax.numpy as jnp
from jax import lax
from jax.experimental import pallas as pl
from jax.experimental.pallas import tpu as pltpu
from jax.sharding import PartitionSpec as P

HEADS = 32
KV_HEADS = 4
HEAD_DIM = 64
GROUP = KV_HEADS
GROUP_HEADS = HEADS // GROUP
PAIR = 2 * HEAD_DIM

epsilon = 1e-05
rope_base = 10000.0
masked_score = -1e30

f32 = jnp.float32
bf16 = jnp.bfloat16


def dot(left, right, contract=((1,), (0,))):
    return lax.dot_general(left, right, (contract, ((), ())), preferred_element_type=f32)


def stack_heads(block, rows):
    lane = lax.broadcasted_iota(jnp.int32, (rows, PAIR), 1)
    parts = []
    for pair in range(GROUP_HEADS // 2):
        both = block[:, pair * PAIR : (pair + 1) * PAIR]
        parts.append(jnp.where(lane < HEAD_DIM, both, jnp.zeros_like(both)))
        parts.append(jnp.where(lane >= HEAD_DIM, both, jnp.zeros_like(both)))
    return jnp.concatenate(parts, axis=0)


def unstack_heads(stacked, rows):
    lane = lax.broadcasted_iota(jnp.int32, (rows, PAIR), 1)
    parts = []
    for pair in range(GROUP_HEADS // 2):
        low = stacked[2 * pair * rows : (2 * pair + 1) * rows]
        high = stacked[(2 * pair + 1) * rows : (2 * pair + 2) * rows]
        parts.append(jnp.where(lane < HEAD_DIM, low, high))
    return jnp.concatenate(parts, axis=1)


def as_row(column):
    wide = jnp.broadcast_to(column, (column.shape[0], 128))
    return jnp.transpose(wide)[:8]


def turn(values):
    width = values.shape[1]
    half_dim = HEAD_DIM // 2
    lane = lax.broadcasted_iota(jnp.int32, values.shape, 1)
    ahead = pltpu.roll(values, width - half_dim, 1)
    behind = pltpu.roll(values, half_dim, 1)
    return jnp.where(lane % HEAD_DIM < half_dim, -ahead, behind)


def rotate(values, cosine, sine):
    return values * cosine + turn(values) * sine


def unrotate(grads, cosine, sine):
    return grads * cosine - turn(grads * sine)


def project_kernel(low_ref, w_ref, cos_ref, sin_ref, q_ref, kv_ref):
    made = dot(low_ref[...], w_ref[...])
    cosine, sine = cos_ref[...], sin_ref[...]
    for i in range(q_ref.shape[1] // PAIR):
        q = rotate(made[:, i * PAIR : (i + 1) * PAIR], cosine, sine).astype(bf16)
        q_ref[:, i * PAIR : (i + 1) * PAIR] = (q.astype(f32) * HEAD_DIM ** (-0.5)).astype(bf16)
    kv = made[:, q_ref.shape[1] :]
    lane = lax.broadcasted_iota(jnp.int32, kv.shape, 1)
    kv_ref[...] = jnp.where(lane < HEAD_DIM, rotate(kv, cosine, sine), kv).astype(bf16)


def project(low, weights, cosine, sine):
    tokens, width = low.shape
    q_width = weights.shape[1] - PAIR
    rows = min(256, tokens)
    return pl.pallas_call(
        project_kernel,
        out_shape=(
            jax.ShapeDtypeStruct((tokens, q_width), bf16),
            jax.ShapeDtypeStruct((tokens, PAIR), bf16),
        ),
        grid=(tokens // rows,),
        in_specs=[
            pl.BlockSpec((rows, width), lambda i: (i, 0)),
            pl.BlockSpec(weights.shape, lambda i: (0, 0)),
            pl.BlockSpec((rows, PAIR), lambda i: (i, 0)),
            pl.BlockSpec((rows, PAIR), lambda i: (i, 0)),
        ],
        out_specs=[
            pl.BlockSpec((rows, q_width), lambda i: (i, 0)),
            pl.BlockSpec((rows, PAIR), lambda i: (i, 0)),
        ],
        name="project",
    )(low, weights, cosine, sine)


def feed_kernel(low_ref, w_ref, grad_hidden_ref, hidden_ref, grad_gate_ref, grad_up_ref, back_ref):
    low = low_ref[...]
    gate = dot(low, w_ref[0])
    up = dot(low, w_ref[1])
    grad_hidden = grad_hidden_ref[...]
    sigmoid_gate = 1.0 / (1.0 + jnp.exp(-gate))
    silu = gate * sigmoid_gate
    hidden_ref[...] = (silu * up).astype(bf16)
    grad_gate = (
        grad_hidden * up * sigmoid_gate * (1.0 + gate * (1.0 - sigmoid_gate))
    ).astype(bf16)
    grad_up = (grad_hidden * silu).astype(bf16)
    grad_gate_ref[...] = grad_gate
    grad_up_ref[...] = grad_up
    back_ref[...] = (
        dot(grad_gate, w_ref[0], ((1,), (1,))) + dot(grad_up, w_ref[1], ((1,), (1,)))
    ).astype(bf16)


def feed(low, weights, grad_hidden):
    tokens, width = low.shape
    block = weights.shape[2]
    rows = min(256, tokens)
    narrow = pl.BlockSpec((rows, block), lambda i: (i, 0))
    wide = pl.BlockSpec((rows, width), lambda i: (i, 0))
    return pl.pallas_call(
        feed_kernel,
        out_shape=(
            jax.ShapeDtypeStruct((tokens, block), bf16),
            jax.ShapeDtypeStruct((tokens, block), bf16),
            jax.ShapeDtypeStruct((tokens, block), bf16),
            jax.ShapeDtypeStruct((tokens, width), bf16),
        ),
        grid=(tokens // rows,),
        in_specs=[wide, pl.BlockSpec(weights.shape, lambda i: (0, 0, 0)), narrow],
        out_specs=[narrow, narrow, narrow, wide],
        name="feed",
    )(low, weights, grad_hidden)


def both_lanes(kv_ref, kk_ref, vv_ref):
    @pl.when(pl.program_id(0) == 0)
    def _():
        for index in range(kv_ref.shape[0]):
            kv = kv_ref[index].astype(f32)
            swapped = pltpu.roll(kv, HEAD_DIM, 1)
            lane = lax.broadcasted_iota(jnp.int32, kv.shape, 1)
            kk_ref[index] = jnp.where(lane < HEAD_DIM, kv, swapped).astype(bf16)
            vv_ref[index] = jnp.where(lane < HEAD_DIM, swapped, kv).astype(bf16)


def attend_kernel(seen_ref, q_ref, kv_ref, qpos_ref, kpos_ref, o_ref, lse_ref, kk_ref, vv_ref):
    rows = q_ref.shape[0]
    both_lanes(kv_ref, kk_ref, vv_ref)
    stacked = stack_heads(q_ref[...], rows)
    qpos = jnp.concatenate([qpos_ref[...]] * GROUP_HEADS, axis=0)

    def unit(index, carry, masked):
        top, total, acc = carry
        scores = dot(stacked, kk_ref[index], ((1,), (1,)))
        if masked:
            scores = jnp.where(kpos_ref[...] <= qpos, scores, masked_score)
        new_top = jnp.maximum(top, jnp.max(scores, axis=1, keepdims=True))
        weights = jnp.exp(scores - new_top)
        keep = jnp.exp(top - new_top)
        total = total * keep + jnp.sum(weights, axis=1, keepdims=True)
        acc = acc * keep + dot(weights.astype(bf16), vv_ref[index])
        return new_top, total, acc

    count = GROUP_HEADS * rows
    start = (
        jnp.full((count, 1), masked_score, f32),
        jnp.zeros((count, 1), f32),
        jnp.zeros((count, PAIR), f32),
    )
    carry = unit(0, start, True)
    top, total, acc = lax.fori_loop(1, seen_ref[0], lambda i, c: unit(i, c, False), carry)
    o_ref[...] = unstack_heads(acc / total, rows).astype(bf16)
    lse_ref[...] = as_row(top + jnp.log(total))


def attend_back_kernel(
    seen_ref, q_ref, do_ref, o_ref, kv_ref, lse_ref, qpos_ref, kpos_ref, cos_ref, sin_ref,
    dq_ref, dkv_ref, qs_ref, dos_ref, delta_ref, dqs_ref, kk_ref, vv_ref, dkk_ref, dvv_ref,
):
    rows = q_ref.shape[0]
    both_lanes(kv_ref, kk_ref, vv_ref)

    @pl.when(pl.program_id(0) == 0)
    def _():
        dkk_ref[...] = jnp.zeros_like(dkk_ref)
        dvv_ref[...] = jnp.zeros_like(dvv_ref)

    qs_ref[...] = stack_heads(q_ref[...], rows)
    grads = stack_heads(do_ref[...], rows)
    dos_ref[...] = grads
    outs = stack_heads(o_ref[...], rows)
    delta_ref[...] = as_row(jnp.sum(grads.astype(f32) * outs.astype(f32), axis=1, keepdims=True))

    def unit(index, masked):
        keys = kk_ref[index]
        scores = dot(keys, qs_ref[...], ((1,), (1,)))
        if masked:
            qpos = jnp.concatenate([qpos_ref[0:1, :]] * GROUP_HEADS, axis=1)
            scores = jnp.where(kpos_ref[...] <= qpos, scores, masked_score)
        probs = jnp.exp(scores - lse_ref[0:1, :])
        prob_grad = dot(vv_ref[index], dos_ref[...], ((1,), (1,)))
        score_grad = (probs * (prob_grad - delta_ref[0:1, :])).astype(bf16)
        dvv_ref[index] += dot(probs.astype(bf16), dos_ref[...])
        dkk_ref[index] += dot(score_grad, qs_ref[...])
        return dot(score_grad, keys, ((0,), (0,)))

    dqs_ref[...] = unit(0, True)

    @pl.loop(1, seen_ref[0])
    def _(index):
        dqs_ref[...] += unit(index, False)

    grads = unstack_heads(dqs_ref[...], rows) * HEAD_DIM ** (-0.5)
    cosine, sine = cos_ref[...], sin_ref[...]
    for i in range(dq_ref.shape[1] // PAIR):
        part = unrotate(grads[:, i * PAIR : (i + 1) * PAIR], cosine, sine)
        dq_ref[:, i * PAIR : (i + 1) * PAIR] = part.astype(bf16)

    @pl.when(pl.program_id(0) == pl.num_programs(0) - 1)
    def _():
        for index in range(kv_ref.shape[0]):
            keys, values = dkk_ref[index], dvv_ref[index]
            keys = keys + pltpu.roll(keys, HEAD_DIM, 1)
            values = values + pltpu.roll(values, HEAD_DIM, 1)
            lane = lax.broadcasted_iota(jnp.int32, keys.shape, 1)
            dkv_ref[index] = jnp.where(lane < HEAD_DIM, keys, values).astype(bf16)


def block_rows(length):
    return min(128, length)


def whole(shape):
    zeros = (0,) * len(shape)
    return pl.BlockSpec(shape, lambda i, seen: zeros)


def attend(seen, q, kv, order):
    length, width = q.shape
    rows = block_rows(length)
    stacked = GROUP_HEADS * rows
    steps = length // rows
    return pl.pallas_call(
        attend_kernel,
        out_shape=(
            jax.ShapeDtypeStruct((length, width), bf16),
            jax.ShapeDtypeStruct((steps, 8, stacked), f32),
        ),
        grid_spec=pltpu.PrefetchScalarGridSpec(
            num_scalar_prefetch=1,
            grid=(steps,),
            in_specs=[
                pl.BlockSpec((rows, width), lambda i, seen: (i, 0)),
                whole(kv.shape),
                pl.BlockSpec((rows, 1), lambda i, seen: (i, 0)),
                whole((1, length)),
            ],
            out_specs=[
                pl.BlockSpec((rows, width), lambda i, seen: (i, 0)),
                pl.BlockSpec((pl.Squeezed(), 8, stacked), lambda i, seen: (i, 0, 0)),
            ],
            scratch_shapes=[pltpu.VMEM(kv.shape, bf16), pltpu.VMEM(kv.shape, bf16)],
        ),
        name="attend",
    )(seen, q, kv, order[:, None], order[None, :])


def attend_back(seen, q, do, o, kv, lse, order, cosine, sine):
    length, width = q.shape
    rows = block_rows(length)
    stacked = GROUP_HEADS * rows
    steps = length // rows
    return pl.pallas_call(
        attend_back_kernel,
        out_shape=(
            jax.ShapeDtypeStruct((length, width), bf16),
            jax.ShapeDtypeStruct(kv.shape, bf16),
        ),
        grid_spec=pltpu.PrefetchScalarGridSpec(
            num_scalar_prefetch=1,
            grid=(steps,),
            in_specs=[
                pl.BlockSpec((rows, width), lambda i, seen: (i, 0)),
                pl.BlockSpec((rows, width), lambda i, seen: (i, 0)),
                pl.BlockSpec((rows, width), lambda i, seen: (i, 0)),
                whole(kv.shape),
                pl.BlockSpec((pl.Squeezed(), 8, stacked), lambda i, seen: (i, 0, 0)),
                pl.BlockSpec((8, rows), lambda i, seen: (0, i)),
                whole((length, 1)),
                pl.BlockSpec((rows, PAIR), lambda i, seen: (i, 0)),
                pl.BlockSpec((rows, PAIR), lambda i, seen: (i, 0)),
            ],
            out_specs=[
                pl.BlockSpec((rows, width), lambda i, seen: (i, 0)),
                whole(kv.shape),
            ],
            scratch_shapes=[
                pltpu.VMEM((stacked, PAIR), bf16),
                pltpu.VMEM((stacked, PAIR), bf16),
                pltpu.VMEM((8, stacked), f32),
                pltpu.VMEM((stacked, PAIR), f32),
                pltpu.VMEM(kv.shape, bf16),
                pltpu.VMEM(kv.shape, bf16),
                pltpu.VMEM(kv.shape, f32),
                pltpu.VMEM(kv.shape, f32),
            ],
        ),
        name="attend_back",
    )(
        seen, q, do, o, kv, lse, jnp.broadcast_to(order[None, :], (8, length)), order[:, None],
        cosine, sine,
    )


def normalize(values):
    inverse = lax.rsqrt(jnp.mean(values * values, axis=-1, keepdims=True) + epsilon)
    return values * inverse, inverse


def norm_back(inner, normed, inverse):
    return inverse * (inner - normed * jnp.mean(inner * normed, axis=-1, keepdims=True))


def rope_tables(positions):
    half_dim = HEAD_DIM // 2
    frequency = rope_base ** (-(jnp.arange(half_dim).astype(f32) * 2.0 / HEAD_DIM))
    angles = positions.astype(f32)[:, None] * frequency
    times = PAIR // half_dim
    return jnp.tile(jnp.cos(angles), (1, times)), jnp.tile(jnp.sin(angles), (1, times))


def unrotate_keys(grads, cosine, sine):
    half_dim = HEAD_DIM // 2
    sines = grads * sine
    turned = jnp.concatenate([-sines[:, half_dim:], sines[:, :half_dim]], axis=1)
    return grads * cosine - turned


def tie(*values):
    return lax.optimization_barrier(values)


def solution(mesh):
    n_dp = mesh.shape["dp"]
    n_seq = mesh.shape["seq"]
    planes = n_seq // GROUP
    halves = n_dp // 2
    both = ("dp", "seq")

    in_plane = [[GROUP * p + w for w in range(GROUP)] for p in range(planes)]
    across_dp = [
        [c * n_seq + GROUP * p + w for c in range(n_dp) for p in range(planes)] for w in range(GROUP)
    ]
    in_plane_dp = [
        [c * n_seq + GROUP * p + w for c in range(n_dp) for w in range(GROUP)] for p in range(planes)
    ]
    across = [[GROUP * p + w for p in range(planes)] for w in range(GROUP)]

    def xor_w(value, j):
        return lax.ppermute(value, "seq", [(s, s ^ j) for s in range(n_seq)])

    def shift_z(value, t):
        return lax.ppermute(value, "seq", [(s, (s + GROUP * t) % n_seq) for s in range(n_seq)])

    def shift_dp(value, t):
        return lax.ppermute(value, "dp", [(c, (c + t) % n_dp) for c in range(n_dp)])

    def gather_w(value):
        first = xor_w(value, 1)
        second = xor_w(value, 2)
        half = value.shape[0] // 2
        third = jnp.concatenate([xor_w(first[:half], 2), xor_w(second[half:], 1)], axis=0)
        return jnp.concatenate([value, first, second, third], axis=0)

    def scatter_w(slots):
        got = [xor_w(slots[j], j) for j in range(1, GROUP)]
        return functools.reduce(jnp.add, [g.astype(f32) for g in got], slots[0].astype(f32))

    def gather_z(value):
        return [value] + [shift_z(value, t) for t in range(1, planes)]

    def scatter_z(slots):
        got = [shift_z(slots[t], -t) for t in range(1, planes)]
        return functools.reduce(jnp.add, [g.astype(f32) for g in got], slots[0].astype(f32))

    def gather_dp(value):
        return jnp.concatenate([value] + [shift_dp(value, t) for t in range(1, n_dp)], axis=0)

    def pick(value, index, count, axis):
        size = value.shape[axis] // count
        return lax.dynamic_slice_in_dim(value, index * size, size, axis)

    def exchange_dp(value, c, axis):
        parts = [pick(value, c, n_dp, axis)]
        for t in range(1, n_dp):
            parts.append(shift_dp(pick(value, (c + t) % n_dp, n_dp, axis), t))
        return jnp.concatenate(parts, axis=0)

    def collect_dp(value, c):
        slots = [value] + [shift_dp(value, t) for t in range(1, n_dp)]
        out = []
        for member in range(n_dp):
            chosen = slots[0]
            for t in range(1, n_dp):
                chosen = jnp.where((c - t) % n_dp == member, slots[t], chosen)
            out.append(chosen)
        return out

    def body(
        inputs, positions, select, cotangent, gain_attn, w_query, w_key, w_value, w_out, gain_mlp,
        w_gate, w_up, w_down,
    ):
        seqs, rows, width = inputs.shape
        tokens = seqs * rows
        shard = w_query.shape[0]
        ff_rows = w_down.shape[0]
        ff_block = w_gate.shape[1] // planes
        q_width = GROUP_HEADS * HEAD_DIM
        s = lax.axis_index("seq")
        c = lax.axis_index("dp")
        p = s // GROUP
        w = s % GROUP

        gain_one = gain_attn.astype(f32)[:, None]
        gain_two = gain_mlp.astype(f32)[:, None]

        def scaled(weight, gain):
            return (weight.astype(f32) * gain).astype(bf16)

        q_cols = scaled(w_query, gain_one).reshape(shard, GROUP, n_dp, q_width // n_dp)
        kv_cols = jnp.concatenate(
            [
                scaled(w_key, gain_one).reshape(shard, GROUP, HEAD_DIM),
                scaled(w_value, gain_one).reshape(shard, GROUP, HEAD_DIM),
            ],
            axis=-1,
        ).reshape(shard, GROUP, n_dp, PAIR // n_dp)
        qkv_cols = jnp.concatenate([q_cols, kv_cols], axis=-1)
        qkv_part = lax.dynamic_index_in_dim(qkv_cols, c, 2, keepdims=False)
        qkv_part = lax.all_to_all(
            jnp.transpose(qkv_part, (1, 0, 2)), "seq", 0, 0, axis_index_groups=in_plane, tiled=True
        )
        part_width = (q_width + PAIR) // n_dp
        qkv_part = qkv_part.reshape(GROUP * shard, part_width)
        own_pos = positions.reshape(1, tokens)
        plane_pos = jnp.concatenate([own_pos] + [xor_w(own_pos, j) for j in range(1, GROUP)], axis=1)
        x_in = inputs.reshape(tokens, width).astype(f32)
        normed_one, inverse_one = normalize(x_in)
        low_one, qkv_part, plane_pos = tie(normed_one.astype(bf16), qkv_part, plane_pos)

        ring = [qkv_part] + [shift_z(qkv_part, -t) for t in range(1, planes)]
        qkv_ring = jnp.concatenate(ring + ring[: planes - 1], axis=0)
        qkv_mine = lax.dynamic_slice_in_dim(
            qkv_ring, ((planes - p) % planes) * GROUP * shard, width, 0
        )
        low_one = gather_w(low_one)

        piece = shard // halves
        gate_up = jnp.where(c // halves == 0, scaled(w_gate, gain_two), scaled(w_up, gain_two))
        out_part, gate_up, qkv_mine = tie(
            pick(w_out, c, n_dp, 1), pick(gate_up, c % halves, halves, 0), qkv_mine
        )
        qkv_full = collect_dp(qkv_mine, c)
        out_part = lax.ppermute(
            out_part, "seq", [(i, GROUP * (i % planes) + i // planes) for i in range(n_seq)]
        )
        gate_up_sent = [
            shift_z(pick(gate_up, (p + t) % planes, planes, 1), t) if t
            else pick(gate_up, p, planes, 1)
            for t in range(planes)
        ]
        down_full = lax.all_gather(
            pick(w_down, c, n_dp, 1), both, axis_index_groups=in_plane_dp, tiled=False
        )
        out_part, down_full = tie(out_part, down_full)
        down_full = down_full.reshape(n_dp, ff_block, width // n_dp)
        out_full = lax.all_gather(out_part, both, axis_index_groups=across_dp, tiled=False)
        out_full = out_full.reshape(n_dp, planes * shard, width // n_dp)

        blocks = [
            (i * GROUP + j) * halves + h
            for h in range(halves) for j in range(GROUP) for i in range(planes)
        ]

        def column_blocks(value, which):
            return jnp.concatenate([value[:, i * piece : (i + 1) * piece] for i in which], axis=1)

        def reorder(value):
            return column_blocks(value, blocks)

        def order_back(value):
            return column_blocks(value, [blocks.index(i) for i in range(len(blocks))])

        cosine, sine = rope_tables(plane_pos.reshape(GROUP * tokens))

        grad_y = (
            cotangent.astype(f32) * select.astype(f32)[..., None]
        ).reshape(tokens, width)
        cut = q_width // n_dp
        plane_tokens = GROUP * tokens
        qkv_weights = jnp.concatenate(
            [one[:, :cut] for one in qkv_full] + [one[:, cut:] for one in qkv_full], axis=1
        )
        q, kv_low = project(low_one, qkv_weights, cosine, sine)
        kv_all = jnp.stack(gather_z(kv_low))
        grad_y_low, kv_all = tie(grad_y.astype(bf16), kv_all)
        *gate_up_sent, q = tie(*gate_up_sent, q)
        gate_up_part = jnp.zeros((planes, piece, ff_block), bf16)
        for t in range(planes):
            gate_up_part = lax.dynamic_update_index_in_dim(
                gate_up_part, gate_up_sent[t], (p - t) % planes, 0
            )
        gate_up_full = lax.all_gather(
            gate_up_part, both, axis_index_groups=in_plane_dp, tiled=False
        )
        gate_up_full = gate_up_full.reshape(2, width, ff_block)
        grad_y_all = jnp.concatenate(gather_z(grad_y_low), axis=0)

        def by_seq(value, axis):
            shape = value.shape
            value = value.reshape(shape[:axis] + (GROUP, seqs, rows) + shape[axis + 1 :])
            value = jnp.moveaxis(value, axis + 1, 0)
            return value.reshape((seqs,) + shape[:axis] + (GROUP * rows,) + shape[axis + 1 :])

        def from_seq(value, axis):
            shape = value.shape[1:]
            value = value.reshape((seqs,) + shape[:axis] + (GROUP, rows) + shape[axis + 1 :])
            value = jnp.moveaxis(value, 0, axis + 1)
            return value.reshape(shape[:axis] + (GROUP * seqs * rows,) + shape[axis + 1 :])

        order = jnp.concatenate([(w ^ j) * rows + jnp.arange(rows) for j in range(GROUP)])
        order = order.astype(jnp.int32)
        seen = (p + 1).astype(jnp.int32).reshape(1)
        q_seq = by_seq(q, 0)
        kv_seq = by_seq(kv_all, 1)
        cos_seq = by_seq(cosine, 0)
        sin_seq = by_seq(sine, 0)
        pieces = [attend(seen, q_seq[i], kv_seq[i], order) for i in range(seqs)]
        o_seq = [one[0] for one in pieces]
        lse_seq = [one[1] for one in pieces]
        o = from_seq(jnp.stack(o_seq), 0)

        branch = jnp.concatenate([dot(o, out_full[i]).astype(bf16) for i in range(n_dp)], axis=1)
        branch = scatter_w([branch[j * tokens : (j + 1) * tokens] for j in range(GROUP)])
        x_mid = x_in + branch

        normed_two, inverse_two = normalize(x_mid)
        low_two = reorder(normed_two.astype(bf16))
        low_two, grad_y_all = tie(low_two, grad_y_all)
        low_two_own, *low_two_sent = gather_z(low_two)
        grad_hidden = functools.reduce(
            jnp.add,
            [
                dot(pick(grad_y_all, i, n_dp, 1), down_full[i], ((1,), (1,)))
                for i in range(n_dp)
            ],
        )
        *low_two_sent, grad_hidden = tie(*low_two_sent, grad_hidden)
        low_two = jnp.concatenate([low_two_own] + low_two_sent, axis=0)
        hidden, grad_gate, grad_up, grad_low_two = feed(low_two, gate_up_full, grad_hidden)
        hidden_later, grad_gate_later, grad_up_later, grad_low_two = tie(
            hidden, grad_gate, grad_up, grad_low_two
        )
        inner_sent = [
            shift_z(grad_low_two[t * tokens : (t + 1) * tokens], -t) for t in range(1, planes)
        ]

        hidden_all = gather_dp(hidden_later)
        down_sum = dot(hidden_all, exchange_dp(grad_y_all, c, 1), ((0,), (0,))).astype(bf16)

        low_two_all = gather_dp(low_two)
        if halves > 1:
            low_two_all = pick(low_two_all, c % halves, halves, 1)

        def of_member(member):
            return jnp.where(member // halves == 0, grad_gate_later, grad_up_later)

        gate_up_grads = [of_member(c)]
        for t in range(1, n_dp):
            gate_up_grads.append(shift_dp(of_member((c + t) % n_dp), t))
        gate_up_grads = jnp.concatenate(gate_up_grads, axis=0)
        gate_up_sum = dot(low_two_all, gate_up_grads, ((0,), (0,))).astype(bf16)

        inner_sent[0], gate_up_sum = tie(inner_sent[0], gate_up_sum)
        *inner_rest, down_sum = tie(*inner_sent[1:], down_sum)
        inner_sent = [inner_sent[0]] + inner_rest
        mixed = jnp.concatenate(
            [dot(hidden_later, down_full[i]).astype(bf16) for i in range(n_dp)], axis=1
        )
        *inner_sent, mixed = tie(*inner_sent, mixed)
        inner_two = functools.reduce(
            jnp.add, [g.astype(f32) for g in inner_sent], grad_low_two[:tokens].astype(f32)
        )
        grad_x_mid = grad_y + norm_back(order_back(inner_two), normed_two, inverse_two)

        mixed, grad_x_low = tie(mixed, grad_x_mid.astype(bf16))
        mixed_sent = [shift_z(mixed[t * tokens : (t + 1) * tokens], -t) for t in range(1, planes)]
        gate_up_sum = lax.psum_scatter(gate_up_sum, "seq", axis_index_groups=in_plane, tiled=True)
        down_sum = lax.psum_scatter(
            down_sum, "seq", axis_index_groups=in_plane, tiled=True
        )
        gate_up_sum = gate_up_sum.reshape(planes, piece, ff_block)

        grad_branch = gather_w(grad_x_low)
        early = planes - 2
        *mixed_sent[:early], grad_branch = tie(*mixed_sent[:early], grad_branch)
        grad_o = functools.reduce(
            jnp.add,
            [dot(pick(grad_branch, i, n_dp, 1), out_full[i], ((1,), (1,))) for i in range(n_dp)],
        ).astype(bf16)

        out_part_sum = dot(gather_dp(o), exchange_dp(grad_branch, c, 1), ((0,), (0,))).astype(bf16)
        grad_o_seq = by_seq(grad_o, 0)
        *late, grad_o_seq, out_part_sum = tie(*mixed_sent[early:], grad_o_seq, out_part_sum)
        mixed_sent = mixed_sent[:early] + list(late)
        gate_up_sum, out_part_sum = tie(gate_up_sum, out_part_sum)
        out_sum = lax.psum_scatter(out_part_sum, "seq", axis_index_groups=across, tiled=True)
        pieces = [
            attend_back(
                seen, q_seq[i], grad_o_seq[i], o_seq[i], kv_seq[i], lse_seq[i], order,
                cos_seq[i], sin_seq[i],
            )
            for i in range(seqs)
        ]
        grad_q = jnp.stack([one[0] for one in pieces])
        mixed = functools.reduce(
            jnp.add, [g.astype(f32) for g in mixed_sent], mixed[:tokens].astype(f32)
        )
        query_pre = from_seq(grad_q, 0)
        grad_kv = from_seq(jnp.stack([one[1] for one in pieces]), 1)
        grad_kv = scatter_z([grad_kv[t] for t in range(planes)])
        grad_kv, gate_up_late = tie(grad_kv, gate_up_sum)
        gate_up_sent = []
        for t in range(planes):
            block = lax.dynamic_index_in_dim(gate_up_late, (p + t) % planes, 0, keepdims=False)
            gate_up_sent.append(shift_z(block, t) if t else block)
        query_pre, out_sum = tie(query_pre, out_sum)
        key_pre = unrotate_keys(
            grad_kv[:, :HEAD_DIM], cosine[:, :HEAD_DIM], sine[:, :HEAD_DIM]
        )
        kv_pre = jnp.concatenate([key_pre, grad_kv[:, HEAD_DIM:]], axis=1).astype(bf16)
        pre = [
            jnp.concatenate(
                [query_pre[:, i * cut : (i + 1) * cut], pick(kv_pre, i, n_dp, 1)], axis=1
            )
            for i in range(n_dp)
        ]
        outputs = (x_mid + mixed).astype(bf16).reshape(seqs, rows, width)

        grad_low_one = dot(
            jnp.concatenate([query_pre, kv_pre], axis=1), qkv_weights, ((1,), (1,))
        ).astype(bf16)
        inner_one = scatter_w([grad_low_one[j * tokens : (j + 1) * tokens] for j in range(GROUP)])
        grad_inputs = grad_x_mid + norm_back(inner_one, normed_one, inverse_one)
        grad_inputs = grad_inputs.reshape(seqs, rows, width)

        qkv_sum = dot(
            gather_dp(low_one),
            exchange_dp(jnp.concatenate(pre, axis=1), c, 1),
            ((0,), (0,)),
        ).astype(bf16)
        *gate_up_sent, down_sum, qkv_sum = tie(*gate_up_sent, down_sum, qkv_sum)
        out_sum = lax.ppermute(
            out_sum, "seq", [(GROUP * (i % planes) + i // planes, i) for i in range(n_seq)]
        )
        grad_w_out = jnp.concatenate(collect_dp(out_sum, c), axis=1).astype(f32)

        qkv_sum = lax.psum_scatter(
            qkv_sum, "seq", axis_index_groups=across, tiled=True
        )
        qkv_sum = qkv_sum.reshape(GROUP, shard, part_width)
        qkv_sum = lax.all_to_all(qkv_sum, "seq", 0, 0, axis_index_groups=in_plane, tiled=True)
        qkv_sum = collect_dp(qkv_sum, c)
        q_sum = jnp.concatenate(
            [one[j][:, :cut] for j in range(GROUP) for one in qkv_sum], axis=1
        ).astype(f32)
        kv_sum = jnp.concatenate(
            [one[j][:, cut:] for j in range(GROUP) for one in qkv_sum], axis=1
        ).astype(f32).reshape(shard, GROUP, PAIR)
        k_sum = kv_sum[..., :HEAD_DIM].reshape(shard, GROUP * HEAD_DIM)
        v_sum = kv_sum[..., HEAD_DIM:].reshape(shard, GROUP * HEAD_DIM)

        grad_w_down = jnp.concatenate(collect_dp(down_sum, c), axis=1).astype(f32)
        gate_up_rows = jnp.zeros((planes, piece, ff_block), bf16)
        for t in range(planes):
            gate_up_rows = lax.dynamic_update_index_in_dim(
                gate_up_rows, gate_up_sent[t], (p - t) % planes, 0
            )
        gate_up_rows = collect_dp(gate_up_rows, c)

        def rows_of(members):
            wide = [jnp.concatenate([one[i] for i in range(planes)], axis=1) for one in members]
            return jnp.concatenate(wide, axis=0).astype(f32)

        gate_rows = rows_of(gate_up_rows[:halves])
        up_rows = rows_of(gate_up_rows[halves:])
        grad_w_gate = gate_rows * gain_two
        grad_w_up = up_rows * gain_two
        grad_gain_mlp = jnp.sum(
            gate_rows * w_gate.astype(f32) + up_rows * w_up.astype(f32), axis=1
        )
        grad_gain_attn = (
            jnp.sum(q_sum * w_query.astype(f32), axis=1)
            + jnp.sum(k_sum * w_key.astype(f32), axis=1)
            + jnp.sum(v_sum * w_value.astype(f32), axis=1)
        )

        return (
            outputs,
            grad_inputs,
            grad_gain_attn,
            q_sum * gain_one,
            k_sum * gain_one,
            v_sum * gain_one,
            grad_w_out,
            grad_gain_mlp,
            grad_w_gate,
            grad_w_up,
            grad_w_down,
        )

    tokens_spec = P("dp", "seq", None)
    in_specs = (
        tokens_spec,
        P("dp", "seq"),
        P("dp", "seq"),
        tokens_spec,
        P("seq"),
        P("seq", None),
        P("seq", None),
        P("seq", None),
        P("seq", None),
        P("seq"),
        P("seq", None),
        P("seq", None),
        P("seq", None),
    )
    out_specs = (
        tokens_spec,
        tokens_spec,
        P("seq"),
        P("seq", None),
        P("seq", None),
        P("seq", None),
        P("seq", None),
        P("seq"),
        P("seq", None),
        P("seq", None),
        P("seq", None),
    )
    return jax.shard_map(body, mesh=mesh, in_specs=in_specs, out_specs=out_specs, check_vma=False)
```

```python
import functools

import jax
import jax.numpy as jnp
from jax import lax
from jax.experimental import pallas as pl
from jax.experimental.pallas import tpu as pltpu
from jax.sharding import PartitionSpec as P

HEADS = 32
KV_HEADS = 4
HEAD_DIM = 64
GROUP = KV_HEADS
GROUP_HEADS = HEADS // GROUP
PAIR = 2 * HEAD_DIM

epsilon = 1e-05
rope_base = 10000.0
masked_score = -1e30

f32 = jnp.float32
bf16 = jnp.bfloat16


def dot(left, right, contract=((1,), (0,))):
    return lax.dot_general(left, right, (contract, ((), ())), preferred_element_type=f32)


def stack_heads(block, rows):
    lane = lax.broadcasted_iota(jnp.int32, (rows, PAIR), 1)
    parts = []
    for pair in range(GROUP_HEADS // 2):
        both = block[:, pair * PAIR : (pair + 1) * PAIR]
        parts.append(jnp.where(lane < HEAD_DIM, both, jnp.zeros_like(both)))
        parts.append(jnp.where(lane >= HEAD_DIM, both, jnp.zeros_like(both)))
    return jnp.concatenate(parts, axis=0)


def unstack_heads(stacked, rows):
    lane = lax.broadcasted_iota(jnp.int32, (rows, PAIR), 1)
    parts = []
    for pair in range(GROUP_HEADS // 2):
        low = stacked[2 * pair * rows : (2 * pair + 1) * rows]
        high = stacked[(2 * pair + 1) * rows : (2 * pair + 2) * rows]
        parts.append(jnp.where(lane < HEAD_DIM, low, high))
    return jnp.concatenate(parts, axis=1)


def as_row(column):
    wide = jnp.broadcast_to(column, (column.shape[0], 128))
    return jnp.transpose(wide)[:8]


def turn(values):
    width = values.shape[1]
    half_dim = HEAD_DIM // 2
    lane = lax.broadcasted_iota(jnp.int32, values.shape, 1)
    ahead = pltpu.roll(values, width - half_dim, 1)
    behind = pltpu.roll(values, half_dim, 1)
    return jnp.where(lane % HEAD_DIM < half_dim, -ahead, behind)


def rotate(values, cosine, sine):
    return values * cosine + turn(values) * sine


def unrotate(grads, cosine, sine):
    return grads * cosine - turn(grads * sine)


def project_kernel(low_ref, w_ref, cos_ref, sin_ref, q_ref, kv_ref):
    made = dot(low_ref[...], w_ref[...])
    cosine, sine = cos_ref[...], sin_ref[...]
    for i in range(q_ref.shape[1] // PAIR):
        q = rotate(made[:, i * PAIR : (i + 1) * PAIR], cosine, sine).astype(bf16)
        q_ref[:, i * PAIR : (i + 1) * PAIR] = (q.astype(f32) * HEAD_DIM ** (-0.5)).astype(bf16)
    kv = made[:, q_ref.shape[1] :]
    lane = lax.broadcasted_iota(jnp.int32, kv.shape, 1)
    kv_ref[...] = jnp.where(lane < HEAD_DIM, rotate(kv, cosine, sine), kv).astype(bf16)


def project(low, weights, cosine, sine):
    tokens, width = low.shape
    q_width = weights.shape[1] - PAIR
    rows = min(256, tokens)
    return pl.pallas_call(
        project_kernel,
        out_shape=(
            jax.ShapeDtypeStruct((tokens, q_width), bf16),
            jax.ShapeDtypeStruct((tokens, PAIR), bf16),
        ),
        grid=(tokens // rows,),
        in_specs=[
            pl.BlockSpec((rows, width), lambda i: (i, 0)),
            pl.BlockSpec(weights.shape, lambda i: (0, 0)),
            pl.BlockSpec((rows, PAIR), lambda i: (i, 0)),
            pl.BlockSpec((rows, PAIR), lambda i: (i, 0)),
        ],
        out_specs=[
            pl.BlockSpec((rows, q_width), lambda i: (i, 0)),
            pl.BlockSpec((rows, PAIR), lambda i: (i, 0)),
        ],
        name="project",
    )(low, weights, cosine, sine)


def feed_kernel(low_ref, w_ref, grad_hidden_ref, hidden_ref, grad_gate_ref, grad_up_ref, back_ref):
    low = low_ref[...]
    gate = dot(low, w_ref[0])
    up = dot(low, w_ref[1])
    grad_hidden = grad_hidden_ref[...]
    sigmoid_gate = 1.0 / (1.0 + jnp.exp(-gate))
    silu = gate * sigmoid_gate
    hidden_ref[...] = (silu * up).astype(bf16)
    grad_gate = (
        grad_hidden * up * sigmoid_gate * (1.0 + gate * (1.0 - sigmoid_gate))
    ).astype(bf16)
    grad_up = (grad_hidden * silu).astype(bf16)
    grad_gate_ref[...] = grad_gate
    grad_up_ref[...] = grad_up
    back_ref[...] = (
        dot(grad_gate, w_ref[0], ((1,), (1,))) + dot(grad_up, w_ref[1], ((1,), (1,)))
    ).astype(bf16)


def feed(low, weights, grad_hidden):
    tokens, width = low.shape
    block = weights.shape[2]
    rows = min(256, tokens)
    narrow = pl.BlockSpec((rows, block), lambda i: (i, 0))
    wide = pl.BlockSpec((rows, width), lambda i: (i, 0))
    return pl.pallas_call(
        feed_kernel,
        out_shape=(
            jax.ShapeDtypeStruct((tokens, block), bf16),
            jax.ShapeDtypeStruct((tokens, block), bf16),
            jax.ShapeDtypeStruct((tokens, block), bf16),
            jax.ShapeDtypeStruct((tokens, width), bf16),
        ),
        grid=(tokens // rows,),
        in_specs=[wide, pl.BlockSpec(weights.shape, lambda i: (0, 0, 0)), narrow],
        out_specs=[narrow, narrow, narrow, wide],
        name="feed",
    )(low, weights, grad_hidden)


def both_lanes(kv_ref, kk_ref, vv_ref):
    @pl.when(pl.program_id(0) == 0)
    def _():
        for index in range(kv_ref.shape[0]):
            kv = kv_ref[index].astype(f32)
            swapped = pltpu.roll(kv, HEAD_DIM, 1)
            lane = lax.broadcasted_iota(jnp.int32, kv.shape, 1)
            kk_ref[index] = jnp.where(lane < HEAD_DIM, kv, swapped).astype(bf16)
            vv_ref[index] = jnp.where(lane < HEAD_DIM, swapped, kv).astype(bf16)


def attend_kernel(seen_ref, q_ref, kv_ref, qpos_ref, kpos_ref, o_ref, lse_ref, kk_ref, vv_ref):
    rows = q_ref.shape[0]
    both_lanes(kv_ref, kk_ref, vv_ref)
    stacked = stack_heads(q_ref[...], rows)
    qpos = jnp.concatenate([qpos_ref[...]] * GROUP_HEADS, axis=0)

    def unit(index, carry, masked):
        top, total, acc = carry
        scores = dot(stacked, kk_ref[index], ((1,), (1,)))
        if masked:
            scores = jnp.where(kpos_ref[...] <= qpos, scores, masked_score)
        new_top = jnp.maximum(top, jnp.max(scores, axis=1, keepdims=True))
        weights = jnp.exp(scores - new_top)
        keep = jnp.exp(top - new_top)
        total = total * keep + jnp.sum(weights, axis=1, keepdims=True)
        acc = acc * keep + dot(weights.astype(bf16), vv_ref[index])
        return new_top, total, acc

    count = GROUP_HEADS * rows
    start = (
        jnp.full((count, 1), masked_score, f32),
        jnp.zeros((count, 1), f32),
        jnp.zeros((count, PAIR), f32),
    )
    carry = unit(0, start, True)
    top, total, acc = lax.fori_loop(1, seen_ref[0], lambda i, c: unit(i, c, False), carry)
    o_ref[...] = unstack_heads(acc / total, rows).astype(bf16)
    lse_ref[...] = as_row(top + jnp.log(total))


def attend_back_kernel(
    seen_ref, q_ref, do_ref, o_ref, kv_ref, lse_ref, qpos_ref, kpos_ref, cos_ref, sin_ref,
    dq_ref, dkv_ref, qs_ref, dos_ref, delta_ref, dqs_ref, kk_ref, vv_ref, dkk_ref, dvv_ref,
):
    rows = q_ref.shape[0]
    both_lanes(kv_ref, kk_ref, vv_ref)

    @pl.when(pl.program_id(0) == 0)
    def _():
        dkk_ref[...] = jnp.zeros_like(dkk_ref)
        dvv_ref[...] = jnp.zeros_like(dvv_ref)

    qs_ref[...] = stack_heads(q_ref[...], rows)
    grads = stack_heads(do_ref[...], rows)
    dos_ref[...] = grads
    outs = stack_heads(o_ref[...], rows)
    delta_ref[...] = as_row(jnp.sum(grads.astype(f32) * outs.astype(f32), axis=1, keepdims=True))

    def unit(index, masked):
        keys = kk_ref[index]
        scores = dot(keys, qs_ref[...], ((1,), (1,)))
        if masked:
            qpos = jnp.concatenate([qpos_ref[0:1, :]] * GROUP_HEADS, axis=1)
            scores = jnp.where(kpos_ref[...] <= qpos, scores, masked_score)
        probs = jnp.exp(scores - lse_ref[0:1, :])
        prob_grad = dot(vv_ref[index], dos_ref[...], ((1,), (1,)))
        score_grad = (probs * (prob_grad - delta_ref[0:1, :])).astype(bf16)
        dvv_ref[index] += dot(probs.astype(bf16), dos_ref[...])
        dkk_ref[index] += dot(score_grad, qs_ref[...])
        return dot(score_grad, keys, ((0,), (0,)))

    dqs_ref[...] = unit(0, True)

    @pl.loop(1, seen_ref[0])
    def _(index):
        dqs_ref[...] += unit(index, False)

    grads = unstack_heads(dqs_ref[...], rows) * HEAD_DIM ** (-0.5)
    cosine, sine = cos_ref[...], sin_ref[...]
    for i in range(dq_ref.shape[1] // PAIR):
        part = unrotate(grads[:, i * PAIR : (i + 1) * PAIR], cosine, sine)
        dq_ref[:, i * PAIR : (i + 1) * PAIR] = part.astype(bf16)

    @pl.when(pl.program_id(0) == pl.num_programs(0) - 1)
    def _():
        for index in range(kv_ref.shape[0]):
            keys, values = dkk_ref[index], dvv_ref[index]
            keys = keys + pltpu.roll(keys, HEAD_DIM, 1)
            values = values + pltpu.roll(values, HEAD_DIM, 1)
            lane = lax.broadcasted_iota(jnp.int32, keys.shape, 1)
            dkv_ref[index] = jnp.where(lane < HEAD_DIM, keys, values).astype(bf16)


def block_rows(length):
    return min(128, length)


def whole(shape):
    zeros = (0,) * len(shape)
    return pl.BlockSpec(shape, lambda i, seen: zeros)


def attend(seen, q, kv, order):
    length, width = q.shape
    rows = block_rows(length)
    stacked = GROUP_HEADS * rows
    steps = length // rows
    return pl.pallas_call(
        attend_kernel,
        out_shape=(
            jax.ShapeDtypeStruct((length, width), bf16),
            jax.ShapeDtypeStruct((steps, 8, stacked), f32),
        ),
        grid_spec=pltpu.PrefetchScalarGridSpec(
            num_scalar_prefetch=1,
            grid=(steps,),
            in_specs=[
                pl.BlockSpec((rows, width), lambda i, seen: (i, 0)),
                whole(kv.shape),
                pl.BlockSpec((rows, 1), lambda i, seen: (i, 0)),
                whole((1, length)),
            ],
            out_specs=[
                pl.BlockSpec((rows, width), lambda i, seen: (i, 0)),
                pl.BlockSpec((pl.Squeezed(), 8, stacked), lambda i, seen: (i, 0, 0)),
            ],
            scratch_shapes=[pltpu.VMEM(kv.shape, bf16), pltpu.VMEM(kv.shape, bf16)],
        ),
        name="attend",
    )(seen, q, kv, order[:, None], order[None, :])


def attend_back(seen, q, do, o, kv, lse, order, cosine, sine):
    length, width = q.shape
    rows = block_rows(length)
    stacked = GROUP_HEADS * rows
    steps = length // rows
    return pl.pallas_call(
        attend_back_kernel,
        out_shape=(
            jax.ShapeDtypeStruct((length, width), bf16),
            jax.ShapeDtypeStruct(kv.shape, bf16),
        ),
        grid_spec=pltpu.PrefetchScalarGridSpec(
            num_scalar_prefetch=1,
            grid=(steps,),
            in_specs=[
                pl.BlockSpec((rows, width), lambda i, seen: (i, 0)),
                pl.BlockSpec((rows, width), lambda i, seen: (i, 0)),
                pl.BlockSpec((rows, width), lambda i, seen: (i, 0)),
                whole(kv.shape),
                pl.BlockSpec((pl.Squeezed(), 8, stacked), lambda i, seen: (i, 0, 0)),
                pl.BlockSpec((8, rows), lambda i, seen: (0, i)),
                whole((length, 1)),
                pl.BlockSpec((rows, PAIR), lambda i, seen: (i, 0)),
                pl.BlockSpec((rows, PAIR), lambda i, seen: (i, 0)),
            ],
            out_specs=[
                pl.BlockSpec((rows, width), lambda i, seen: (i, 0)),
                whole(kv.shape),
            ],
            scratch_shapes=[
                pltpu.VMEM((stacked, PAIR), bf16),
                pltpu.VMEM((stacked, PAIR), bf16),
                pltpu.VMEM((8, stacked), f32),
                pltpu.VMEM((stacked, PAIR), f32),
                pltpu.VMEM(kv.shape, bf16),
                pltpu.VMEM(kv.shape, bf16),
                pltpu.VMEM(kv.shape, f32),
                pltpu.VMEM(kv.shape, f32),
            ],
        ),
        name="attend_back",
    )(
        seen, q, do, o, kv, lse, jnp.broadcast_to(order[None, :], (8, length)), order[:, None],
        cosine, sine,
    )


def normalize(values):
    inverse = lax.rsqrt(jnp.mean(values * values, axis=-1, keepdims=True) + epsilon)
    return values * inverse, inverse


def norm_back(inner, normed, inverse):
    return inverse * (inner - normed * jnp.mean(inner * normed, axis=-1, keepdims=True))


def rope_tables(positions):
    half_dim = HEAD_DIM // 2
    frequency = rope_base ** (-(jnp.arange(half_dim).astype(f32) * 2.0 / HEAD_DIM))
    angles = positions.astype(f32)[:, None] * frequency
    times = PAIR // half_dim
    return jnp.tile(jnp.cos(angles), (1, times)), jnp.tile(jnp.sin(angles), (1, times))


def unrotate_keys(grads, cosine, sine):
    half_dim = HEAD_DIM // 2
    sines = grads * sine
    turned = jnp.concatenate([-sines[:, half_dim:], sines[:, :half_dim]], axis=1)
    return grads * cosine - turned


def tie(*values):
    return lax.optimization_barrier(values)


def solution(mesh):
    n_dp = mesh.shape["dp"]
    n_seq = mesh.shape["seq"]
    planes = n_seq // GROUP
    halves = n_dp // 2
    both = ("dp", "seq")

    in_plane = [[GROUP * p + w for w in range(GROUP)] for p in range(planes)]
    across_dp = [
        [c * n_seq + GROUP * p + w for c in range(n_dp) for p in range(planes)] for w in range(GROUP)
    ]
    in_plane_dp = [
        [c * n_seq + GROUP * p + w for c in range(n_dp) for w in range(GROUP)] for p in range(planes)
    ]
    across = [[GROUP * p + w for p in range(planes)] for w in range(GROUP)]

    def xor_w(value, j):
        return lax.ppermute(value, "seq", [(s, s ^ j) for s in range(n_seq)])

    def shift_z(value, t):
        return lax.ppermute(value, "seq", [(s, (s + GROUP * t) % n_seq) for s in range(n_seq)])

    def shift_dp(value, t):
        return lax.ppermute(value, "dp", [(c, (c + t) % n_dp) for c in range(n_dp)])

    def gather_w(value):
        first = xor_w(value, 1)
        second = xor_w(value, 2)
        half = value.shape[0] // 2
        third = jnp.concatenate([xor_w(first[:half], 2), xor_w(second[half:], 1)], axis=0)
        return jnp.concatenate([value, first, second, third], axis=0)

    def scatter_w(slots):
        got = [xor_w(slots[j], j) for j in range(1, GROUP)]
        return functools.reduce(jnp.add, [g.astype(f32) for g in got], slots[0].astype(f32))

    def gather_z(value):
        return [value] + [shift_z(value, t) for t in range(1, planes)]

    def scatter_z(slots):
        got = [shift_z(slots[t], -t) for t in range(1, planes)]
        return functools.reduce(jnp.add, [g.astype(f32) for g in got], slots[0].astype(f32))

    def gather_dp(value):
        return jnp.concatenate([value] + [shift_dp(value, t) for t in range(1, n_dp)], axis=0)

    def pick(value, index, count, axis):
        size = value.shape[axis] // count
        return lax.dynamic_slice_in_dim(value, index * size, size, axis)

    def exchange_dp(value, c, axis):
        parts = [pick(value, c, n_dp, axis)]
        for t in range(1, n_dp):
            parts.append(shift_dp(pick(value, (c + t) % n_dp, n_dp, axis), t))
        return jnp.concatenate(parts, axis=0)

    def collect_dp(value, c):
        slots = [value] + [shift_dp(value, t) for t in range(1, n_dp)]
        out = []
        for member in range(n_dp):
            chosen = slots[0]
            for t in range(1, n_dp):
                chosen = jnp.where((c - t) % n_dp == member, slots[t], chosen)
            out.append(chosen)
        return out

    def body(
        inputs, positions, select, cotangent, gain_attn, w_query, w_key, w_value, w_out, gain_mlp,
        w_gate, w_up, w_down,
    ):
        seqs, rows, width = inputs.shape
        tokens = seqs * rows
        shard = w_query.shape[0]
        ff_rows = w_down.shape[0]
        ff_block = w_gate.shape[1] // planes
        q_width = GROUP_HEADS * HEAD_DIM
        s = lax.axis_index("seq")
        c = lax.axis_index("dp")
        p = s // GROUP
        w = s % GROUP

        gain_one = gain_attn.astype(f32)[:, None]
        gain_two = gain_mlp.astype(f32)[:, None]

        def scaled(weight, gain):
            return (weight.astype(f32) * gain).astype(bf16)

        q_cols = scaled(w_query, gain_one).reshape(shard, GROUP, n_dp, q_width // n_dp)
        kv_cols = jnp.concatenate(
            [
                scaled(w_key, gain_one).reshape(shard, GROUP, HEAD_DIM),
                scaled(w_value, gain_one).reshape(shard, GROUP, HEAD_DIM),
            ],
            axis=-1,
        ).reshape(shard, GROUP, n_dp, PAIR // n_dp)
        qkv_cols = jnp.concatenate([q_cols, kv_cols], axis=-1)
        qkv_part = lax.dynamic_index_in_dim(qkv_cols, c, 2, keepdims=False)
        qkv_part = lax.all_to_all(
            jnp.transpose(qkv_part, (1, 0, 2)), "seq", 0, 0, axis_index_groups=in_plane, tiled=True
        )
        part_width = (q_width + PAIR) // n_dp
        qkv_part = qkv_part.reshape(GROUP * shard, part_width)
        own_pos = positions.reshape(1, tokens)
        plane_pos = jnp.concatenate([own_pos] + [xor_w(own_pos, j) for j in range(1, GROUP)], axis=1)
        x_in = inputs.reshape(tokens, width).astype(f32)
        normed_one, inverse_one = normalize(x_in)
        low_one, qkv_part, plane_pos = tie(normed_one.astype(bf16), qkv_part, plane_pos)

        ring = [qkv_part] + [shift_z(qkv_part, -t) for t in range(1, planes)]
        qkv_ring = jnp.concatenate(ring + ring[: planes - 1], axis=0)
        qkv_mine = lax.dynamic_slice_in_dim(
            qkv_ring, ((planes - p) % planes) * GROUP * shard, width, 0
        )
        low_one = gather_w(low_one)

        piece = shard // halves
        gate_up = jnp.where(c // halves == 0, scaled(w_gate, gain_two), scaled(w_up, gain_two))
        out_part, gate_up, qkv_mine = tie(
            pick(w_out, c, n_dp, 1), pick(gate_up, c % halves, halves, 0), qkv_mine
        )
        qkv_full = collect_dp(qkv_mine, c)
        out_part = lax.ppermute(
            out_part, "seq", [(i, GROUP * (i % planes) + i // planes) for i in range(n_seq)]
        )
        gate_up_sent = [
            shift_z(pick(gate_up, (p + t) % planes, planes, 1), t) if t
            else pick(gate_up, p, planes, 1)
            for t in range(planes)
        ]
        down_full = lax.all_gather(
            pick(w_down, c, n_dp, 1), both, axis_index_groups=in_plane_dp, tiled=False
        )
        out_part, down_full = tie(out_part, down_full)
        down_full = down_full.reshape(n_dp, ff_block, width // n_dp)
        out_full = lax.all_gather(out_part, both, axis_index_groups=across_dp, tiled=False)
        out_full = out_full.reshape(n_dp, planes * shard, width // n_dp)

        blocks = [
            (i * GROUP + j) * halves + h
            for h in range(halves) for j in range(GROUP) for i in range(planes)
        ]

        def column_blocks(value, which):
            return jnp.concatenate([value[:, i * piece : (i + 1) * piece] for i in which], axis=1)

        def reorder(value):
            return column_blocks(value, blocks)

        def order_back(value):
            return column_blocks(value, [blocks.index(i) for i in range(len(blocks))])

        cosine, sine = rope_tables(plane_pos.reshape(GROUP * tokens))

        grad_y = (
            cotangent.astype(f32) * select.astype(f32)[..., None]
        ).reshape(tokens, width)
        cut = q_width // n_dp
        plane_tokens = GROUP * tokens
        qkv_weights = jnp.concatenate(
            [one[:, :cut] for one in qkv_full] + [one[:, cut:] for one in qkv_full], axis=1
        )
        q, kv_low = project(low_one, qkv_weights, cosine, sine)
        kv_all = jnp.stack(gather_z(kv_low))
        grad_y_low, kv_all = tie(grad_y.astype(bf16), kv_all)
        *gate_up_sent, q = tie(*gate_up_sent, q)
        gate_up_part = jnp.zeros((planes, piece, ff_block), bf16)
        for t in range(planes):
            gate_up_part = lax.dynamic_update_index_in_dim(
                gate_up_part, gate_up_sent[t], (p - t) % planes, 0
            )
        gate_up_full = lax.all_gather(
            gate_up_part, both, axis_index_groups=in_plane_dp, tiled=False
        )
        gate_up_full = gate_up_full.reshape(2, width, ff_block)
        grad_y_all = jnp.concatenate(gather_z(grad_y_low), axis=0)

        def by_seq(value, axis):
            shape = value.shape
            value = value.reshape(shape[:axis] + (GROUP, seqs, rows) + shape[axis + 1 :])
            value = jnp.moveaxis(value, axis + 1, 0)
            return value.reshape((seqs,) + shape[:axis] + (GROUP * rows,) + shape[axis + 1 :])

        def from_seq(value, axis):
            shape = value.shape[1:]
            value = value.reshape((seqs,) + shape[:axis] + (GROUP, rows) + shape[axis + 1 :])
            value = jnp.moveaxis(value, 0, axis + 1)
            return value.reshape(shape[:axis] + (GROUP * seqs * rows,) + shape[axis + 1 :])

        order = jnp.concatenate([(w ^ j) * rows + jnp.arange(rows) for j in range(GROUP)])
        order = order.astype(jnp.int32)
        seen = (p + 1).astype(jnp.int32).reshape(1)
        q_seq = by_seq(q, 0)
        kv_seq = by_seq(kv_all, 1)
        cos_seq = by_seq(cosine, 0)
        sin_seq = by_seq(sine, 0)
        pieces = [attend(seen, q_seq[i], kv_seq[i], order) for i in range(seqs)]
        o_seq = [one[0] for one in pieces]
        lse_seq = [one[1] for one in pieces]
        o = from_seq(jnp.stack(o_seq), 0)

        branch = jnp.concatenate([dot(o, out_full[i]).astype(bf16) for i in range(n_dp)], axis=1)
        branch = scatter_w([branch[j * tokens : (j + 1) * tokens] for j in range(GROUP)])
        x_mid = x_in + branch

        normed_two, inverse_two = normalize(x_mid)
        low_two = reorder(normed_two.astype(bf16))
        low_two, grad_y_all = tie(low_two, grad_y_all)
        low_two_own, *low_two_sent = gather_z(low_two)
        grad_hidden = functools.reduce(
            jnp.add,
            [
                dot(pick(grad_y_all, i, n_dp, 1), down_full[i], ((1,), (1,)))
                for i in range(n_dp)
            ],
        )
        *low_two_sent, grad_hidden = tie(*low_two_sent, grad_hidden)
        low_two = jnp.concatenate([low_two_own] + low_two_sent, axis=0)
        hidden, grad_gate, grad_up, grad_low_two = feed(low_two, gate_up_full, grad_hidden)
        hidden_later, grad_gate_later, grad_up_later, grad_low_two = tie(
            hidden, grad_gate, grad_up, grad_low_two
        )
        inner_sent = [
            shift_z(grad_low_two[t * tokens : (t + 1) * tokens], -t) for t in range(1, planes)
        ]

        hidden_all = gather_dp(hidden_later)
        down_sum = dot(hidden_all, exchange_dp(grad_y_all, c, 1), ((0,), (0,))).astype(bf16)

        low_two_all = gather_dp(low_two)
        if halves > 1:
            low_two_all = pick(low_two_all, c % halves, halves, 1)

        def of_member(member):
            return jnp.where(member // halves == 0, grad_gate_later, grad_up_later)

        gate_up_grads = [of_member(c)]
        for t in range(1, n_dp):
            gate_up_grads.append(shift_dp(of_member((c + t) % n_dp), t))
        gate_up_grads = jnp.concatenate(gate_up_grads, axis=0)
        gate_up_sum = dot(low_two_all, gate_up_grads, ((0,), (0,))).astype(bf16)

        inner_sent[0], gate_up_sum = tie(inner_sent[0], gate_up_sum)
        *inner_rest, down_sum = tie(*inner_sent[1:], down_sum)
        inner_sent = [inner_sent[0]] + inner_rest
        mixed = jnp.concatenate(
            [dot(hidden_later, down_full[i]).astype(bf16) for i in range(n_dp)], axis=1
        )
        *inner_sent, mixed = tie(*inner_sent, mixed)
        inner_two = functools.reduce(
            jnp.add, [g.astype(f32) for g in inner_sent], grad_low_two[:tokens].astype(f32)
        )
        grad_x_mid = grad_y + norm_back(order_back(inner_two), normed_two, inverse_two)

        mixed, grad_x_low = tie(mixed, grad_x_mid.astype(bf16))
        mixed_sent = [shift_z(mixed[t * tokens : (t + 1) * tokens], -t) for t in range(1, planes)]
        gate_up_sum = lax.psum_scatter(gate_up_sum, "seq", axis_index_groups=in_plane, tiled=True)
        down_sum = lax.psum_scatter(
            down_sum, "seq", axis_index_groups=in_plane, tiled=True
        )
        gate_up_sum = gate_up_sum.reshape(planes, piece, ff_block)

        grad_branch = gather_w(grad_x_low)
        early = planes - 2
        *mixed_sent[:early], grad_branch = tie(*mixed_sent[:early], grad_branch)
        grad_o = functools.reduce(
            jnp.add,
            [dot(pick(grad_branch, i, n_dp, 1), out_full[i], ((1,), (1,))) for i in range(n_dp)],
        ).astype(bf16)

        out_part_sum = dot(gather_dp(o), exchange_dp(grad_branch, c, 1), ((0,), (0,))).astype(bf16)
        grad_o_seq = by_seq(grad_o, 0)
        *late, grad_o_seq, out_part_sum = tie(*mixed_sent[early:], grad_o_seq, out_part_sum)
        mixed_sent = mixed_sent[:early] + list(late)
        gate_up_sum, out_part_sum = tie(gate_up_sum, out_part_sum)
        out_sum = lax.psum_scatter(out_part_sum, "seq", axis_index_groups=across, tiled=True)
        grad_o_seq, gate_up_late = tie(grad_o_seq, gate_up_sum)
        gate_up_sent = []
        for t in range(planes):
            block = lax.dynamic_index_in_dim(gate_up_late, (p + t) % planes, 0, keepdims=False)
            gate_up_sent.append(shift_z(block, t) if t else block)
        pieces = [
            attend_back(
                seen, q_seq[i], grad_o_seq[i], o_seq[i], kv_seq[i], lse_seq[i], order,
                cos_seq[i], sin_seq[i],
            )
            for i in range(seqs)
        ]
        grad_q = jnp.stack([one[0] for one in pieces])
        mixed = functools.reduce(
            jnp.add, [g.astype(f32) for g in mixed_sent], mixed[:tokens].astype(f32)
        )
        query_pre = from_seq(grad_q, 0)
        grad_kv = from_seq(jnp.stack([one[1] for one in pieces]), 1)
        *gate_up_sent, grad_kv = tie(*gate_up_sent, grad_kv)
        grad_kv = scatter_z([grad_kv[t] for t in range(planes)])
        query_pre, out_sum = tie(query_pre, out_sum)
        key_pre = unrotate_keys(
            grad_kv[:, :HEAD_DIM], cosine[:, :HEAD_DIM], sine[:, :HEAD_DIM]
        )
        kv_pre = jnp.concatenate([key_pre, grad_kv[:, HEAD_DIM:]], axis=1).astype(bf16)
        pre = [
            jnp.concatenate(
                [query_pre[:, i * cut : (i + 1) * cut], pick(kv_pre, i, n_dp, 1)], axis=1
            )
            for i in range(n_dp)
        ]
        outputs = (x_mid + mixed).astype(bf16).reshape(seqs, rows, width)

        grad_low_one = dot(
            jnp.concatenate([query_pre, kv_pre], axis=1), qkv_weights, ((1,), (1,))
        ).astype(bf16)
        inner_one = scatter_w([grad_low_one[j * tokens : (j + 1) * tokens] for j in range(GROUP)])
        grad_inputs = grad_x_mid + norm_back(inner_one, normed_one, inverse_one)
        grad_inputs = grad_inputs.reshape(seqs, rows, width)

        qkv_sum = dot(
            gather_dp(low_one),
            exchange_dp(jnp.concatenate(pre, axis=1), c, 1),
            ((0,), (0,)),
        ).astype(bf16)
        down_sum, qkv_sum = tie(down_sum, qkv_sum)
        out_sum = lax.ppermute(
            out_sum, "seq", [(GROUP * (i % planes) + i // planes, i) for i in range(n_seq)]
        )
        grad_w_out = jnp.concatenate(collect_dp(out_sum, c), axis=1).astype(f32)

        qkv_sum = lax.psum_scatter(
            qkv_sum, "seq", axis_index_groups=across, tiled=True
        )
        grad_w_down = jnp.concatenate(collect_dp(down_sum, c), axis=1).astype(f32)
        gate_up_rows = jnp.zeros((planes, piece, ff_block), bf16)
        for t in range(planes):
            gate_up_rows = lax.dynamic_update_index_in_dim(
                gate_up_rows, gate_up_sent[t], (p - t) % planes, 0
            )
        gate_up_rows = collect_dp(gate_up_rows, c)

        def rows_of(members):
            wide = [jnp.concatenate([one[i] for i in range(planes)], axis=1) for one in members]
            return jnp.concatenate(wide, axis=0).astype(f32)

        gate_rows = rows_of(gate_up_rows[:halves])
        up_rows = rows_of(gate_up_rows[halves:])
        grad_w_gate = gate_rows * gain_two
        grad_w_up = up_rows * gain_two
        grad_gain_mlp = jnp.sum(
            gate_rows * w_gate.astype(f32) + up_rows * w_up.astype(f32), axis=1
        )
        qkv_sum, grad_w_gate, grad_w_up, grad_w_down, grad_gain_mlp = tie(
            qkv_sum, grad_w_gate, grad_w_up, grad_w_down, grad_gain_mlp
        )
        qkv_sum = qkv_sum.reshape(GROUP, shard, part_width)
        qkv_sum = lax.all_to_all(qkv_sum, "seq", 0, 0, axis_index_groups=in_plane, tiled=True)
        qkv_sum = collect_dp(qkv_sum, c)
        q_sum = jnp.concatenate(
            [one[j][:, :cut] for j in range(GROUP) for one in qkv_sum], axis=1
        ).astype(f32)
        kv_sum = jnp.concatenate(
            [one[j][:, cut:] for j in range(GROUP) for one in qkv_sum], axis=1
        ).astype(f32).reshape(shard, GROUP, PAIR)
        k_sum = kv_sum[..., :HEAD_DIM].reshape(shard, GROUP * HEAD_DIM)
        v_sum = kv_sum[..., HEAD_DIM:].reshape(shard, GROUP * HEAD_DIM)

        grad_gain_attn = (
            jnp.sum(q_sum * w_query.astype(f32), axis=1)
            + jnp.sum(k_sum * w_key.astype(f32), axis=1)
            + jnp.sum(v_sum * w_value.astype(f32), axis=1)
        )

        return (
            outputs,
            grad_inputs,
            grad_gain_attn,
            q_sum * gain_one,
            k_sum * gain_one,
            v_sum * gain_one,
            grad_w_out,
            grad_gain_mlp,
            grad_w_gate,
            grad_w_up,
            grad_w_down,
        )

    tokens_spec = P("dp", "seq", None)
    in_specs = (
        tokens_spec,
        P("dp", "seq"),
        P("dp", "seq"),
        tokens_spec,
        P("seq"),
        P("seq", None),
        P("seq", None),
        P("seq", None),
        P("seq", None),
        P("seq"),
        P("seq", None),
        P("seq", None),
        P("seq", None),
    )
    out_specs = (
        tokens_spec,
        tokens_spec,
        P("seq"),
        P("seq", None),
        P("seq", None),
        P("seq", None),
        P("seq", None),
        P("seq"),
        P("seq", None),
        P("seq", None),
        P("seq", None),
    )
    return jax.shard_map(body, mesh=mesh, in_specs=in_specs, out_specs=out_specs, check_vma=False)
```

```python
import functools

import jax
import jax.numpy as jnp
from jax import lax
from jax.experimental import pallas as pl
from jax.experimental.pallas import tpu as pltpu
from jax.sharding import PartitionSpec as P

HEADS = 32
KV_HEADS = 4
HEAD_DIM = 64
GROUP = KV_HEADS
GROUP_HEADS = HEADS // GROUP
PAIR = 2 * HEAD_DIM

epsilon = 1e-05
rope_base = 10000.0
masked_score = -1e30

f32 = jnp.float32
bf16 = jnp.bfloat16


def dot(left, right, contract=((1,), (0,))):
    return lax.dot_general(left, right, (contract, ((), ())), preferred_element_type=f32)


def stack_heads(block, rows):
    lane = lax.broadcasted_iota(jnp.int32, (rows, PAIR), 1)
    parts = []
    for pair in range(GROUP_HEADS // 2):
        both = block[:, pair * PAIR : (pair + 1) * PAIR]
        parts.append(jnp.where(lane < HEAD_DIM, both, jnp.zeros_like(both)))
        parts.append(jnp.where(lane >= HEAD_DIM, both, jnp.zeros_like(both)))
    return jnp.concatenate(parts, axis=0)


def unstack_heads(stacked, rows):
    lane = lax.broadcasted_iota(jnp.int32, (rows, PAIR), 1)
    parts = []
    for pair in range(GROUP_HEADS // 2):
        low = stacked[2 * pair * rows : (2 * pair + 1) * rows]
        high = stacked[(2 * pair + 1) * rows : (2 * pair + 2) * rows]
        parts.append(jnp.where(lane < HEAD_DIM, low, high))
    return jnp.concatenate(parts, axis=1)


def as_row(column):
    wide = jnp.broadcast_to(column, (column.shape[0], 128))
    return jnp.transpose(wide)[:8]


def turn(values):
    width = values.shape[1]
    half_dim = HEAD_DIM // 2
    lane = lax.broadcasted_iota(jnp.int32, values.shape, 1)
    ahead = pltpu.roll(values, width - half_dim, 1)
    behind = pltpu.roll(values, half_dim, 1)
    return jnp.where(lane % HEAD_DIM < half_dim, -ahead, behind)


def rotate(values, cosine, sine):
    return values * cosine + turn(values) * sine


def unrotate(grads, cosine, sine):
    return grads * cosine - turn(grads * sine)


def project_kernel(low_ref, w_ref, cos_ref, sin_ref, q_ref, kv_ref):
    made = dot(low_ref[...], w_ref[...])
    cosine, sine = cos_ref[...], sin_ref[...]
    for i in range(q_ref.shape[1] // PAIR):
        q = rotate(made[:, i * PAIR : (i + 1) * PAIR], cosine, sine).astype(bf16)
        q_ref[:, i * PAIR : (i + 1) * PAIR] = (q.astype(f32) * HEAD_DIM ** (-0.5)).astype(bf16)
    kv = made[:, q_ref.shape[1] :]
    lane = lax.broadcasted_iota(jnp.int32, kv.shape, 1)
    kv_ref[...] = jnp.where(lane < HEAD_DIM, rotate(kv, cosine, sine), kv).astype(bf16)


def project(low, weights, cosine, sine):
    tokens, width = low.shape
    q_width = weights.shape[1] - PAIR
    rows = min(256, tokens)
    return pl.pallas_call(
        project_kernel,
        out_shape=(
            jax.ShapeDtypeStruct((tokens, q_width), bf16),
            jax.ShapeDtypeStruct((tokens, PAIR), bf16),
        ),
        grid=(tokens // rows,),
        in_specs=[
            pl.BlockSpec((rows, width), lambda i: (i, 0)),
            pl.BlockSpec(weights.shape, lambda i: (0, 0)),
            pl.BlockSpec((rows, PAIR), lambda i: (i, 0)),
            pl.BlockSpec((rows, PAIR), lambda i: (i, 0)),
        ],
        out_specs=[
            pl.BlockSpec((rows, q_width), lambda i: (i, 0)),
            pl.BlockSpec((rows, PAIR), lambda i: (i, 0)),
        ],
        name="project",
    )(low, weights, cosine, sine)


def feed_kernel(low_ref, w_ref, grad_hidden_ref, hidden_ref, grad_gate_ref, grad_up_ref, back_ref):
    low = low_ref[...]
    gate = dot(low, w_ref[0])
    up = dot(low, w_ref[1])
    grad_hidden = grad_hidden_ref[...]
    sigmoid_gate = 1.0 / (1.0 + jnp.exp(-gate))
    silu = gate * sigmoid_gate
    hidden_ref[...] = (silu * up).astype(bf16)
    grad_gate = (
        grad_hidden * up * sigmoid_gate * (1.0 + gate * (1.0 - sigmoid_gate))
    ).astype(bf16)
    grad_up = (grad_hidden * silu).astype(bf16)
    grad_gate_ref[...] = grad_gate
    grad_up_ref[...] = grad_up
    back_ref[...] = (
        dot(grad_gate, w_ref[0], ((1,), (1,))) + dot(grad_up, w_ref[1], ((1,), (1,)))
    ).astype(bf16)


def feed(low, weights, grad_hidden):
    tokens, width = low.shape
    block = weights.shape[2]
    rows = min(256, tokens)
    narrow = pl.BlockSpec((rows, block), lambda i: (i, 0))
    wide = pl.BlockSpec((rows, width), lambda i: (i, 0))
    return pl.pallas_call(
        feed_kernel,
        out_shape=(
            jax.ShapeDtypeStruct((tokens, block), bf16),
            jax.ShapeDtypeStruct((tokens, block), bf16),
            jax.ShapeDtypeStruct((tokens, block), bf16),
            jax.ShapeDtypeStruct((tokens, width), bf16),
        ),
        grid=(tokens // rows,),
        in_specs=[wide, pl.BlockSpec(weights.shape, lambda i: (0, 0, 0)), narrow],
        out_specs=[narrow, narrow, narrow, wide],
        name="feed",
    )(low, weights, grad_hidden)


def both_lanes(kv_ref, kk_ref, vv_ref):
    @pl.when(pl.program_id(0) == 0)
    def _():
        for index in range(kv_ref.shape[0]):
            kv = kv_ref[index].astype(f32)
            swapped = pltpu.roll(kv, HEAD_DIM, 1)
            lane = lax.broadcasted_iota(jnp.int32, kv.shape, 1)
            kk_ref[index] = jnp.where(lane < HEAD_DIM, kv, swapped).astype(bf16)
            vv_ref[index] = jnp.where(lane < HEAD_DIM, swapped, kv).astype(bf16)


def attend_kernel(seen_ref, q_ref, kv_ref, qpos_ref, kpos_ref, o_ref, lse_ref, kk_ref, vv_ref):
    rows = q_ref.shape[0]
    both_lanes(kv_ref, kk_ref, vv_ref)
    stacked = stack_heads(q_ref[...], rows)
    qpos = jnp.concatenate([qpos_ref[...]] * GROUP_HEADS, axis=0)

    def unit(index, carry, masked):
        top, total, acc = carry
        scores = dot(stacked, kk_ref[index], ((1,), (1,)))
        if masked:
            scores = jnp.where(kpos_ref[...] <= qpos, scores, masked_score)
        new_top = jnp.maximum(top, jnp.max(scores, axis=1, keepdims=True))
        weights = jnp.exp(scores - new_top)
        keep = jnp.exp(top - new_top)
        total = total * keep + jnp.sum(weights, axis=1, keepdims=True)
        acc = acc * keep + dot(weights.astype(bf16), vv_ref[index])
        return new_top, total, acc

    count = GROUP_HEADS * rows
    start = (
        jnp.full((count, 1), masked_score, f32),
        jnp.zeros((count, 1), f32),
        jnp.zeros((count, PAIR), f32),
    )
    carry = unit(0, start, True)
    top, total, acc = lax.fori_loop(1, seen_ref[0], lambda i, c: unit(i, c, False), carry)
    o_ref[...] = unstack_heads(acc / total, rows).astype(bf16)
    lse_ref[...] = as_row(top + jnp.log(total))


def attend_back_kernel(
    seen_ref, q_ref, do_ref, o_ref, kv_ref, lse_ref, qpos_ref, kpos_ref, cos_ref, sin_ref,
    dq_ref, dkv_ref, qs_ref, dos_ref, delta_ref, dqs_ref, kk_ref, vv_ref, dkk_ref, dvv_ref,
):
    rows = q_ref.shape[0]
    both_lanes(kv_ref, kk_ref, vv_ref)

    @pl.when(pl.program_id(0) == 0)
    def _():
        dkk_ref[...] = jnp.zeros_like(dkk_ref)
        dvv_ref[...] = jnp.zeros_like(dvv_ref)

    qs_ref[...] = stack_heads(q_ref[...], rows)
    grads = stack_heads(do_ref[...], rows)
    dos_ref[...] = grads
    outs = stack_heads(o_ref[...], rows)
    delta_ref[...] = as_row(jnp.sum(grads.astype(f32) * outs.astype(f32), axis=1, keepdims=True))

    def unit(index, masked):
        keys = kk_ref[index]
        scores = dot(keys, qs_ref[...], ((1,), (1,)))
        if masked:
            qpos = jnp.concatenate([qpos_ref[0:1, :]] * GROUP_HEADS, axis=1)
            scores = jnp.where(kpos_ref[...] <= qpos, scores, masked_score)
        probs = jnp.exp(scores - lse_ref[0:1, :])
        prob_grad = dot(vv_ref[index], dos_ref[...], ((1,), (1,)))
        score_grad = (probs * (prob_grad - delta_ref[0:1, :])).astype(bf16)
        dvv_ref[index] += dot(probs.astype(bf16), dos_ref[...])
        dkk_ref[index] += dot(score_grad, qs_ref[...])
        return dot(score_grad, keys, ((0,), (0,)))

    dqs_ref[...] = unit(0, True)

    @pl.loop(1, seen_ref[0])
    def _(index):
        dqs_ref[...] += unit(index, False)

    grads = unstack_heads(dqs_ref[...], rows) * HEAD_DIM ** (-0.5)
    cosine, sine = cos_ref[...], sin_ref[...]
    for i in range(dq_ref.shape[1] // PAIR):
        part = unrotate(grads[:, i * PAIR : (i + 1) * PAIR], cosine, sine)
        dq_ref[:, i * PAIR : (i + 1) * PAIR] = part.astype(bf16)

    @pl.when(pl.program_id(0) == pl.num_programs(0) - 1)
    def _():
        for index in range(kv_ref.shape[0]):
            keys, values = dkk_ref[index], dvv_ref[index]
            keys = keys + pltpu.roll(keys, HEAD_DIM, 1)
            values = values + pltpu.roll(values, HEAD_DIM, 1)
            lane = lax.broadcasted_iota(jnp.int32, keys.shape, 1)
            dkv_ref[index] = jnp.where(lane < HEAD_DIM, keys, values).astype(bf16)


def block_rows(length):
    return min(128, length)


def whole(shape):
    zeros = (0,) * len(shape)
    return pl.BlockSpec(shape, lambda i, seen: zeros)


def attend(seen, q, kv, order):
    length, width = q.shape
    rows = block_rows(length)
    stacked = GROUP_HEADS * rows
    steps = length // rows
    return pl.pallas_call(
        attend_kernel,
        out_shape=(
            jax.ShapeDtypeStruct((length, width), bf16),
            jax.ShapeDtypeStruct((steps, 8, stacked), f32),
        ),
        grid_spec=pltpu.PrefetchScalarGridSpec(
            num_scalar_prefetch=1,
            grid=(steps,),
            in_specs=[
                pl.BlockSpec((rows, width), lambda i, seen: (i, 0)),
                whole(kv.shape),
                pl.BlockSpec((rows, 1), lambda i, seen: (i, 0)),
                whole((1, length)),
            ],
            out_specs=[
                pl.BlockSpec((rows, width), lambda i, seen: (i, 0)),
                pl.BlockSpec((pl.Squeezed(), 8, stacked), lambda i, seen: (i, 0, 0)),
            ],
            scratch_shapes=[pltpu.VMEM(kv.shape, bf16), pltpu.VMEM(kv.shape, bf16)],
        ),
        name="attend",
    )(seen, q, kv, order[:, None], order[None, :])


def attend_back(seen, q, do, o, kv, lse, order, cosine, sine):
    length, width = q.shape
    rows = block_rows(length)
    stacked = GROUP_HEADS * rows
    steps = length // rows
    return pl.pallas_call(
        attend_back_kernel,
        out_shape=(
            jax.ShapeDtypeStruct((length, width), bf16),
            jax.ShapeDtypeStruct(kv.shape, bf16),
        ),
        grid_spec=pltpu.PrefetchScalarGridSpec(
            num_scalar_prefetch=1,
            grid=(steps,),
            in_specs=[
                pl.BlockSpec((rows, width), lambda i, seen: (i, 0)),
                pl.BlockSpec((rows, width), lambda i, seen: (i, 0)),
                pl.BlockSpec((rows, width), lambda i, seen: (i, 0)),
                whole(kv.shape),
                pl.BlockSpec((pl.Squeezed(), 8, stacked), lambda i, seen: (i, 0, 0)),
                pl.BlockSpec((8, rows), lambda i, seen: (0, i)),
                whole((length, 1)),
                pl.BlockSpec((rows, PAIR), lambda i, seen: (i, 0)),
                pl.BlockSpec((rows, PAIR), lambda i, seen: (i, 0)),
            ],
            out_specs=[
                pl.BlockSpec((rows, width), lambda i, seen: (i, 0)),
                whole(kv.shape),
            ],
            scratch_shapes=[
                pltpu.VMEM((stacked, PAIR), bf16),
                pltpu.VMEM((stacked, PAIR), bf16),
                pltpu.VMEM((8, stacked), f32),
                pltpu.VMEM((stacked, PAIR), f32),
                pltpu.VMEM(kv.shape, bf16),
                pltpu.VMEM(kv.shape, bf16),
                pltpu.VMEM(kv.shape, f32),
                pltpu.VMEM(kv.shape, f32),
            ],
        ),
        name="attend_back",
    )(
        seen, q, do, o, kv, lse, jnp.broadcast_to(order[None, :], (8, length)), order[:, None],
        cosine, sine,
    )


def normalize(values):
    inverse = lax.rsqrt(jnp.mean(values * values, axis=-1, keepdims=True) + epsilon)
    return values * inverse, inverse


def norm_back(inner, normed, inverse):
    return inverse * (inner - normed * jnp.mean(inner * normed, axis=-1, keepdims=True))


def rope_tables(positions):
    half_dim = HEAD_DIM // 2
    frequency = rope_base ** (-(jnp.arange(half_dim).astype(f32) * 2.0 / HEAD_DIM))
    angles = positions.astype(f32)[:, None] * frequency
    times = PAIR // half_dim
    return jnp.tile(jnp.cos(angles), (1, times)), jnp.tile(jnp.sin(angles), (1, times))


def unrotate_keys(grads, cosine, sine):
    half_dim = HEAD_DIM // 2
    sines = grads * sine
    turned = jnp.concatenate([-sines[:, half_dim:], sines[:, :half_dim]], axis=1)
    return grads * cosine - turned


def tie(*values):
    return lax.optimization_barrier(values)


def solution(mesh):
    n_dp = mesh.shape["dp"]
    n_seq = mesh.shape["seq"]
    planes = n_seq // GROUP
    halves = n_dp // 2
    both = ("dp", "seq")

    in_plane = [[GROUP * p + w for w in range(GROUP)] for p in range(planes)]
    across_dp = [
        [c * n_seq + GROUP * p + w for c in range(n_dp) for p in range(planes)] for w in range(GROUP)
    ]
    in_plane_dp = [
        [c * n_seq + GROUP * p + w for c in range(n_dp) for w in range(GROUP)] for p in range(planes)
    ]
    across = [[GROUP * p + w for p in range(planes)] for w in range(GROUP)]

    def xor_w(value, j):
        return lax.ppermute(value, "seq", [(s, s ^ j) for s in range(n_seq)])

    def shift_z(value, t):
        return lax.ppermute(value, "seq", [(s, (s + GROUP * t) % n_seq) for s in range(n_seq)])

    def shift_dp(value, t):
        return lax.ppermute(value, "dp", [(c, (c + t) % n_dp) for c in range(n_dp)])

    def gather_w(value):
        first = xor_w(value, 1)
        second = xor_w(value, 2)
        half = value.shape[0] // 2
        third = jnp.concatenate([xor_w(first[:half], 2), xor_w(second[half:], 1)], axis=0)
        return jnp.concatenate([value, first, second, third], axis=0)

    def scatter_w(slots):
        got = [xor_w(slots[j], j) for j in range(1, GROUP)]
        return functools.reduce(jnp.add, [g.astype(f32) for g in got], slots[0].astype(f32))

    def gather_z(value):
        return [value] + [shift_z(value, t) for t in range(1, planes)]

    def scatter_z(slots):
        got = [shift_z(slots[t], -t) for t in range(1, planes)]
        return functools.reduce(jnp.add, [g.astype(f32) for g in got], slots[0].astype(f32))

    def gather_dp(value):
        return jnp.concatenate([value] + [shift_dp(value, t) for t in range(1, n_dp)], axis=0)

    def pick(value, index, count, axis):
        size = value.shape[axis] // count
        return lax.dynamic_slice_in_dim(value, index * size, size, axis)

    def exchange_dp(value, c, axis):
        parts = [pick(value, c, n_dp, axis)]
        for t in range(1, n_dp):
            parts.append(shift_dp(pick(value, (c + t) % n_dp, n_dp, axis), t))
        return jnp.concatenate(parts, axis=0)

    def collect_dp(value, c):
        slots = [value] + [shift_dp(value, t) for t in range(1, n_dp)]
        out = []
        for member in range(n_dp):
            chosen = slots[0]
            for t in range(1, n_dp):
                chosen = jnp.where((c - t) % n_dp == member, slots[t], chosen)
            out.append(chosen)
        return out

    def body(
        inputs, positions, select, cotangent, gain_attn, w_query, w_key, w_value, w_out, gain_mlp,
        w_gate, w_up, w_down,
    ):
        seqs, rows, width = inputs.shape
        tokens = seqs * rows
        shard = w_query.shape[0]
        ff_rows = w_down.shape[0]
        ff_block = w_gate.shape[1] // planes
        q_width = GROUP_HEADS * HEAD_DIM
        s = lax.axis_index("seq")
        c = lax.axis_index("dp")
        p = s // GROUP
        w = s % GROUP

        gain_one = gain_attn.astype(f32)[:, None]
        gain_two = gain_mlp.astype(f32)[:, None]

        def scaled(weight, gain):
            return (weight.astype(f32) * gain).astype(bf16)

        q_cols = scaled(w_query, gain_one).reshape(shard, GROUP, n_dp, q_width // n_dp)
        kv_cols = jnp.concatenate(
            [
                scaled(w_key, gain_one).reshape(shard, GROUP, HEAD_DIM),
                scaled(w_value, gain_one).reshape(shard, GROUP, HEAD_DIM),
            ],
            axis=-1,
        ).reshape(shard, GROUP, n_dp, PAIR // n_dp)
        qkv_cols = jnp.concatenate([q_cols, kv_cols], axis=-1)
        qkv_part = lax.dynamic_index_in_dim(qkv_cols, c, 2, keepdims=False)
        qkv_part = lax.all_to_all(
            jnp.transpose(qkv_part, (1, 0, 2)), "seq", 0, 0, axis_index_groups=in_plane, tiled=True
        )
        part_width = (q_width + PAIR) // n_dp
        qkv_part = qkv_part.reshape(GROUP * shard, part_width)
        own_pos = positions.reshape(1, tokens)
        plane_pos = jnp.concatenate([own_pos] + [xor_w(own_pos, j) for j in range(1, GROUP)], axis=1)
        x_in = inputs.reshape(tokens, width).astype(f32)
        normed_one, inverse_one = normalize(x_in)
        low_one, qkv_part, plane_pos = tie(normed_one.astype(bf16), qkv_part, plane_pos)

        ring = [qkv_part] + [shift_z(qkv_part, -t) for t in range(1, planes)]
        qkv_ring = jnp.concatenate(ring + ring[: planes - 1], axis=0)
        qkv_mine = lax.dynamic_slice_in_dim(
            qkv_ring, ((planes - p) % planes) * GROUP * shard, width, 0
        )
        low_one = gather_w(low_one)

        piece = shard // halves
        gate_up = jnp.where(c // halves == 0, scaled(w_gate, gain_two), scaled(w_up, gain_two))
        out_part, gate_up, qkv_mine = tie(
            pick(w_out, c, n_dp, 1), pick(gate_up, c % halves, halves, 0), qkv_mine
        )
        qkv_full = collect_dp(qkv_mine, c)
        out_part = lax.ppermute(
            out_part, "seq", [(i, GROUP * (i % planes) + i // planes) for i in range(n_seq)]
        )
        gate_up_sent = [
            shift_z(pick(gate_up, (p + t) % planes, planes, 1), t) if t
            else pick(gate_up, p, planes, 1)
            for t in range(planes)
        ]
        down_full = lax.all_gather(
            pick(w_down, c, n_dp, 1), both, axis_index_groups=in_plane_dp, tiled=False
        )
        out_part, down_full = tie(out_part, down_full)
        down_full = down_full.reshape(n_dp, ff_block, width // n_dp)
        out_full = lax.all_gather(out_part, both, axis_index_groups=across_dp, tiled=False)
        out_full = out_full.reshape(n_dp, planes * shard, width // n_dp)

        blocks = [
            (i * GROUP + j) * halves + h
            for h in range(halves) for j in range(GROUP) for i in range(planes)
        ]

        def column_blocks(value, which):
            return jnp.concatenate([value[:, i * piece : (i + 1) * piece] for i in which], axis=1)

        def reorder(value):
            return column_blocks(value, blocks)

        def order_back(value):
            return column_blocks(value, [blocks.index(i) for i in range(len(blocks))])

        cosine, sine = rope_tables(plane_pos.reshape(GROUP * tokens))

        grad_y = (
            cotangent.astype(f32) * select.astype(f32)[..., None]
        ).reshape(tokens, width)
        cut = q_width // n_dp
        plane_tokens = GROUP * tokens
        qkv_weights = jnp.concatenate(
            [one[:, :cut] for one in qkv_full] + [one[:, cut:] for one in qkv_full], axis=1
        )
        q, kv_low = project(low_one, qkv_weights, cosine, sine)
        kv_all = jnp.stack(gather_z(kv_low))
        grad_y_low, kv_all = tie(grad_y.astype(bf16), kv_all)
        *gate_up_sent, q = tie(*gate_up_sent, q)
        gate_up_part = jnp.zeros((planes, piece, ff_block), bf16)
        for t in range(planes):
            gate_up_part = lax.dynamic_update_index_in_dim(
                gate_up_part, gate_up_sent[t], (p - t) % planes, 0
            )
        gate_up_full = lax.all_gather(
            gate_up_part, both, axis_index_groups=in_plane_dp, tiled=False
        )
        gate_up_full = gate_up_full.reshape(2, width, ff_block)
        grad_y_all = jnp.concatenate(gather_z(grad_y_low), axis=0)

        def by_seq(value, axis):
            shape = value.shape
            value = value.reshape(shape[:axis] + (GROUP, seqs, rows) + shape[axis + 1 :])
            value = jnp.moveaxis(value, axis + 1, 0)
            return value.reshape((seqs,) + shape[:axis] + (GROUP * rows,) + shape[axis + 1 :])

        def from_seq(value, axis):
            shape = value.shape[1:]
            value = value.reshape((seqs,) + shape[:axis] + (GROUP, rows) + shape[axis + 1 :])
            value = jnp.moveaxis(value, 0, axis + 1)
            return value.reshape(shape[:axis] + (GROUP * seqs * rows,) + shape[axis + 1 :])

        order = jnp.concatenate([(w ^ j) * rows + jnp.arange(rows) for j in range(GROUP)])
        order = order.astype(jnp.int32)
        seen = (p + 1).astype(jnp.int32).reshape(1)
        q_seq = by_seq(q, 0)
        kv_seq = by_seq(kv_all, 1)
        cos_seq = by_seq(cosine, 0)
        sin_seq = by_seq(sine, 0)
        pieces = [attend(seen, q_seq[i], kv_seq[i], order) for i in range(seqs)]
        o_seq = [one[0] for one in pieces]
        lse_seq = [one[1] for one in pieces]
        o = from_seq(jnp.stack(o_seq), 0)

        branch = jnp.concatenate([dot(o, out_full[i]).astype(bf16) for i in range(n_dp)], axis=1)
        branch = scatter_w([branch[j * tokens : (j + 1) * tokens] for j in range(GROUP)])
        x_mid = x_in + branch

        normed_two, inverse_two = normalize(x_mid)
        low_two = reorder(normed_two.astype(bf16))
        low_two, grad_y_all = tie(low_two, grad_y_all)
        low_two_own, *low_two_sent = gather_z(low_two)
        grad_hidden = functools.reduce(
            jnp.add,
            [
                dot(pick(grad_y_all, i, n_dp, 1), down_full[i], ((1,), (1,)))
                for i in range(n_dp)
            ],
        )
        *low_two_sent, grad_hidden = tie(*low_two_sent, grad_hidden)
        low_two = jnp.concatenate([low_two_own] + low_two_sent, axis=0)
        hidden, grad_gate, grad_up, grad_low_two = feed(low_two, gate_up_full, grad_hidden)
        hidden_later, grad_gate_later, grad_up_later, grad_low_two = tie(
            hidden, grad_gate, grad_up, grad_low_two
        )
        inner_sent = [
            shift_z(grad_low_two[t * tokens : (t + 1) * tokens], -t) for t in range(1, planes)
        ]

        hidden_all = gather_dp(hidden_later)
        down_sum = dot(hidden_all, exchange_dp(grad_y_all, c, 1), ((0,), (0,))).astype(bf16)

        low_two_all = gather_dp(low_two)
        if halves > 1:
            low_two_all = pick(low_two_all, c % halves, halves, 1)

        def of_member(member):
            return jnp.where(member // halves == 0, grad_gate_later, grad_up_later)

        gate_up_grads = [of_member(c)]
        for t in range(1, n_dp):
            gate_up_grads.append(shift_dp(of_member((c + t) % n_dp), t))
        gate_up_grads = jnp.concatenate(gate_up_grads, axis=0)
        gate_up_sum = dot(low_two_all, gate_up_grads, ((0,), (0,))).astype(bf16)

        inner_sent[0], gate_up_sum = tie(inner_sent[0], gate_up_sum)
        *inner_rest, down_sum = tie(*inner_sent[1:], down_sum)
        inner_sent = [inner_sent[0]] + inner_rest
        mixed = jnp.concatenate(
            [dot(hidden_later, down_full[i]).astype(bf16) for i in range(n_dp)], axis=1
        )
        *inner_sent, mixed = tie(*inner_sent, mixed)
        inner_two = functools.reduce(
            jnp.add, [g.astype(f32) for g in inner_sent], grad_low_two[:tokens].astype(f32)
        )
        grad_x_mid = grad_y + norm_back(order_back(inner_two), normed_two, inverse_two)

        mixed, grad_x_low = tie(mixed, grad_x_mid.astype(bf16))
        mixed_sent = [shift_z(mixed[t * tokens : (t + 1) * tokens], -t) for t in range(1, planes)]
        gate_up_sum = lax.psum_scatter(gate_up_sum, "seq", axis_index_groups=in_plane, tiled=True)
        down_sum = lax.psum_scatter(
            down_sum, "seq", axis_index_groups=in_plane, tiled=True
        )
        gate_up_sum = gate_up_sum.reshape(planes, piece, ff_block)

        grad_branch = gather_w(grad_x_low)
        early = planes - 2
        *mixed_sent[:early], grad_branch = tie(*mixed_sent[:early], grad_branch)
        grad_o = functools.reduce(
            jnp.add,
            [dot(pick(grad_branch, i, n_dp, 1), out_full[i], ((1,), (1,))) for i in range(n_dp)],
        ).astype(bf16)

        out_part_sum = dot(gather_dp(o), exchange_dp(grad_branch, c, 1), ((0,), (0,))).astype(bf16)
        grad_o_seq = by_seq(grad_o, 0)
        *late, grad_o_seq, out_part_sum = tie(*mixed_sent[early:], grad_o_seq, out_part_sum)
        mixed_sent = mixed_sent[:early] + list(late)
        gate_up_sum, down_sum, out_part_sum = tie(gate_up_sum, down_sum, out_part_sum)
        out_sum = lax.psum_scatter(out_part_sum, "seq", axis_index_groups=across, tiled=True)
        grad_o_seq, gate_up_late = tie(grad_o_seq, gate_up_sum)
        gate_up_sent = []
        for t in range(planes):
            block = lax.dynamic_index_in_dim(gate_up_late, (p + t) % planes, 0, keepdims=False)
            gate_up_sent.append(shift_z(block, t) if t else block)
        pieces = [
            attend_back(
                seen, q_seq[i], grad_o_seq[i], o_seq[i], kv_seq[i], lse_seq[i], order,
                cos_seq[i], sin_seq[i],
            )
            for i in range(seqs)
        ]
        grad_q = jnp.stack([one[0] for one in pieces])
        mixed = functools.reduce(
            jnp.add, [g.astype(f32) for g in mixed_sent], mixed[:tokens].astype(f32)
        )
        query_pre = from_seq(grad_q, 0)
        grad_kv = from_seq(jnp.stack([one[1] for one in pieces]), 1)
        *gate_up_sent, grad_kv = tie(*gate_up_sent, grad_kv)
        grad_kv = scatter_z([grad_kv[t] for t in range(planes)])
        query_pre, out_sum = tie(query_pre, out_sum)
        key_pre = unrotate_keys(
            grad_kv[:, :HEAD_DIM], cosine[:, :HEAD_DIM], sine[:, :HEAD_DIM]
        )
        kv_pre = jnp.concatenate([key_pre, grad_kv[:, HEAD_DIM:]], axis=1).astype(bf16)
        pre = [
            jnp.concatenate(
                [query_pre[:, i * cut : (i + 1) * cut], pick(kv_pre, i, n_dp, 1)], axis=1
            )
            for i in range(n_dp)
        ]
        outputs = (x_mid + mixed).astype(bf16).reshape(seqs, rows, width)

        grad_low_one = dot(
            jnp.concatenate([query_pre, kv_pre], axis=1), qkv_weights, ((1,), (1,))
        ).astype(bf16)
        inner_one = scatter_w([grad_low_one[j * tokens : (j + 1) * tokens] for j in range(GROUP)])
        grad_inputs = grad_x_mid + norm_back(inner_one, normed_one, inverse_one)
        grad_inputs = grad_inputs.reshape(seqs, rows, width)

        qkv_sum = dot(
            gather_dp(low_one),
            exchange_dp(jnp.concatenate(pre, axis=1), c, 1),
            ((0,), (0,)),
        ).astype(bf16)
        down_sum, qkv_sum = tie(down_sum, qkv_sum)
        out_sum = lax.ppermute(
            out_sum, "seq", [(GROUP * (i % planes) + i // planes, i) for i in range(n_seq)]
        )
        grad_w_out = jnp.concatenate(collect_dp(out_sum, c), axis=1).astype(f32)

        qkv_sum = lax.psum_scatter(
            qkv_sum, "seq", axis_index_groups=across, tiled=True
        )
        grad_w_down = jnp.concatenate(collect_dp(down_sum, c), axis=1).astype(f32)
        gate_up_rows = jnp.zeros((planes, piece, ff_block), bf16)
        for t in range(planes):
            gate_up_rows = lax.dynamic_update_index_in_dim(
                gate_up_rows, gate_up_sent[t], (p - t) % planes, 0
            )
        gate_up_rows = collect_dp(gate_up_rows, c)

        def rows_of(members):
            wide = [jnp.concatenate([one[i] for i in range(planes)], axis=1) for one in members]
            return jnp.concatenate(wide, axis=0).astype(f32)

        gate_rows = rows_of(gate_up_rows[:halves])
        up_rows = rows_of(gate_up_rows[halves:])
        grad_w_gate = gate_rows * gain_two
        grad_w_up = up_rows * gain_two
        grad_gain_mlp = jnp.sum(
            gate_rows * w_gate.astype(f32) + up_rows * w_up.astype(f32), axis=1
        )
        qkv_sum, grad_w_gate, grad_w_up, grad_w_down, grad_gain_mlp = tie(
            qkv_sum, grad_w_gate, grad_w_up, grad_w_down, grad_gain_mlp
        )
        qkv_sum = qkv_sum.reshape(GROUP, shard, part_width)
        qkv_sum = lax.all_to_all(qkv_sum, "seq", 0, 0, axis_index_groups=in_plane, tiled=True)
        qkv_sum = collect_dp(qkv_sum, c)
        q_sum = jnp.concatenate(
            [one[j][:, :cut] for j in range(GROUP) for one in qkv_sum], axis=1
        ).astype(f32)
        kv_sum = jnp.concatenate(
            [one[j][:, cut:] for j in range(GROUP) for one in qkv_sum], axis=1
        ).astype(f32).reshape(shard, GROUP, PAIR)
        k_sum = kv_sum[..., :HEAD_DIM].reshape(shard, GROUP * HEAD_DIM)
        v_sum = kv_sum[..., HEAD_DIM:].reshape(shard, GROUP * HEAD_DIM)

        grad_gain_attn = (
            jnp.sum(q_sum * w_query.astype(f32), axis=1)
            + jnp.sum(k_sum * w_key.astype(f32), axis=1)
            + jnp.sum(v_sum * w_value.astype(f32), axis=1)
        )

        return (
            outputs,
            grad_inputs,
            grad_gain_attn,
            q_sum * gain_one,
            k_sum * gain_one,
            v_sum * gain_one,
            grad_w_out,
            grad_gain_mlp,
            grad_w_gate,
            grad_w_up,
            grad_w_down,
        )

    tokens_spec = P("dp", "seq", None)
    in_specs = (
        tokens_spec,
        P("dp", "seq"),
        P("dp", "seq"),
        tokens_spec,
        P("seq"),
        P("seq", None),
        P("seq", None),
        P("seq", None),
        P("seq", None),
        P("seq"),
        P("seq", None),
        P("seq", None),
        P("seq", None),
    )
    out_specs = (
        tokens_spec,
        tokens_spec,
        P("seq"),
        P("seq", None),
        P("seq", None),
        P("seq", None),
        P("seq", None),
        P("seq"),
        P("seq", None),
        P("seq", None),
        P("seq", None),
    )
    return jax.shard_map(body, mesh=mesh, in_specs=in_specs, out_specs=out_specs, check_vma=False)
```
